32 devices in a mesh: ctx: 8 (over z, x), fsdp: 4 (over y, core).
Axes of the slice: x: 2, y: 2, z: 4, core: 2. Of those that a mesh axis runs over, the one named last changes fastest.
Arguments:
- inputs: bfloat16 [8, 1024, 768], P('fsdp', 'ctx'), may hold values from -6 to 6
- cotangent: bfloat16 [8, 1024, 768], P('fsdp', 'ctx'), may hold values from -6 to 6
- lengths: int32 [8], P('fsdp'), may hold values from 256 to 1024, as said below
- w_query: bfloat16 [768, 768], P('fsdp'), may hold values from -0.21875 to 0.21875
- b_query: bfloat16 [768], P('fsdp'), may hold values from -3 to 3
- w_key: bfloat16 [768, 768], P('fsdp'), may hold values from -0.21875 to 0.21875
- w_value: bfloat16 [768, 768], P('fsdp'), may hold values from -0.21875 to 0.21875
- b_value: bfloat16 [768], P('fsdp'), may hold values from -0.119628906 to 0.119628906
- w_output: bfloat16 [768, 768], P('fsdp'), may hold values from -3.5 to 3.5
- b_output: bfloat16 [768], P('fsdp'), may hold values from -2 to 2
- gain_one: bfloat16 [768], P('fsdp'), may hold values from 0.5 to 1.5
- bias_one: bfloat16 [768], P('fsdp'), may hold values from -1.1953125 to 1.1953125
- w_inner: bfloat16 [768, 3072], P('fsdp'), may hold values from -0.21875 to 0.21875
- b_inner: bfloat16 [3072], P('fsdp'), may hold values from -3 to 3
- w_outer: bfloat16 [3072, 768], P('fsdp'), may hold values from -0.109375 to 0.109375
- b_outer: bfloat16 [768], P('fsdp'), may hold values from -2 to 2
- gain_two: bfloat16 [768], P('fsdp'), may hold values from 0.5 to 1.5
- bias_two: bfloat16 [768], P('fsdp'), may hold values from -1.1953125 to 1.1953125
Outputs:
- outputs: bfloat16 [8, 1024, 768], P('fsdp', 'ctx')
- input_grad: float32 [8, 1024, 768], P('fsdp', 'ctx')
- grad_w_query: float32 [768, 768], P('fsdp')
- grad_b_query: float32 [768], P('fsdp')
- grad_w_key: float32 [768, 768], P('fsdp')
- grad_w_value: float32 [768, 768], P('fsdp')
- grad_b_value: float32 [768], P('fsdp')
- grad_w_output: float32 [768, 768], P('fsdp')
- grad_b_output: float32 [768], P('fsdp')
- grad_gain_one: float32 [768], P('fsdp')
- grad_bias_one: float32 [768], P('fsdp')
- grad_w_inner: float32 [768, 3072], P('fsdp')
- grad_b_inner: float32 [3072], P('fsdp')
- grad_w_outer: float32 [3072, 768], P('fsdp')
- grad_b_outer: float32 [768], P('fsdp')
- grad_gain_two: float32 [768], P('fsdp')
- grad_bias_two: float32 [768], P('fsdp')
The draws below stay inside these ranges and needn't reach their ends.
Inputs may be any that keep to these rules, and one draw needn't show every extreme that they name: Slot s has 1024 positions, of which the first lengths[s] are real tokens; in every draw some slot is full.
All inputs are finite; a program needn't handle non-finite values.
Results may differ from the reference program's by a relative error of at most 0.024.
Values may be sent and summed in bfloat16 or wider, within the bound.
No kernel may reach another device: no remote copies, remote signals or barrier semaphores. Data moves between devices by JAX's collectives and lax.ppermute only.
A program may use at most 192 MiB of HBM per device.

```python
import jax
import jax.numpy as jnp
from jax import lax

D = 768
H = 12
HD = 64
FF = 3072
SEQ_DEV = 128
SEQ_LEN = 1024
BATCH = 8
N_CTX = 8


def draw_lengths(key, part):
    ragged = jax.random.randint(jax.random.fold_in(key, 11), (BATCH,), SEQ_LEN // 4, SEQ_LEN + 1)
    full_slot = jax.random.randint(jax.random.fold_in(key, 12), (), 0, BATCH)
    return jnp.where(lax.iota(jnp.int32, BATCH) == full_slot, SEQ_LEN, ragged).astype(jnp.int32)


def levels(stream_key, dims, shards, smallest, top_value):
    def one(axis_at, shards_of):
        steps = jax.random.uniform(jax.random.fold_in(jax.random.fold_in(stream_key, 6), axis_at), (shards_of,), jnp.float32, smallest / len(shards), top_value / len(shards))
        return jnp.repeat(jnp.exp(steps), dims[axis_at] // shards_of).reshape((-1,) + (1,) * (len(dims) - axis_at - 1))

    gain = one(*shards[0])
    for cut in shards[1:]:
        gain = gain * one(*cut)
    return gain


def scatter_about(stream_key, dims, width, reach, split=(), kind=jnp.bfloat16):
    values = width * jax.random.normal(stream_key, dims, jnp.float32)
    if split:
        values = values * levels(stream_key, dims, split, -0.22, 0.18)
    return jnp.clip(values, -reach, reach).astype(kind)


def setup_inputs(seed: int = 0) -> dict:
    seeds = jax.random.split(jax.random.key(seed), 19)
    inputs = scatter_about(seeds[0], (BATCH, SEQ_LEN, D), 1.0, 6.0, ((0, 4), (1, 8)))
    cotangent = scatter_about(seeds[1], (BATCH, SEQ_LEN, D), 1.0, 6.0, ((0, 4), (1, 8)))
    lengths = draw_lengths(jax.random.fold_in(seeds[18], 71), 0)
    w_query = scatter_about(seeds[3], (D, D), D ** -0.5, 0.21875, ((0, 4),))
    b_query = scatter_about(seeds[4], (D,), 0.5, 3.0, ((0, 4),))
    w_key = scatter_about(seeds[5], (D, D), D ** -0.5, 0.21875, ((0, 4),))
    w_value = scatter_about(seeds[6], (D, D), D ** -0.5, 0.21875, ((0, 4),))
    b_value = scatter_about(seeds[7], (D,), 0.02, 0.119628906, ((0, 4),))
    w_output = scatter_about(seeds[8], (D, D), (max(1, 4 * D // (SEQ_DEV * N_CTX))) ** -0.5, 3.5, ((0, 4),))
    b_output = scatter_about(seeds[9], (D,), 0.3, 2.0, ((0, 4),))
    gain_one = jnp.clip(1.0 + 0.1 * jax.random.normal(seeds[10], (D,), jnp.float32), 0.5, 1.5).astype(jnp.bfloat16)
    bias_one = scatter_about(seeds[11], (D,), 0.2, 1.1953125, ((0, 4),))
    w_inner = scatter_about(seeds[12], (D, FF), D ** -0.5, 0.21875, ((0, 4),))
    b_inner = scatter_about(seeds[13], (FF,), 0.5, 3.0, ((0, 4),))
    w_outer = scatter_about(seeds[14], (FF, D), FF ** -0.5, 0.109375, ((0, 4),))
    b_outer = scatter_about(seeds[15], (D,), 0.3, 2.0, ((0, 4),))
    gain_two = jnp.clip(1.0 + 0.1 * jax.random.normal(seeds[16], (D,), jnp.float32), 0.5, 1.5).astype(jnp.bfloat16)
    bias_two = scatter_about(seeds[17], (D,), 0.2, 1.1953125, ((0, 4),))
    return {"inputs": inputs, "cotangent": cotangent, "lengths": lengths, "w_query": w_query, "b_query": b_query, "w_key": w_key, "w_value": w_value, "b_value": b_value, "w_output": w_output, "b_output": b_output, "gain_one": gain_one, "bias_one": bias_one, "w_inner": w_inner, "b_inner": b_inner, "w_outer": w_outer, "b_outer": b_outer, "gain_two": gain_two, "bias_two": bias_two}


EPSILON = 1e-05
NEG_FILL = -1e+30
SCALE = 0.125
ROOT_HALF = 0.7071067811865476

@jax.custom_vjp
def low(v):
    return lax.optimization_barrier(v.astype(jnp.bfloat16)).astype(jnp.float32)

@jax.custom_vjp
def low_back(v):
    return v

def low_keep(v):
    return (low(v), None)

def low_pass(kept, grad):
    return (grad,)

def back_keep(v):
    return (v, None)

def back_low(kept, grad):
    return (low(grad),)
low.defvjp(low_keep, low_pass)
low_back.defvjp(back_keep, back_low)

def product(left_side, right_side):
    return jnp.dot(left_side, right_side, precision=lax.Precision.HIGHEST, preferred_element_type=jnp.float32)

def layer_norm(resid, norm_gain, norm_bias):
    row_mean = lax.optimization_barrier(jnp.mean(resid, axis=-1, keepdims=True))
    centered = resid - row_mean
    inv_std = lax.rsqrt(lax.optimization_barrier(jnp.mean(centered * centered, axis=-1, keepdims=True)) + EPSILON)
    return centered * inv_std * norm_gain + norm_bias

def gelu_exact(pre_act):
    return 0.5 * pre_act * (1.0 + lax.erf(pre_act * ROOT_HALF))

def forward_one(params, tokens, seq_len):
    w_query, b_query, w_key, w_value, b_value, w_output, b_output, gain_one, bias_one, w_inner, b_inner, w_outer, b_outer, gain_two, bias_two = params
    length_all = tokens.shape[0]
    queries = low_back(low(product(tokens, w_query) + b_query))
    keys = low_back(low(product(tokens, w_key)))
    values = low_back(low(product(tokens, w_value) + b_value))
    key_ok = lax.iota(jnp.int32, length_all) < seq_len
    block_len = min(512, length_all)
    query_blocks = queries.reshape(length_all // block_len, block_len, H, HD)
    key_heads = keys.reshape(length_all, H, HD)
    value_heads = values.reshape(length_all, H, HD)

    def attend_block(query_block):
        raw_scores = jnp.einsum('qhd,khd->hqk', query_block, key_heads, precision=lax.Precision.HIGHEST)
        scores = jnp.where(key_ok[None, None, :], low_back(raw_scores * SCALE), NEG_FILL)
        shifted = jnp.exp(scores - lax.optimization_barrier(jnp.max(scores, axis=-1, keepdims=True)))
        probabilities = low(shifted / lax.optimization_barrier(jnp.sum(shifted, axis=-1, keepdims=True)))
        return jnp.einsum('hqk,khd->qhd', probabilities, value_heads, precision=lax.Precision.HIGHEST)
    attended = lax.map(jax.checkpoint(attend_block), query_blocks).reshape(length_all, D)
    context = low_back(low(attended))
    branch = low_back(product(context, w_output) + b_output)
    hidden = layer_norm(tokens + branch, gain_one, bias_one)
    inner_pre = low_back(product(low(hidden), w_inner) + b_inner)
    activated = low(gelu_exact(inner_pre))
    outer_out = low_back(product(activated, w_outer) + b_outer)
    return layer_norm(hidden + outer_out, gain_two, bias_two)

def reference(inputs, cotangent, lengths, w_query, b_query, w_key, w_value, b_value, w_output, b_output, gain_one, bias_one, w_inner, b_inner, w_outer, b_outer, gain_two, bias_two):
    params = tuple((member.astype(jnp.float32) for member in (w_query, b_query, w_key, w_value, b_value, w_output, b_output, gain_one, bias_one, w_inner, b_inner, w_outer, b_outer, gain_two, bias_two)))

    def one_sequence(totals, inputs_now):
        tokens, grad_out, seq_len = inputs_now
        tokens = tokens.astype(jnp.float32)

        def apply_layer(param_set, token_set):
            return forward_one(param_set, token_set, seq_len)
        result, pullback = jax.vjp(apply_layer, params, tokens)
        keep_rows = (lax.iota(jnp.int32, tokens.shape[0]) < seq_len).astype(jnp.float32)[:, None]
        grad_params, grad_tokens = pullback(grad_out.astype(jnp.float32) * keep_rows)
        totals = jax.tree.map(lambda held, fresh: held + fresh, totals, grad_params)
        return (totals, (result.astype(jnp.bfloat16), grad_tokens))
    zero_grads = jax.tree.map(jnp.zeros_like, params)
    totals, stacked = lax.scan(one_sequence, zero_grads, (inputs, cotangent, lengths))
    return (stacked[0], stacked[1], totals[0], totals[1], totals[2], totals[3], totals[4], totals[5], totals[6], totals[7], totals[8], totals[9], totals[10], totals[11], totals[12], totals[13], totals[14])
```

```python
from functools import partial

import jax
import jax.numpy as jnp
from jax import lax
from jax.experimental import pallas as pl
from jax.experimental.pallas import tpu as pltpu
from jax.sharding import PartitionSpec as P

D = 768
H = 12
HD = 64
SEQ_MB = 1
MICRO = 2


EPSILON = 1e-05
NEG_FILL = -1e30
SCALE = 0.125
ROOT_HALF = 0.7071067811865476
INV_ROOT_TAU = 0.3989422804014327
key_block = 512


def matmul(left_side, right_side):
    return jnp.dot(left_side, right_side, preferred_element_type=jnp.float32)


def left_product(left_side, right_side):
    return lax.dot_general(
        left_side, right_side, (((0,), (0,)), ((), ())), preferred_element_type=jnp.float32
    )


def right_product(left_side, right_side):
    return lax.dot_general(
        left_side, right_side, (((1,), (1,)), ((), ())), preferred_element_type=jnp.float32
    )


def split_heads(token_rows):
    return token_rows.reshape(token_rows.shape[0], token_rows.shape[1], H, HD)


def head_scores(query_rows, key_rows):
    return (
        jnp.einsum(
            "bqhd,bkhd->bhqk",
            split_heads(query_rows),
            split_heads(key_rows),
            preferred_element_type=jnp.float32,
        )
        * SCALE
    )


def live_mask(seq_lens, first_pos, num_rows):
    return (first_pos + lax.iota(jnp.int32, num_rows))[None, :] < seq_lens[:, None]


def layer_norm(resid, norm_gain, norm_bias):
    row_mean = jnp.mean(resid, axis=-1, keepdims=True)
    centered = resid - row_mean
    inv_std = lax.rsqrt(jnp.mean(centered * centered, axis=-1, keepdims=True) + EPSILON)
    normed = centered * inv_std
    return (normed * norm_gain + norm_bias, normed, inv_std)


def norm_back(grad_out, normed, inv_std, norm_gain):
    grad_norm = grad_out * norm_gain
    grad_in = inv_std * (
        grad_norm
        - jnp.mean(grad_norm, axis=-1, keepdims=True)
        - normed * jnp.mean(grad_norm * normed, axis=-1, keepdims=True)
    )
    return (grad_in, jnp.sum(grad_out * normed, axis=0), jnp.sum(grad_out, axis=0))


def gelu_exact(pre_act):
    return 0.5 * pre_act * (1.0 + lax.erf(pre_act * ROOT_HALF))


def gelu_slope(pre_act):
    return 0.5 * (1.0 + lax.erf(pre_act * ROOT_HALF)) + pre_act * INV_ROOT_TAU * jnp.exp(
        -0.5 * pre_act * pre_act
    )


def in_blocks(step_fn, running, pieces):
    num_rows = pieces[0].shape[1]

    def advance(block_index, current):
        offset = block_index * key_block
        sliced = tuple(
            (lax.dynamic_slice_in_dim(member, offset, key_block, 1) for member in pieces)
        )
        return step_fn(current, sliced, offset)

    return lax.fori_loop(0, num_rows // key_block, advance, running)


def attend_step(running, sliced, first_pos, queries, seq_lens, skip_empty):
    key_rows, value_rows = sliced
    live_keys = live_mask(seq_lens, first_pos, key_rows.shape[1])
    run_max, run_sum, run_out = running
    key_mask = live_keys[:, None, None, :]
    scores = jnp.where(key_mask, head_scores(queries, key_rows), NEG_FILL)
    new_max = jnp.maximum(run_max, jnp.max(scores, axis=-1))
    weights = jnp.where(key_mask, jnp.exp(scores - new_max[..., None]), 0.0)
    rescale = jnp.exp(run_max - new_max)
    new_sum = run_sum * rescale + jnp.sum(weights, axis=-1)
    new_out = run_out * rescale[..., None] + jnp.einsum(
        "bhqk,bkhd->bhqd",
        weights.astype(jnp.bfloat16),
        split_heads(value_rows),
        preferred_element_type=jnp.float32,
    )
    return (new_max, new_sum, new_out)


def query_grad_step(
    running,
    sliced,
    first_pos,
    queries,
    grad_context,
    log_total,
    row_delta,
    seq_lens,
    live_queries,
    skip_empty,
):
    key_rows, value_rows = sliced
    live_keys = live_mask(seq_lens, first_pos, key_rows.shape[1])
    key_mask = live_keys[:, None, None, :]
    probabilities = jnp.where(
        key_mask, jnp.exp(head_scores(queries, key_rows) - log_total[..., None]), 0.0
    )
    grad_probs = jnp.einsum(
        "bqhd,bkhd->bhqk",
        split_heads(grad_context),
        split_heads(value_rows),
        preferred_element_type=jnp.float32,
    )
    grad_scores = (probabilities * (grad_probs - row_delta[..., None])).astype(jnp.bfloat16)
    return running + jnp.einsum(
        "bhqk,bkhd->bqhd", grad_scores, split_heads(key_rows), preferred_element_type=jnp.float32
    )


def key_grad_step(
    running,
    sliced,
    first_pos,
    key_rows,
    value_rows,
    stat_total,
    stat_delta,
    seq_lens,
    live_keys,
    skip_empty,
):
    query_rows, grad_rows = sliced
    num_rows = query_rows.shape[1]
    grad_k, grad_v = running
    log_total = lax.dynamic_slice_in_dim(stat_total, first_pos, num_rows, 1).transpose(0, 2, 1)
    row_delta = lax.dynamic_slice_in_dim(stat_delta, first_pos, num_rows, 1).transpose(0, 2, 1)
    key_mask = live_keys[:, None, None, :]
    probabilities = jnp.where(
        key_mask, jnp.exp(head_scores(query_rows, key_rows) - log_total[..., None]), 0.0
    )
    grad_probs = jnp.einsum(
        "bqhd,bkhd->bhqk",
        split_heads(grad_rows),
        split_heads(value_rows),
        preferred_element_type=jnp.float32,
    )
    grad_scores = (probabilities * (grad_probs - row_delta[..., None])).astype(jnp.bfloat16)
    grad_v = grad_v + jnp.einsum(
        "bhqk,bqhd->bkhd",
        probabilities.astype(jnp.bfloat16),
        split_heads(grad_rows),
        preferred_element_type=jnp.float32,
    )
    grad_k = grad_k + jnp.einsum(
        "bhqk,bqhd->bkhd", grad_scores, split_heads(query_rows), preferred_element_type=jnp.float32
    )
    return (grad_k, grad_v)


def body(
    inputs,
    cotangent,
    lengths,
    w_query,
    b_query,
    w_key,
    w_value,
    b_value,
    w_output,
    b_output,
    gain_one,
    bias_one,
    w_inner,
    b_inner,
    w_outer,
    b_outer,
    gain_two,
    bias_two,
):
    gathered = (
        lax.all_gather(w_query, "fsdp", axis=0, tiled=True),
        lax.all_gather(b_query, "fsdp", axis=0, tiled=True),
        lax.all_gather(w_key, "fsdp", axis=0, tiled=True),
        lax.all_gather(w_value, "fsdp", axis=0, tiled=True),
        lax.all_gather(b_value, "fsdp", axis=0, tiled=True),
        lax.all_gather(w_output, "fsdp", axis=0, tiled=True),
        lax.all_gather(b_output, "fsdp", axis=0, tiled=True),
        lax.all_gather(gain_one, "fsdp", axis=0, tiled=True),
        lax.all_gather(bias_one, "fsdp", axis=0, tiled=True),
        lax.all_gather(w_inner, "fsdp", axis=0, tiled=True),
        lax.all_gather(b_inner, "fsdp", axis=0, tiled=True),
        lax.all_gather(w_outer, "fsdp", axis=0, tiled=True),
        lax.all_gather(b_outer, "fsdp", axis=0, tiled=True),
        lax.all_gather(gain_two, "fsdp", axis=0, tiled=True),
        lax.all_gather(bias_two, "fsdp", axis=0, tiled=True),
    )
    (
        query_weight,
        query_bias,
        key_weight,
        value_weight,
        value_bias,
        out_weight,
        out_bias,
        gain_first,
        shift_first,
        inner_weight,
        inner_bias,
        outer_weight,
        outer_bias,
        gain_second,
        shift_second,
    ) = gathered
    joint_weight = jnp.concatenate([query_weight, key_weight, value_weight], axis=1)
    joint_bias = jnp.concatenate(
        [
            query_bias.astype(jnp.float32),
            jnp.zeros((D,), jnp.float32),
            value_bias.astype(jnp.float32),
        ]
    )
    out_bias_f = out_bias.astype(jnp.float32)
    inner_bias_f = inner_bias.astype(jnp.float32)
    outer_bias_f = outer_bias.astype(jnp.float32)
    gain_first_f = gain_first.astype(jnp.float32)
    shift_first_f = shift_first.astype(jnp.float32)
    gain_second_f = gain_second.astype(jnp.float32)
    shift_second_f = shift_second.astype(jnp.float32)
    seq_dev = inputs.shape[1]
    row_count = SEQ_MB * seq_dev
    positions = lax.axis_index("ctx") * seq_dev + lax.iota(jnp.int32, seq_dev)
    accum = None
    out_list = []
    grad_list = []
    for micro_index in range(MICRO):
        first_seq = micro_index * SEQ_MB
        seq_lens = lengths[first_seq : first_seq + SEQ_MB]
        token_rows = inputs[first_seq : first_seq + SEQ_MB].reshape(row_count, D)
        grad_rows = (
            cotangent[first_seq : first_seq + SEQ_MB].reshape(row_count, D).astype(jnp.float32)
        )
        query_ok = positions[None, :] < seq_lens[:, None]
        row_keep = query_ok.reshape(row_count, 1).astype(jnp.float32)
        projected = (matmul(token_rows, joint_weight) + joint_bias).astype(jnp.bfloat16)
        queries = projected[:, :D].reshape(SEQ_MB, seq_dev, D)
        keys_local = projected[:, D : 2 * D].reshape(SEQ_MB, seq_dev, D)
        values_local = projected[:, 2 * D :].reshape(SEQ_MB, seq_dev, D)
        start_state = (
            jnp.full((SEQ_MB, H, seq_dev), NEG_FILL, jnp.float32),
            jnp.zeros((SEQ_MB, H, seq_dev), jnp.float32),
            jnp.zeros((SEQ_MB, H, seq_dev, HD), jnp.float32),
        )
        attend_fn = partial(attend_step, queries=queries, seq_lens=seq_lens, skip_empty=False)
        run_max, run_sum, run_out = in_blocks(
            attend_fn,
            start_state,
            (
                lax.all_gather(keys_local, "ctx", axis=1, tiled=True),
                lax.all_gather(values_local, "ctx", axis=1, tiled=True),
            ),
        )
        attended = run_out / run_sum[..., None]
        log_total = run_max + jnp.log(run_sum)
        context = attended.transpose(0, 2, 1, 3).reshape(row_count, D).astype(jnp.bfloat16)
        first_sum = token_rows.astype(jnp.float32) + matmul(context, out_weight) + out_bias_f
        hidden, normed_one, inv_one = layer_norm(first_sum, gain_first_f, shift_first_f)
        hidden_low = hidden.astype(jnp.bfloat16)
        inner_pre = matmul(hidden_low, inner_weight) + inner_bias_f
        activated = gelu_exact(inner_pre).astype(jnp.bfloat16)
        outer_out = matmul(activated, outer_weight) + outer_bias_f
        result, normed_two, inv_two = layer_norm(hidden + outer_out, gain_second_f, shift_second_f)
        out_list.append(result.astype(jnp.bfloat16).reshape(SEQ_MB, seq_dev, D))
        grad_out = grad_rows * row_keep
        grad_second, grad_gain_b, grad_shift_b = norm_back(
            grad_out, normed_two, inv_two, gain_second_f
        )
        grad_outer = grad_second.astype(jnp.bfloat16)
        grad_outer_w = left_product(activated, grad_outer)
        grad_outer_b = jnp.sum(grad_outer.astype(jnp.float32), axis=0)
        grad_inner = (right_product(grad_outer, outer_weight) * gelu_slope(inner_pre)).astype(
            jnp.bfloat16
        )
        grad_inner_w = left_product(hidden_low, grad_inner)
        grad_inner_b = jnp.sum(grad_inner.astype(jnp.float32), axis=0)
        grad_hidden = grad_second + right_product(grad_inner, inner_weight)
        grad_first, grad_gain_a, grad_shift_a = norm_back(
            grad_hidden, normed_one, inv_one, gain_first_f
        )
        grad_branch = grad_first.astype(jnp.bfloat16)
        grad_out_w = left_product(context, grad_branch)
        grad_out_b = jnp.sum(grad_branch.astype(jnp.float32), axis=0)
        grad_context = (
            right_product(grad_branch, out_weight).astype(jnp.bfloat16).reshape(SEQ_MB, seq_dev, D)
        )
        row_delta = jnp.einsum(
            "bqhd,bhqd->bhq", split_heads(grad_context).astype(jnp.float32), attended
        )
        stat_total, stat_delta = (
            lax.all_gather(log_total.transpose(0, 2, 1), "ctx", axis=1, tiled=True),
            lax.all_gather(row_delta.transpose(0, 2, 1), "ctx", axis=1, tiled=True),
        )
        query_fn = partial(
            query_grad_step,
            queries=queries,
            grad_context=grad_context,
            log_total=log_total,
            row_delta=row_delta,
            seq_lens=seq_lens,
            live_queries=query_ok,
            skip_empty=False,
        )
        key_fn = partial(
            key_grad_step,
            key_rows=keys_local,
            value_rows=values_local,
            stat_total=stat_total,
            stat_delta=stat_delta,
            seq_lens=seq_lens,
            live_keys=query_ok,
            skip_empty=False,
        )
        grad_zero = jnp.zeros((SEQ_MB, seq_dev, H, HD), jnp.float32)
        grad_q = in_blocks(
            query_fn,
            grad_zero,
            (
                lax.all_gather(keys_local, "ctx", axis=1, tiled=True),
                lax.all_gather(values_local, "ctx", axis=1, tiled=True),
            ),
        )
        grad_k, grad_v = in_blocks(
            key_fn,
            (grad_zero, grad_zero),
            (
                lax.all_gather(queries, "ctx", axis=1, tiled=True),
                lax.all_gather(grad_context, "ctx", axis=1, tiled=True),
            ),
        )
        joint_grad = jnp.concatenate(
            [
                (grad_q * SCALE).reshape(row_count, D).astype(jnp.bfloat16),
                (grad_k * SCALE).reshape(row_count, D).astype(jnp.bfloat16),
                grad_v.reshape(row_count, D).astype(jnp.bfloat16),
            ],
            axis=1,
        )
        grad_joint_w = left_product(token_rows, joint_grad)
        grad_joint_b = jnp.sum(joint_grad.astype(jnp.float32), axis=0)
        input_rows = grad_first + right_product(joint_grad, joint_weight)
        grad_list.append(input_rows.reshape(SEQ_MB, seq_dev, D))
        micro_grads = (
            grad_joint_w,
            grad_joint_b,
            grad_out_w,
            grad_out_b,
            grad_gain_a,
            grad_shift_a,
            grad_inner_w,
            grad_inner_b,
            grad_outer_w,
            grad_outer_b,
            grad_gain_b,
            grad_shift_b,
        )
        if accum is None:
            accum = micro_grads
        else:
            accum = tuple((held + fresh for held, fresh in zip(accum, micro_grads)))
    (
        joint_w,
        joint_b,
        out_w,
        out_b,
        gain_a,
        shift_a,
        inner_w,
        inner_b,
        outer_w,
        outer_b,
        gain_b,
        shift_b,
    ) = accum
    grad_set = (
        joint_w[:, :D],
        joint_b[:D],
        joint_w[:, D : 2 * D],
        joint_w[:, 2 * D :],
        joint_b[2 * D :],
        out_w,
        out_b,
        gain_a,
        shift_a,
        inner_w,
        inner_b,
        outer_w,
        outer_b,
        gain_b,
        shift_b,
    )
    shard_grads = (
        lax.psum_scatter(
            grad_set[0].astype(jnp.bfloat16), "fsdp", scatter_dimension=0, tiled=True
        ).astype(jnp.float32),
        lax.psum_scatter(
            grad_set[1].astype(jnp.bfloat16), "fsdp", scatter_dimension=0, tiled=True
        ).astype(jnp.float32),
        lax.psum_scatter(
            grad_set[2].astype(jnp.bfloat16), "fsdp", scatter_dimension=0, tiled=True
        ).astype(jnp.float32),
        lax.psum_scatter(
            grad_set[3].astype(jnp.bfloat16), "fsdp", scatter_dimension=0, tiled=True
        ).astype(jnp.float32),
        lax.psum_scatter(
            grad_set[4].astype(jnp.bfloat16), "fsdp", scatter_dimension=0, tiled=True
        ).astype(jnp.float32),
        lax.psum_scatter(
            grad_set[5].astype(jnp.bfloat16), "fsdp", scatter_dimension=0, tiled=True
        ).astype(jnp.float32),
        lax.psum_scatter(
            grad_set[6].astype(jnp.bfloat16), "fsdp", scatter_dimension=0, tiled=True
        ).astype(jnp.float32),
        lax.psum_scatter(
            grad_set[7].astype(jnp.bfloat16), "fsdp", scatter_dimension=0, tiled=True
        ).astype(jnp.float32),
        lax.psum_scatter(
            grad_set[8].astype(jnp.bfloat16), "fsdp", scatter_dimension=0, tiled=True
        ).astype(jnp.float32),
        lax.psum_scatter(
            grad_set[9].astype(jnp.bfloat16), "fsdp", scatter_dimension=0, tiled=True
        ).astype(jnp.float32),
        lax.psum_scatter(
            grad_set[10].astype(jnp.bfloat16), "fsdp", scatter_dimension=0, tiled=True
        ).astype(jnp.float32),
        lax.psum_scatter(
            grad_set[11].astype(jnp.bfloat16), "fsdp", scatter_dimension=0, tiled=True
        ).astype(jnp.float32),
        lax.psum_scatter(
            grad_set[12].astype(jnp.bfloat16), "fsdp", scatter_dimension=0, tiled=True
        ).astype(jnp.float32),
        lax.psum_scatter(
            grad_set[13].astype(jnp.bfloat16), "fsdp", scatter_dimension=0, tiled=True
        ).astype(jnp.float32),
        lax.psum_scatter(
            grad_set[14].astype(jnp.bfloat16), "fsdp", scatter_dimension=0, tiled=True
        ).astype(jnp.float32),
    )
    summed = lax.psum(
        (
            shard_grads[0],
            shard_grads[1],
            shard_grads[2],
            shard_grads[3],
            shard_grads[4],
            shard_grads[5],
            shard_grads[6],
            shard_grads[7],
            shard_grads[8],
            shard_grads[9],
            shard_grads[10],
            shard_grads[11],
            shard_grads[12],
            shard_grads[13],
            shard_grads[14],
        ),
        "ctx",
    )
    outputs = jnp.concatenate(out_list, axis=0)
    input_grad = jnp.concatenate(grad_list, axis=0)
    return (outputs, input_grad) + tuple(summed)


HALF = D // 2
ROWS = 128


def flat(z, x, y, k):
    return (z * 2 + x) * 4 + y * 2 + k


def table(move):
    return [
        (flat(z, x, y, k), flat(*move(z, x, y, k)))
        for z in range(4)
        for x in range(2)
        for y in range(2)
        for k in range(2)
    ]


def permute(move):
    pairs = table(move)
    return lambda block: lax.ppermute(block, ("ctx", "fsdp"), pairs)


def permute_back(move):
    pairs = [(b, a) for a, b in table(move)]
    return lambda block: lax.ppermute(block, ("ctx", "fsdp"), pairs)


def to_seq(turn):
    return lambda z, x, y, k: (2 * k + (z // 2 + turn) % 2, x, y, z % 2)


swap_core = permute(lambda z, x, y, k: (z, x, y, k ^ 1))
swap_y = permute(lambda z, x, y, k: (z, x, y ^ 1, k))
swap_x = permute(lambda z, x, y, k: (z, x ^ 1, y, k))
swap_z1 = permute(lambda z, x, y, k: (z ^ 1, x, y, k))
swap_z2 = permute(lambda z, x, y, k: (z ^ 2, x, y, k))
seq_send = (permute(to_seq(0)), permute(to_seq(1)))
seq_return = (permute_back(to_seq(0)), permute_back(to_seq(1)))


def low(value):
    return value.astype(jnp.bfloat16)


def wide(value):
    return value.astype(jnp.float32)


def pick(array, index, axis=0):
    return lax.dynamic_index_in_dim(array, index, axis, keepdims=False)


def dot_nt(a, b):
    return lax.dot_general(a, b, (((1,), (1,)), ((), ())), preferred_element_type=jnp.float32)


def dot_tn(a, b):
    return lax.dot_general(a, b, (((0,), (0,)), ((), ())), preferred_element_type=jnp.float32)


def attend_kernel(
    info, b0, b1, b2, b3, b4, b5, b6, b7, w0, w1, w2, w3, bias,
    xs, ws, q_out, k_out, v_out, p_out, cu, cv, cxu, cxv, key_bias,
):
    step = pl.program_id(0)

    @pl.when(step == 0)
    def _():
        for n, block in enumerate((b0, b1, b2, b3, b4, b5, b6, b7)):
            xs[n * ROWS : (n + 1) * ROWS, :] = block[...]
            place = info[n] + lax.broadcasted_iota(jnp.int32, (1, ROWS), 1)
            key_bias[:, n * ROWS : (n + 1) * ROWS] = jnp.where(place < info[8], 0.0, NEG_FILL)
        for n, piece in enumerate((w0, w1, w2, w3)):
            ws[pl.ds(pl.multiple_of(info[9 + n], 64), 192), :] = piece[...]
        q_out[...] = low(
            wide(low(matmul(xs[: 4 * ROWS, :], ws[:, :HALF]) + bias[:, :HALF])) * SCALE
        )
        k_out[...] = low(matmul(xs[...], ws[:, HALF : 2 * HALF]))
        v_out[...] = low(matmul(xs[...], ws[:, 2 * HALF :]) + bias[:, 2 * HALF :])

    lanes = pl.ds(pl.multiple_of(step * 128, 128), 128)
    first = lax.broadcasted_iota(jnp.int32, (1, 128), 1) < HD
    queries = q_out[:, lanes]
    keys = k_out[:, lanes]
    values = v_out[:, lanes]
    for part in range(2):
        rows = slice(part * 256, part * 256 + 256)
        found = []
        for head in range(2):
            mine = first if head == 0 else jnp.logical_not(first)
            scores = dot_nt(jnp.where(mine, queries[rows], 0), keys) + key_bias[...]
            top = jnp.max(scores, axis=1, keepdims=True)
            weights = jnp.exp(scores - top)
            total = jnp.sum(weights, axis=1, keepdims=True)
            probs = low(weights * (1.0 / total))
            p_out[head, rows, :] = probs
            found.append(matmul(probs, values))
        context = low(jnp.where(first, found[0], found[1]))
        one, two = (cu, cv) if part == 0 else (cxu, cxv)
        one[...] = context[:ROWS]
        two[...] = context[ROWS:]


def attend_back_kernel(
    info, xs, ws, queries_ref, keys_ref, values_ref, probs_ref, gu, gv, gxu, gxv,
    dx_own, dx_other, keep, send, dq, dk, dv, dw,
):
    step = pl.program_id(0)
    lanes = pl.ds(pl.multiple_of(step * 128, 128), 128)
    first = lax.broadcasted_iota(jnp.int32, (1, 128), 1) < HD
    keys = keys_ref[:, lanes]
    values = values_ref[:, lanes]
    grad_k = jnp.zeros((8 * ROWS, 128), jnp.float32)
    grad_v = jnp.zeros((8 * ROWS, 128), jnp.float32)
    for part in range(2):
        rows = slice(part * 256, part * 256 + 256)
        one, two = (gu, gv) if part == 0 else (gxu, gxv)
        grad_rows = jnp.concatenate([one[...], two[...]], axis=0)
        queries = queries_ref[rows, lanes]
        grad_q = jnp.zeros((256, 128), jnp.float32)
        for head in range(2):
            mine = first if head == 0 else jnp.logical_not(first)
            grad_mine = jnp.where(mine, grad_rows, 0)
            probs = probs_ref[head, rows, :]
            grad_probs = dot_nt(grad_mine, values)
            product = wide(probs) * grad_probs
            delta = jnp.sum(product, axis=1, keepdims=True)
            grad_scores = low(product - wide(probs) * delta)
            grad_q = grad_q + matmul(grad_scores, jnp.where(mine, keys, 0))
            grad_k = grad_k + dot_tn(grad_scores, jnp.where(mine, queries, 0))
            grad_v = grad_v + dot_tn(probs, grad_mine)
        dq[rows, lanes] = low(grad_q * SCALE)
    dk[:, lanes] = low(grad_k)
    dv[:, lanes] = low(grad_v)

    @pl.when(step == pl.num_programs(0) - 1)
    def _():
        own = slice(0, 4 * ROWS)
        other = slice(4 * ROWS, 8 * ROWS)
        w_q, w_k, w_v = ws[:, :HALF], ws[:, HALF : 2 * HALF], ws[:, 2 * HALF :]
        dx_other[...] = low(dot_nt(dk[other, :], w_k) + dot_nt(dv[other, :], w_v))
        dx_own[...] = dot_nt(dq[...], w_q) + dot_nt(dk[own, :], w_k) + dot_nt(dv[own, :], w_v)
        dw[:, :HALF] = low(dot_tn(xs[own, :], dq[...]))
        dw[:, HALF : 2 * HALF] = low(dot_tn(xs[...], dk[...]))
        dw[:, 2 * HALF :] = low(dot_tn(xs[...], dv[...]))
        col_sums = jnp.concatenate(
            [
                jnp.sum(wide(dq[...]), axis=0, keepdims=True),
                jnp.zeros((1, HALF), jnp.float32),
                jnp.sum(wide(dv[...]), axis=0, keepdims=True),
            ],
            axis=1,
        )
        tail = low(jnp.where(lax.broadcasted_iota(jnp.int32, (16, 1), 0) == 0, col_sums, 0.0))
        fsdp, z_bit = info[13], info[14]
        for other_f in range(4):
            place = send if other_f % 2 else keep
            for half in range(2):
                start = pl.multiple_of(192 * (fsdp ^ other_f) + 96 * half, 32)
                place[other_f // 2, half ^ z_bit, :96, :] = dw[pl.ds(start, 96), :]
                place[other_f // 2, half ^ z_bit, 96:, :] = tail if half == 0 else tail * 0


def whole(shape):
    return pl.BlockSpec(shape, lambda *_: (0,) * len(shape))


def lane_block(rows):
    return pl.BlockSpec((rows, 128), lambda step, *_: (0, step))


VMEM_LIMIT = 56 * 1024 * 1024


def attend(info, blocks, pieces, bias):
    shape = jax.ShapeDtypeStruct
    half = jnp.bfloat16
    return pl.pallas_call(
        attend_kernel,
        out_shape=[
            shape((8 * ROWS, D), half),
            shape((D, 3 * HALF), half),
            shape((4 * ROWS, HALF), half),
            shape((8 * ROWS, HALF), half),
            shape((8 * ROWS, HALF), half),
            shape((6, 4 * ROWS, 8 * ROWS), half),
        ]
        + [shape((ROWS, HALF), half)] * 4,
        grid_spec=pltpu.PrefetchScalarGridSpec(
            num_scalar_prefetch=1,
            grid=(3,),
            in_specs=[whole((ROWS, D))] * 8 + [whole((192, 3 * HALF))] * 4 + [whole((1, 3 * HALF))],
            out_specs=[
                whole((8 * ROWS, D)),
                whole((D, 3 * HALF)),
                whole((4 * ROWS, HALF)),
                whole((8 * ROWS, HALF)),
                whole((8 * ROWS, HALF)),
                pl.BlockSpec((2, 4 * ROWS, 8 * ROWS), lambda step, *_: (step, 0, 0)),
            ]
            + [lane_block(ROWS)] * 4,
            scratch_shapes=[pltpu.VMEM((1, 8 * ROWS), jnp.float32)],
        ),
        compiler_params=pltpu.CompilerParams(
            dimension_semantics=("arbitrary",), vmem_limit_bytes=VMEM_LIMIT
        ),
        cost_estimate=pl.CostEstimate(
            flops=10_000_000_000, bytes_accessed=20_000_000, transcendentals=3_200_000
        ),
        name="attend",
    )(info, *blocks, *pieces, bias)


def attend_back(info, xs, ws, queries, keys, values, probs, grads):
    shape = jax.ShapeDtypeStruct
    half = jnp.bfloat16
    joint = (2, 2, 112, 3 * HALF)
    return pl.pallas_call(
        attend_back_kernel,
        out_shape=[
            shape((4 * ROWS, D), jnp.float32),
            shape((4 * ROWS, D), half),
            shape(joint, half),
            shape(joint, half),
        ],
        grid_spec=pltpu.PrefetchScalarGridSpec(
            num_scalar_prefetch=1,
            grid=(3,),
            in_specs=[
                whole((8 * ROWS, D)),
                whole((D, 3 * HALF)),
                whole((4 * ROWS, HALF)),
                whole((8 * ROWS, HALF)),
                whole((8 * ROWS, HALF)),
                pl.BlockSpec((2, 4 * ROWS, 8 * ROWS), lambda step, *_: (step, 0, 0)),
            ]
            + [lane_block(ROWS)] * 4,
            out_specs=[whole((4 * ROWS, D)), whole((4 * ROWS, D)), whole(joint), whole(joint)],
            scratch_shapes=[
                pltpu.VMEM((4 * ROWS, HALF), half),
                pltpu.VMEM((8 * ROWS, HALF), half),
                pltpu.VMEM((8 * ROWS, HALF), half),
                pltpu.VMEM((D, 3 * HALF), half),
            ],
        ),
        compiler_params=pltpu.CompilerParams(
            dimension_semantics=("arbitrary",), vmem_limit_bytes=VMEM_LIMIT
        ),
        cost_estimate=pl.CostEstimate(
            flops=14_000_000_000, bytes_accessed=20_000_000, transcendentals=0
        ),
        name="attend_back",
    )(info, xs, ws, queries, keys, values, probs, *grads)


def middle_one_kernel(
    info, cm0, cm1, co0, co1, x0, x1, o0, o1, o2, o3, i0, i1, i2, i3, vec, bias,
    hidden_out, normed_out, inv_out, act, slope, ctx, low_rows,
):
    step = pl.program_id(0)
    f, x = info[0], info[1]

    @pl.when(step == 0)
    def _():
        for side, (one, two) in enumerate(((cm0, cm1), (co0, co1))):
            rows = jnp.concatenate([one[...], two[...]], axis=0)
            for part in range(2):
                ctx[2 * (x ^ side) + part] = rows[:, 192 * part : 192 * part + 192]
        total = wide(jnp.concatenate([x0[...], x1[...]], axis=0)) + vec[0:1, :]
        for n, piece in enumerate((o0, o1, o2, o3)):
            total = total + matmul(ctx[f ^ n], piece[...])
        hidden, normed, inv = layer_norm(total, vec[1:2, :], vec[2:3, :])
        hidden_out[...] = hidden
        normed_out[...] = normed
        inv_out[...] = inv
        rows = low(hidden)
        for n in range(4):
            low_rows[n] = rows[:, 192 * n : 192 * n + 192]

    pre = bias[0]
    for n, piece in enumerate((i0, i1, i2, i3)):
        pre = pre + matmul(low_rows[f ^ n], piece[...])
    bell = 0.5 * (1.0 + lax.erf(pre * ROOT_HALF))
    act[0] = low(pre * bell)
    slope[0] = low(bell + pre * INV_ROOT_TAU * jnp.exp(-0.5 * pre * pre))


def middle_two_kernel(
    info, act, slope, hidden, normed_one, inv_one, cot, vec,
    o0, o1, o2, o3, i0, i1, i2, i3, w0, w1, w2, w3,
    out, first_out, gm0, gm1, go0, go1, outer_out, inner_out, branch_out, sums,
    o_all, i_all, w_all, spread, gc, o_sem, i_sem, w_sem,
):
    f, x = info[0], info[1]
    copies = {}
    for name, refs, held, sems in (
        ("w", (w0, w1, w2, w3), w_all, w_sem),
        ("i", (i0, i1, i2, i3), i_all, i_sem),
        ("o", (o0, o1, o2, o3), o_all, o_sem),
    ):
        for n, ref in enumerate(refs):
            copies[name, n] = pltpu.make_async_copy(ref, held.at[n], sems.at[n])
            copies[name, n].start()
    b_2, g_2, s_2, g_1 = vec[3:4, :], vec[4:5, :], vec[5:6, :], vec[1:2, :]
    total = hidden[...] + b_2
    for n in range(4):
        copies["w", n].wait()
        total = total + matmul(act[n], w_all[n])
    result, normed, inv = layer_norm(total, g_2, s_2)
    out[...] = low(result)
    row = lax.broadcasted_iota(jnp.int32, (2 * ROWS, 1), 0)
    end = jnp.where(row < ROWS, info[4], info[5] + ROWS)
    grad = wide(cot[...]) * jnp.where(row + info[3] < end, 1.0, 0.0)
    sums[...] = jnp.zeros_like(sums)

    def put(index, value):
        sums[index : index + 1, :] = jnp.sum(value, axis=0, keepdims=True)

    def back(grad, normed, inv, gain):
        scaled = grad * gain
        return inv * (
            scaled
            - jnp.mean(scaled, axis=-1, keepdims=True)
            - normed * jnp.mean(scaled * normed, axis=-1, keepdims=True)
        )

    put(4, grad * normed)
    put(5, grad)
    grad_second = back(grad, normed, inv, g_2)
    grad_outer = low(grad_second)
    outer_out[...] = grad_outer
    put(3, wide(grad_outer))
    for n in range(4):
        copies["i", n].wait()
    parts = [None] * 4
    for e in range(4):
        inner = low(dot_nt(grad_outer, w_all[e]) * wide(slope[e]))
        inner_out[e] = inner
        sums[pl.ds(8 + (f ^ e), 1), :] = jnp.sum(wide(inner), axis=0, keepdims=True)
        columns = pl.ds(pl.multiple_of(D * (f ^ e), 128), D)
        for n in range(4):
            fresh = dot_nt(inner, i_all[n, :, columns])
            parts[n] = fresh if e == 0 else parts[n] + fresh
    for n in range(4):
        spread[f ^ n] = parts[n]
    grad_hidden = grad_second + jnp.concatenate([spread[n] for n in range(4)], axis=1)
    normed = normed_one[...]
    put(1, grad_hidden * normed)
    put(2, grad_hidden)
    grad_first = back(grad_hidden, normed, inv_one[...], g_1)
    first_out[...] = grad_first
    branch = low(grad_first)
    branch_out[...] = branch
    put(0, wide(branch))
    for n in range(4):
        copies["o", n].wait()
        gc[f ^ n] = low(dot_nt(branch, o_all[n]))
    for side, (one, two) in enumerate(((gm0, gm1), (go0, go1))):
        rows = jnp.concatenate([gc[2 * (x ^ side)], gc[2 * (x ^ side) + 1]], axis=1)
        one[...] = rows[:ROWS]
        two[...] = rows[ROWS:]


def middle_three_kernel(
    info, act, inner, outer, hidden, branch, cm0, cm1, co0, co1, sums,
    outer_keep, outer_send, inner_keep, inner_send, held, out_held, vec_held,
):
    step = pl.program_id(0)
    f, x, spot = info[0], info[1], info[2]
    block = f ^ step

    @pl.when(step == 0)
    def _():
        for side, (one, two) in enumerate(((cm0, cm1), (co0, co1))):
            rows = jnp.concatenate([one[...], two[...]], axis=0)
            start = pl.multiple_of(HALF * (x ^ side), 128)
            out_held[pl.ds(start, HALF), :] = low(dot_tn(rows, branch[...]))
        vec_held[...] = jnp.zeros_like(vec_held)
        top = lax.broadcasted_iota(jnp.int32, (16, 1), 0) == 0
        for n in range(4):
            cut = slice(192 * n, 192 * n + 192)
            lines = (
                sums[8 + n : 9 + n, :],
                jnp.concatenate([sums[m : m + 1, cut] for m in range(4)], axis=1),
                jnp.concatenate(
                    [sums[4:5, cut], sums[5:6, cut], jnp.zeros((1, HALF), jnp.float32)], axis=1
                ),
            )
            for m, line in enumerate(lines):
                vec_held[m, n] = low(jnp.where(top, line, 0.0))

    grad = low(dot_tn(act[0], outer[...]))
    for place, wanted in ((outer_send, step < 2), (outer_keep, step >= 2)):

        @pl.when(wanted)
        def _(place=place):
            for n in range(4):
                place[0, n ^ spot] = grad[192 * n : 192 * n + 192]

    held[...] = low(dot_tn(low(hidden[...]), inner[0]))
    for n in range(4):
        place = inner_send if n % 2 else inner_keep
        start = 192 * (f ^ n)
        place[n // 2, 0, :192, :] = held[pl.ds(pl.multiple_of(start, 64), 192), :]
        place[n // 2, 0, 192:240, :] = out_held[pl.ds(pl.multiple_of(start + 48 * block, 16), 48), :]
        place[n // 2, 0, 240:, :] = vec_held[block, f ^ n]


MIDDLE = 2 * ROWS


def middle_one(info, ctx, rows, out_pieces, inner_pieces, vec, bias):
    shape = jax.ShapeDtypeStruct
    return pl.pallas_call(
        middle_one_kernel,
        out_shape=[
            shape((MIDDLE, D), jnp.float32),
            shape((MIDDLE, D), jnp.float32),
            shape((MIDDLE, 1), jnp.float32),
            shape((4, MIDDLE, D), jnp.bfloat16),
            shape((4, MIDDLE, D), jnp.bfloat16),
        ],
        grid_spec=pltpu.PrefetchScalarGridSpec(
            num_scalar_prefetch=1,
            grid=(4,),
            in_specs=[whole((ROWS, HALF))] * 4
            + [whole((ROWS, D))] * 2
            + [whole((192, D))] * 4
            + [pl.BlockSpec((192, D), lambda step, info: (0, info[0] ^ step))] * 4
            + [whole((8, D)), pl.BlockSpec((1, 1, D), lambda step, info: (info[0] ^ step, 0, 0))],
            out_specs=[whole((MIDDLE, D)), whole((MIDDLE, D)), whole((MIDDLE, 1))]
            + [pl.BlockSpec((1, MIDDLE, D), lambda step, info: (step, 0, 0))] * 2,
            scratch_shapes=[
                pltpu.VMEM((4, MIDDLE, 192), jnp.bfloat16),
                pltpu.VMEM((4, MIDDLE, 192), jnp.bfloat16),
            ],
        ),
        compiler_params=pltpu.CompilerParams(
            dimension_semantics=("arbitrary",), vmem_limit_bytes=VMEM_LIMIT
        ),
        cost_estimate=pl.CostEstimate(
            flops=1_600_000_000, bytes_accessed=12_000_000, transcendentals=1_600_000
        ),
        name="middle_one",
    )(info, *ctx, *rows, *out_pieces, *inner_pieces, vec, bias)


def middle_two(info, act, slope, hidden, normed, inv, cot, vec, out_p, inner_p, outer_p):
    shape = jax.ShapeDtypeStruct
    half = jnp.bfloat16
    return pl.pallas_call(
        middle_two_kernel,
        out_shape=[shape((MIDDLE, D), half), shape((MIDDLE, D), jnp.float32)]
        + [shape((ROWS, HALF), half)] * 4
        + [
            shape((MIDDLE, D), half),
            shape((4, MIDDLE, D), half),
            shape((MIDDLE, D), half),
            shape((16, D), jnp.float32),
        ],
        grid_spec=pltpu.PrefetchScalarGridSpec(
            num_scalar_prefetch=1,
            grid=(1,),
            in_specs=[whole((4, MIDDLE, D))] * 2
            + [whole((MIDDLE, D))] * 2
            + [whole((MIDDLE, 1)), whole((MIDDLE, D)), whole((8, D))]
            + [pl.BlockSpec(memory_space=pl.ANY)] * 12,
            out_specs=[whole((MIDDLE, D))] * 2
            + [whole((ROWS, HALF))] * 4
            + [whole((MIDDLE, D)), whole((4, MIDDLE, D)), whole((MIDDLE, D)), whole((16, D))],
            scratch_shapes=[
                pltpu.VMEM((4, 192, D), half),
                pltpu.VMEM((4, 192, 4 * D), half),
                pltpu.VMEM((4, D, D), half),
                pltpu.VMEM((4, MIDDLE, 192), jnp.float32),
                pltpu.VMEM((4, MIDDLE, 192), half),
                pltpu.SemaphoreType.DMA((4,)),
                pltpu.SemaphoreType.DMA((4,)),
                pltpu.SemaphoreType.DMA((4,)),
            ],
        ),
        compiler_params=pltpu.CompilerParams(
            dimension_semantics=("arbitrary",), vmem_limit_bytes=VMEM_LIMIT
        ),
        cost_estimate=pl.CostEstimate(
            flops=4_000_000_000, bytes_accessed=20_000_000, transcendentals=0
        ),
        name="middle_two",
    )(info, act, slope, hidden, normed, inv, cot, vec, *out_p, *inner_p, *outer_p)


def middle_three(info, act, inner, outer, hidden, branch, ctx, sums):
    shape = jax.ShapeDtypeStruct
    half = jnp.bfloat16
    return pl.pallas_call(
        middle_three_kernel,
        out_shape=[shape((2, 4, 192, D), half)] * 2 + [shape((2, 4, 256, D), half)] * 2,
        grid_spec=pltpu.PrefetchScalarGridSpec(
            num_scalar_prefetch=1,
            grid=(4,),
            in_specs=[
                pl.BlockSpec(
                    (1, MIDDLE, D),
                    lambda step, info: (jnp.where(step < 2, 2 * step + 1, 2 * step - 4), 0, 0),
                ),
                pl.BlockSpec((1, MIDDLE, D), lambda step, info: (step, 0, 0)),
            ]
            + [whole((MIDDLE, D))] * 3
            + [whole((ROWS, HALF))] * 4
            + [whole((16, D))],
            out_specs=[
                pl.BlockSpec(
                    (1, 4, 192, D), lambda step, info: (jnp.maximum(step - 2, 0), 0, 0, 0)
                ),
                pl.BlockSpec((1, 4, 192, D), lambda step, info: (jnp.minimum(step, 1), 0, 0, 0)),
            ]
            + [
                pl.BlockSpec(
                    (2, 1, 256, D), lambda step, info: (0, info[0] ^ step ^ info[2], 0, 0)
                )
            ]
            * 2,
            scratch_shapes=[
                pltpu.VMEM((D, D), half),
                pltpu.VMEM((D, D), half),
                pltpu.VMEM((4, 4, 16, D), half),
            ],
        ),
        compiler_params=pltpu.CompilerParams(
            dimension_semantics=("arbitrary",), vmem_limit_bytes=VMEM_LIMIT
        ),
        cost_estimate=pl.CostEstimate(
            flops=3_000_000_000, bytes_accessed=16_000_000, transcendentals=0
        ),
        name="middle_three",
    )(info, act, inner, outer, hidden, branch, *ctx, sums)


def place_outer_kernel(info, p0, p1, p2, p3, out):
    for n, piece in enumerate((p0, p1, p2, p3)):
        out[pl.ds(pl.multiple_of(192 * (n ^ info[2]), 64), 192), :] = wide(piece[...])


def place_inner_kernel(info, p0, p1, p2, p3, inner, out, vec):
    for n, piece in enumerate((p0, p1, p2, p3)):
        at = n ^ info[2]
        inner[:, pl.ds(pl.multiple_of(D * at, 128), D)] = wide(piece[:192, :])
        out[pl.ds(pl.multiple_of(48 * at, 16), 48), :] = wide(piece[192:240, :])
        vec[at] = wide(piece[240:, :])


def place_joint_kernel(info, p0, p1, p2, p3, query, key, value, vec):
    x, z_bit = info[1], info[2] % 2
    for n, piece in enumerate((p0, p1, p2, p3)):
        rows = pl.ds(pl.multiple_of(96 * (n % 2 ^ z_bit), 32), 96)
        columns = pl.ds(pl.multiple_of(HALF * (n // 2 ^ x), 128), HALF)
        for m, out in enumerate((query, key, value)):
            out[rows, columns] = wide(piece[:96, HALF * m : HALF * m + HALF])
        vec[n // 2 ^ x, n % 2 ^ z_bit] = wide(piece[96:, :])


def placed(kernel, name, info, pieces, shapes):
    return pl.pallas_call(
        kernel,
        out_shape=[jax.ShapeDtypeStruct(shape, jnp.float32) for shape in shapes],
        grid_spec=pltpu.PrefetchScalarGridSpec(
            num_scalar_prefetch=1,
            grid=(1,),
            in_specs=[whole(piece.shape) for piece in pieces],
            out_specs=[whole(shape) for shape in shapes],
        ),
        compiler_params=pltpu.CompilerParams(
            dimension_semantics=("arbitrary",), vmem_limit_bytes=VMEM_LIMIT
        ),
        name=name,
    )(info, *pieces)


def unshuffle(array, bit):
    return jnp.where(bit == 0, array, array[::-1])


def fsdp_sum(keep, send):
    by_y = wide(keep) + wide(swap_core(send))
    return by_y[0] + wide(swap_y(low(by_y[1])))


def halved(shard, swap):
    half = shard.shape[0] // 2
    return shard[:half] + wide(swap(low(shard[half:])))


def z_sum(pair):
    one = low(halved(pair, swap_z1)[0])
    one = low(wide(one) + wide(swap_z2(one)))
    return [one, swap_z1(one)]


def ctx_sum(shard):
    pair = z_sum(halved(shard, swap_x))
    return pair + [swap_x(one) for one in pair]


def fast_body(
    inputs, cotangent, lengths, w_query, b_query, w_key, w_value, b_value, w_output, b_output,
    gain_one, bias_one, w_inner, b_inner, w_outer, b_outer, gain_two, bias_two,
):
    c, f = lax.axis_index("ctx"), lax.axis_index("fsdp")
    z, x, y, k = c // 2, c % 2, f // 2, f % 2
    zh = z // 2

    turned = unshuffle(inputs, zh)
    bu, bv = seq_send[0](turned[0]), seq_send[1](turned[1])
    bxu, bxv = swap_x(bu), swap_x(bv)
    blocks = [bu, bv, bxu, bxv]
    blocks = blocks + [swap_core(b) for b in blocks]
    z_low, z_high = 2 * (z % 2), 2 * (1 - z % 2)
    spots = []
    for kk in (k, 1 - k):
        for xx in (x, 1 - x):
            spots += [((z_low + kk) * 2 + xx) * ROWS, ((z_high + kk) * 2 + xx) * ROWS]

    ends = jnp.stack([lengths // 128, lengths % 128]).reshape(4).astype(jnp.bfloat16)
    small = jnp.concatenate(
        [b_query, b_value, b_output, gain_one, bias_one, b_outer, gain_two, bias_two, b_inner, ends]
        + [jnp.zeros((124,), jnp.bfloat16)]
    ).reshape(19, 128)
    small = jnp.stack([small, swap_y(small)])
    small = jnp.stack([small, swap_core(small)], axis=1)
    small = unshuffle(small, y)
    small = jnp.where(k == 0, small, small[:, ::-1]).reshape(4, 19 * 128)
    small = small.astype(jnp.float32)
    vectors = [small[:, 192 * n : 192 * n + 192].reshape(D) for n in range(8)]
    b_q, b_v, b_o, g_1, s_1, b_2, g_2, s_2 = vectors
    b_1 = small[:, 1536:2304].reshape(4, 1, D)
    ends = small[:, 2304:2308].astype(jnp.int32).reshape(4, 2, 2)
    ends = (128 * ends[:, 0] + ends[:, 1]).reshape(8)
    vec = jnp.stack([b_o, g_1, s_1, b_2, g_2, s_2, g_2, s_2])
    info = jnp.stack(
        spots + [pick(ends, 4 * y + z)] + [192 * (f ^ n) for n in range(4)] + [f, z % 2]
    ).astype(jnp.int32)
    turned_ends = unshuffle(lengths, zh)
    spot = jnp.stack(
        [f, x, 2 * x + z % 2, c * ROWS, turned_ends[0], turned_ends[1]]
    ).astype(jnp.int32)
    x_bias = jnp.concatenate(
        [
            lax.dynamic_slice_in_dim(b_q, x * HALF, HALF),
            jnp.zeros((HALF,), jnp.float32),
            lax.dynamic_slice_in_dim(b_v, x * HALF, HALF),
        ]
    )[None]
    w_x = jnp.concatenate(
        [lax.dynamic_slice_in_dim(w, x * HALF, HALF, 1) for w in (w_query, w_key, w_value)], axis=1
    )

    def gathered(shard, after=None):
        if after is not None:
            shard, after = lax.optimization_barrier((shard, after))
        far = swap_y(shard)
        return [shard, swap_core(shard), far, swap_core(far)]

    qkv_p = gathered(w_x)
    out_p = gathered(w_output, qkv_p[2])
    inner_p = gathered(w_inner, out_p[2])
    outer_p = gathered(w_outer, inner_p[2])

    xs, ws, queries, keys, values, probs, cu, cv, cxu, cxv = attend(info, blocks, qkv_p, x_bias)

    mine = [seq_return[0](cu), seq_return[1](cv)]
    cxu, cxv = swap_x(cxu), swap_x(cxv)
    ctx = mine + [seq_return[0](cxu), seq_return[1](cxv)]

    hidden, normed, inv, act, slope = middle_one(
        spot, ctx, [turned[0], turned[1]], out_p, inner_p, vec, b_1
    )
    cot = unshuffle(cotangent, zh).reshape(MIDDLE, D)
    result, grad_first, gm0, gm1, go0, go1, outer, inner, branch, sums = middle_two(
        spot, act, slope, hidden, normed, inv, cot, vec, out_p, inner_p, outer_p
    )
    outputs = unshuffle(result.reshape(2, ROWS, D), zh)
    sent = [seq_send[0](go0), seq_send[1](go1)]
    kept = [seq_send[0](gm0), seq_send[1](gm1)]
    came = [swap_x(block) for block in sent]
    outer_keep, outer_send, inner_keep, inner_send = middle_three(
        spot, act, inner, outer, hidden, branch, ctx, sums
    )
    dx_own, dx_other, joint_keep, joint_send = attend_back(
        info, xs, ws, queries, keys, values, probs, kept + came
    )

    dx = dx_own + wide(swap_core(dx_other))
    dx = low(halved(dx, swap_x))
    dx = jnp.concatenate([seq_return[n](dx[n * ROWS : (n + 1) * ROWS]) for n in range(2)], axis=0)
    input_grad = unshuffle((grad_first + wide(dx)).reshape(2, ROWS, D), zh)

    outer_blocks = ctx_sum(fsdp_sum(outer_keep, outer_send))
    inner_blocks = ctx_sum(fsdp_sum(inner_keep, inner_send))
    joint = z_sum(fsdp_sum(joint_keep, joint_send))
    joint_blocks = joint + [swap_x(one) for one in joint]
    (outer_grad,) = placed(place_outer_kernel, "place_outer", spot, outer_blocks, [(D, D)])
    inner_grad, out_grad, lines = placed(
        place_inner_kernel, "place_inner", spot, inner_blocks,
        [(192, 4 * D), (192, D), (4, 16, D)],
    )
    q_grad, k_grad, v_grad, joint_lines = placed(
        place_joint_kernel, "place_joint", spot, joint_blocks,
        [(192, D)] * 3 + [(2, 2, 16, 3 * HALF)],
    )
    grad_b1 = lines[0, 0]
    grad_bo, grad_g1, grad_s1, grad_b2 = (lines[1, 0, 192 * n : 192 * n + 192] for n in range(4))
    grad_g2, grad_s2 = (lines[2, 0, 192 * n : 192 * n + 192] for n in range(2))
    joint_sums = joint_lines[:, 0, 0]

    def own(vector):
        return lax.dynamic_slice_in_dim(vector.reshape(D), f * 192, 192)

    grad_bq, grad_bv = own(joint_sums[:, :HALF]), own(joint_sums[:, 2 * HALF :])
    return (
        outputs, input_grad, q_grad, grad_bq, k_grad, v_grad, grad_bv, out_grad, grad_bo,
        grad_g1, grad_s1, inner_grad, grad_b1, outer_grad, grad_b2, grad_g2, grad_s2,
    )


def solution(mesh):
    placed = (
        P("fsdp", "ctx", None),
        P("fsdp", "ctx", None),
        P("fsdp"),
        P("fsdp", None),
        P("fsdp"),
        P("fsdp", None),
        P("fsdp", None),
        P("fsdp"),
        P("fsdp", None),
        P("fsdp"),
        P("fsdp"),
        P("fsdp"),
        P("fsdp", None),
        P("fsdp"),
        P("fsdp", None),
        P("fsdp"),
        P("fsdp"),
        P("fsdp"),
    )
    fast = dict(mesh.shape) == {"ctx": 8, "fsdp": 4}
    return jax.shard_map(
        fast_body if fast else body,
        mesh=mesh,
        in_specs=placed,
        out_specs=(
            P("fsdp", "ctx", None),
            P("fsdp", "ctx", None),
            P("fsdp", None),
            P("fsdp"),
            P("fsdp", None),
            P("fsdp", None),
            P("fsdp"),
            P("fsdp", None),
            P("fsdp"),
            P("fsdp"),
            P("fsdp"),
            P("fsdp", None),
            P("fsdp"),
            P("fsdp", None),
            P("fsdp"),
            P("fsdp"),
            P("fsdp"),
        ),
        check_vma=False,
    )
```

```python
from functools import partial

import jax
import jax.numpy as jnp
from jax import lax
from jax.experimental import pallas as pl
from jax.experimental.pallas import tpu as pltpu
from jax.sharding import PartitionSpec as P

D = 768
H = 12
HD = 64
SEQ_MB = 1
MICRO = 2


EPSILON = 1e-05
NEG_FILL = -1e30
SCALE = 0.125
ROOT_HALF = 0.7071067811865476
INV_ROOT_TAU = 0.3989422804014327
key_block = 512


def matmul(left_side, right_side):
    return jnp.dot(left_side, right_side, preferred_element_type=jnp.float32)


def left_product(left_side, right_side):
    return lax.dot_general(
        left_side, right_side, (((0,), (0,)), ((), ())), preferred_element_type=jnp.float32
    )


def right_product(left_side, right_side):
    return lax.dot_general(
        left_side, right_side, (((1,), (1,)), ((), ())), preferred_element_type=jnp.float32
    )


def split_heads(token_rows):
    return token_rows.reshape(token_rows.shape[0], token_rows.shape[1], H, HD)


def head_scores(query_rows, key_rows):
    return (
        jnp.einsum(
            "bqhd,bkhd->bhqk",
            split_heads(query_rows),
            split_heads(key_rows),
            preferred_element_type=jnp.float32,
        )
        * SCALE
    )


def live_mask(seq_lens, first_pos, num_rows):
    return (first_pos + lax.iota(jnp.int32, num_rows))[None, :] < seq_lens[:, None]


def layer_norm(resid, norm_gain, norm_bias):
    row_mean = jnp.mean(resid, axis=-1, keepdims=True)
    centered = resid - row_mean
    inv_std = lax.rsqrt(jnp.mean(centered * centered, axis=-1, keepdims=True) + EPSILON)
    normed = centered * inv_std
    return (normed * norm_gain + norm_bias, normed, inv_std)


def norm_back(grad_out, normed, inv_std, norm_gain):
    grad_norm = grad_out * norm_gain
    grad_in = inv_std * (
        grad_norm
        - jnp.mean(grad_norm, axis=-1, keepdims=True)
        - normed * jnp.mean(grad_norm * normed, axis=-1, keepdims=True)
    )
    return (grad_in, jnp.sum(grad_out * normed, axis=0), jnp.sum(grad_out, axis=0))


def gelu_exact(pre_act):
    return 0.5 * pre_act * (1.0 + lax.erf(pre_act * ROOT_HALF))


def gelu_slope(pre_act):
    return 0.5 * (1.0 + lax.erf(pre_act * ROOT_HALF)) + pre_act * INV_ROOT_TAU * jnp.exp(
        -0.5 * pre_act * pre_act
    )


def in_blocks(step_fn, running, pieces):
    num_rows = pieces[0].shape[1]

    def advance(block_index, current):
        offset = block_index * key_block
        sliced = tuple(
            (lax.dynamic_slice_in_dim(member, offset, key_block, 1) for member in pieces)
        )
        return step_fn(current, sliced, offset)

    return lax.fori_loop(0, num_rows // key_block, advance, running)


def attend_step(running, sliced, first_pos, queries, seq_lens, skip_empty):
    key_rows, value_rows = sliced
    live_keys = live_mask(seq_lens, first_pos, key_rows.shape[1])
    run_max, run_sum, run_out = running
    key_mask = live_keys[:, None, None, :]
    scores = jnp.where(key_mask, head_scores(queries, key_rows), NEG_FILL)
    new_max = jnp.maximum(run_max, jnp.max(scores, axis=-1))
    weights = jnp.where(key_mask, jnp.exp(scores - new_max[..., None]), 0.0)
    rescale = jnp.exp(run_max - new_max)
    new_sum = run_sum * rescale + jnp.sum(weights, axis=-1)
    new_out = run_out * rescale[..., None] + jnp.einsum(
        "bhqk,bkhd->bhqd",
        weights.astype(jnp.bfloat16),
        split_heads(value_rows),
        preferred_element_type=jnp.float32,
    )
    return (new_max, new_sum, new_out)


def query_grad_step(
    running,
    sliced,
    first_pos,
    queries,
    grad_context,
    log_total,
    row_delta,
    seq_lens,
    live_queries,
    skip_empty,
):
    key_rows, value_rows = sliced
    live_keys = live_mask(seq_lens, first_pos, key_rows.shape[1])
    key_mask = live_keys[:, None, None, :]
    probabilities = jnp.where(
        key_mask, jnp.exp(head_scores(queries, key_rows) - log_total[..., None]), 0.0
    )
    grad_probs = jnp.einsum(
        "bqhd,bkhd->bhqk",
        split_heads(grad_context),
        split_heads(value_rows),
        preferred_element_type=jnp.float32,
    )
    grad_scores = (probabilities * (grad_probs - row_delta[..., None])).astype(jnp.bfloat16)
    return running + jnp.einsum(
        "bhqk,bkhd->bqhd", grad_scores, split_heads(key_rows), preferred_element_type=jnp.float32
    )


def key_grad_step(
    running,
    sliced,
    first_pos,
    key_rows,
    value_rows,
    stat_total,
    stat_delta,
    seq_lens,
    live_keys,
    skip_empty,
):
    query_rows, grad_rows = sliced
    num_rows = query_rows.shape[1]
    grad_k, grad_v = running
    log_total = lax.dynamic_slice_in_dim(stat_total, first_pos, num_rows, 1).transpose(0, 2, 1)
    row_delta = lax.dynamic_slice_in_dim(stat_delta, first_pos, num_rows, 1).transpose(0, 2, 1)
    key_mask = live_keys[:, None, None, :]
    probabilities = jnp.where(
        key_mask, jnp.exp(head_scores(query_rows, key_rows) - log_total[..., None]), 0.0
    )
    grad_probs = jnp.einsum(
        "bqhd,bkhd->bhqk",
        split_heads(grad_rows),
        split_heads(value_rows),
        preferred_element_type=jnp.float32,
    )
    grad_scores = (probabilities * (grad_probs - row_delta[..., None])).astype(jnp.bfloat16)
    grad_v = grad_v + jnp.einsum(
        "bhqk,bqhd->bkhd",
        probabilities.astype(jnp.bfloat16),
        split_heads(grad_rows),
        preferred_element_type=jnp.float32,
    )
    grad_k = grad_k + jnp.einsum(
        "bhqk,bqhd->bkhd", grad_scores, split_heads(query_rows), preferred_element_type=jnp.float32
    )
    return (grad_k, grad_v)


def body(
    inputs,
    cotangent,
    lengths,
    w_query,
    b_query,
    w_key,
    w_value,
    b_value,
    w_output,
    b_output,
    gain_one,
    bias_one,
    w_inner,
    b_inner,
    w_outer,
    b_outer,
    gain_two,
    bias_two,
):
    gathered = (
        lax.all_gather(w_query, "fsdp", axis=0, tiled=True),
        lax.all_gather(b_query, "fsdp", axis=0, tiled=True),
        lax.all_gather(w_key, "fsdp", axis=0, tiled=True),
        lax.all_gather(w_value, "fsdp", axis=0, tiled=True),
        lax.all_gather(b_value, "fsdp", axis=0, tiled=True),
        lax.all_gather(w_output, "fsdp", axis=0, tiled=True),
        lax.all_gather(b_output, "fsdp", axis=0, tiled=True),
        lax.all_gather(gain_one, "fsdp", axis=0, tiled=True),
        lax.all_gather(bias_one, "fsdp", axis=0, tiled=True),
        lax.all_gather(w_inner, "fsdp", axis=0, tiled=True),
        lax.all_gather(b_inner, "fsdp", axis=0, tiled=True),
        lax.all_gather(w_outer, "fsdp", axis=0, tiled=True),
        lax.all_gather(b_outer, "fsdp", axis=0, tiled=True),
        lax.all_gather(gain_two, "fsdp", axis=0, tiled=True),
        lax.all_gather(bias_two, "fsdp", axis=0, tiled=True),
    )
    (
        query_weight,
        query_bias,
        key_weight,
        value_weight,
        value_bias,
        out_weight,
        out_bias,
        gain_first,
        shift_first,
        inner_weight,
        inner_bias,
        outer_weight,
        outer_bias,
        gain_second,
        shift_second,
    ) = gathered
    joint_weight = jnp.concatenate([query_weight, key_weight, value_weight], axis=1)
    joint_bias = jnp.concatenate(
        [
            query_bias.astype(jnp.float32),
            jnp.zeros((D,), jnp.float32),
            value_bias.astype(jnp.float32),
        ]
    )
    out_bias_f = out_bias.astype(jnp.float32)
    inner_bias_f = inner_bias.astype(jnp.float32)
    outer_bias_f = outer_bias.astype(jnp.float32)
    gain_first_f = gain_first.astype(jnp.float32)
    shift_first_f = shift_first.astype(jnp.float32)
    gain_second_f = gain_second.astype(jnp.float32)
    shift_second_f = shift_second.astype(jnp.float32)
    seq_dev = inputs.shape[1]
    row_count = SEQ_MB * seq_dev
    positions = lax.axis_index("ctx") * seq_dev + lax.iota(jnp.int32, seq_dev)
    accum = None
    out_list = []
    grad_list = []
    for micro_index in range(MICRO):
        first_seq = micro_index * SEQ_MB
        seq_lens = lengths[first_seq : first_seq + SEQ_MB]
        token_rows = inputs[first_seq : first_seq + SEQ_MB].reshape(row_count, D)
        grad_rows = (
            cotangent[first_seq : first_seq + SEQ_MB].reshape(row_count, D).astype(jnp.float32)
        )
        query_ok = positions[None, :] < seq_lens[:, None]
        row_keep = query_ok.reshape(row_count, 1).astype(jnp.float32)
        projected = (matmul(token_rows, joint_weight) + joint_bias).astype(jnp.bfloat16)
        queries = projected[:, :D].reshape(SEQ_MB, seq_dev, D)
        keys_local = projected[:, D : 2 * D].reshape(SEQ_MB, seq_dev, D)
        values_local = projected[:, 2 * D :].reshape(SEQ_MB, seq_dev, D)
        start_state = (
            jnp.full((SEQ_MB, H, seq_dev), NEG_FILL, jnp.float32),
            jnp.zeros((SEQ_MB, H, seq_dev), jnp.float32),
            jnp.zeros((SEQ_MB, H, seq_dev, HD), jnp.float32),
        )
        attend_fn = partial(attend_step, queries=queries, seq_lens=seq_lens, skip_empty=False)
        run_max, run_sum, run_out = in_blocks(
            attend_fn,
            start_state,
            (
                lax.all_gather(keys_local, "ctx", axis=1, tiled=True),
                lax.all_gather(values_local, "ctx", axis=1, tiled=True),
            ),
        )
        attended = run_out / run_sum[..., None]
        log_total = run_max + jnp.log(run_sum)
        context = attended.transpose(0, 2, 1, 3).reshape(row_count, D).astype(jnp.bfloat16)
        first_sum = token_rows.astype(jnp.float32) + matmul(context, out_weight) + out_bias_f
        hidden, normed_one, inv_one = layer_norm(first_sum, gain_first_f, shift_first_f)
        hidden_low = hidden.astype(jnp.bfloat16)
        inner_pre = matmul(hidden_low, inner_weight) + inner_bias_f
        activated = gelu_exact(inner_pre).astype(jnp.bfloat16)
        outer_out = matmul(activated, outer_weight) + outer_bias_f
        result, normed_two, inv_two = layer_norm(hidden + outer_out, gain_second_f, shift_second_f)
        out_list.append(result.astype(jnp.bfloat16).reshape(SEQ_MB, seq_dev, D))
        grad_out = grad_rows * row_keep
        grad_second, grad_gain_b, grad_shift_b = norm_back(
            grad_out, normed_two, inv_two, gain_second_f
        )
        grad_outer = grad_second.astype(jnp.bfloat16)
        grad_outer_w = left_product(activated, grad_outer)
        grad_outer_b = jnp.sum(grad_outer.astype(jnp.float32), axis=0)
        grad_inner = (right_product(grad_outer, outer_weight) * gelu_slope(inner_pre)).astype(
            jnp.bfloat16
        )
        grad_inner_w = left_product(hidden_low, grad_inner)
        grad_inner_b = jnp.sum(grad_inner.astype(jnp.float32), axis=0)
        grad_hidden = grad_second + right_product(grad_inner, inner_weight)
        grad_first, grad_gain_a, grad_shift_a = norm_back(
            grad_hidden, normed_one, inv_one, gain_first_f
        )
        grad_branch = grad_first.astype(jnp.bfloat16)
        grad_out_w = left_product(context, grad_branch)
        grad_out_b = jnp.sum(grad_branch.astype(jnp.float32), axis=0)
        grad_context = (
            right_product(grad_branch, out_weight).astype(jnp.bfloat16).reshape(SEQ_MB, seq_dev, D)
        )
        row_delta = jnp.einsum(
            "bqhd,bhqd->bhq", split_heads(grad_context).astype(jnp.float32), attended
        )
        stat_total, stat_delta = (
            lax.all_gather(log_total.transpose(0, 2, 1), "ctx", axis=1, tiled=True),
            lax.all_gather(row_delta.transpose(0, 2, 1), "ctx", axis=1, tiled=True),
        )
        query_fn = partial(
            query_grad_step,
            queries=queries,
            grad_context=grad_context,
            log_total=log_total,
            row_delta=row_delta,
            seq_lens=seq_lens,
            live_queries=query_ok,
            skip_empty=False,
        )
        key_fn = partial(
            key_grad_step,
            key_rows=keys_local,
            value_rows=values_local,
            stat_total=stat_total,
            stat_delta=stat_delta,
            seq_lens=seq_lens,
            live_keys=query_ok,
            skip_empty=False,
        )
        grad_zero = jnp.zeros((SEQ_MB, seq_dev, H, HD), jnp.float32)
        grad_q = in_blocks(
            query_fn,
            grad_zero,
            (
                lax.all_gather(keys_local, "ctx", axis=1, tiled=True),
                lax.all_gather(values_local, "ctx", axis=1, tiled=True),
            ),
        )
        grad_k, grad_v = in_blocks(
            key_fn,
            (grad_zero, grad_zero),
            (
                lax.all_gather(queries, "ctx", axis=1, tiled=True),
                lax.all_gather(grad_context, "ctx", axis=1, tiled=True),
            ),
        )
        joint_grad = jnp.concatenate(
            [
                (grad_q * SCALE).reshape(row_count, D).astype(jnp.bfloat16),
                (grad_k * SCALE).reshape(row_count, D).astype(jnp.bfloat16),
                grad_v.reshape(row_count, D).astype(jnp.bfloat16),
            ],
            axis=1,
        )
        grad_joint_w = left_product(token_rows, joint_grad)
        grad_joint_b = jnp.sum(joint_grad.astype(jnp.float32), axis=0)
        input_rows = grad_first + right_product(joint_grad, joint_weight)
        grad_list.append(input_rows.reshape(SEQ_MB, seq_dev, D))
        micro_grads = (
            grad_joint_w,
            grad_joint_b,
            grad_out_w,
            grad_out_b,
            grad_gain_a,
            grad_shift_a,
            grad_inner_w,
            grad_inner_b,
            grad_outer_w,
            grad_outer_b,
            grad_gain_b,
            grad_shift_b,
        )
        if accum is None:
            accum = micro_grads
        else:
            accum = tuple((held + fresh for held, fresh in zip(accum, micro_grads)))
    (
        joint_w,
        joint_b,
        out_w,
        out_b,
        gain_a,
        shift_a,
        inner_w,
        inner_b,
        outer_w,
        outer_b,
        gain_b,
        shift_b,
    ) = accum
    grad_set = (
        joint_w[:, :D],
        joint_b[:D],
        joint_w[:, D : 2 * D],
        joint_w[:, 2 * D :],
        joint_b[2 * D :],
        out_w,
        out_b,
        gain_a,
        shift_a,
        inner_w,
        inner_b,
        outer_w,
        outer_b,
        gain_b,
        shift_b,
    )
    shard_grads = (
        lax.psum_scatter(
            grad_set[0].astype(jnp.bfloat16), "fsdp", scatter_dimension=0, tiled=True
        ).astype(jnp.float32),
        lax.psum_scatter(
            grad_set[1].astype(jnp.bfloat16), "fsdp", scatter_dimension=0, tiled=True
        ).astype(jnp.float32),
        lax.psum_scatter(
            grad_set[2].astype(jnp.bfloat16), "fsdp", scatter_dimension=0, tiled=True
        ).astype(jnp.float32),
        lax.psum_scatter(
            grad_set[3].astype(jnp.bfloat16), "fsdp", scatter_dimension=0, tiled=True
        ).astype(jnp.float32),
        lax.psum_scatter(
            grad_set[4].astype(jnp.bfloat16), "fsdp", scatter_dimension=0, tiled=True
        ).astype(jnp.float32),
        lax.psum_scatter(
            grad_set[5].astype(jnp.bfloat16), "fsdp", scatter_dimension=0, tiled=True
        ).astype(jnp.float32),
        lax.psum_scatter(
            grad_set[6].astype(jnp.bfloat16), "fsdp", scatter_dimension=0, tiled=True
        ).astype(jnp.float32),
        lax.psum_scatter(
            grad_set[7].astype(jnp.bfloat16), "fsdp", scatter_dimension=0, tiled=True
        ).astype(jnp.float32),
        lax.psum_scatter(
            grad_set[8].astype(jnp.bfloat16), "fsdp", scatter_dimension=0, tiled=True
        ).astype(jnp.float32),
        lax.psum_scatter(
            grad_set[9].astype(jnp.bfloat16), "fsdp", scatter_dimension=0, tiled=True
        ).astype(jnp.float32),
        lax.psum_scatter(
            grad_set[10].astype(jnp.bfloat16), "fsdp", scatter_dimension=0, tiled=True
        ).astype(jnp.float32),
        lax.psum_scatter(
            grad_set[11].astype(jnp.bfloat16), "fsdp", scatter_dimension=0, tiled=True
        ).astype(jnp.float32),
        lax.psum_scatter(
            grad_set[12].astype(jnp.bfloat16), "fsdp", scatter_dimension=0, tiled=True
        ).astype(jnp.float32),
        lax.psum_scatter(
            grad_set[13].astype(jnp.bfloat16), "fsdp", scatter_dimension=0, tiled=True
        ).astype(jnp.float32),
        lax.psum_scatter(
            grad_set[14].astype(jnp.bfloat16), "fsdp", scatter_dimension=0, tiled=True
        ).astype(jnp.float32),
    )
    summed = lax.psum(
        (
            shard_grads[0],
            shard_grads[1],
            shard_grads[2],
            shard_grads[3],
            shard_grads[4],
            shard_grads[5],
            shard_grads[6],
            shard_grads[7],
            shard_grads[8],
            shard_grads[9],
            shard_grads[10],
            shard_grads[11],
            shard_grads[12],
            shard_grads[13],
            shard_grads[14],
        ),
        "ctx",
    )
    outputs = jnp.concatenate(out_list, axis=0)
    input_grad = jnp.concatenate(grad_list, axis=0)
    return (outputs, input_grad) + tuple(summed)


HALF = D // 2
ROWS = 128


def flat(z, x, y, k):
    return (z * 2 + x) * 4 + y * 2 + k


def table(move):
    return [
        (flat(z, x, y, k), flat(*move(z, x, y, k)))
        for z in range(4)
        for x in range(2)
        for y in range(2)
        for k in range(2)
    ]


def permute(move):
    pairs = table(move)
    return lambda block: lax.ppermute(block, ("ctx", "fsdp"), pairs)


def permute_back(move):
    pairs = [(b, a) for a, b in table(move)]
    return lambda block: lax.ppermute(block, ("ctx", "fsdp"), pairs)


def to_seq(turn):
    return lambda z, x, y, k: (2 * k + (z // 2 + turn) % 2, x, y, z % 2)


swap_core = permute(lambda z, x, y, k: (z, x, y, k ^ 1))
swap_y = permute(lambda z, x, y, k: (z, x, y ^ 1, k))
swap_x = permute(lambda z, x, y, k: (z, x ^ 1, y, k))
swap_z1 = permute(lambda z, x, y, k: (z ^ 1, x, y, k))
swap_z2 = permute(lambda z, x, y, k: (z ^ 2, x, y, k))
seq_send = (permute(to_seq(0)), permute(to_seq(1)))
seq_return = (permute_back(to_seq(0)), permute_back(to_seq(1)))


def low(value):
    return value.astype(jnp.bfloat16)


def wide(value):
    return value.astype(jnp.float32)


def pick(array, index, axis=0):
    return lax.dynamic_index_in_dim(array, index, axis, keepdims=False)


def dot_nt(a, b):
    return lax.dot_general(a, b, (((1,), (1,)), ((), ())), preferred_element_type=jnp.float32)


def dot_tn(a, b):
    return lax.dot_general(a, b, (((0,), (0,)), ((), ())), preferred_element_type=jnp.float32)


def coords(info):
    c, f = info[0] >> 2, info[0] & 3
    return c >> 1, c & 1, f >> 1, f & 1, c, f


def pack_kernel(
    info, lens, rows, grads, w_q, w_k, w_v, v0, v1, v2, v3, v4, v5, v6, v7, wide_vec,
    t0, t1, cot, w_x, small, held,
):
    z, x, _, _, _, _ = coords(info)
    zh = z >> 1
    t0[...] = rows[zh]
    t1[...] = rows[1 - zh]
    cot[:ROWS] = grads[zh]
    cot[ROWS:] = grads[1 - zh]
    columns = pl.ds(pl.multiple_of(x * HALF, 128), HALF)
    for n, weight in enumerate((w_q, w_k, w_v)):
        w_x[:, HALF * n : HALF * n + HALF] = weight[:, columns]
    held[...] = jnp.zeros_like(held)
    for n, vector in enumerate((v0, v1, v2, v3, v4, v5, v6, v7)):
        held[n : n + 1, :192] = wide(vector[...]).reshape(1, 192)
    held[8:9, :] = wide(wide_vec[...]).reshape(1, D)
    lane = lax.broadcasted_iota(jnp.int32, (1, D), 1)
    ends = jnp.zeros((1, D), jnp.int32)
    for n in range(2):
        ends = jnp.where(lane == n, lens[n] >> 7, ends)
        ends = jnp.where(lane == 2 + n, lens[n] & 127, ends)
    held[9:10, :] = wide(ends)
    small[...] = low(held[...])


def attend_kernel(
    info, b0, b1, b2, b3, b4, b5, b6, b7, w0, w1, w2, w3, s0, s1, s2, s3,
    xs, ws, q_out, k_out, v_out, p_out, cu, cv, cxu, cxv, key_bias, small,
):
    step = pl.program_id(0)
    z, x, y, k, _, f = coords(info)

    @pl.when(step == 0)
    def _():
        for n, piece in enumerate((s0, s1, s2, s3)):
            small[f ^ n] = wide(piece[...])
        line = small[2 * y + (z >> 1)][9:10, :]
        lane = lax.broadcasted_iota(jnp.int32, (1, D), 1)
        part = jnp.where(lane == (z & 1), 128.0 * line, 0.0)
        part = part + jnp.where(lane == 2 + (z & 1), line, 0.0)
        end = jnp.sum(part, axis=1, keepdims=True)
        z_low = 2 * (z & 1)
        blocks = (b0, b1, b2, b3, b4, b5, b6, b7)
        for n, block in enumerate(blocks):
            z_block = (z_low if n % 2 == 0 else 2 - z_low) + (k if n < 4 else 1 - k)
            x_block = x if n % 4 < 2 else 1 - x
            xs[n * ROWS : (n + 1) * ROWS, :] = block[...]
            place = (2 * z_block + x_block) * ROWS + lax.broadcasted_iota(jnp.int32, (1, ROWS), 1)
            key_bias[:, n * ROWS : (n + 1) * ROWS] = jnp.where(wide(place) < end, 0.0, NEG_FILL)
        for n, piece in enumerate((w0, w1, w2, w3)):
            ws[pl.ds(pl.multiple_of(192 * (f ^ n), 64), 192), :] = piece[...]

        def bias(row):
            return jnp.concatenate(
                [small[2 * x + n][row : row + 1, :192] for n in range(2)], axis=1
            )

        q_out[...] = low(wide(low(matmul(xs[: 4 * ROWS, :], ws[:, :HALF]) + bias(0))) * SCALE)
        k_out[...] = low(matmul(xs[...], ws[:, HALF : 2 * HALF]))
        v_out[...] = low(matmul(xs[...], ws[:, 2 * HALF :]) + bias(1))

    lanes = pl.ds(pl.multiple_of(step * 128, 128), 128)
    first = lax.broadcasted_iota(jnp.int32, (1, 128), 1) < HD
    queries = q_out[:, lanes]
    keys = k_out[:, lanes]
    values = v_out[:, lanes]
    for part in range(2):
        rows = slice(part * 256, part * 256 + 256)
        found = []
        for head in range(2):
            mine = first if head == 0 else jnp.logical_not(first)
            scores = dot_nt(jnp.where(mine, queries[rows], 0), keys) + key_bias[...]
            top = jnp.max(scores, axis=1, keepdims=True)
            weights = jnp.exp(scores - top)
            total = jnp.sum(weights, axis=1, keepdims=True)
            probs = low(weights * (1.0 / total))
            p_out[head, rows, :] = probs
            found.append(matmul(probs, values))
        context = low(jnp.where(first, found[0], found[1]))
        one, two = (cu, cv) if part == 0 else (cxu, cxv)
        one[...] = context[:ROWS]
        two[...] = context[ROWS:]


def pair_back(queries_ref, keys, values, probs_ref, grads):
    first = lax.broadcasted_iota(jnp.int32, (1, 128), 1) < HD
    grad_k = jnp.zeros((8 * ROWS, 128), jnp.float32)
    grad_v = jnp.zeros((8 * ROWS, 128), jnp.float32)
    grad_qs = []
    for part in range(2):
        rows = slice(part * 256, part * 256 + 256)
        one, two = grads[2 * part : 2 * part + 2]
        grad_rows = jnp.concatenate([one[...], two[...]], axis=0)
        queries = queries_ref[rows, :]
        grad_q = jnp.zeros((256, 128), jnp.float32)
        for head in range(2):
            mine = first if head == 0 else jnp.logical_not(first)
            grad_mine = jnp.where(mine, grad_rows, 0)
            probs = probs_ref[head, rows, :]
            grad_probs = dot_nt(grad_mine, values)
            product = wide(probs) * grad_probs
            delta = jnp.sum(product, axis=1, keepdims=True)
            grad_scores = low(product - wide(probs) * delta)
            grad_q = grad_q + matmul(grad_scores, jnp.where(mine, keys, 0))
            grad_k = grad_k + dot_tn(grad_scores, jnp.where(mine, queries, 0))
            grad_v = grad_v + dot_tn(probs, grad_mine)
        grad_qs.append(low(grad_q * SCALE))
    return grad_qs, low(grad_k), low(grad_v)


def attend_back_kernel(queries, keys, values, probs, gu, gv, gxu, gxv, dq, dk, dv):
    grad_qs, dk[...], dv[...] = pair_back(
        queries, keys[...], values[...], probs, (gu, gv, gxu, gxv)
    )
    dq[:256, :], dq[256:, :] = grad_qs


def attend_last_kernel(
    info, xs, ws, queries, keys, values, probs, gu, gv, gxu, gxv, dq_in, dk_in, dv_in,
    dx_own, dx_other, keep, send, dq, dk, dv, dw,
):
    cut = 2 * 128
    grad_qs, grad_k, grad_v = pair_back(
        queries, keys[...], values[...], probs, (gu, gv, gxu, gxv)
    )
    dq[:, :cut], dk[:, :cut], dv[:, :cut] = dq_in[...], dk_in[...], dv_in[...]
    dq[:256, cut:], dq[256:, cut:] = grad_qs
    dk[:, cut:], dv[:, cut:] = grad_k, grad_v
    own = slice(0, 4 * ROWS)
    other = slice(4 * ROWS, 8 * ROWS)
    w_q, w_k, w_v = ws[:, :HALF], ws[:, HALF : 2 * HALF], ws[:, 2 * HALF :]
    dx_other[...] = low(dot_nt(dk[other, :], w_k) + dot_nt(dv[other, :], w_v))
    dx_own[...] = dot_nt(dq[...], w_q) + dot_nt(dk[own, :], w_k) + dot_nt(dv[own, :], w_v)
    dw[:, :HALF] = low(dot_tn(xs[own, :], dq[...]))
    dw[:, HALF : 2 * HALF] = low(dot_tn(xs[...], dk[...]))
    dw[:, 2 * HALF :] = low(dot_tn(xs[...], dv[...]))
    col_sums = jnp.concatenate(
        [
            jnp.sum(wide(dq[...]), axis=0, keepdims=True),
            jnp.zeros((1, HALF), jnp.float32),
            jnp.sum(wide(dv[...]), axis=0, keepdims=True),
        ],
        axis=1,
    )
    tail = low(jnp.where(lax.broadcasted_iota(jnp.int32, (16, 1), 0) == 0, col_sums, 0.0))
    z, _, _, _, _, f = coords(info)
    for n in range(4):
        place = send if n % 2 else keep
        for half in range(2):
            start = pl.multiple_of(192 * (f ^ n) + 96 * half, 32)
            place[n // 2, half ^ (z & 1), :96, :] = dw[pl.ds(start, 96), :]
            place[n // 2, half ^ (z & 1), 96:, :] = tail if half == 0 else tail * 0


def middle_one_kernel(
    info, cm0, cm1, co0, co1, x0, x1, o0, o1, o2, o3, inner_weight, s0, s1, s2, s3,
    hidden_out, normed_out, inv_out, act, slope, vec, ctx, low_rows, small, order,
):
    step = pl.program_id(0)
    _, x, _, _, _, f = coords(info)

    @pl.when(step == 0)
    def _():
        for n, piece in enumerate((s0, s1, s2, s3)):
            small[f ^ n] = wide(piece[...])
            order[n] = wide(piece[...])
        for n in range(8):
            vec[n : n + 1, :] = jnp.concatenate(
                [small[m][n : n + 1, :192] for m in range(4)], axis=1
            )
        for side, (one, two) in enumerate(((cm0, cm1), (co0, co1))):
            rows = jnp.concatenate([one[...], two[...]], axis=0)
            for part in range(2):
                ctx[2 * (x ^ side) + part] = rows[:, 192 * part : 192 * part + 192]
        total = wide(jnp.concatenate([x0[...], x1[...]], axis=0)) + vec[2:3, :]
        for n, piece in enumerate((o0, o1, o2, o3)):
            total = total + matmul(ctx[f ^ n], piece[...])
        hidden, normed, inv = layer_norm(total, vec[3:4, :], vec[4:5, :])
        hidden_out[...] = hidden
        normed_out[...] = normed
        inv_out[...] = inv
        low_rows[...] = low(hidden)

    pre = matmul(low_rows[...], inner_weight[...]) + order[step][8:9, :]
    bell = 0.5 * (1.0 + lax.erf(pre * ROOT_HALF))
    act[0] = low(pre * bell)
    slope[0] = low(bell + pre * INV_ROOT_TAU * jnp.exp(-0.5 * pre * pre))


def norm_grad(grad, normed, inv, gain):
    scaled = grad * gain
    return inv * (
        scaled
        - jnp.mean(scaled, axis=-1, keepdims=True)
        - normed * jnp.mean(scaled * normed, axis=-1, keepdims=True)
    )


def column_sum(value):
    return jnp.sum(value, axis=0, keepdims=True)


def middle_two_kernel(
    info, lens, act, act_block, hidden, cot, vec, w0, w1, w2, w3,
    out, second_out, outer_out, sums, keep, send, w_all, w_sem,
):
    step = pl.program_id(0)
    z, x, _, _, c, f = coords(info)

    @pl.when(step == 0)
    def _():
        copies = [
            pltpu.make_async_copy(ref, w_all.at[n], w_sem.at[n])
            for n, ref in enumerate((w0, w1, w2, w3))
        ]
        for copy in copies:
            copy.start()
        b_2, g_2, s_2 = vec[5:6, :], vec[6:7, :], vec[7:8, :]
        total = hidden[...] + b_2
        for n in range(4):
            copies[n].wait()
            total = total + matmul(act[n], w_all[n])
        result, normed, inv = layer_norm(total, g_2, s_2)
        zh = z >> 1
        out[zh] = low(result[:ROWS])
        out[1 - zh] = low(result[ROWS:])
        row = lax.broadcasted_iota(jnp.int32, (2 * ROWS, 1), 0)
        end = jnp.where(row < ROWS, lens[zh], lens[1 - zh] + ROWS)
        grad = wide(cot[...]) * jnp.where(row + c * ROWS < end, 1.0, 0.0)
        grad_second = norm_grad(grad, normed, inv, g_2)
        second_out[...] = grad_second
        grad_outer = low(grad_second)
        outer_out[...] = grad_outer
        sums[...] = jnp.zeros_like(sums)
        for n, value in enumerate((wide(grad_outer), grad * normed, grad)):
            sums[n : n + 1, :] = column_sum(value)

    @pl.when(step > 0)
    def _():
        grad = low(dot_tn(act_block[0], outer_out[...]))
        for place, wanted in ((send, step < 3), (keep, step >= 3)):

            @pl.when(wanted)
            def _(place=place):
                for n in range(4):
                    place[0, n ^ (2 * (z & 1) + x)] = grad[192 * n : 192 * n + 192]


def middle_three_kernel(
    info, outer, second, slope, normed_one, inv_one, vec, inner_weight,
    o0, o1, o2, o3, w0, w1, w2, w3,
    first_out, gm0, gm1, go0, go1, inner_out, branch_out, sums,
    o_all, i_all, w_all, gc, o_sem, i_sem, w_sem,
):
    _, x, _, _, _, f = coords(info)
    copies = {}
    for e in range(4):
        columns = pl.ds(pl.multiple_of(D * (f ^ e), 128), D)
        copies["w", e] = pltpu.make_async_copy((w0, w1, w2, w3)[e], w_all.at[e], w_sem.at[e])
        copies["i", e] = pltpu.make_async_copy(
            inner_weight.at[:, columns], i_all.at[e], i_sem.at[e]
        )
        copies["w", e].start()
        copies["i", e].start()
    for n, ref in enumerate((o0, o1, o2, o3)):
        copies["o", n] = pltpu.make_async_copy(ref, o_all.at[n], o_sem.at[n])
        copies["o", n].start()
    sums[...] = jnp.zeros_like(sums)
    grad_hidden = second[...]
    for e in range(4):
        copies["w", e].wait()
        inner = low(dot_nt(outer[...], w_all[e]) * wide(slope[e]))
        inner_out[e] = inner
        sums[pl.ds(8 + (f ^ e), 1), :] = column_sum(wide(inner))
        copies["i", e].wait()
        grad_hidden = grad_hidden + dot_nt(inner, i_all[e])
    grad_first = norm_grad(grad_hidden, normed_one[...], inv_one[...], vec[3:4, :])
    first_out[...] = grad_first
    branch = low(grad_first)
    branch_out[...] = branch
    for n, value in enumerate((wide(branch), grad_hidden * normed_one[...], grad_hidden)):
        sums[n : n + 1, :] = column_sum(value)
    for n in range(4):
        copies["o", n].wait()
        gc[f ^ n] = low(dot_nt(branch, o_all[n]))
    for side, (one, two) in enumerate(((gm0, gm1), (go0, go1))):
        rows = jnp.concatenate([gc[2 * (x ^ side)], gc[2 * (x ^ side) + 1]], axis=1)
        one[...] = rows[:ROWS]
        two[...] = rows[ROWS:]


def middle_four_kernel(
    info, inner, hidden, branch, cm0, cm1, co0, co1, sums_one, sums_two,
    keep, send, held, out_held, vec_held,
):
    step = pl.program_id(0)
    _, x, _, _, _, f = coords(info)
    block = f ^ step

    @pl.when(step == 0)
    def _():
        for side, (one, two) in enumerate(((cm0, cm1), (co0, co1))):
            rows = jnp.concatenate([one[...], two[...]], axis=0)
            start = pl.multiple_of(HALF * (x ^ side), 128)
            out_held[pl.ds(start, HALF), :] = low(dot_tn(rows, branch[...]))
        vec_held[...] = jnp.zeros_like(vec_held)
        top = lax.broadcasted_iota(jnp.int32, (16, 1), 0) == 0
        for n in range(4):
            cut = slice(192 * n, 192 * n + 192)
            lines = (
                sums_two[8 + n : 9 + n, :],
                jnp.concatenate(
                    [sums_two[m : m + 1, cut] for m in range(3)] + [sums_one[0:1, cut]], axis=1
                ),
                jnp.concatenate(
                    [sums_one[1:2, cut], sums_one[2:3, cut], jnp.zeros((1, HALF), jnp.float32)],
                    axis=1,
                ),
            )
            for m, line in enumerate(lines):
                vec_held[m, n] = low(jnp.where(top, line, 0.0))

    held[...] = low(dot_tn(low(hidden[...]), inner[0]))
    for n in range(4):
        place = send if n % 2 else keep
        start = 192 * (f ^ n)
        place[n // 2, 0, :192, :] = held[pl.ds(pl.multiple_of(start, 64), 192), :]
        place[n // 2, 0, 192:240, :] = out_held[pl.ds(pl.multiple_of(start + 48 * block, 16), 48), :]
        place[n // 2, 0, 240:, :] = vec_held[block, f ^ n]


MIDDLE = 2 * ROWS
VMEM_LIMIT = 56 * 1024 * 1024
BF, FP = jnp.bfloat16, jnp.float32


def whole(shape):
    return pl.BlockSpec(tuple(shape), lambda *_: (0,) * len(shape))


def lane_block(rows, start=0):
    return pl.BlockSpec((rows, 128), lambda step, *_: (0, step + start))


def call(kernel, name, grid, scalars, operands, outs, scratch=(), work=(1, 1)):
    return pl.pallas_call(
        kernel,
        out_shape=[jax.ShapeDtypeStruct(shape, kind) for shape, kind, _ in outs],
        grid_spec=pltpu.PrefetchScalarGridSpec(
            num_scalar_prefetch=len(scalars),
            grid=(grid,),
            in_specs=[spec or whole(array.shape) for array, spec in operands],
            out_specs=[spec or whole(shape) for shape, _, spec in outs],
            scratch_shapes=list(scratch),
        ),
        compiler_params=pltpu.CompilerParams(
            dimension_semantics=("arbitrary",), vmem_limit_bytes=VMEM_LIMIT
        ),
        cost_estimate=pl.CostEstimate(
            flops=work[0] * 1_000_000_000, bytes_accessed=work[1] * 1_000_000, transcendentals=0
        ),
        name=name,
    )(*scalars, *[array for array, _ in operands])


def plain(arrays):
    return [(array, None) for array in arrays]


def anywhere(arrays):
    return [(array, pl.BlockSpec(memory_space=pl.ANY)) for array in arrays]


def probs_block(start=0):
    return pl.BlockSpec((2, 4 * ROWS, 8 * ROWS), lambda step, *_: (step + start, 0, 0))


def pack(info, lens, inputs, cotangent, weights, vectors):
    return call(
        pack_kernel, "pack", 1, (info, lens), plain([inputs, cotangent, *weights, *vectors]),
        [
            ((ROWS, D), BF, None), ((ROWS, D), BF, None), ((MIDDLE, D), BF, None),
            ((192, 3 * HALF), BF, None), ((16, D), BF, None),
        ],
        [pltpu.VMEM((16, D), FP)], (1, 4),
    )


def attend(info, blocks, pieces, small):
    return call(
        attend_kernel, "attend", 3, (info,), plain([*blocks, *pieces, *small]),
        [
            ((8 * ROWS, D), BF, None), ((D, 3 * HALF), BF, None), ((4 * ROWS, HALF), BF, None),
            ((8 * ROWS, HALF), BF, None), ((8 * ROWS, HALF), BF, None),
            ((6, 4 * ROWS, 8 * ROWS), BF, probs_block()),
        ]
        + [((ROWS, HALF), BF, lane_block(ROWS))] * 4,
        [pltpu.VMEM((1, 8 * ROWS), FP), pltpu.VMEM((4, 16, D), FP)], (10, 15),
    )


def attend_back(queries, keys, values, probs, grads):
    return call(
        attend_back_kernel, "attend_back", 2, (),
        [
            (queries, lane_block(4 * ROWS)), (keys, lane_block(8 * ROWS)),
            (values, lane_block(8 * ROWS)), (probs, probs_block()),
        ]
        + [(grad, lane_block(ROWS)) for grad in grads],
        [
            ((4 * ROWS, 256), BF, lane_block(4 * ROWS)),
            ((8 * ROWS, 256), BF, lane_block(8 * ROWS)),
            ((8 * ROWS, 256), BF, lane_block(8 * ROWS)),
        ],
        (), (8, 10),
    )


def attend_last(info, xs, ws, queries, keys, values, probs, grads, parts):
    joint = (2, 2, 112, 3 * HALF)
    return call(
        attend_last_kernel, "attend_last", 1, (info,),
        plain([xs, ws])
        + [
            (queries, lane_block(4 * ROWS, 2)), (keys, lane_block(8 * ROWS, 2)),
            (values, lane_block(8 * ROWS, 2)), (probs, probs_block(2)),
        ]
        + [(grad, lane_block(ROWS, 2)) for grad in grads]
        + plain(parts),
        [((4 * ROWS, D), FP, None), ((4 * ROWS, D), BF, None), (joint, BF, None), (joint, BF, None)],
        [
            pltpu.VMEM((4 * ROWS, HALF), BF), pltpu.VMEM((8 * ROWS, HALF), BF),
            pltpu.VMEM((8 * ROWS, HALF), BF), pltpu.VMEM((D, 3 * HALF), BF),
        ],
        (8, 10),
    )


def middle_one(info, ctx, rows, out_p, inner_weight, small):
    block = pl.BlockSpec((1, MIDDLE, D), lambda step, *_: (step, 0, 0))
    return call(
        middle_one_kernel, "middle_one", 4, (info,),
        plain([*ctx, *rows, *out_p])
        + [(inner_weight, pl.BlockSpec((D, D), lambda step, info: (0, (info[0] & 3) ^ step)))]
        + plain(small),
        [
            ((MIDDLE, D), FP, None), ((MIDDLE, D), FP, None), ((MIDDLE, 1), FP, None),
            ((4, MIDDLE, D), BF, block), ((4, MIDDLE, D), BF, block), ((8, D), FP, None),
        ],
        [
            pltpu.VMEM((4, MIDDLE, 192), BF), pltpu.VMEM((MIDDLE, D), BF),
            pltpu.VMEM((4, 16, D), FP), pltpu.VMEM((4, 16, D), FP),
        ],
        (4, 10),
    )


def middle_two(info, lens, act, hidden, cot, vec, outer_p):
    def turn(step, *_):
        at = jnp.maximum(step - 1, 0)
        return (jnp.where(at < 2, 2 * at + 1, 2 * at - 4), 0, 0)

    blocks = (2, 4, 192, D)
    return call(
        middle_two_kernel, "middle_two", 5, (info, lens),
        [(act, None), (act, pl.BlockSpec((1, MIDDLE, D), turn))]
        + plain([hidden, cot, vec])
        + anywhere(outer_p),
        [
            ((2, ROWS, D), BF, None), ((MIDDLE, D), FP, None), ((MIDDLE, D), BF, None),
            ((8, D), FP, None),
            (blocks, BF, pl.BlockSpec((1, 4, 192, D), lambda s, *_: (jnp.maximum(s - 3, 0), 0, 0, 0))),
            (blocks, BF, pl.BlockSpec((1, 4, 192, D), lambda s, *_: (jnp.where(s < 2, 0, 1), 0, 0, 0))),
        ],
        [pltpu.VMEM((4, D, D), BF), pltpu.SemaphoreType.DMA((4,))], (4, 10),
    )


def middle_three(info, outer, second, slope, normed, inv, vec, inner_weight, out_p, outer_p):
    return call(
        middle_three_kernel, "middle_three", 1, (info,),
        plain([outer, second, slope, normed, inv, vec]) + anywhere([inner_weight, *out_p, *outer_p]),
        [((MIDDLE, D), FP, None)]
        + [((ROWS, HALF), BF, None)] * 4
        + [((4, MIDDLE, D), BF, None), ((MIDDLE, D), BF, None), ((16, D), FP, None)],
        [
            pltpu.VMEM((4, 192, D), BF), pltpu.VMEM((4, D, D), BF), pltpu.VMEM((4, D, D), BF),
            pltpu.VMEM((4, MIDDLE, 192), BF), pltpu.SemaphoreType.DMA((4,)),
            pltpu.SemaphoreType.DMA((4,)), pltpu.SemaphoreType.DMA((4,)),
        ],
        (4, 14),
    )


def middle_four(info, inner, hidden, branch, ctx, sums):
    def spot(step, info):
        z, x, _, _, _, f = coords(info)
        return (0, f ^ step ^ (2 * x + (z & 1)), 0, 0)

    block = pl.BlockSpec((2, 1, 256, D), spot)
    return call(
        middle_four_kernel, "middle_four", 4, (info,),
        [(inner, pl.BlockSpec((1, MIDDLE, D), lambda step, *_: (step, 0, 0)))]
        + plain([hidden, branch, *ctx, *sums]),
        [((2, 4, 256, D), BF, block)] * 2,
        [pltpu.VMEM((D, D), BF), pltpu.VMEM((D, D), BF), pltpu.VMEM((4, 4, 16, D), BF)],
        (4, 8),
    )


def place_outer_kernel(info, p0, p1, p2, p3, out):
    z, x, _, _, _, _ = coords(info)
    for n, piece in enumerate((p0, p1, p2, p3)):
        out[pl.ds(pl.multiple_of(192 * (n ^ (2 * (z & 1) + x)), 64), 192), :] = wide(piece[...])


def place_inner_kernel(info, p0, p1, p2, p3, inner, out, vec):
    z, x, _, _, _, _ = coords(info)
    for n, piece in enumerate((p0, p1, p2, p3)):
        at = n ^ (2 * x + (z & 1))
        inner[:, pl.ds(pl.multiple_of(D * at, 128), D)] = wide(piece[:192, :])
        out[pl.ds(pl.multiple_of(48 * at, 16), 48), :] = wide(piece[192:240, :])
        vec[at] = wide(piece[240:, :])


def place_joint_kernel(info, p0, p1, p2, p3, query, key, value, vec):
    z, x, _, _, _, _ = coords(info)
    z_bit = z & 1
    for n, piece in enumerate((p0, p1, p2, p3)):
        rows = pl.ds(pl.multiple_of(96 * (n % 2 ^ z_bit), 32), 96)
        columns = pl.ds(pl.multiple_of(HALF * (n // 2 ^ x), 128), HALF)
        for m, out in enumerate((query, key, value)):
            out[rows, columns] = wide(piece[:96, HALF * m : HALF * m + HALF])
        vec[n // 2 ^ x, n % 2 ^ z_bit] = wide(piece[96:, :])


def placed(kernel, name, info, pieces, shapes):
    return call(
        kernel, name, 1, (info,), plain(pieces), [(shape, FP, None) for shape in shapes], (), (1, 6)
    )


def unshuffle(array, bit):
    return jnp.where(bit == 0, array, array[::-1])


def tied(values, *events):
    return lax.optimization_barrier((values, events))[0]


def z_level(low_half):
    one = low(wide(low_half) + wide(swap_z2(low_half)))
    return one


def fast_body(
    inputs, cotangent, lengths, w_query, b_query, w_key, w_value, b_value, w_output, b_output,
    gain_one, bias_one, w_inner, b_inner, w_outer, b_outer, gain_two, bias_two,
):
    info = lax.axis_index(("ctx", "fsdp")).astype(jnp.int32).reshape(1)
    f = lax.axis_index("fsdp")
    zh = lax.axis_index("ctx") // 4

    inner_weight = lax.all_gather(w_inner, "fsdp", axis=0, tiled=True)
    t0, t1, cot, w_x, small = pack(
        info, lengths, inputs, cotangent, (w_query, w_key, w_value),
        (b_query, b_value, b_output, gain_one, bias_one, b_outer, gain_two, bias_two, b_inner),
    )

    bu, bv = seq_send[0](t0), seq_send[1](t1)
    w_y, small_y, out_y = swap_y(w_x), swap_y(small), swap_y(tied(w_output, t0))
    bu, bv, small_y = tied((bu, bv, small_y))
    bxu, bxv = swap_x(bu), swap_x(bv)
    bku, bkv = swap_core(bu), swap_core(bv)
    bku, bkv, bxu, bxv, w_y, out_y = tied((bku, bkv, bxu, bxv, w_y, out_y))
    outer_y = swap_y(tied(w_outer, out_y))
    rest = [swap_core(b) for b in (bxu, bxv)] + [swap_core(tied(w_x, w_y)), swap_core(w_y)]
    rest, small_y = tied((rest, small_y))
    small_k, small_ky = swap_core(tied(small, rest)), swap_core(small_y)
    blocks = [bu, bv, bxu, bxv, bku, bkv, rest[0], rest[1]]
    qkv_p = [w_x, rest[2], w_y, rest[3]]
    smalls = [small, small_k, small_y, small_ky]

    xs, ws, queries, keys, values, probs, cu, cv, cxu, cxv = attend(info, blocks, qkv_p, smalls)

    cu, cv = seq_return[0](cu), seq_return[1](cv)
    cxu, cxv = swap_x(cxu), swap_x(cxv)
    cu, cv, cxu, cxv = tied((cu, cv, cxu, cxv))
    cxu, cxv = seq_return[0](cxu), seq_return[1](cxv)
    out_k, out_ky = swap_core(tied(w_output, cu)), swap_core(tied(out_y, cu))
    cxu, cxv, out_k, out_ky, outer_y = tied((cxu, cxv, out_k, out_ky, outer_y))
    ctx = [cu, cv, cxu, cxv]
    out_p = [w_output, out_k, out_y, out_ky]
    outer_k, outer_ky = swap_core(tied(w_outer, cxu)), swap_core(outer_y)

    hidden, normed, inv, act, slope, vec = middle_one(
        info, ctx, [t0, t1], out_p, inner_weight, smalls
    )
    outer_p = [w_outer, outer_k, outer_y, outer_ky]
    outputs, second, outer, sums_two, o_keep, o_send = middle_two(
        info, lengths, act, hidden, cot, vec, outer_p
    )
    o_came = swap_core(o_send)
    grad_first, gm0, gm1, go0, go1, inner, branch, sums_one = middle_three(
        info, outer, second, slope, normed, inv, vec, inner_weight, out_p, outer_p
    )
    go0, go1 = seq_send[0](go0), seq_send[1](go1)
    gm0, gm1 = seq_send[0](gm0), seq_send[1](gm1)
    o_far = low(wide(o_keep[1]) + wide(o_came[1]))
    o_near = wide(o_keep[0]) + wide(o_came[0])
    o_came = swap_y(o_far[2:])
    inner, o_far, o_near = tied((inner, o_far, o_near))
    i_keep, i_send = middle_four(info, inner, hidden, branch, ctx, (sums_two, sums_one))
    go0, go1, gm0, gm1, i_send, o_came = tied((go0, go1, gm0, gm1, i_send, o_came))
    go0, go1 = swap_x(go0), swap_x(go1)
    i_came = swap_core(i_send)
    o_zed = swap_z1(low(o_near[2:] + wide(o_came)))
    o_came = swap_y(tied(o_far[:2], o_came))
    go0, go1, i_came = tied((go0, go1, i_came))
    i_far = low(wide(i_keep[1, 2:]) + wide(i_came[1, 2:]))
    i_far2 = low(wide(i_keep[1, :2]) + wide(i_came[1, :2]))
    i_near = wide(i_keep[0]) + wide(i_came[0])
    grads, i_far, i_far2, i_near = tied(([gm0, gm1, go0, go1], i_far, i_far2, i_near))
    parts = attend_back(queries, keys, values, probs, grads)
    i_came = swap_y(i_far)
    parts, o_came, o_zed = tied((parts, o_came, o_zed))
    o_sum = o_near[:2] + wide(o_came) + wide(o_zed)
    o_came = swap_x(low(o_sum[1]))
    dx_own, dx_other, j_keep, j_send = attend_last(
        info, xs, ws, queries, keys, values, probs, grads, tied(parts, o_sum)
    )
    dx_own, dx_other, j_keep, j_send, o_came, i_came = tied(
        (dx_own, dx_other, j_keep, j_send, o_came, i_came)
    )
    dx_came, j_came = swap_core(dx_other), swap_core(j_send)
    i_sum = i_near[2:] + wide(i_came)
    o_sum = low(o_sum[0] + wide(o_came))
    i_came = swap_x(low(i_sum))
    i_came2 = swap_y(tied(i_far2, i_sum))
    o_came = swap_z2(o_sum)
    dx_came, j_came = tied((dx_came, j_came))
    dx = dx_own + wide(dx_came)
    j_far = low(wide(j_keep[1]) + wide(j_came[1]))
    j_near = wide(j_keep[0]) + wide(j_came[0])
    dx_came = swap_x(low(dx[2 * ROWS :]))
    i_came, i_came2, dx_came, o_came = tied((i_came, i_came2, dx_came, o_came))
    j_came = swap_y(tied(j_far, i_came2))
    o_sum = low(wide(o_sum) + wide(o_came))
    i_sum = i_near[:2] + wide(i_came2) + wide(i_came)
    dx = low(dx[: 2 * ROWS] + wide(dx_came))
    i_came = swap_z1(low(i_sum[1]))
    dx0, dx1 = seq_return[0](dx[:ROWS]), seq_return[1](dx[ROWS:])
    o_x = swap_x(o_sum)
    i_came, dx0, dx1, j_came, o_x = tied((i_came, dx0, dx1, j_came, o_x))
    i_sum = low(i_sum[0] + wide(i_came))
    j_sum = j_near + wide(j_came)
    input_grad = grad_first + wide(jnp.concatenate([dx0, dx1], axis=0))
    input_grad = unshuffle(input_grad.reshape(2, ROWS, D), zh)
    i_came = swap_z2(i_sum)
    j_came = swap_z1(low(j_sum[1]))
    o_z, o_zx = swap_z1(o_sum), swap_z1(o_x)
    j_came, i_came, o_z, o_zx = tied((j_came, i_came, o_z, o_zx))
    j_sum = low(j_sum[0] + wide(j_came))
    i_sum = low(wide(i_sum) + wide(i_came))
    (outer_grad,) = placed(place_outer_kernel, "place_outer", info, [o_sum, o_x, o_z, o_zx], [(D, D)])
    j_came = swap_z2(j_sum)
    i_z, i_x = swap_z1(i_sum), swap_x(i_sum)
    j_came, i_z, i_x = tied((j_came, i_z, i_x))
    j_sum = low(wide(j_sum) + wide(j_came))
    i_zx = swap_x(i_z)
    j_z, j_x = swap_z1(j_sum), swap_x(j_sum)
    j_z, j_x, i_zx = tied((j_z, j_x, i_zx))
    j_zx = swap_x(j_z)
    inner_grad, out_grad, lines = placed(
        place_inner_kernel, "place_inner", info, [i_sum, i_z, i_x, i_zx],
        [(192, 4 * D), (192, D), (4, 16, D)],
    )
    q_grad, k_grad, v_grad, joint_lines = placed(
        place_joint_kernel, "place_joint", info, [j_sum, j_z, j_x, j_zx],
        [(192, D)] * 3 + [(2, 2, 16, 3 * HALF)],
    )
    grad_b1 = lines[0, 0]
    grad_bo, grad_g1, grad_s1, grad_b2 = (lines[1, 0, 192 * n : 192 * n + 192] for n in range(4))
    grad_g2, grad_s2 = (lines[2, 0, 192 * n : 192 * n + 192] for n in range(2))
    joint_sums = joint_lines[:, 0, 0]

    def own(vector):
        return lax.dynamic_slice_in_dim(vector.reshape(D), f * 192, 192)

    grad_bq, grad_bv = own(joint_sums[:, :HALF]), own(joint_sums[:, 2 * HALF :])
    return (
        outputs, input_grad, q_grad, grad_bq, k_grad, v_grad, grad_bv, out_grad, grad_bo,
        grad_g1, grad_s1, inner_grad, grad_b1, outer_grad, grad_b2, grad_g2, grad_s2,
    )


def solution(mesh):
    placed = (
        P("fsdp", "ctx", None),
        P("fsdp", "ctx", None),
        P("fsdp"),
        P("fsdp", None),
        P("fsdp"),
        P("fsdp", None),
        P("fsdp", None),
        P("fsdp"),
        P("fsdp", None),
        P("fsdp"),
        P("fsdp"),
        P("fsdp"),
        P("fsdp", None),
        P("fsdp"),
        P("fsdp", None),
        P("fsdp"),
        P("fsdp"),
        P("fsdp"),
    )
    fast = dict(mesh.shape) == {"ctx": 8, "fsdp": 4}
    return jax.shard_map(
        fast_body if fast else body,
        mesh=mesh,
        in_specs=placed,
        out_specs=(
            P("fsdp", "ctx", None),
            P("fsdp", "ctx", None),
            P("fsdp", None),
            P("fsdp"),
            P("fsdp", None),
            P("fsdp", None),
            P("fsdp"),
            P("fsdp", None),
            P("fsdp"),
            P("fsdp"),
            P("fsdp"),
            P("fsdp", None),
            P("fsdp"),
            P("fsdp", None),
            P("fsdp"),
            P("fsdp"),
            P("fsdp"),
        ),
        check_vma=False,
    )
```

```python
from functools import partial

import jax
import jax.numpy as jnp
from jax import lax
from jax.experimental import pallas as pl
from jax.experimental.pallas import tpu as pltpu
from jax.sharding import PartitionSpec as P

D = 768
H = 12
HD = 64
SEQ_MB = 1
MICRO = 2


EPSILON = 1e-05
NEG_FILL = -1e30
SCALE = 0.125
ROOT_HALF = 0.7071067811865476
INV_ROOT_TAU = 0.3989422804014327
key_block = 512


def matmul(left_side, right_side):
    return jnp.dot(left_side, right_side, preferred_element_type=jnp.float32)


def left_product(left_side, right_side):
    return lax.dot_general(
        left_side, right_side, (((0,), (0,)), ((), ())), preferred_element_type=jnp.float32
    )


def right_product(left_side, right_side):
    return lax.dot_general(
        left_side, right_side, (((1,), (1,)), ((), ())), preferred_element_type=jnp.float32
    )


def split_heads(token_rows):
    return token_rows.reshape(token_rows.shape[0], token_rows.shape[1], H, HD)


def head_scores(query_rows, key_rows):
    return (
        jnp.einsum(
            "bqhd,bkhd->bhqk",
            split_heads(query_rows),
            split_heads(key_rows),
            preferred_element_type=jnp.float32,
        )
        * SCALE
    )


def live_mask(seq_lens, first_pos, num_rows):
    return (first_pos + lax.iota(jnp.int32, num_rows))[None, :] < seq_lens[:, None]


def layer_norm(resid, norm_gain, norm_bias):
    row_mean = jnp.mean(resid, axis=-1, keepdims=True)
    centered = resid - row_mean
    inv_std = lax.rsqrt(jnp.mean(centered * centered, axis=-1, keepdims=True) + EPSILON)
    normed = centered * inv_std
    return (normed * norm_gain + norm_bias, normed, inv_std)


def norm_back(grad_out, normed, inv_std, norm_gain):
    grad_norm = grad_out * norm_gain
    grad_in = inv_std * (
        grad_norm
        - jnp.mean(grad_norm, axis=-1, keepdims=True)
        - normed * jnp.mean(grad_norm * normed, axis=-1, keepdims=True)
    )
    return (grad_in, jnp.sum(grad_out * normed, axis=0), jnp.sum(grad_out, axis=0))


def gelu_exact(pre_act):
    return 0.5 * pre_act * (1.0 + lax.erf(pre_act * ROOT_HALF))


def gelu_slope(pre_act):
    return 0.5 * (1.0 + lax.erf(pre_act * ROOT_HALF)) + pre_act * INV_ROOT_TAU * jnp.exp(
        -0.5 * pre_act * pre_act
    )


def in_blocks(step_fn, running, pieces):
    num_rows = pieces[0].shape[1]

    def advance(block_index, current):
        offset = block_index * key_block
        sliced = tuple(
            (lax.dynamic_slice_in_dim(member, offset, key_block, 1) for member in pieces)
        )
        return step_fn(current, sliced, offset)

    return lax.fori_loop(0, num_rows // key_block, advance, running)


def attend_step(running, sliced, first_pos, queries, seq_lens, skip_empty):
    key_rows, value_rows = sliced
    live_keys = live_mask(seq_lens, first_pos, key_rows.shape[1])
    run_max, run_sum, run_out = running
    key_mask = live_keys[:, None, None, :]
    scores = jnp.where(key_mask, head_scores(queries, key_rows), NEG_FILL)
    new_max = jnp.maximum(run_max, jnp.max(scores, axis=-1))
    weights = jnp.where(key_mask, jnp.exp(scores - new_max[..., None]), 0.0)
    rescale = jnp.exp(run_max - new_max)
    new_sum = run_sum * rescale + jnp.sum(weights, axis=-1)
    new_out = run_out * rescale[..., None] + jnp.einsum(
        "bhqk,bkhd->bhqd",
        weights.astype(jnp.bfloat16),
        split_heads(value_rows),
        preferred_element_type=jnp.float32,
    )
    return (new_max, new_sum, new_out)


def query_grad_step(
    running,
    sliced,
    first_pos,
    queries,
    grad_context,
    log_total,
    row_delta,
    seq_lens,
    live_queries,
    skip_empty,
):
    key_rows, value_rows = sliced
    live_keys = live_mask(seq_lens, first_pos, key_rows.shape[1])
    key_mask = live_keys[:, None, None, :]
    probabilities = jnp.where(
        key_mask, jnp.exp(head_scores(queries, key_rows) - log_total[..., None]), 0.0
    )
    grad_probs = jnp.einsum(
        "bqhd,bkhd->bhqk",
        split_heads(grad_context),
        split_heads(value_rows),
        preferred_element_type=jnp.float32,
    )
    grad_scores = (probabilities * (grad_probs - row_delta[..., None])).astype(jnp.bfloat16)
    return running + jnp.einsum(
        "bhqk,bkhd->bqhd", grad_scores, split_heads(key_rows), preferred_element_type=jnp.float32
    )


def key_grad_step(
    running,
    sliced,
    first_pos,
    key_rows,
    value_rows,
    stat_total,
    stat_delta,
    seq_lens,
    live_keys,
    skip_empty,
):
    query_rows, grad_rows = sliced
    num_rows = query_rows.shape[1]
    grad_k, grad_v = running
    log_total = lax.dynamic_slice_in_dim(stat_total, first_pos, num_rows, 1).transpose(0, 2, 1)
    row_delta = lax.dynamic_slice_in_dim(stat_delta, first_pos, num_rows, 1).transpose(0, 2, 1)
    key_mask = live_keys[:, None, None, :]
    probabilities = jnp.where(
        key_mask, jnp.exp(head_scores(query_rows, key_rows) - log_total[..., None]), 0.0
    )
    grad_probs = jnp.einsum(
        "bqhd,bkhd->bhqk",
        split_heads(grad_rows),
        split_heads(value_rows),
        preferred_element_type=jnp.float32,
    )
    grad_scores = (probabilities * (grad_probs - row_delta[..., None])).astype(jnp.bfloat16)
    grad_v = grad_v + jnp.einsum(
        "bhqk,bqhd->bkhd",
        probabilities.astype(jnp.bfloat16),
        split_heads(grad_rows),
        preferred_element_type=jnp.float32,
    )
    grad_k = grad_k + jnp.einsum(
        "bhqk,bqhd->bkhd", grad_scores, split_heads(query_rows), preferred_element_type=jnp.float32
    )
    return (grad_k, grad_v)


def body(
    inputs,
    cotangent,
    lengths,
    w_query,
    b_query,
    w_key,
    w_value,
    b_value,
    w_output,
    b_output,
    gain_one,
    bias_one,
    w_inner,
    b_inner,
    w_outer,
    b_outer,
    gain_two,
    bias_two,
):
    gathered = (
        lax.all_gather(w_query, "fsdp", axis=0, tiled=True),
        lax.all_gather(b_query, "fsdp", axis=0, tiled=True),
        lax.all_gather(w_key, "fsdp", axis=0, tiled=True),
        lax.all_gather(w_value, "fsdp", axis=0, tiled=True),
        lax.all_gather(b_value, "fsdp", axis=0, tiled=True),
        lax.all_gather(w_output, "fsdp", axis=0, tiled=True),
        lax.all_gather(b_output, "fsdp", axis=0, tiled=True),
        lax.all_gather(gain_one, "fsdp", axis=0, tiled=True),
        lax.all_gather(bias_one, "fsdp", axis=0, tiled=True),
        lax.all_gather(w_inner, "fsdp", axis=0, tiled=True),
        lax.all_gather(b_inner, "fsdp", axis=0, tiled=True),
        lax.all_gather(w_outer, "fsdp", axis=0, tiled=True),
        lax.all_gather(b_outer, "fsdp", axis=0, tiled=True),
        lax.all_gather(gain_two, "fsdp", axis=0, tiled=True),
        lax.all_gather(bias_two, "fsdp", axis=0, tiled=True),
    )
    (
        query_weight,
        query_bias,
        key_weight,
        value_weight,
        value_bias,
        out_weight,
        out_bias,
        gain_first,
        shift_first,
        inner_weight,
        inner_bias,
        outer_weight,
        outer_bias,
        gain_second,
        shift_second,
    ) = gathered
    joint_weight = jnp.concatenate([query_weight, key_weight, value_weight], axis=1)
    joint_bias = jnp.concatenate(
        [
            query_bias.astype(jnp.float32),
            jnp.zeros((D,), jnp.float32),
            value_bias.astype(jnp.float32),
        ]
    )
    out_bias_f = out_bias.astype(jnp.float32)
    inner_bias_f = inner_bias.astype(jnp.float32)
    outer_bias_f = outer_bias.astype(jnp.float32)
    gain_first_f = gain_first.astype(jnp.float32)
    shift_first_f = shift_first.astype(jnp.float32)
    gain_second_f = gain_second.astype(jnp.float32)
    shift_second_f = shift_second.astype(jnp.float32)
    seq_dev = inputs.shape[1]
    row_count = SEQ_MB * seq_dev
    positions = lax.axis_index("ctx") * seq_dev + lax.iota(jnp.int32, seq_dev)
    accum = None
    out_list = []
    grad_list = []
    for micro_index in range(MICRO):
        first_seq = micro_index * SEQ_MB
        seq_lens = lengths[first_seq : first_seq + SEQ_MB]
        token_rows = inputs[first_seq : first_seq + SEQ_MB].reshape(row_count, D)
        grad_rows = (
            cotangent[first_seq : first_seq + SEQ_MB].reshape(row_count, D).astype(jnp.float32)
        )
        query_ok = positions[None, :] < seq_lens[:, None]
        row_keep = query_ok.reshape(row_count, 1).astype(jnp.float32)
        projected = (matmul(token_rows, joint_weight) + joint_bias).astype(jnp.bfloat16)
        queries = projected[:, :D].reshape(SEQ_MB, seq_dev, D)
        keys_local = projected[:, D : 2 * D].reshape(SEQ_MB, seq_dev, D)
        values_local = projected[:, 2 * D :].reshape(SEQ_MB, seq_dev, D)
        start_state = (
            jnp.full((SEQ_MB, H, seq_dev), NEG_FILL, jnp.float32),
            jnp.zeros((SEQ_MB, H, seq_dev), jnp.float32),
            jnp.zeros((SEQ_MB, H, seq_dev, HD), jnp.float32),
        )
        attend_fn = partial(attend_step, queries=queries, seq_lens=seq_lens, skip_empty=False)
        run_max, run_sum, run_out = in_blocks(
            attend_fn,
            start_state,
            (
                lax.all_gather(keys_local, "ctx", axis=1, tiled=True),
                lax.all_gather(values_local, "ctx", axis=1, tiled=True),
            ),
        )
        attended = run_out / run_sum[..., None]
        log_total = run_max + jnp.log(run_sum)
        context = attended.transpose(0, 2, 1, 3).reshape(row_count, D).astype(jnp.bfloat16)
        first_sum = token_rows.astype(jnp.float32) + matmul(context, out_weight) + out_bias_f
        hidden, normed_one, inv_one = layer_norm(first_sum, gain_first_f, shift_first_f)
        hidden_low = hidden.astype(jnp.bfloat16)
        inner_pre = matmul(hidden_low, inner_weight) + inner_bias_f
        activated = gelu_exact(inner_pre).astype(jnp.bfloat16)
        outer_out = matmul(activated, outer_weight) + outer_bias_f
        result, normed_two, inv_two = layer_norm(hidden + outer_out, gain_second_f, shift_second_f)
        out_list.append(result.astype(jnp.bfloat16).reshape(SEQ_MB, seq_dev, D))
        grad_out = grad_rows * row_keep
        grad_second, grad_gain_b, grad_shift_b = norm_back(
            grad_out, normed_two, inv_two, gain_second_f
        )
        grad_outer = grad_second.astype(jnp.bfloat16)
        grad_outer_w = left_product(activated, grad_outer)
        grad_outer_b = jnp.sum(grad_outer.astype(jnp.float32), axis=0)
        grad_inner = (right_product(grad_outer, outer_weight) * gelu_slope(inner_pre)).astype(
            jnp.bfloat16
        )
        grad_inner_w = left_product(hidden_low, grad_inner)
        grad_inner_b = jnp.sum(grad_inner.astype(jnp.float32), axis=0)
        grad_hidden = grad_second + right_product(grad_inner, inner_weight)
        grad_first, grad_gain_a, grad_shift_a = norm_back(
            grad_hidden, normed_one, inv_one, gain_first_f
        )
        grad_branch = grad_first.astype(jnp.bfloat16)
        grad_out_w = left_product(context, grad_branch)
        grad_out_b = jnp.sum(grad_branch.astype(jnp.float32), axis=0)
        grad_context = (
            right_product(grad_branch, out_weight).astype(jnp.bfloat16).reshape(SEQ_MB, seq_dev, D)
        )
        row_delta = jnp.einsum(
            "bqhd,bhqd->bhq", split_heads(grad_context).astype(jnp.float32), attended
        )
        stat_total, stat_delta = (
            lax.all_gather(log_total.transpose(0, 2, 1), "ctx", axis=1, tiled=True),
            lax.all_gather(row_delta.transpose(0, 2, 1), "ctx", axis=1, tiled=True),
        )
        query_fn = partial(
            query_grad_step,
            queries=queries,
            grad_context=grad_context,
            log_total=log_total,
            row_delta=row_delta,
            seq_lens=seq_lens,
            live_queries=query_ok,
            skip_empty=False,
        )
        key_fn = partial(
            key_grad_step,
            key_rows=keys_local,
            value_rows=values_local,
            stat_total=stat_total,
            stat_delta=stat_delta,
            seq_lens=seq_lens,
            live_keys=query_ok,
            skip_empty=False,
        )
        grad_zero = jnp.zeros((SEQ_MB, seq_dev, H, HD), jnp.float32)
        grad_q = in_blocks(
            query_fn,
            grad_zero,
            (
                lax.all_gather(keys_local, "ctx", axis=1, tiled=True),
                lax.all_gather(values_local, "ctx", axis=1, tiled=True),
            ),
        )
        grad_k, grad_v = in_blocks(
            key_fn,
            (grad_zero, grad_zero),
            (
                lax.all_gather(queries, "ctx", axis=1, tiled=True),
                lax.all_gather(grad_context, "ctx", axis=1, tiled=True),
            ),
        )
        joint_grad = jnp.concatenate(
            [
                (grad_q * SCALE).reshape(row_count, D).astype(jnp.bfloat16),
                (grad_k * SCALE).reshape(row_count, D).astype(jnp.bfloat16),
                grad_v.reshape(row_count, D).astype(jnp.bfloat16),
            ],
            axis=1,
        )
        grad_joint_w = left_product(token_rows, joint_grad)
        grad_joint_b = jnp.sum(joint_grad.astype(jnp.float32), axis=0)
        input_rows = grad_first + right_product(joint_grad, joint_weight)
        grad_list.append(input_rows.reshape(SEQ_MB, seq_dev, D))
        micro_grads = (
            grad_joint_w,
            grad_joint_b,
            grad_out_w,
            grad_out_b,
            grad_gain_a,
            grad_shift_a,
            grad_inner_w,
            grad_inner_b,
            grad_outer_w,
            grad_outer_b,
            grad_gain_b,
            grad_shift_b,
        )
        if accum is None:
            accum = micro_grads
        else:
            accum = tuple((held + fresh for held, fresh in zip(accum, micro_grads)))
    (
        joint_w,
        joint_b,
        out_w,
        out_b,
        gain_a,
        shift_a,
        inner_w,
        inner_b,
        outer_w,
        outer_b,
        gain_b,
        shift_b,
    ) = accum
    grad_set = (
        joint_w[:, :D],
        joint_b[:D],
        joint_w[:, D : 2 * D],
        joint_w[:, 2 * D :],
        joint_b[2 * D :],
        out_w,
        out_b,
        gain_a,
        shift_a,
        inner_w,
        inner_b,
        outer_w,
        outer_b,
        gain_b,
        shift_b,
    )
    shard_grads = (
        lax.psum_scatter(
            grad_set[0].astype(jnp.bfloat16), "fsdp", scatter_dimension=0, tiled=True
        ).astype(jnp.float32),
        lax.psum_scatter(
            grad_set[1].astype(jnp.bfloat16), "fsdp", scatter_dimension=0, tiled=True
        ).astype(jnp.float32),
        lax.psum_scatter(
            grad_set[2].astype(jnp.bfloat16), "fsdp", scatter_dimension=0, tiled=True
        ).astype(jnp.float32),
        lax.psum_scatter(
            grad_set[3].astype(jnp.bfloat16), "fsdp", scatter_dimension=0, tiled=True
        ).astype(jnp.float32),
        lax.psum_scatter(
            grad_set[4].astype(jnp.bfloat16), "fsdp", scatter_dimension=0, tiled=True
        ).astype(jnp.float32),
        lax.psum_scatter(
            grad_set[5].astype(jnp.bfloat16), "fsdp", scatter_dimension=0, tiled=True
        ).astype(jnp.float32),
        lax.psum_scatter(
            grad_set[6].astype(jnp.bfloat16), "fsdp", scatter_dimension=0, tiled=True
        ).astype(jnp.float32),
        lax.psum_scatter(
            grad_set[7].astype(jnp.bfloat16), "fsdp", scatter_dimension=0, tiled=True
        ).astype(jnp.float32),
        lax.psum_scatter(
            grad_set[8].astype(jnp.bfloat16), "fsdp", scatter_dimension=0, tiled=True
        ).astype(jnp.float32),
        lax.psum_scatter(
            grad_set[9].astype(jnp.bfloat16), "fsdp", scatter_dimension=0, tiled=True
        ).astype(jnp.float32),
        lax.psum_scatter(
            grad_set[10].astype(jnp.bfloat16), "fsdp", scatter_dimension=0, tiled=True
        ).astype(jnp.float32),
        lax.psum_scatter(
            grad_set[11].astype(jnp.bfloat16), "fsdp", scatter_dimension=0, tiled=True
        ).astype(jnp.float32),
        lax.psum_scatter(
            grad_set[12].astype(jnp.bfloat16), "fsdp", scatter_dimension=0, tiled=True
        ).astype(jnp.float32),
        lax.psum_scatter(
            grad_set[13].astype(jnp.bfloat16), "fsdp", scatter_dimension=0, tiled=True
        ).astype(jnp.float32),
        lax.psum_scatter(
            grad_set[14].astype(jnp.bfloat16), "fsdp", scatter_dimension=0, tiled=True
        ).astype(jnp.float32),
    )
    summed = lax.psum(
        (
            shard_grads[0],
            shard_grads[1],
            shard_grads[2],
            shard_grads[3],
            shard_grads[4],
            shard_grads[5],
            shard_grads[6],
            shard_grads[7],
            shard_grads[8],
            shard_grads[9],
            shard_grads[10],
            shard_grads[11],
            shard_grads[12],
            shard_grads[13],
            shard_grads[14],
        ),
        "ctx",
    )
    outputs = jnp.concatenate(out_list, axis=0)
    input_grad = jnp.concatenate(grad_list, axis=0)
    return (outputs, input_grad) + tuple(summed)


HALF = D // 2
ROWS = 128


def flat(z, x, y, k):
    return (z * 2 + x) * 4 + y * 2 + k


def table(move):
    return [
        (flat(z, x, y, k), flat(*move(z, x, y, k)))
        for z in range(4)
        for x in range(2)
        for y in range(2)
        for k in range(2)
    ]


def permute(move):
    pairs = table(move)
    return lambda block: lax.ppermute(block, ("ctx", "fsdp"), pairs)


def permute_back(move):
    pairs = [(b, a) for a, b in table(move)]
    return lambda block: lax.ppermute(block, ("ctx", "fsdp"), pairs)


def to_seq(turn):
    return lambda z, x, y, k: (2 * k + (z // 2 + turn) % 2, x, y, z % 2)


swap_core = permute(lambda z, x, y, k: (z, x, y, k ^ 1))
swap_y = permute(lambda z, x, y, k: (z, x, y ^ 1, k))
swap_x = permute(lambda z, x, y, k: (z, x ^ 1, y, k))
swap_z1 = permute(lambda z, x, y, k: (z ^ 1, x, y, k))
swap_z2 = permute(lambda z, x, y, k: (z ^ 2, x, y, k))
seq_send = (permute(to_seq(0)), permute(to_seq(1)))
seq_return = (permute_back(to_seq(0)), permute_back(to_seq(1)))


def low(value):
    return value.astype(jnp.bfloat16)


def wide(value):
    return value.astype(jnp.float32)


def pick(array, index, axis=0):
    return lax.dynamic_index_in_dim(array, index, axis, keepdims=False)


def dot_nt(a, b):
    return lax.dot_general(a, b, (((1,), (1,)), ((), ())), preferred_element_type=jnp.float32)


def dot_tn(a, b):
    return lax.dot_general(a, b, (((0,), (0,)), ((), ())), preferred_element_type=jnp.float32)


def coords(info):
    c, f = info[0] >> 2, info[0] & 3
    return c >> 1, c & 1, f >> 1, f & 1, c, f


def pack_kernel(
    info, lens, rows, grads, w_q, w_k, w_v, w_o, v0, v1, v2, v3, v4, v5, v6, v7, wide_vec,
    t0, t1, cot, first, held,
):
    z, x, _, _, _, _ = coords(info)
    zh = z >> 1
    t0[...] = rows[zh]
    t1[...] = rows[1 - zh]
    cot[:ROWS] = grads[zh]
    cot[ROWS:] = grads[1 - zh]
    columns = pl.ds(pl.multiple_of(x * HALF, 128), HALF)
    first[:192, :D] = w_o[...]
    for n, weight in enumerate((w_q, w_k, w_v)):
        first[:192, D + HALF * n : D + HALF * n + HALF] = weight[:, columns]
    held[...] = jnp.zeros_like(held)
    for n, vector in enumerate((v0, v1, v2, v3, v4, v5, v6, v7)):
        held[n : n + 1, :192] = wide(vector[...]).reshape(1, 192)
    held[8:9, :] = wide(wide_vec[...]).reshape(1, D)
    lane = lax.broadcasted_iota(jnp.int32, (1, D), 1)
    ends = jnp.zeros((1, D), jnp.int32)
    for n in range(2):
        ends = jnp.where(lane == n, lens[n] >> 7, ends)
        ends = jnp.where(lane == 2 + n, lens[n] & 127, ends)
    held[9:10, :] = wide(ends)
    first[192:, :D] = low(held[...])
    first[192:, D:] = jnp.zeros((16, 3 * HALF), jnp.bfloat16)


def attend_kernel(
    info, b0, b1, b2, b3, b4, b5, b6, b7, s0, s1, s2, s3, w0, w1, w2, w3,
    xs, ws, q_out, k_out, v_out, p_out, cu, cv, cx, key_bias, small, sems,
):
    step = pl.program_id(0)
    z, x, y, k, _, f = coords(info)

    @pl.when(step == 0)
    def _():
        copies = [
            pltpu.make_async_copy(
                piece.at[:192, D:], ws.at[pl.ds(pl.multiple_of(192 * (f ^ n), 64), 192), :], sems.at[n]
            )
            for n, piece in enumerate((w0, w1, w2, w3))
        ]
        for copy in copies:
            copy.start()
        for n, piece in enumerate((s0, s1, s2, s3)):
            small[f ^ n] = wide(piece[...])
        line = small[2 * y + (z >> 1)][9:10, :]
        lane = lax.broadcasted_iota(jnp.int32, (1, D), 1)
        part = jnp.where(lane == (z & 1), 128.0 * line, 0.0)
        part = part + jnp.where(lane == 2 + (z & 1), line, 0.0)
        end = jnp.sum(part, axis=1, keepdims=True)
        z_low = 2 * (z & 1)
        blocks = (b0, b1, b2, b3, b4, b5, b6, b7)
        for n, block in enumerate(blocks):
            z_block = (z_low if n % 2 == 0 else 2 - z_low) + (k if n < 4 else 1 - k)
            x_block = x if n % 4 < 2 else 1 - x
            xs[n * ROWS : (n + 1) * ROWS, :] = block[...]
            place = (2 * z_block + x_block) * ROWS + lax.broadcasted_iota(jnp.int32, (1, ROWS), 1)
            key_bias[:, n * ROWS : (n + 1) * ROWS] = jnp.where(wide(place) < end, 0.0, NEG_FILL)
        for copy in copies:
            copy.wait()

        def bias(row):
            return jnp.concatenate(
                [small[2 * x + n][row : row + 1, :192] for n in range(2)], axis=1
            )

        q_out[...] = low(wide(low(matmul(xs[: 4 * ROWS, :], ws[:, :HALF]) + bias(0))) * SCALE)
        k_out[...] = low(matmul(xs[...], ws[:, HALF : 2 * HALF]))
        v_out[...] = low(matmul(xs[...], ws[:, 2 * HALF :]) + bias(1))

    lanes = pl.ds(pl.multiple_of(step * 128, 128), 128)
    first = lax.broadcasted_iota(jnp.int32, (1, 128), 1) < HD
    queries = q_out[:, lanes]
    keys = k_out[:, lanes]
    values = v_out[:, lanes]
    for part in range(2):
        rows = slice(part * 256, part * 256 + 256)
        found = []
        for head in range(2):
            mine = first if head == 0 else jnp.logical_not(first)
            scores = dot_nt(jnp.where(mine, queries[rows], 0), keys) + key_bias[...]
            top = jnp.max(scores, axis=1, keepdims=True)
            weights = jnp.exp(scores - top)
            total = jnp.sum(weights, axis=1, keepdims=True)
            probs = low(weights * (1.0 / total))
            p_out[head, rows, :] = probs
            found.append(matmul(probs, values))
        context = low(jnp.where(first, found[0], found[1]))
        if part == 0:
            cu[...] = context[:ROWS]
            cv[...] = context[ROWS:]
        else:
            cx[0] = context[:ROWS]
            cx[1] = context[ROWS:]


def pair_back(queries_ref, keys, values, probs_ref, grads):
    first = lax.broadcasted_iota(jnp.int32, (1, 128), 1) < HD
    grad_k = jnp.zeros((8 * ROWS, 128), jnp.float32)
    grad_v = jnp.zeros((8 * ROWS, 128), jnp.float32)
    grad_qs = []
    for part in range(2):
        rows = slice(part * 256, part * 256 + 256)
        one, two = grads[2 * part : 2 * part + 2]
        grad_rows = jnp.concatenate([one[...], two[...]], axis=0)
        queries = queries_ref[rows, :]
        grad_q = jnp.zeros((256, 128), jnp.float32)
        for head in range(2):
            mine = first if head == 0 else jnp.logical_not(first)
            grad_mine = jnp.where(mine, grad_rows, 0)
            probs = probs_ref[head, rows, :]
            grad_probs = dot_nt(grad_mine, values)
            product = wide(probs) * grad_probs
            delta = jnp.sum(product, axis=1, keepdims=True)
            grad_scores = low(product - wide(probs) * delta)
            grad_q = grad_q + matmul(grad_scores, jnp.where(mine, keys, 0))
            grad_k = grad_k + dot_tn(grad_scores, jnp.where(mine, queries, 0))
            grad_v = grad_v + dot_tn(probs, grad_mine)
        grad_qs.append(low(grad_q * SCALE))
    return grad_qs, low(grad_k), low(grad_v)


def attend_back_kernel(queries, keys, values, probs, gu, gv, gxu, gxv, dq, dk, dv):
    grad_qs, dk[...], dv[...] = pair_back(
        queries, keys[...], values[...], probs, (gu, gv, gxu, gxv)
    )
    dq[:256, :], dq[256:, :] = grad_qs


def joint_kernel(
    info, xs, dq0, dq1, dq2, dk0, dk1, dk2, dv0, dv1, dv2, keep, send, grads, dw
):
    for n, (q, k, v) in enumerate(((dq0, dk0, dv0), (dq1, dk1, dv1), (dq2, dk2, dv2))):
        start = 128 * n
        grads[: 4 * ROWS, start : start + 128] = q[...]
        grads[:, HALF + start : HALF + start + 128] = k[...]
        grads[:, 2 * HALF + start : 2 * HALF + start + 128] = v[...]
    own = slice(0, 4 * ROWS)
    dw[:, :HALF] = low(dot_tn(xs[own, :], grads[own, :HALF]))
    dw[:, HALF:] = low(dot_tn(xs[...], grads[:, HALF:]))
    col_sums = jnp.concatenate(
        [
            column_sum(wide(grads[own, :HALF])),
            jnp.zeros((1, HALF), jnp.float32),
            column_sum(wide(grads[:, 2 * HALF :])),
        ],
        axis=1,
    )
    tail = low(jnp.where(lax.broadcasted_iota(jnp.int32, (16, 1), 0) == 0, col_sums, 0.0))
    z, _, _, _, _, f = coords(info)
    for n in range(4):
        place = send if n % 2 else keep
        for half in range(2):
            start = pl.multiple_of(192 * (f ^ n) + 96 * half, 32)
            place[n // 2, half ^ (z & 1), :96, :] = dw[pl.ds(start, 96), :]
            place[n // 2, half ^ (z & 1), 96:, :] = tail if half == 0 else tail * 0


def rows_back_kernel(
    ws, dq0, dq1, dq2, dk0, dk1, dk2, dv0, dv1, dv2, dx_own, dx_other, grads
):
    for n, (q, k, v) in enumerate(((dq0, dk0, dv0), (dq1, dk1, dv1), (dq2, dk2, dv2))):
        start = 128 * n
        grads[: 4 * ROWS, start : start + 128] = q[...]
        grads[:, HALF + start : HALF + start + 128] = k[...]
        grads[:, 2 * HALF + start : 2 * HALF + start + 128] = v[...]
    dx_other[...] = low(dot_nt(grads[4 * ROWS :, HALF:], ws[:, HALF:]))
    dx_own[...] = dot_nt(grads[: 4 * ROWS, :], ws[...])


def middle_one_kernel(
    info, cm0, cm1, co0, co1, x0, x1, o0, o1, o2, o3, i0, i1, i2, i3,
    hidden_out, normed_out, inv_out, act, slope, vec,
    ctx, low_rows, small, order, inner_weight, sems,
):
    step = pl.program_id(0)
    _, x, _, _, _, f = coords(info)

    def copy(e, n):
        return pltpu.make_async_copy(
            (i0, i1, i2, i3)[n].at[:, pl.ds(pl.multiple_of(D * (f ^ e), 128), D)],
            inner_weight.at[e, pl.ds(pl.multiple_of(192 * (f ^ n), 64), 192), :],
            sems.at[e, n],
        )

    @pl.when(step == 0)
    def _():
        for e in range(4):
            for n in range(4):
                copy(e, n).start()
        for n, piece in enumerate((o0, o1, o2, o3)):
            small[f ^ n] = wide(piece[192:, :])
            order[n] = wide(piece[192:, :])
        for n in range(8):
            vec[n : n + 1, :] = jnp.concatenate(
                [small[m][n : n + 1, :192] for m in range(4)], axis=1
            )
        for side, (one, two) in enumerate(((cm0, cm1), (co0, co1))):
            rows = jnp.concatenate([one[...], two[...]], axis=0)
            for part in range(2):
                ctx[2 * (x ^ side) + part] = rows[:, 192 * part : 192 * part + 192]
        total = wide(jnp.concatenate([x0[...], x1[...]], axis=0)) + vec[2:3, :]
        for n, piece in enumerate((o0, o1, o2, o3)):
            total = total + matmul(ctx[f ^ n], piece[:192, :])
        hidden, normed, inv = layer_norm(total, vec[3:4, :], vec[4:5, :])
        hidden_out[...] = hidden
        normed_out[...] = normed
        inv_out[...] = inv
        low_rows[...] = low(hidden)

    for n in range(4):
        copy(step, n).wait()
    pre = matmul(low_rows[...], inner_weight[step]) + order[step][8:9, :]
    bell = 0.5 * (1.0 + lax.erf(pre * ROOT_HALF))
    act[0] = low(pre * bell)
    slope[0] = low(bell + pre * INV_ROOT_TAU * jnp.exp(-0.5 * pre * pre))


def norm_grad(grad, normed, inv, gain):
    scaled = grad * gain
    return inv * (
        scaled
        - jnp.mean(scaled, axis=-1, keepdims=True)
        - normed * jnp.mean(scaled * normed, axis=-1, keepdims=True)
    )


def column_sum(value):
    return jnp.sum(value, axis=0, keepdims=True)


def outer_copies(refs, held, sems):
    w0, w1, y0, y1, ky0, ky1 = refs
    half = D // 2
    plan = [
        [(w0, held.at[0], 0)],
        [(w1, held.at[1], 1)],
        [(y0, held.at[2, :half], 2), (y1, held.at[2, half:], 3)],
        [(ky0, held.at[3, :half], 4), (ky1, held.at[3, half:], 5)],
    ]
    copies = [[pltpu.make_async_copy(a, b, sems.at[n]) for a, b, n in block] for block in plan]
    for block in copies:
        for copy in block:
            copy.start()
    return copies


def middle_two_kernel(
    info, lens, act, act_block, hidden, cot, vec, w0, w1, w2, w3, w4, w5,
    out, second_out, outer_out, sums, keep, send, w_all, w_sem,
):
    step = pl.program_id(0)
    z, x, _, _, c, f = coords(info)

    @pl.when(step == 0)
    def _():
        copies = outer_copies((w0, w1, w2, w3, w4, w5), w_all, w_sem)
        b_2, g_2, s_2 = vec[5:6, :], vec[6:7, :], vec[7:8, :]
        total = hidden[...] + b_2
        for n in range(4):
            for copy in copies[n]:
                copy.wait()
            total = total + matmul(act[n], w_all[n])
        result, normed, inv = layer_norm(total, g_2, s_2)
        zh = z >> 1
        out[zh] = low(result[:ROWS])
        out[1 - zh] = low(result[ROWS:])
        row = lax.broadcasted_iota(jnp.int32, (2 * ROWS, 1), 0)
        end = jnp.where(row < ROWS, lens[zh], lens[1 - zh] + ROWS)
        grad = wide(cot[...]) * jnp.where(row + c * ROWS < end, 1.0, 0.0)
        grad_second = norm_grad(grad, normed, inv, g_2)
        second_out[...] = grad_second
        grad_outer = low(grad_second)
        outer_out[...] = grad_outer
        sums[...] = jnp.zeros_like(sums)
        for n, value in enumerate((wide(grad_outer), grad * normed, grad)):
            sums[n : n + 1, :] = column_sum(value)

    @pl.when(step > 0)
    def _():
        grad = low(dot_tn(act_block[0], outer_out[...]))
        for place, wanted in ((send, step < 3), (keep, step >= 3)):

            @pl.when(wanted)
            def _(place=place):
                for n in range(4):
                    place[0, n ^ (2 * (z & 1) + x)] = grad[192 * n : 192 * n + 192]


def inner_back_kernel(
    info, outer, slope, w0, w1, w2, w3, w4, w5, inner_out, sums, w_all, sems
):
    f = info[0] & 3
    copies = outer_copies((w0, w1, w2, w3, w4, w5), w_all, sems)
    for e in range(4):
        for copy in copies[e]:
            copy.wait()
        inner = low(dot_nt(outer[...], w_all[e]) * wide(slope[e]))
        inner_out[e] = inner
        sums[pl.ds(f ^ e, 1), :] = column_sum(wide(inner))


def middle_three_kernel(
    info, second, inner, normed_one, inv_one, vec, o0, o1, o2, o3, i0, i1, i2, i3,
    first_out, gm0, gm1, go0, go1, branch_out, sums, o_all, i_all, gc, o_sem, i_sem,
):
    _, x, _, _, _, f = coords(info)
    copies = {}
    for e in range(4):
        columns = pl.ds(pl.multiple_of(D * (f ^ e), 128), D)
        for n, ref in enumerate((i0, i1, i2, i3)):
            rows = pl.ds(pl.multiple_of(192 * (f ^ n), 64), 192)
            copies["i", e, n] = pltpu.make_async_copy(
                ref.at[:, columns], i_all.at[e, rows, :], i_sem.at[e, n]
            )
            copies["i", e, n].start()
    for n, ref in enumerate((o0, o1, o2, o3)):
        copies["o", n] = pltpu.make_async_copy(ref.at[:192, :D], o_all.at[n], o_sem.at[n])
        copies["o", n].start()
    grad_hidden = second[...]
    for e in range(4):
        for n in range(4):
            copies["i", e, n].wait()
        grad_hidden = grad_hidden + dot_nt(inner[e], i_all[e])
    grad_first = norm_grad(grad_hidden, normed_one[...], inv_one[...], vec[3:4, :])
    first_out[...] = grad_first
    branch = low(grad_first)
    branch_out[...] = branch
    for n, value in enumerate((wide(branch), grad_hidden * normed_one[...], grad_hidden)):
        sums[n : n + 1, :] = column_sum(value)
    for n in range(4):
        copies["o", n].wait()
        gc[f ^ n] = low(dot_nt(branch, o_all[n]))
    for side, (one, two) in enumerate(((gm0, gm1), (go0, go1))):
        rows = jnp.concatenate([gc[2 * (x ^ side)], gc[2 * (x ^ side) + 1]], axis=1)
        one[...] = rows[:ROWS]
        two[...] = rows[ROWS:]


def middle_four_kernel(
    info, inner, hidden, branch, cm0, cm1, co0, co1, sums_two, sums_in, sums_one,
    keep, send, held, out_held, vec_held,
):
    step = pl.program_id(0)
    _, x, _, _, _, f = coords(info)
    block = f ^ step

    @pl.when(step == 0)
    def _():
        for side, (one, two) in enumerate(((cm0, cm1), (co0, co1))):
            rows = jnp.concatenate([one[...], two[...]], axis=0)
            start = pl.multiple_of(HALF * (x ^ side), 128)
            out_held[pl.ds(start, HALF), :] = low(dot_tn(rows, branch[...]))
        vec_held[...] = jnp.zeros_like(vec_held)
        top = lax.broadcasted_iota(jnp.int32, (16, 1), 0) == 0
        for n in range(4):
            cut = slice(192 * n, 192 * n + 192)
            lines = (
                sums_in[n : n + 1, :],
                jnp.concatenate(
                    [sums_one[m : m + 1, cut] for m in range(3)] + [sums_two[0:1, cut]], axis=1
                ),
                jnp.concatenate(
                    [sums_two[1:2, cut], sums_two[2:3, cut], jnp.zeros((1, HALF), jnp.float32)],
                    axis=1,
                ),
            )
            for m, line in enumerate(lines):
                vec_held[m, n] = low(jnp.where(top, line, 0.0))

    held[...] = low(dot_tn(low(hidden[...]), inner[0]))
    for n in range(4):
        place = send if n % 2 else keep
        start = 192 * (f ^ n)
        place[n // 2, 0, :192, :] = held[pl.ds(pl.multiple_of(start, 64), 192), :]
        place[n // 2, 0, 192:240, :] = out_held[pl.ds(pl.multiple_of(start + 48 * block, 16), 48), :]
        place[n // 2, 0, 240:, :] = vec_held[block, f ^ n]


MIDDLE = 2 * ROWS
VMEM_LIMIT = 56 * 1024 * 1024
BF, FP = jnp.bfloat16, jnp.float32


def whole(shape):
    return pl.BlockSpec(tuple(shape), lambda *_: (0,) * len(shape))


def lane_block(rows, start=0):
    return pl.BlockSpec((rows, 128), lambda step, *_: (0, step + start))


def call(kernel, name, grid, scalars, operands, outs, scratch=(), work=(1, 1)):
    return pl.pallas_call(
        kernel,
        out_shape=[jax.ShapeDtypeStruct(shape, kind) for shape, kind, _ in outs],
        grid_spec=pltpu.PrefetchScalarGridSpec(
            num_scalar_prefetch=len(scalars),
            grid=(grid,),
            in_specs=[spec or whole(array.shape) for array, spec in operands],
            out_specs=[spec or whole(shape) for shape, _, spec in outs],
            scratch_shapes=list(scratch),
        ),
        compiler_params=pltpu.CompilerParams(
            dimension_semantics=("arbitrary",), vmem_limit_bytes=VMEM_LIMIT
        ),
        cost_estimate=pl.CostEstimate(
            flops=1000, bytes_accessed=1000, transcendentals=0
        ),
        name=name,
    )(*scalars, *[array for array, _ in operands])


def plain(arrays):
    return [(array, None) for array in arrays]


def anywhere(arrays):
    return [(array, pl.BlockSpec(memory_space=pl.ANY)) for array in arrays]


def probs_block(start=0):
    return pl.BlockSpec((2, 4 * ROWS, 8 * ROWS), lambda step, *_: (step + start, 0, 0))


def pack(info, lens, inputs, cotangent, weights, vectors):
    return call(
        pack_kernel, "pack", 1, (info, lens), plain([inputs, cotangent, *weights, *vectors]),
        [
            ((ROWS, D), BF, None), ((ROWS, D), BF, None), ((MIDDLE, D), BF, None),
            ((208, D + 3 * HALF), BF, None),
        ],
        [pltpu.VMEM((16, D), FP)], (1, 4),
    )


def first_columns(pieces):
    return [(piece, pl.BlockSpec((208, D), lambda *_: (0, 0))) for piece in pieces]


def attend(info, blocks, pieces):
    return call(
        attend_kernel, "attend", 3, (info,),
        plain(blocks)
        + [(piece, pl.BlockSpec((16, D), lambda *_: (12, 0))) for piece in pieces]
        + anywhere(pieces),
        [
            ((8 * ROWS, D), BF, None), ((D, 3 * HALF), BF, None), ((4 * ROWS, HALF), BF, None),
            ((8 * ROWS, HALF), BF, None), ((8 * ROWS, HALF), BF, None),
            ((6, 4 * ROWS, 8 * ROWS), BF, probs_block()),
        ]
        + [((ROWS, HALF), BF, lane_block(ROWS))] * 2
        + [((2, ROWS, HALF), BF, pl.BlockSpec((2, ROWS, 128), lambda step, *_: (0, 0, step)))],
        [
            pltpu.VMEM((1, 8 * ROWS), FP), pltpu.VMEM((4, 16, D), FP),
            pltpu.SemaphoreType.DMA((4,)),
        ],
        (10, 15),
    )


def attend_back(queries, keys, values, probs, grads, start, pairs):
    return call(
        attend_back_kernel, "attend_back", pairs, (),
        [
            (queries, lane_block(4 * ROWS, start)), (keys, lane_block(8 * ROWS, start)),
            (values, lane_block(8 * ROWS, start)), (probs, probs_block(start)),
        ]
        + [(grad, lane_block(ROWS, start)) for grad in grads],
        [
            ((4 * ROWS, 128 * pairs), BF, lane_block(4 * ROWS)),
            ((8 * ROWS, 128 * pairs), BF, lane_block(8 * ROWS)),
            ((8 * ROWS, 128 * pairs), BF, lane_block(8 * ROWS)),
        ],
        (), (4 * pairs, 5 * pairs),
    )


def by_name(pairs):
    return [part for name in zip(*pairs) for part in name]


def joint_grads(info, xs, pairs):
    joint = (2, 2, 112, 3 * HALF)
    return call(
        joint_kernel, "joint_grads", 1, (info,), plain([xs, *by_name(pairs)]),
        [(joint, BF, None), (joint, BF, None)],
        [pltpu.VMEM((8 * ROWS, 3 * HALF), BF), pltpu.VMEM((D, 3 * HALF), BF)],
    )


def rows_back(ws, pairs):
    return call(
        rows_back_kernel, "rows_back", 1, (), plain([ws, *by_name(pairs)]),
        [((4 * ROWS, D), FP, None), ((4 * ROWS, D), BF, None)],
        [pltpu.VMEM((8 * ROWS, 3 * HALF), BF)],
    )


def middle_one(info, ctx, rows, out_p, inner_p):
    block = pl.BlockSpec((1, MIDDLE, D), lambda step, *_: (step, 0, 0))
    return call(
        middle_one_kernel, "middle_one", 4, (info,),
        plain([*ctx, *rows]) + first_columns(out_p) + anywhere(inner_p),
        [
            ((MIDDLE, D), FP, None), ((MIDDLE, D), FP, None), ((MIDDLE, 1), FP, None),
            ((4, MIDDLE, D), BF, block), ((4, MIDDLE, D), BF, block), ((8, D), FP, None),
        ],
        [
            pltpu.VMEM((4, MIDDLE, 192), BF), pltpu.VMEM((MIDDLE, D), BF),
            pltpu.VMEM((4, 16, D), FP), pltpu.VMEM((4, 16, D), FP), pltpu.VMEM((4, D, D), BF),
            pltpu.SemaphoreType.DMA((4, 4)),
        ],
        (4, 10),
    )


def middle_two(info, lens, act, hidden, cot, vec, outer_p):
    def turn(step, *_):
        at = jnp.maximum(step - 1, 0)
        return (jnp.where(at < 2, 2 * at + 1, 2 * at - 4), 0, 0)

    blocks = (2, 4, 192, D)
    return call(
        middle_two_kernel, "middle_two", 5, (info, lens),
        [(act, None), (act, pl.BlockSpec((1, MIDDLE, D), turn))]
        + plain([hidden, cot, vec])
        + anywhere(outer_p),
        [
            ((2, ROWS, D), BF, None), ((MIDDLE, D), FP, None), ((MIDDLE, D), BF, None),
            ((8, D), FP, None),
            (blocks, BF, pl.BlockSpec((1, 4, 192, D), lambda s, *_: (jnp.maximum(s - 3, 0), 0, 0, 0))),
            (blocks, BF, pl.BlockSpec((1, 4, 192, D), lambda s, *_: (jnp.where(s < 2, 0, 1), 0, 0, 0))),
        ],
        [pltpu.VMEM((4, D, D), BF), pltpu.SemaphoreType.DMA((6,))], (4, 10),
    )


def inner_back(info, outer, slope, outer_p):
    return call(
        inner_back_kernel, "inner_back", 1, (info,), plain([outer, slope]) + anywhere(outer_p),
        [((4, MIDDLE, D), BF, None), ((4, D), FP, None)],
        [pltpu.VMEM((4, D, D), BF), pltpu.SemaphoreType.DMA((6,))], (2, 7),
    )


def middle_three(info, second, inner, normed, inv, vec, out_p, inner_p):
    return call(
        middle_three_kernel, "middle_three", 1, (info,),
        plain([second, inner, normed, inv, vec]) + anywhere([*out_p, *inner_p]),
        [((MIDDLE, D), FP, None)]
        + [((ROWS, HALF), BF, None)] * 4
        + [((MIDDLE, D), BF, None), ((8, D), FP, None)],
        [
            pltpu.VMEM((4, 192, D), BF), pltpu.VMEM((4, D, D), BF),
            pltpu.VMEM((4, MIDDLE, 192), BF), pltpu.SemaphoreType.DMA((4,)),
            pltpu.SemaphoreType.DMA((4, 4)),
        ],
        (2, 7),
    )


def middle_four(info, inner, hidden, branch, ctx, sums):
    def spot(step, info):
        z, x, _, _, _, f = coords(info)
        return (0, f ^ step ^ (2 * x + (z & 1)), 0, 0)

    block = pl.BlockSpec((2, 1, 256, D), spot)
    return call(
        middle_four_kernel, "middle_four", 4, (info,),
        [(inner, pl.BlockSpec((1, MIDDLE, D), lambda step, *_: (step, 0, 0)))]
        + plain([hidden, branch, *ctx, *sums]),
        [((2, 4, 256, D), BF, block)] * 2,
        [pltpu.VMEM((D, D), BF), pltpu.VMEM((D, D), BF), pltpu.VMEM((4, 4, 16, D), BF)],
        (4, 8),
    )


def place_outer_kernel(info, p0, p1, p2, p3, out):
    z, x, _, _, _, _ = coords(info)
    for n, piece in enumerate((p0, p1, p2, p3)):
        out[pl.ds(pl.multiple_of(192 * (n ^ (2 * (z & 1) + x)), 64), 192), :] = wide(piece[...])


def place_inner_kernel(
    info, p0, p1, p2, p3, inner, out, b_in, b_out, g_one, s_one, b_two, g_two, s_two, held
):
    z, x, _, _, _, _ = coords(info)
    for n, piece in enumerate((p0, p1, p2, p3)):
        at = n ^ (2 * x + (z & 1))
        inner[:, pl.ds(pl.multiple_of(D * at, 128), D)] = wide(piece[:192, :])
        out[pl.ds(pl.multiple_of(48 * at, 16), 48), :] = wide(piece[192:240, :])
        held[at] = wide(piece[240:, :])
    b_in[...] = held[0][0:1, :].reshape(D)
    for n, vector in enumerate((b_out, g_one, s_one, b_two, g_two, s_two)):
        cut = 192 * (n % 4)
        vector[...] = held[1 + n // 4][0:1, cut : cut + 192].reshape(192)


def place_joint_kernel(info, p0, p1, p2, p3, query, key, value, b_query, b_value, held):
    z, x, _, _, _, f = coords(info)
    z_bit = z & 1
    for n, piece in enumerate((p0, p1, p2, p3)):
        rows = pl.ds(pl.multiple_of(96 * (n % 2 ^ z_bit), 32), 96)
        columns = pl.ds(pl.multiple_of(HALF * (n // 2 ^ x), 128), HALF)
        for m, out in enumerate((query, key, value)):
            out[rows, columns] = wide(piece[:96, HALF * m : HALF * m + HALF])
        line = wide(piece[96:, :])
        line = jnp.where(f & 1 == 0, line, jnp.concatenate([line[:, 192:], line[:, :192]], axis=1))
        held[n // 2 ^ x, n % 2 ^ z_bit] = line
    mine = held[f >> 1, 0][0:1, :]
    b_query[...] = mine[:, :192].reshape(192)
    b_value[...] = mine[:, 2 * HALF : 2 * HALF + 192].reshape(192)


def placed(kernel, name, info, pieces, shapes, held=()):
    return call(
        kernel, name, 1, (info,), plain(pieces), [(shape, FP, None) for shape in shapes],
        [pltpu.VMEM(shape, FP) for shape in held], (1, 6),
    )


def unshuffle(array, bit):
    return jnp.where(bit == 0, array, array[::-1])


def tied(values, *events):
    return lax.optimization_barrier((values, events))[0]


def fast_body(
    inputs, cotangent, lengths, w_query, b_query, w_key, w_value, b_value, w_output, b_output,
    gain_one, bias_one, w_inner, b_inner, w_outer, b_outer, gain_two, bias_two,
):
    info = lax.axis_index(("ctx", "fsdp")).astype(jnp.int32).reshape(1)
    zh = lax.axis_index("ctx") // 4

    t0, t1, cot, first = pack(
        info, lengths, inputs, cotangent, (w_query, w_key, w_value, w_output),
        (b_query, b_value, b_output, gain_one, bias_one, b_outer, gain_two, bias_two, b_inner),
    )

    bu, bv = seq_send[0](t0), seq_send[1](t1)
    first_y, first_k = swap_y(first), swap_core(first)
    bu, bv, first_k = tied((bu, bv, first_k))
    bxu, bxv, bku = swap_x(bu), swap_x(bv), swap_core(bu)
    inner_y = swap_y(tied(w_inner, bu))
    bxu, bxv, bku, first_y = tied((bxu, bxv, bku, first_y))
    w_cut = w_outer.reshape(2, D // 2, D)
    outer_y1 = swap_y(tied(w_cut[0], first_y))
    bkv, *rest = [swap_core(b) for b in (bv, bxu, bxv, first_y)]
    bkv, *rest = tied([bkv] + rest)
    blocks = [bu, bv, bxu, bxv, bku, bkv, *rest[:2]]
    first_p = [first, first_k, first_y, rest[2]]
    xs, ws, queries, keys, values, probs, cu, cv, cx = attend(info, blocks, first_p)

    cu, cv = seq_return[0](cu), seq_return[1](cv)
    cx = swap_x(cx)
    cu, cv, cx, inner_y, outer_y1 = tied((cu, cv, cx, inner_y, outer_y1))
    outer_y2 = swap_y(tied(w_cut[1], outer_y1))
    cxu, cxv = seq_return[0](cx[0]), seq_return[1](cx[1])
    inner_k, inner_ky = swap_core(tied(w_inner, cx)), swap_core(inner_y)
    cxu, cxv, inner_k, inner_ky, outer_y2 = tied((cxu, cxv, inner_k, inner_ky, outer_y2))
    ctx = [cu, cv, cxu, cxv]
    inner_p = [w_inner, inner_k, inner_y, inner_ky]
    outer_k = swap_core(tied(w_outer, cxu))
    outer_ky1, outer_ky2 = swap_core(tied(outer_y1, cxu)), swap_core(outer_y2)
    hidden, normed, inv, act, slope, vec = middle_one(info, ctx, [t0, t1], first_p, inner_p)
    act, outer_k, outer_ky1, outer_ky2 = tied((act, outer_k, outer_ky1, outer_ky2))
    outer_p = [w_outer, outer_k, outer_y1, outer_y2, outer_ky1, outer_ky2]
    outputs, second_grad, outer, sums_two, o_keep, o_send = middle_two(
        info, lengths, act, hidden, cot, vec, outer_p
    )
    o_came = swap_core(o_send)
    inner, sums_in = inner_back(info, outer, slope, outer_p)
    o_came, inner = tied((o_came, inner))
    o_far = low(wide(o_keep[1]) + wide(o_came[1]))
    o_near = wide(o_keep[0]) + wide(o_came[0])
    inner, o_far, o_near = tied((inner, o_far, o_near))
    o_came = swap_y(o_far[1:])
    grad_first, gm0, gm1, go0, go1, branch, sums_one = middle_three(
        info, second_grad, inner, normed, inv, vec, first_p, inner_p
    )
    go0, go1 = seq_send[0](go0), seq_send[1](go1)
    gm0, gm1 = seq_send[0](gm0), seq_send[1](gm1)
    i_keep, i_send = middle_four(
        info, inner, hidden, branch, ctx, (sums_two, sums_in, sums_one)
    )
    go0, go1, gm0, gm1, i_send, o_came = tied((go0, go1, gm0, gm1, i_send, o_came))
    go0, go1 = swap_x(go0), swap_x(go1)
    i_came = swap_core(i_send)
    o_zed = swap_z1(low(o_near[2:] + wide(o_came[1:])))
    o_last = swap_y(tied(o_far[:1], o_came))
    go0, go1, i_came, o_last = tied((go0, go1, i_came, o_last))
    i_far = low(wide(i_keep[1, 2:]) + wide(i_came[1, 2:]))
    i_far2 = low(wide(i_keep[1, :2]) + wide(i_came[1, :2]))
    i_near = wide(i_keep[0]) + wide(i_came[0])
    grads, i_far, i_far2, i_near = tied(([gm0, gm1, go0, go1], i_far, i_far2, i_near))
    i_came = swap_y(i_far)
    pair_0 = attend_back(queries, keys, values, probs, grads, 0, 1)
    pair_0, o_zed = tied((pair_0, o_zed))
    o_one = o_near[1] + wide(o_came[0]) + wide(o_zed[1])
    o_sum = o_near[0] + wide(o_last[0]) + wide(o_zed[0])
    o_came = swap_x(low(o_one))
    pair_1 = attend_back(tied(queries, o_one), keys, values, probs, grads, 1, 1)
    pair_1, o_came, i_came = tied((pair_1, o_came, i_came))
    o_sum = low(o_sum + wide(o_came))
    i_sum = i_near[2:] + wide(i_came)
    o_came = swap_z2(o_sum)
    i_came = swap_x(low(i_sum))
    i_came2 = swap_y(tied(i_far2, i_sum))
    pair_2 = attend_back(tied(queries, o_sum, i_sum), keys, values, probs, grads, 2, 1)
    pairs = (pair_0, pair_1, pair_2)
    dx_own, dx_other = rows_back(ws, pairs)
    j_keep, j_send = joint_grads(info, tied(xs, dx_other), pairs)
    dx_own, dx_other, j_keep, j_send, i_came, i_came2, o_came = tied(
        (dx_own, dx_other, j_keep, j_send, i_came, i_came2, o_came)
    )
    j_came, dx_came = swap_core(j_send), swap_core(dx_other)
    o_sum = low(wide(o_sum) + wide(o_came))
    i_sum = i_near[:2] + wide(i_came2) + wide(i_came)
    j_came, dx_came, o_sum, i_sum = tied((j_came, dx_came, o_sum, i_sum))
    j_far = low(wide(j_keep[1]) + wide(j_came[1]))
    j_near = wide(j_keep[0]) + wide(j_came[0])
    dx = dx_own[: 2 * ROWS] + wide(dx_came[: 2 * ROWS])
    dx_send = low(dx_own[2 * ROWS :] + wide(dx_came[2 * ROWS :]))
    j_came = swap_y(j_far)
    i_came = swap_z1(low(i_sum[1]))
    dx_came = swap_x(dx_send)
    j_came, i_came, dx_came = tied((j_came, i_came, dx_came))
    j_sum = j_near + wide(j_came)
    i_sum = low(i_sum[0] + wide(i_came))
    dx = low(dx + wide(dx_came))
    j_came = swap_z1(low(j_sum[1]))
    i_came = swap_z2(i_sum)
    o_x = swap_x(tied(o_sum, i_sum))
    j_came, o_x = tied((j_came, o_x))
    j_sum = low(j_sum[0] + wide(j_came))
    j_came = swap_z2(j_sum)
    o_z, o_zx = swap_z1(tied(o_sum, j_sum)), swap_z1(tied(o_x, j_sum))
    i_came, o_z, o_zx = tied((i_came, o_z, o_zx))
    i_sum = low(wide(i_sum) + wide(i_came))
    i_z, i_x = swap_z1(i_sum), swap_x(i_sum)
    j_came, i_sum = tied((j_came, i_sum))
    j_sum = low(wide(j_sum) + wide(j_came))
    j_x, j_z = swap_x(j_sum), swap_z1(j_sum)
    (outer_grad,) = placed(
        place_outer_kernel, "place_outer", info, tied([o_sum, o_x, o_z, o_zx], j_sum), [(D, D)]
    )
    i_z, i_x, j_x, j_z, outer_grad = tied((i_z, i_x, j_x, j_z, outer_grad))
    i_zx, j_zx = swap_x(i_z), swap_z1(j_x)
    dx0, dx1 = seq_return[0](tied(dx[:ROWS], i_z)), seq_return[1](tied(dx[ROWS:], i_z))
    input_grad = grad_first + wide(jnp.concatenate([dx0, dx1], axis=0))
    input_grad = unshuffle(input_grad.reshape(2, ROWS, D), zh)
    inner_grad, out_grad, grad_b1, grad_bo, grad_g1, grad_s1, grad_b2, grad_g2, grad_s2 = placed(
        place_inner_kernel, "place_inner", info, [i_sum, i_z, i_x, i_zx],
        [(192, 4 * D), (192, D), (D,)] + [(192,)] * 6, [(4, 16, D)],
    )
    q_grad, k_grad, v_grad, grad_bq, grad_bv = placed(
        place_joint_kernel, "place_joint", info, [j_sum, j_z, j_x, j_zx],
        [(192, D)] * 3 + [(192,)] * 2, [(2, 2, 16, 3 * HALF)],
    )
    return (
        outputs, input_grad, q_grad, grad_bq, k_grad, v_grad, grad_bv, out_grad, grad_bo,
        grad_g1, grad_s1, inner_grad, grad_b1, outer_grad, grad_b2, grad_g2, grad_s2,
    )


def solution(mesh):
    placed = (
        P("fsdp", "ctx", None),
        P("fsdp", "ctx", None),
        P("fsdp"),
        P("fsdp", None),
        P("fsdp"),
        P("fsdp", None),
        P("fsdp", None),
        P("fsdp"),
        P("fsdp", None),
        P("fsdp"),
        P("fsdp"),
        P("fsdp"),
        P("fsdp", None),
        P("fsdp"),
        P("fsdp", None),
        P("fsdp"),
        P("fsdp"),
        P("fsdp"),
    )
    fast = dict(mesh.shape) == {"ctx": 8, "fsdp": 4}
    return jax.shard_map(
        fast_body if fast else body,
        mesh=mesh,
        in_specs=placed,
        out_specs=(
            P("fsdp", "ctx", None),
            P("fsdp", "ctx", None),
            P("fsdp", None),
            P("fsdp"),
            P("fsdp", None),
            P("fsdp", None),
            P("fsdp"),
            P("fsdp", None),
            P("fsdp"),
            P("fsdp"),
            P("fsdp"),
            P("fsdp", None),
            P("fsdp"),
            P("fsdp", None),
            P("fsdp"),
            P("fsdp"),
            P("fsdp"),
        ),
        check_vma=False,
    )
```

```python
from functools import partial

import jax
import jax.numpy as jnp
from jax import lax
from jax.experimental import pallas as pl
from jax.experimental.pallas import tpu as pltpu
from jax.sharding import PartitionSpec as P

D = 768
H = 12
HD = 64
SEQ_MB = 1
MICRO = 2


EPSILON = 1e-05
NEG_FILL = -1e30
SCALE = 0.125
ROOT_HALF = 0.7071067811865476
INV_ROOT_TAU = 0.3989422804014327
key_block = 512


def matmul(left_side, right_side):
    return jnp.dot(left_side, right_side, preferred_element_type=jnp.float32)


def left_product(left_side, right_side):
    return lax.dot_general(
        left_side, right_side, (((0,), (0,)), ((), ())), preferred_element_type=jnp.float32
    )


def right_product(left_side, right_side):
    return lax.dot_general(
        left_side, right_side, (((1,), (1,)), ((), ())), preferred_element_type=jnp.float32
    )


def split_heads(token_rows):
    return token_rows.reshape(token_rows.shape[0], token_rows.shape[1], H, HD)


def head_scores(query_rows, key_rows):
    return (
        jnp.einsum(
            "bqhd,bkhd->bhqk",
            split_heads(query_rows),
            split_heads(key_rows),
            preferred_element_type=jnp.float32,
        )
        * SCALE
    )


def live_mask(seq_lens, first_pos, num_rows):
    return (first_pos + lax.iota(jnp.int32, num_rows))[None, :] < seq_lens[:, None]


def layer_norm(resid, norm_gain, norm_bias):
    row_mean = jnp.mean(resid, axis=-1, keepdims=True)
    centered = resid - row_mean
    inv_std = lax.rsqrt(jnp.mean(centered * centered, axis=-1, keepdims=True) + EPSILON)
    normed = centered * inv_std
    return (normed * norm_gain + norm_bias, normed, inv_std)


def norm_back(grad_out, normed, inv_std, norm_gain):
    grad_norm = grad_out * norm_gain
    grad_in = inv_std * (
        grad_norm
        - jnp.mean(grad_norm, axis=-1, keepdims=True)
        - normed * jnp.mean(grad_norm * normed, axis=-1, keepdims=True)
    )
    return (grad_in, jnp.sum(grad_out * normed, axis=0), jnp.sum(grad_out, axis=0))


def gelu_exact(pre_act):
    return 0.5 * pre_act * (1.0 + lax.erf(pre_act * ROOT_HALF))


def gelu_slope(pre_act):
    return 0.5 * (1.0 + lax.erf(pre_act * ROOT_HALF)) + pre_act * INV_ROOT_TAU * jnp.exp(
        -0.5 * pre_act * pre_act
    )


def in_blocks(step_fn, running, pieces):
    num_rows = pieces[0].shape[1]

    def advance(block_index, current):
        offset = block_index * key_block
        sliced = tuple(
            (lax.dynamic_slice_in_dim(member, offset, key_block, 1) for member in pieces)
        )
        return step_fn(current, sliced, offset)

    return lax.fori_loop(0, num_rows // key_block, advance, running)


def attend_step(running, sliced, first_pos, queries, seq_lens, skip_empty):
    key_rows, value_rows = sliced
    live_keys = live_mask(seq_lens, first_pos, key_rows.shape[1])
    run_max, run_sum, run_out = running
    key_mask = live_keys[:, None, None, :]
    scores = jnp.where(key_mask, head_scores(queries, key_rows), NEG_FILL)
    new_max = jnp.maximum(run_max, jnp.max(scores, axis=-1))
    weights = jnp.where(key_mask, jnp.exp(scores - new_max[..., None]), 0.0)
    rescale = jnp.exp(run_max - new_max)
    new_sum = run_sum * rescale + jnp.sum(weights, axis=-1)
    new_out = run_out * rescale[..., None] + jnp.einsum(
        "bhqk,bkhd->bhqd",
        weights.astype(jnp.bfloat16),
        split_heads(value_rows),
        preferred_element_type=jnp.float32,
    )
    return (new_max, new_sum, new_out)


def query_grad_step(
    running,
    sliced,
    first_pos,
    queries,
    grad_context,
    log_total,
    row_delta,
    seq_lens,
    live_queries,
    skip_empty,
):
    key_rows, value_rows = sliced
    live_keys = live_mask(seq_lens, first_pos, key_rows.shape[1])
    key_mask = live_keys[:, None, None, :]
    probabilities = jnp.where(
        key_mask, jnp.exp(head_scores(queries, key_rows) - log_total[..., None]), 0.0
    )
    grad_probs = jnp.einsum(
        "bqhd,bkhd->bhqk",
        split_heads(grad_context),
        split_heads(value_rows),
        preferred_element_type=jnp.float32,
    )
    grad_scores = (probabilities * (grad_probs - row_delta[..., None])).astype(jnp.bfloat16)
    return running + jnp.einsum(
        "bhqk,bkhd->bqhd", grad_scores, split_heads(key_rows), preferred_element_type=jnp.float32
    )


def key_grad_step(
    running,
    sliced,
    first_pos,
    key_rows,
    value_rows,
    stat_total,
    stat_delta,
    seq_lens,
    live_keys,
    skip_empty,
):
    query_rows, grad_rows = sliced
    num_rows = query_rows.shape[1]
    grad_k, grad_v = running
    log_total = lax.dynamic_slice_in_dim(stat_total, first_pos, num_rows, 1).transpose(0, 2, 1)
    row_delta = lax.dynamic_slice_in_dim(stat_delta, first_pos, num_rows, 1).transpose(0, 2, 1)
    key_mask = live_keys[:, None, None, :]
    probabilities = jnp.where(
        key_mask, jnp.exp(head_scores(query_rows, key_rows) - log_total[..., None]), 0.0
    )
    grad_probs = jnp.einsum(
        "bqhd,bkhd->bhqk",
        split_heads(grad_rows),
        split_heads(value_rows),
        preferred_element_type=jnp.float32,
    )
    grad_scores = (probabilities * (grad_probs - row_delta[..., None])).astype(jnp.bfloat16)
    grad_v = grad_v + jnp.einsum(
        "bhqk,bqhd->bkhd",
        probabilities.astype(jnp.bfloat16),
        split_heads(grad_rows),
        preferred_element_type=jnp.float32,
    )
    grad_k = grad_k + jnp.einsum(
        "bhqk,bqhd->bkhd", grad_scores, split_heads(query_rows), preferred_element_type=jnp.float32
    )
    return (grad_k, grad_v)


def body(
    inputs,
    cotangent,
    lengths,
    w_query,
    b_query,
    w_key,
    w_value,
    b_value,
    w_output,
    b_output,
    gain_one,
    bias_one,
    w_inner,
    b_inner,
    w_outer,
    b_outer,
    gain_two,
    bias_two,
):
    gathered = (
        lax.all_gather(w_query, "fsdp", axis=0, tiled=True),
        lax.all_gather(b_query, "fsdp", axis=0, tiled=True),
        lax.all_gather(w_key, "fsdp", axis=0, tiled=True),
        lax.all_gather(w_value, "fsdp", axis=0, tiled=True),
        lax.all_gather(b_value, "fsdp", axis=0, tiled=True),
        lax.all_gather(w_output, "fsdp", axis=0, tiled=True),
        lax.all_gather(b_output, "fsdp", axis=0, tiled=True),
        lax.all_gather(gain_one, "fsdp", axis=0, tiled=True),
        lax.all_gather(bias_one, "fsdp", axis=0, tiled=True),
        lax.all_gather(w_inner, "fsdp", axis=0, tiled=True),
        lax.all_gather(b_inner, "fsdp", axis=0, tiled=True),
        lax.all_gather(w_outer, "fsdp", axis=0, tiled=True),
        lax.all_gather(b_outer, "fsdp", axis=0, tiled=True),
        lax.all_gather(gain_two, "fsdp", axis=0, tiled=True),
        lax.all_gather(bias_two, "fsdp", axis=0, tiled=True),
    )
    (
        query_weight,
        query_bias,
        key_weight,
        value_weight,
        value_bias,
        out_weight,
        out_bias,
        gain_first,
        shift_first,
        inner_weight,
        inner_bias,
        outer_weight,
        outer_bias,
        gain_second,
        shift_second,
    ) = gathered
    joint_weight = jnp.concatenate([query_weight, key_weight, value_weight], axis=1)
    joint_bias = jnp.concatenate(
        [
            query_bias.astype(jnp.float32),
            jnp.zeros((D,), jnp.float32),
            value_bias.astype(jnp.float32),
        ]
    )
    out_bias_f = out_bias.astype(jnp.float32)
    inner_bias_f = inner_bias.astype(jnp.float32)
    outer_bias_f = outer_bias.astype(jnp.float32)
    gain_first_f = gain_first.astype(jnp.float32)
    shift_first_f = shift_first.astype(jnp.float32)
    gain_second_f = gain_second.astype(jnp.float32)
    shift_second_f = shift_second.astype(jnp.float32)
    seq_dev = inputs.shape[1]
    row_count = SEQ_MB * seq_dev
    positions = lax.axis_index("ctx") * seq_dev + lax.iota(jnp.int32, seq_dev)
    accum = None
    out_list = []
    grad_list = []
    for micro_index in range(MICRO):
        first_seq = micro_index * SEQ_MB
        seq_lens = lengths[first_seq : first_seq + SEQ_MB]
        token_rows = inputs[first_seq : first_seq + SEQ_MB].reshape(row_count, D)
        grad_rows = (
            cotangent[first_seq : first_seq + SEQ_MB].reshape(row_count, D).astype(jnp.float32)
        )
        query_ok = positions[None, :] < seq_lens[:, None]
        row_keep = query_ok.reshape(row_count, 1).astype(jnp.float32)
        projected = (matmul(token_rows, joint_weight) + joint_bias).astype(jnp.bfloat16)
        queries = projected[:, :D].reshape(SEQ_MB, seq_dev, D)
        keys_local = projected[:, D : 2 * D].reshape(SEQ_MB, seq_dev, D)
        values_local = projected[:, 2 * D :].reshape(SEQ_MB, seq_dev, D)
        start_state = (
            jnp.full((SEQ_MB, H, seq_dev), NEG_FILL, jnp.float32),
            jnp.zeros((SEQ_MB, H, seq_dev), jnp.float32),
            jnp.zeros((SEQ_MB, H, seq_dev, HD), jnp.float32),
        )
        attend_fn = partial(attend_step, queries=queries, seq_lens=seq_lens, skip_empty=False)
        run_max, run_sum, run_out = in_blocks(
            attend_fn,
            start_state,
            (
                lax.all_gather(keys_local, "ctx", axis=1, tiled=True),
                lax.all_gather(values_local, "ctx", axis=1, tiled=True),
            ),
        )
        attended = run_out / run_sum[..., None]
        log_total = run_max + jnp.log(run_sum)
        context = attended.transpose(0, 2, 1, 3).reshape(row_count, D).astype(jnp.bfloat16)
        first_sum = token_rows.astype(jnp.float32) + matmul(context, out_weight) + out_bias_f
        hidden, normed_one, inv_one = layer_norm(first_sum, gain_first_f, shift_first_f)
        hidden_low = hidden.astype(jnp.bfloat16)
        inner_pre = matmul(hidden_low, inner_weight) + inner_bias_f
        activated = gelu_exact(inner_pre).astype(jnp.bfloat16)
        outer_out = matmul(activated, outer_weight) + outer_bias_f
        result, normed_two, inv_two = layer_norm(hidden + outer_out, gain_second_f, shift_second_f)
        out_list.append(result.astype(jnp.bfloat16).reshape(SEQ_MB, seq_dev, D))
        grad_out = grad_rows * row_keep
        grad_second, grad_gain_b, grad_shift_b = norm_back(
            grad_out, normed_two, inv_two, gain_second_f
        )
        grad_outer = grad_second.astype(jnp.bfloat16)
        grad_outer_w = left_product(activated, grad_outer)
        grad_outer_b = jnp.sum(grad_outer.astype(jnp.float32), axis=0)
        grad_inner = (right_product(grad_outer, outer_weight) * gelu_slope(inner_pre)).astype(
            jnp.bfloat16
        )
        grad_inner_w = left_product(hidden_low, grad_inner)
        grad_inner_b = jnp.sum(grad_inner.astype(jnp.float32), axis=0)
        grad_hidden = grad_second + right_product(grad_inner, inner_weight)
        grad_first, grad_gain_a, grad_shift_a = norm_back(
            grad_hidden, normed_one, inv_one, gain_first_f
        )
        grad_branch = grad_first.astype(jnp.bfloat16)
        grad_out_w = left_product(context, grad_branch)
        grad_out_b = jnp.sum(grad_branch.astype(jnp.float32), axis=0)
        grad_context = (
            right_product(grad_branch, out_weight).astype(jnp.bfloat16).reshape(SEQ_MB, seq_dev, D)
        )
        row_delta = jnp.einsum(
            "bqhd,bhqd->bhq", split_heads(grad_context).astype(jnp.float32), attended
        )
        stat_total, stat_delta = (
            lax.all_gather(log_total.transpose(0, 2, 1), "ctx", axis=1, tiled=True),
            lax.all_gather(row_delta.transpose(0, 2, 1), "ctx", axis=1, tiled=True),
        )
        query_fn = partial(
            query_grad_step,
            queries=queries,
            grad_context=grad_context,
            log_total=log_total,
            row_delta=row_delta,
            seq_lens=seq_lens,
            live_queries=query_ok,
            skip_empty=False,
        )
        key_fn = partial(
            key_grad_step,
            key_rows=keys_local,
            value_rows=values_local,
            stat_total=stat_total,
            stat_delta=stat_delta,
            seq_lens=seq_lens,
            live_keys=query_ok,
            skip_empty=False,
        )
        grad_zero = jnp.zeros((SEQ_MB, seq_dev, H, HD), jnp.float32)
        grad_q = in_blocks(
            query_fn,
            grad_zero,
            (
                lax.all_gather(keys_local, "ctx", axis=1, tiled=True),
                lax.all_gather(values_local, "ctx", axis=1, tiled=True),
            ),
        )
        grad_k, grad_v = in_blocks(
            key_fn,
            (grad_zero, grad_zero),
            (
                lax.all_gather(queries, "ctx", axis=1, tiled=True),
                lax.all_gather(grad_context, "ctx", axis=1, tiled=True),
            ),
        )
        joint_grad = jnp.concatenate(
            [
                (grad_q * SCALE).reshape(row_count, D).astype(jnp.bfloat16),
                (grad_k * SCALE).reshape(row_count, D).astype(jnp.bfloat16),
                grad_v.reshape(row_count, D).astype(jnp.bfloat16),
            ],
            axis=1,
        )
        grad_joint_w = left_product(token_rows, joint_grad)
        grad_joint_b = jnp.sum(joint_grad.astype(jnp.float32), axis=0)
        input_rows = grad_first + right_product(joint_grad, joint_weight)
        grad_list.append(input_rows.reshape(SEQ_MB, seq_dev, D))
        micro_grads = (
            grad_joint_w,
            grad_joint_b,
            grad_out_w,
            grad_out_b,
            grad_gain_a,
            grad_shift_a,
            grad_inner_w,
            grad_inner_b,
            grad_outer_w,
            grad_outer_b,
            grad_gain_b,
            grad_shift_b,
        )
        if accum is None:
            accum = micro_grads
        else:
            accum = tuple((held + fresh for held, fresh in zip(accum, micro_grads)))
    (
        joint_w,
        joint_b,
        out_w,
        out_b,
        gain_a,
        shift_a,
        inner_w,
        inner_b,
        outer_w,
        outer_b,
        gain_b,
        shift_b,
    ) = accum
    grad_set = (
        joint_w[:, :D],
        joint_b[:D],
        joint_w[:, D : 2 * D],
        joint_w[:, 2 * D :],
        joint_b[2 * D :],
        out_w,
        out_b,
        gain_a,
        shift_a,
        inner_w,
        inner_b,
        outer_w,
        outer_b,
        gain_b,
        shift_b,
    )
    shard_grads = (
        lax.psum_scatter(
            grad_set[0].astype(jnp.bfloat16), "fsdp", scatter_dimension=0, tiled=True
        ).astype(jnp.float32),
        lax.psum_scatter(
            grad_set[1].astype(jnp.bfloat16), "fsdp", scatter_dimension=0, tiled=True
        ).astype(jnp.float32),
        lax.psum_scatter(
            grad_set[2].astype(jnp.bfloat16), "fsdp", scatter_dimension=0, tiled=True
        ).astype(jnp.float32),
        lax.psum_scatter(
            grad_set[3].astype(jnp.bfloat16), "fsdp", scatter_dimension=0, tiled=True
        ).astype(jnp.float32),
        lax.psum_scatter(
            grad_set[4].astype(jnp.bfloat16), "fsdp", scatter_dimension=0, tiled=True
        ).astype(jnp.float32),
        lax.psum_scatter(
            grad_set[5].astype(jnp.bfloat16), "fsdp", scatter_dimension=0, tiled=True
        ).astype(jnp.float32),
        lax.psum_scatter(
            grad_set[6].astype(jnp.bfloat16), "fsdp", scatter_dimension=0, tiled=True
        ).astype(jnp.float32),
        lax.psum_scatter(
            grad_set[7].astype(jnp.bfloat16), "fsdp", scatter_dimension=0, tiled=True
        ).astype(jnp.float32),
        lax.psum_scatter(
            grad_set[8].astype(jnp.bfloat16), "fsdp", scatter_dimension=0, tiled=True
        ).astype(jnp.float32),
        lax.psum_scatter(
            grad_set[9].astype(jnp.bfloat16), "fsdp", scatter_dimension=0, tiled=True
        ).astype(jnp.float32),
        lax.psum_scatter(
            grad_set[10].astype(jnp.bfloat16), "fsdp", scatter_dimension=0, tiled=True
        ).astype(jnp.float32),
        lax.psum_scatter(
            grad_set[11].astype(jnp.bfloat16), "fsdp", scatter_dimension=0, tiled=True
        ).astype(jnp.float32),
        lax.psum_scatter(
            grad_set[12].astype(jnp.bfloat16), "fsdp", scatter_dimension=0, tiled=True
        ).astype(jnp.float32),
        lax.psum_scatter(
            grad_set[13].astype(jnp.bfloat16), "fsdp", scatter_dimension=0, tiled=True
        ).astype(jnp.float32),
        lax.psum_scatter(
            grad_set[14].astype(jnp.bfloat16), "fsdp", scatter_dimension=0, tiled=True
        ).astype(jnp.float32),
    )
    summed = lax.psum(
        (
            shard_grads[0],
            shard_grads[1],
            shard_grads[2],
            shard_grads[3],
            shard_grads[4],
            shard_grads[5],
            shard_grads[6],
            shard_grads[7],
            shard_grads[8],
            shard_grads[9],
            shard_grads[10],
            shard_grads[11],
            shard_grads[12],
            shard_grads[13],
            shard_grads[14],
        ),
        "ctx",
    )
    outputs = jnp.concatenate(out_list, axis=0)
    input_grad = jnp.concatenate(grad_list, axis=0)
    return (outputs, input_grad) + tuple(summed)


HALF = D // 2
ROWS = 128


def flat(z, x, y, k):
    return (z * 2 + x) * 4 + y * 2 + k


def table(move):
    return [
        (flat(z, x, y, k), flat(*move(z, x, y, k)))
        for z in range(4)
        for x in range(2)
        for y in range(2)
        for k in range(2)
    ]


def permute(move):
    pairs = table(move)
    return lambda block: lax.ppermute(block, ("ctx", "fsdp"), pairs)


def permute_back(move):
    pairs = [(b, a) for a, b in table(move)]
    return lambda block: lax.ppermute(block, ("ctx", "fsdp"), pairs)


def to_seq(turn):
    return lambda z, x, y, k: (2 * k + (z // 2 + turn) % 2, x, y, z % 2)


swap_core = permute(lambda z, x, y, k: (z, x, y, k ^ 1))
swap_y = permute(lambda z, x, y, k: (z, x, y ^ 1, k))
swap_x = permute(lambda z, x, y, k: (z, x ^ 1, y, k))
swap_z1 = permute(lambda z, x, y, k: (z ^ 1, x, y, k))
swap_z2 = permute(lambda z, x, y, k: (z ^ 2, x, y, k))
seq_send = (permute(to_seq(0)), permute(to_seq(1)))
seq_return = (permute_back(to_seq(0)), permute_back(to_seq(1)))


def low(value):
    return value.astype(jnp.bfloat16)


def wide(value):
    return value.astype(jnp.float32)


def pick(array, index, axis=0):
    return lax.dynamic_index_in_dim(array, index, axis, keepdims=False)


def dot_nt(a, b):
    return lax.dot_general(a, b, (((1,), (1,)), ((), ())), preferred_element_type=jnp.float32)


def dot_tn(a, b):
    return lax.dot_general(a, b, (((0,), (0,)), ((), ())), preferred_element_type=jnp.float32)


def coords(info):
    c, f = info[0] >> 2, info[0] & 3
    return c >> 1, c & 1, f >> 1, f & 1, c, f


def pack_kernel(
    info, lens, rows, grads, w_q, w_k, w_v, w_o, w_in, v0, v1, v2, v3, v4, v5, v6, v7, wide_vec,
    t0, t1, cot, first, half, held, sem,
):
    z, x, _, _, _, _ = coords(info)
    zh = z >> 1
    copy = pltpu.make_async_copy(
        w_in.at[:, pl.ds(pl.multiple_of(x * 2 * D, 128), 2 * D)], half, sem
    )
    copy.start()
    t0[...] = rows[zh]
    t1[...] = rows[1 - zh]
    cot[:ROWS] = grads[zh]
    cot[ROWS:] = grads[1 - zh]
    columns = pl.ds(pl.multiple_of(x * HALF, 128), HALF)
    first[:192, :D] = w_o[...]
    for n, weight in enumerate((w_q, w_k, w_v)):
        first[:192, D + HALF * n : D + HALF * n + HALF] = weight[:, columns]
    held[...] = jnp.zeros_like(held)
    for n, vector in enumerate((v0, v1, v2, v3, v4, v5, v6, v7)):
        held[n : n + 1, :192] = wide(vector[...]).reshape(1, 192)
    held[8:9, :] = wide(wide_vec[...]).reshape(1, D)
    lane = lax.broadcasted_iota(jnp.int32, (1, D), 1)
    ends = jnp.zeros((1, D), jnp.int32)
    for n in range(2):
        ends = jnp.where(lane == n, lens[n] >> 7, ends)
        ends = jnp.where(lane == 2 + n, lens[n] & 127, ends)
    held[9:10, :] = wide(ends)
    first[192:, :D] = low(held[...])
    first[192:, D:] = jnp.zeros((16, 3 * HALF), jnp.bfloat16)
    copy.wait()


def attend_kernel(
    info, b0, b1, b2, b3, b4, b5, b6, b7, s0, s1, s2, s3, w0, w1, w2, w3,
    xs, ws, q_out, k_out, v_out, p_out, cu, cv, cx, key_bias, small, sems,
):
    step = pl.program_id(0)
    z, x, y, k, _, f = coords(info)

    @pl.when(step == 0)
    def _():
        copies = [
            pltpu.make_async_copy(
                piece.at[:192, D:], ws.at[pl.ds(pl.multiple_of(192 * (f ^ n), 64), 192), :], sems.at[n]
            )
            for n, piece in enumerate((w0, w1, w2, w3))
        ]
        for copy in copies:
            copy.start()
        for n, piece in enumerate((s0, s1, s2, s3)):
            small[f ^ n] = wide(piece[...])
        line = small[2 * y + (z >> 1)][9:10, :]
        lane = lax.broadcasted_iota(jnp.int32, (1, D), 1)
        part = jnp.where(lane == (z & 1), 128.0 * line, 0.0)
        part = part + jnp.where(lane == 2 + (z & 1), line, 0.0)
        end = jnp.sum(part, axis=1, keepdims=True)
        z_low = 2 * (z & 1)
        blocks = (b0, b1, b2, b3, b4, b5, b6, b7)
        for n, block in enumerate(blocks):
            z_block = (z_low if n % 2 == 0 else 2 - z_low) + (k if n < 4 else 1 - k)
            x_block = x if n % 4 < 2 else 1 - x
            xs[n * ROWS : (n + 1) * ROWS, :] = block[...]
            place = (2 * z_block + x_block) * ROWS + lax.broadcasted_iota(jnp.int32, (1, ROWS), 1)
            key_bias[:, n * ROWS : (n + 1) * ROWS] = jnp.where(wide(place) < end, 0.0, NEG_FILL)
        for copy in copies:
            copy.wait()

        def bias(row):
            return jnp.concatenate(
                [small[2 * x + n][row : row + 1, :192] for n in range(2)], axis=1
            )

        q_out[...] = low(wide(low(matmul(xs[: 4 * ROWS, :], ws[:, :HALF]) + bias(0))) * SCALE)
        k_out[...] = low(matmul(xs[...], ws[:, HALF : 2 * HALF]))
        v_out[...] = low(matmul(xs[...], ws[:, 2 * HALF :]) + bias(1))

    lanes = pl.ds(pl.multiple_of(step * 128, 128), 128)
    first = lax.broadcasted_iota(jnp.int32, (1, 128), 1) < HD
    queries = q_out[:, lanes]
    keys = k_out[:, lanes]
    values = v_out[:, lanes]
    for part in range(2):
        rows = slice(part * 256, part * 256 + 256)
        found = []
        for head in range(2):
            mine = first if head == 0 else jnp.logical_not(first)
            scores = dot_nt(jnp.where(mine, queries[rows], 0), keys) + key_bias[...]
            top = jnp.max(scores, axis=1, keepdims=True)
            weights = jnp.exp(scores - top)
            total = jnp.sum(weights, axis=1, keepdims=True)
            probs = low(weights * (1.0 / total))
            p_out[head, rows, :] = probs
            found.append(matmul(probs, values))
        context = low(jnp.where(first, found[0], found[1]))
        if part == 0:
            cu[...] = context[:ROWS]
            cv[...] = context[ROWS:]
        else:
            cx[0] = context[:ROWS]
            cx[1] = context[ROWS:]


def pair_back(queries_ref, keys, values, probs_ref, grads):
    first = lax.broadcasted_iota(jnp.int32, (1, 128), 1) < HD
    grad_k = jnp.zeros((8 * ROWS, 128), jnp.float32)
    grad_v = jnp.zeros((8 * ROWS, 128), jnp.float32)
    grad_qs = []
    for part in range(2):
        rows = slice(part * 256, part * 256 + 256)
        one, two = grads[2 * part : 2 * part + 2]
        grad_rows = jnp.concatenate([one[...], two[...]], axis=0)
        queries = queries_ref[rows, :]
        grad_q = jnp.zeros((256, 128), jnp.float32)
        for head in range(2):
            mine = first if head == 0 else jnp.logical_not(first)
            grad_mine = jnp.where(mine, grad_rows, 0)
            probs = probs_ref[head, rows, :]
            grad_probs = dot_nt(grad_mine, values)
            product = wide(probs) * grad_probs
            delta = jnp.sum(product, axis=1, keepdims=True)
            grad_scores = low(product - wide(probs) * delta)
            grad_q = grad_q + matmul(grad_scores, jnp.where(mine, keys, 0))
            grad_k = grad_k + dot_tn(grad_scores, jnp.where(mine, queries, 0))
            grad_v = grad_v + dot_tn(probs, grad_mine)
        grad_qs.append(low(grad_q * SCALE))
    return grad_qs, low(grad_k), low(grad_v)


def attend_back_kernel(queries, keys, values, probs, gu, gv, gxu, gxv, dq, dk, dv):
    grad_qs, dk[...], dv[...] = pair_back(
        queries, keys[...], values[...], probs, (gu, gv, gxu, gxv)
    )
    dq[:256, :], dq[256:, :] = grad_qs


def joint_kernel(
    info, xs, dq0, dq1, dq2, dk0, dk1, dk2, dv0, dv1, dv2, keep, send, grads, dw
):
    for n, (q, k, v) in enumerate(((dq0, dk0, dv0), (dq1, dk1, dv1), (dq2, dk2, dv2))):
        start = 128 * n
        grads[: 4 * ROWS, start : start + 128] = q[...]
        grads[:, HALF + start : HALF + start + 128] = k[...]
        grads[:, 2 * HALF + start : 2 * HALF + start + 128] = v[...]
    own = slice(0, 4 * ROWS)
    dw[:, :HALF] = low(dot_tn(xs[own, :], grads[own, :HALF]))
    dw[:, HALF:] = low(dot_tn(xs[...], grads[:, HALF:]))
    col_sums = jnp.concatenate(
        [
            column_sum(wide(grads[own, :HALF])),
            jnp.zeros((1, HALF), jnp.float32),
            column_sum(wide(grads[:, 2 * HALF :])),
        ],
        axis=1,
    )
    tail = low(jnp.where(lax.broadcasted_iota(jnp.int32, (16, 1), 0) == 0, col_sums, 0.0))
    z, _, _, _, _, f = coords(info)
    for n in range(4):
        place = send if n % 2 else keep
        for half in range(2):
            start = pl.multiple_of(192 * (f ^ n) + 96 * half, 32)
            place[n // 2, half ^ (z & 1), :96, :] = dw[pl.ds(start, 96), :]
            place[n // 2, half ^ (z & 1), 96:, :] = tail if half == 0 else tail * 0


def rows_back_kernel(
    ws, dq0, dq1, dq2, dk0, dk1, dk2, dv0, dv1, dv2, dx_own, dx_other, grads
):
    for n, (q, k, v) in enumerate(((dq0, dk0, dv0), (dq1, dk1, dv1), (dq2, dk2, dv2))):
        start = 128 * n
        grads[: 4 * ROWS, start : start + 128] = q[...]
        grads[:, HALF + start : HALF + start + 128] = k[...]
        grads[:, 2 * HALF + start : 2 * HALF + start + 128] = v[...]
    dx_other[...] = low(dot_nt(grads[4 * ROWS :, HALF:], ws[:, HALF:]))
    dx_own[...] = dot_nt(grads[: 4 * ROWS, :], ws[...])


def middle_one_kernel(
    info, cm0, cm1, co0, co1, x0, x1, o0, o1, o2, o3, i0, i1, i2, i3,
    hidden_out, normed_out, inv_out, act, slope, vec,
    ctx, low_rows, small, order, inner_weight, sems,
):
    step = pl.program_id(0)
    _, x, _, _, _, f = coords(info)

    def copy(e, n):
        return pltpu.make_async_copy(
            (i0, i1, i2, i3)[n].at[:, pl.ds(pl.multiple_of(D * (f ^ e), 128), D)],
            inner_weight.at[e, pl.ds(pl.multiple_of(192 * (f ^ n), 64), 192), :],
            sems.at[e, n],
        )

    @pl.when(step == 0)
    def _():
        for e in range(4):
            for n in range(4):
                copy(e, n).start()
        for n, piece in enumerate((o0, o1, o2, o3)):
            small[f ^ n] = wide(piece[192:, :])
            order[n] = wide(piece[192:, :])
        for n in range(8):
            vec[n : n + 1, :] = jnp.concatenate(
                [small[m][n : n + 1, :192] for m in range(4)], axis=1
            )
        for side, (one, two) in enumerate(((cm0, cm1), (co0, co1))):
            rows = jnp.concatenate([one[...], two[...]], axis=0)
            for part in range(2):
                ctx[2 * (x ^ side) + part] = rows[:, 192 * part : 192 * part + 192]
        total = wide(jnp.concatenate([x0[...], x1[...]], axis=0)) + vec[2:3, :]
        for n, piece in enumerate((o0, o1, o2, o3)):
            total = total + matmul(ctx[f ^ n], piece[:192, :])
        hidden, normed, inv = layer_norm(total, vec[3:4, :], vec[4:5, :])
        hidden_out[...] = hidden
        normed_out[...] = normed
        inv_out[...] = inv
        low_rows[...] = low(hidden)

    for n in range(4):
        copy(step, n).wait()
    pre = matmul(low_rows[...], inner_weight[step]) + order[step][8:9, :]
    bell = 0.5 * (1.0 + lax.erf(pre * ROOT_HALF))
    act[0] = low(pre * bell)
    slope[0] = low(bell + pre * INV_ROOT_TAU * jnp.exp(-0.5 * pre * pre))


def norm_grad(grad, normed, inv, gain):
    scaled = grad * gain
    return inv * (
        scaled
        - jnp.mean(scaled, axis=-1, keepdims=True)
        - normed * jnp.mean(scaled * normed, axis=-1, keepdims=True)
    )


def column_sum(value):
    return jnp.sum(value, axis=0, keepdims=True)


def outer_copies(refs, held, sems):
    copies = [
        pltpu.make_async_copy(ref, held.at[n], sems.at[n]) for n, ref in enumerate(refs)
    ]
    for copy in copies:
        copy.start()
    return copies


def middle_two_kernel(
    info, lens, act, act_block, hidden, cot, vec, w0, w1, w2, w3,
    out, second_out, outer_out, sums, keep, send, w_all, w_sem,
):
    step = pl.program_id(0)
    z, x, _, _, c, f = coords(info)

    @pl.when(step == 0)
    def _():
        copies = outer_copies((w0, w1, w2, w3), w_all, w_sem)
        b_2, g_2, s_2 = vec[5:6, :], vec[6:7, :], vec[7:8, :]
        total = hidden[...] + b_2
        for n in range(4):
            copies[n].wait()
            total = total + matmul(act[n], w_all[n])
        result, normed, inv = layer_norm(total, g_2, s_2)
        zh = z >> 1
        out[zh] = low(result[:ROWS])
        out[1 - zh] = low(result[ROWS:])
        row = lax.broadcasted_iota(jnp.int32, (2 * ROWS, 1), 0)
        end = jnp.where(row < ROWS, lens[zh], lens[1 - zh] + ROWS)
        grad = wide(cot[...]) * jnp.where(row + c * ROWS < end, 1.0, 0.0)
        grad_second = norm_grad(grad, normed, inv, g_2)
        second_out[...] = grad_second
        grad_outer = low(grad_second)
        outer_out[...] = grad_outer
        sums[...] = jnp.zeros_like(sums)
        for n, value in enumerate((wide(grad_outer), grad * normed, grad)):
            sums[n : n + 1, :] = column_sum(value)

    @pl.when(step > 0)
    def _():
        grad = low(dot_tn(act_block[0], outer_out[...]))
        for place, wanted in ((send, step < 3), (keep, step >= 3)):

            @pl.when(wanted)
            def _(place=place):
                for n in range(4):
                    place[0, n ^ (2 * x + (z & 1))] = grad[192 * n : 192 * n + 192]


def inner_back_kernel(
    info, outer, slope, w0, w1, w2, w3, inner_out, sums, w_all, sems
):
    f = info[0] & 3
    copies = outer_copies((w0, w1, w2, w3), w_all, sems)
    for e in range(4):
        copies[e].wait()
        inner = low(dot_nt(outer[...], w_all[e]) * wide(slope[e]))
        inner_out[e] = inner
        sums[pl.ds(f ^ e, 1), :] = column_sum(wide(inner))


def middle_three_kernel(
    info, second, inner, normed_one, inv_one, vec, o0, o1, o2, o3, i0, i1, i2, i3,
    first_out, g0, g1, branch_out, sums, o_all, i_all, gc, o_sem, i_sem,
):
    _, x, _, _, _, f = coords(info)
    copies = {}
    for e in range(4):
        columns = pl.ds(pl.multiple_of(D * (f ^ e), 128), D)
        for n, ref in enumerate((i0, i1, i2, i3)):
            rows = pl.ds(pl.multiple_of(192 * (f ^ n), 64), 192)
            copies["i", e, n] = pltpu.make_async_copy(
                ref.at[:, columns], i_all.at[e, rows, :], i_sem.at[e, n]
            )
            copies["i", e, n].start()
    for n, ref in enumerate((o0, o1, o2, o3)):
        copies["o", n] = pltpu.make_async_copy(ref.at[:192, :D], o_all.at[n], o_sem.at[n])
        copies["o", n].start()
    grad_hidden = second[...]
    for e in range(4):
        for n in range(4):
            copies["i", e, n].wait()
        grad_hidden = grad_hidden + dot_nt(inner[e], i_all[e])
    grad_first = norm_grad(grad_hidden, normed_one[...], inv_one[...], vec[3:4, :])
    first_out[...] = grad_first
    branch = low(grad_first)
    branch_out[...] = branch
    for n, value in enumerate((wide(branch), grad_hidden * normed_one[...], grad_hidden)):
        sums[n : n + 1, :] = column_sum(value)
    for n in range(4):
        copies["o", n].wait()
        gc[f ^ n] = low(dot_nt(branch, o_all[n]))
    for side in range(2):
        rows = jnp.concatenate([gc[2 * (x ^ side)], gc[2 * (x ^ side) + 1]], axis=1)
        g0[1 - side] = rows[:ROWS]
        g1[1 - side] = rows[ROWS:]


def middle_four_kernel(
    info, inner, hidden, branch, cm0, cm1, co0, co1, sums_two, sums_in, sums_one,
    keep, send, held, out_held, vec_held,
):
    step = pl.program_id(0)
    _, x, _, _, _, f = coords(info)
    block = f ^ step

    @pl.when(step == 0)
    def _():
        for side, (one, two) in enumerate(((cm0, cm1), (co0, co1))):
            rows = jnp.concatenate([one[...], two[...]], axis=0)
            start = pl.multiple_of(HALF * (x ^ side), 128)
            out_held[pl.ds(start, HALF), :] = low(dot_tn(rows, branch[...]))
        vec_held[...] = jnp.zeros_like(vec_held)
        top = lax.broadcasted_iota(jnp.int32, (16, 1), 0) == 0
        for n in range(4):
            cut = slice(192 * n, 192 * n + 192)
            lines = (
                sums_in[n : n + 1, :],
                jnp.concatenate(
                    [sums_one[m : m + 1, cut] for m in range(3)] + [sums_two[0:1, cut]], axis=1
                ),
                jnp.concatenate(
                    [sums_two[1:2, cut], sums_two[2:3, cut], jnp.zeros((1, HALF), jnp.float32)],
                    axis=1,
                ),
            )
            for m, line in enumerate(lines):
                vec_held[m, n] = low(jnp.where(top, line, 0.0))

    held[...] = low(dot_tn(low(hidden[...]), inner[0]))
    for n in range(4):
        place = send if n % 2 else keep
        start = 192 * (f ^ n)
        place[n // 2, 0, :192, :] = held[pl.ds(pl.multiple_of(start, 64), 192), :]
        place[n // 2, 0, 192:240, :] = out_held[pl.ds(pl.multiple_of(start + 48 * block, 16), 48), :]
        place[n // 2, 0, 240:, :] = vec_held[block, f ^ n]


MIDDLE = 2 * ROWS
VMEM_LIMIT = 30 * 1024 * 1024
BF, FP = jnp.bfloat16, jnp.float32


def whole(shape):
    return pl.BlockSpec(tuple(shape), lambda *_: (0,) * len(shape))


def lane_block(rows, start=0):
    return pl.BlockSpec((rows, 128), lambda step, *_: (0, step + start))


def call(kernel, name, grid, scalars, operands, outs, scratch=(), work=(1, 1)):
    return pl.pallas_call(
        kernel,
        out_shape=[jax.ShapeDtypeStruct(shape, kind) for shape, kind, _ in outs],
        grid_spec=pltpu.PrefetchScalarGridSpec(
            num_scalar_prefetch=len(scalars),
            grid=(grid,),
            in_specs=[spec or whole(array.shape) for array, spec in operands],
            out_specs=[spec or whole(shape) for shape, _, spec in outs],
            scratch_shapes=list(scratch),
        ),
        compiler_params=pltpu.CompilerParams(
            dimension_semantics=("arbitrary",), vmem_limit_bytes=VMEM_LIMIT
        ),
        cost_estimate=pl.CostEstimate(
            flops=1000, bytes_accessed=1000, transcendentals=0
        ),
        name=name,
    )(*scalars, *[array for array, _ in operands])


def plain(arrays):
    return [(array, None) for array in arrays]


def anywhere(arrays):
    return [(array, pl.BlockSpec(memory_space=pl.ANY)) for array in arrays]


def probs_block(start=0):
    return pl.BlockSpec((2, 4 * ROWS, 8 * ROWS), lambda step, *_: (step + start, 0, 0))


def pack(info, lens, inputs, cotangent, weights, vectors):
    return call(
        pack_kernel, "pack", 1, (info, lens),
        plain([inputs, cotangent, *weights[:4]]) + anywhere(weights[4:]) + plain(vectors),
        [
            ((ROWS, D), BF, None), ((ROWS, D), BF, None), ((MIDDLE, D), BF, None),
            ((208, D + 3 * HALF), BF, None), ((192, 2 * D), BF, pl.BlockSpec(memory_space=pl.ANY)),
        ],
        [pltpu.VMEM((16, D), FP), pltpu.SemaphoreType.DMA], (1, 4),
    )


def first_columns(pieces):
    return [(piece, pl.BlockSpec((208, D), lambda *_: (0, 0))) for piece in pieces]


def attend(info, blocks, pieces):
    return call(
        attend_kernel, "attend", 3, (info,),
        plain(blocks)
        + [(piece, pl.BlockSpec((16, D), lambda *_: (12, 0))) for piece in pieces]
        + anywhere(pieces),
        [
            ((8 * ROWS, D), BF, None), ((D, 3 * HALF), BF, None), ((4 * ROWS, HALF), BF, None),
            ((8 * ROWS, HALF), BF, None), ((8 * ROWS, HALF), BF, None),
            ((6, 4 * ROWS, 8 * ROWS), BF, probs_block()),
        ]
        + [((ROWS, HALF), BF, lane_block(ROWS))] * 2
        + [((2, ROWS, HALF), BF, pl.BlockSpec((2, ROWS, 128), lambda step, *_: (0, 0, step)))],
        [
            pltpu.VMEM((1, 8 * ROWS), FP), pltpu.VMEM((4, 16, D), FP),
            pltpu.SemaphoreType.DMA((4,)),
        ],
        (10, 15),
    )


def attend_back(queries, keys, values, probs, grads, start, pairs):
    return call(
        attend_back_kernel, "attend_back", pairs, (),
        [
            (queries, lane_block(4 * ROWS, start)), (keys, lane_block(8 * ROWS, start)),
            (values, lane_block(8 * ROWS, start)), (probs, probs_block(start)),
        ]
        + [(grad, pl.BlockSpec((None, ROWS, 128), lambda s, n=n: (n, 0, s + start))) for grad, n in grads],
        [
            ((4 * ROWS, 128 * pairs), BF, lane_block(4 * ROWS)),
            ((8 * ROWS, 128 * pairs), BF, lane_block(8 * ROWS)),
            ((8 * ROWS, 128 * pairs), BF, lane_block(8 * ROWS)),
        ],
        (), (4 * pairs, 5 * pairs),
    )


def by_name(pairs):
    return [part for name in zip(*pairs) for part in name]


def joint_grads(info, xs, pairs):
    joint = (2, 2, 112, 3 * HALF)
    return call(
        joint_kernel, "joint_grads", 1, (info,), plain([xs, *by_name(pairs)]),
        [(joint, BF, None), (joint, BF, None)],
        [pltpu.VMEM((8 * ROWS, 3 * HALF), BF), pltpu.VMEM((D, 3 * HALF), BF)],
    )


def rows_back(ws, pairs):
    return call(
        rows_back_kernel, "rows_back", 1, (), plain([ws, *by_name(pairs)]),
        [((4 * ROWS, D), FP, None), ((4 * ROWS, D), BF, None)],
        [pltpu.VMEM((8 * ROWS, 3 * HALF), BF)],
    )


def middle_one(info, ctx, rows, out_p, inner_p):
    block = pl.BlockSpec((1, MIDDLE, D), lambda step, *_: (step, 0, 0))
    return call(
        middle_one_kernel, "middle_one", 4, (info,),
        plain([*ctx, *rows]) + first_columns(out_p) + anywhere(inner_p),
        [
            ((MIDDLE, D), FP, None), ((MIDDLE, D), FP, None), ((MIDDLE, 1), FP, None),
            ((4, MIDDLE, D), BF, block), ((4, MIDDLE, D), BF, block), ((8, D), FP, None),
        ],
        [
            pltpu.VMEM((4, MIDDLE, 192), BF), pltpu.VMEM((MIDDLE, D), BF),
            pltpu.VMEM((4, 16, D), FP), pltpu.VMEM((4, 16, D), FP), pltpu.VMEM((4, D, D), BF),
            pltpu.SemaphoreType.DMA((4, 4)),
        ],
        (4, 10),
    )


def middle_two(info, lens, act, hidden, cot, vec, outer_p):
    def turn(step, *_):
        at = jnp.maximum(step - 1, 0)
        return (jnp.where(at < 2, 2 * at + 1, 2 * at - 4), 0, 0)

    blocks = (2, 4, 192, D)
    return call(
        middle_two_kernel, "middle_two", 5, (info, lens),
        [(act, None), (act, pl.BlockSpec((1, MIDDLE, D), turn))]
        + plain([hidden, cot, vec])
        + anywhere(outer_p),
        [
            ((2, ROWS, D), BF, None), ((MIDDLE, D), FP, None), ((MIDDLE, D), BF, None),
            ((8, D), FP, None),
            (blocks, BF, pl.BlockSpec((1, 4, 192, D), lambda s, *_: (jnp.maximum(s - 3, 0), 0, 0, 0))),
            (blocks, BF, pl.BlockSpec((1, 4, 192, D), lambda s, *_: (jnp.where(s < 2, 0, 1), 0, 0, 0))),
        ],
        [pltpu.VMEM((4, D, D), BF), pltpu.SemaphoreType.DMA((4,))], (4, 10),
    )


def inner_back(info, outer, slope, outer_p):
    return call(
        inner_back_kernel, "inner_back", 1, (info,), plain([outer, slope]) + anywhere(outer_p),
        [((4, MIDDLE, D), BF, None), ((4, D), FP, None)],
        [pltpu.VMEM((4, D, D), BF), pltpu.SemaphoreType.DMA((4,))], (2, 7),
    )


def middle_three(info, second, inner, normed, inv, vec, out_p, inner_p):
    return call(
        middle_three_kernel, "middle_three", 1, (info,),
        plain([second, inner, normed, inv, vec]) + anywhere([*out_p, *inner_p]),
        [((MIDDLE, D), FP, None)]
        + [((2, ROWS, HALF), BF, None)] * 2
        + [((MIDDLE, D), BF, None), ((8, D), FP, None)],
        [
            pltpu.VMEM((4, 192, D), BF), pltpu.VMEM((4, D, D), BF),
            pltpu.VMEM((4, MIDDLE, 192), BF), pltpu.SemaphoreType.DMA((4,)),
            pltpu.SemaphoreType.DMA((4, 4)),
        ],
        (2, 7),
    )


def middle_four(info, inner, hidden, branch, ctx, sums):
    def spot(step, info):
        z, x, _, _, _, f = coords(info)
        return (0, f ^ step ^ (2 * (z & 1) + x), 0, 0)

    block = pl.BlockSpec((2, 1, 256, D), spot)
    return call(
        middle_four_kernel, "middle_four", 4, (info,),
        [(inner, pl.BlockSpec((1, MIDDLE, D), lambda step, *_: (step, 0, 0)))]
        + plain([hidden, branch, *ctx, *sums]),
        [((2, 4, 256, D), BF, block)] * 2,
        [pltpu.VMEM((D, D), BF), pltpu.VMEM((D, D), BF), pltpu.VMEM((4, 4, 16, D), BF)],
        (4, 8),
    )


def place_outer_kernel(info, p0, p1, p2, p3, out):
    z, x, _, _, _, _ = coords(info)
    for n, piece in enumerate((p0, p1, p2, p3)):
        out[pl.ds(pl.multiple_of(192 * (n ^ (2 * x + (z & 1))), 64), 192), :] = wide(piece[...])


def place_inner_kernel(
    info, p0, p1, p2, p3, inner, out, b_in, b_out, g_one, s_one, b_two, g_two, s_two, held
):
    z, x, _, _, _, _ = coords(info)
    for n, piece in enumerate((p0, p1, p2, p3)):
        at = n ^ (2 * (z & 1) + x)
        inner[:, pl.ds(pl.multiple_of(D * at, 128), D)] = wide(piece[:192, :])
        out[pl.ds(pl.multiple_of(48 * at, 16), 48), :] = wide(piece[192:240, :])
        held[at] = wide(piece[240:, :])
    b_in[...] = held[0][0:1, :].reshape(D)
    for n, vector in enumerate((b_out, g_one, s_one, b_two, g_two, s_two)):
        cut = 192 * (n % 4)
        vector[...] = held[1 + n // 4][0:1, cut : cut + 192].reshape(192)


def place_joint_kernel(info, p0, p1, p2, p3, query, key, value, b_query, b_value, held):
    z, x, _, _, _, f = coords(info)
    z_bit = z & 1
    for n, piece in enumerate((p0, p1, p2, p3)):
        rows = pl.ds(pl.multiple_of(96 * (n % 2 ^ z_bit), 32), 96)
        columns = pl.ds(pl.multiple_of(HALF * (n // 2 ^ x), 128), HALF)
        for m, out in enumerate((query, key, value)):
            out[rows, columns] = wide(piece[:96, HALF * m : HALF * m + HALF])
        line = wide(piece[96:, :])
        line = jnp.where(f & 1 == 0, line, jnp.concatenate([line[:, 192:], line[:, :192]], axis=1))
        held[n // 2 ^ x, n % 2 ^ z_bit] = line
    mine = held[f >> 1, 0][0:1, :]
    b_query[...] = mine[:, :192].reshape(192)
    b_value[...] = mine[:, 2 * HALF : 2 * HALF + 192].reshape(192)


def placed(kernel, name, info, pieces, shapes, held=()):
    return call(
        kernel, name, 1, (info,), plain(pieces), [(shape, FP, None) for shape in shapes],
        [pltpu.VMEM(shape, FP) for shape in held], (1, 6),
    )


def unshuffle(array, bit):
    return jnp.where(bit == 0, array, array[::-1])


def tied(values, *events):
    return lax.optimization_barrier((values, events))[0]


def fast_body(
    inputs, cotangent, lengths, w_query, b_query, w_key, w_value, b_value, w_output, b_output,
    gain_one, bias_one, w_inner, b_inner, w_outer, b_outer, gain_two, bias_two,
):
    info = lax.axis_index(("ctx", "fsdp")).astype(jnp.int32).reshape(1)
    zh, x = lax.axis_index("ctx") // 4, lax.axis_index("ctx") % 2

    t0, t1, cot, first, half = pack(
        info, lengths, inputs, cotangent, (w_query, w_key, w_value, w_output, w_inner),
        (b_query, b_value, b_output, gain_one, bias_one, b_outer, gain_two, bias_two, b_inner),
    )

    bu, bv = seq_send[0](t0), seq_send[1](t1)
    first_y, first_k = swap_y(first), swap_core(first)
    half_y = swap_y(half)
    bu, bv, first_k = tied((bu, bv, first_k))
    bxu, bxv, bku = swap_x(bu), swap_x(bv), swap_core(bu)
    bxu, bxv, bku, first_y, half_y = tied((bxu, bxv, bku, first_y, half_y))
    bkv, *rest = [swap_core(b) for b in (bv, bxu, bxv, first_y)]
    bkv, *rest = tied([bkv] + rest)
    blocks = [bu, bv, bxu, bxv, bku, bkv, *rest[:2]]
    first_p = [first, first_k, first_y, rest[2]]
    outer_y = swap_y(tied(w_outer, half_y))
    half_x = swap_x(tied(half_y, bkv))
    xs, ws, queries, keys, values, probs, cu, cv, cx = attend(info, blocks, first_p)

    cu, cv, cx, half_x = tied((cu, cv, cx, half_x))
    cu, cv = seq_return[0](cu), seq_return[1](cv)
    cx = swap_x(cx)
    inner_y = jnp.where(
        x == 0, jnp.concatenate([half_y, half_x], 1), jnp.concatenate([half_x, half_y], 1)
    )
    cu, cv, cx, outer_y, inner_y = tied((cu, cv, cx, outer_y, inner_y))
    cxu, cxv = seq_return[0](cx[0]), seq_return[1](cx[1])
    inner_k, inner_ky = swap_core(tied(w_inner, cx)), swap_core(inner_y)
    cxu, cxv, inner_k, inner_ky = tied((cxu, cxv, inner_k, inner_ky))
    outer_k, outer_ky = swap_core(tied(w_outer, cxu)), swap_core(tied(outer_y, cxu))
    ctx = [cu, cv, cxu, cxv]
    inner_p = [w_inner, inner_k, inner_y, inner_ky]
    hidden, normed, inv, act, slope, vec = middle_one(info, ctx, [t0, t1], first_p, inner_p)
    act, outer_k, outer_ky = tied((act, outer_k, outer_ky))
    outer_p = [w_outer, outer_k, outer_y, outer_ky]
    outputs, second_grad, outer, sums_two, o_keep, o_send = middle_two(
        info, lengths, act, hidden, cot, vec, outer_p
    )
    o_came = swap_core(o_send)
    inner, sums_in = inner_back(info, outer, slope, outer_p)
    o_came, inner = tied((o_came, inner))
    o_y = low(wide(o_keep[1, :2]) + wide(o_came[1, :2]))
    o_z = low(wide(o_keep[:, 3]) + wide(o_came[:, 3]))
    inner, o_y, o_z = tied((inner, o_y, o_z))
    o_y, o_z = swap_y(o_y), swap_z1(o_z)
    grad_first, g0, g1, branch, sums_one = middle_three(
        info, second_grad, inner, normed, inv, vec, first_p, inner_p
    )
    g0, g1 = seq_send[0](g0), seq_send[1](g1)
    i_keep, i_send = middle_four(
        info, inner, hidden, branch, ctx, (sums_two, sums_in, sums_one)
    )
    g0, g1, i_send, o_y, o_z = tied((g0, g1, i_send, o_y, o_z))
    go = jnp.stack([g0[0], g1[0]])
    go, o_y, o_z, i_send = tied((go, o_y, o_z, i_send))
    go = swap_x(go)
    i_came = swap_core(i_send)
    o_z2 = swap_z1(low(wide(o_keep[0, 1]) + wide(o_came[0, 1]) + wide(o_y[1])))
    o_y2 = swap_y(low(wide(o_keep[1, 2]) + wide(o_came[1, 2]) + wide(o_z[1])))
    go, i_came, o_z2, o_y2 = tied((go, i_came, o_z2, o_y2))
    o_one = wide(o_keep[0, 0]) + wide(o_came[0, 0]) + wide(o_y[0]) + wide(o_z2)
    o_two = low(wide(o_keep[0, 2]) + wide(o_came[0, 2]) + wide(o_z[0]) + wide(o_y2))
    i_y = low(wide(i_keep[1, :2]) + wide(i_came[1, :2]))
    i_x = low(wide(i_keep[:, 3]) + wide(i_came[:, 3]))
    go, i_y, i_x = tied((go, i_y, i_x))
    i_y, i_x = swap_y(i_y), swap_x(i_x)
    grads = [(g0, 1), (g1, 1), (go, 0), (go, 1)]
    pair_0 = attend_back(queries, keys, values, probs, grads, 0, 1)
    pair_1 = attend_back(tied(queries, pair_0), keys, values, probs, grads, 1, 1)
    pair_2 = attend_back(tied(queries, pair_1), keys, values, probs, grads, 2, 1)
    pairs = (pair_0, pair_1, pair_2)
    dx_own, dx_other = rows_back(ws, pairs)
    dx_own, dx_other, i_y, i_x = tied((dx_own, dx_other, i_y, i_x))
    i_x2 = swap_x(low(wide(i_keep[0, 1]) + wide(i_came[0, 1]) + wide(i_y[1])))
    i_y2 = swap_y(low(wide(i_keep[1, 2]) + wide(i_came[1, 2]) + wide(i_x[1])))
    o_came = swap_x(tied(o_two, dx_other))
    j_keep, j_send = joint_grads(info, tied(xs, dx_other), pairs)
    j_keep, j_send, i_x2, i_y2, o_came = tied((j_keep, j_send, i_x2, i_y2, o_came))
    i_one = wide(i_keep[0, 0]) + wide(i_came[0, 0]) + wide(i_y[0]) + wide(i_x2)
    i_two = low(wide(i_keep[0, 2]) + wide(i_came[0, 2]) + wide(i_x[0]) + wide(i_y2))
    o_sum = low(o_one + wide(o_came))
    i_came = swap_z1(i_two)
    j_came, dx_came = swap_core(j_send), swap_core(dx_other)
    o_came = swap_z2(o_sum)
    j_came, dx_came, i_came = tied((j_came, dx_came, i_came))
    i_sum = low(i_one + wide(i_came))
    dx = dx_own[: 2 * ROWS] + wide(dx_came[: 2 * ROWS])
    dx_send = low(dx_own[2 * ROWS :] + wide(dx_came[2 * ROWS :]))
    j_y = swap_y(low(wide(j_keep[1, :, :56]) + wide(j_came[1, :, :56])))
    j_z = swap_z1(low(wide(j_keep[:, 1, 56:]) + wide(j_came[:, 1, 56:])))
    j_one = wide(j_keep[0, :, :56]) + wide(j_came[0, :, :56])
    j_two = wide(j_keep[:, 0, 56:]) + wide(j_came[:, 0, 56:])
    i_came = swap_z2(i_sum)
    dx_came = swap_x(dx_send)
    j_y, j_z, dx_came, o_came = tied((j_y, j_z, dx_came, o_came))
    j_one, j_two = j_one + wide(j_y), j_two + wide(j_z)
    dx = low(dx + wide(dx_came))
    o_sum = low(wide(o_sum) + wide(o_came))
    j_z, j_y = swap_z1(low(j_one[1])), swap_y(low(j_two[1]))
    o_x = swap_x(o_sum)
    j_z, j_y, o_x, i_came = tied((j_z, j_y, o_x, i_came))
    j_sum = low(jnp.concatenate([j_one[0] + wide(j_z), j_two[0] + wide(j_y)], axis=0))
    i_sum = low(wide(i_sum) + wide(i_came))
    j_came = swap_z2(j_sum)
    i_z, i_x, o_z = swap_z1(i_sum), swap_x(i_sum), swap_z1(tied(o_sum, i_sum))
    j_came, i_z, i_x, o_z = tied((j_came, i_z, i_x, o_z))
    j_sum = low(wide(j_sum) + wide(j_came))
    j_x, j_z = swap_x(j_sum), swap_z1(j_sum)
    i_zx = swap_x(i_z)
    dx0, dx1 = seq_return[0](tied(dx[:ROWS], i_z)), seq_return[1](tied(dx[ROWS:], i_z))
    j_x, j_z, i_zx, dx0, dx1 = tied((j_x, j_z, i_zx, dx0, dx1))
    j_zx = swap_z1(j_x)
    o_zx = swap_z1(tied(o_x, j_x))
    input_grad = grad_first + wide(jnp.concatenate([dx0, dx1], axis=0))
    input_grad = unshuffle(input_grad.reshape(2, ROWS, D), zh)
    inner_grad, out_grad, grad_b1, grad_bo, grad_g1, grad_s1, grad_b2, grad_g2, grad_s2 = placed(
        place_inner_kernel, "place_inner", info, [i_sum, i_x, i_z, i_zx],
        [(192, 4 * D), (192, D), (D,)] + [(192,)] * 6, [(4, 16, D)],
    )
    (outer_grad,) = placed(place_outer_kernel, "place_outer", info, [o_sum, o_z, o_x, o_zx], [(D, D)])
    q_grad, k_grad, v_grad, grad_bq, grad_bv = placed(
        place_joint_kernel, "place_joint", info, [j_sum, j_z, j_x, j_zx],
        [(192, D)] * 3 + [(192,)] * 2, [(2, 2, 16, 3 * HALF)],
    )
    return (
        outputs, input_grad, q_grad, grad_bq, k_grad, v_grad, grad_bv, out_grad, grad_bo,
        grad_g1, grad_s1, inner_grad, grad_b1, outer_grad, grad_b2, grad_g2, grad_s2,
    )


def solution(mesh):
    placed = (
        P("fsdp", "ctx", None),
        P("fsdp", "ctx", None),
        P("fsdp"),
        P("fsdp", None),
        P("fsdp"),
        P("fsdp", None),
        P("fsdp", None),
        P("fsdp"),
        P("fsdp", None),
        P("fsdp"),
        P("fsdp"),
        P("fsdp"),
        P("fsdp", None),
        P("fsdp"),
        P("fsdp", None),
        P("fsdp"),
        P("fsdp"),
        P("fsdp"),
    )
    fast = dict(mesh.shape) == {"ctx": 8, "fsdp": 4}
    return jax.shard_map(
        fast_body if fast else body,
        mesh=mesh,
        in_specs=placed,
        out_specs=(
            P("fsdp", "ctx", None),
            P("fsdp", "ctx", None),
            P("fsdp", None),
            P("fsdp"),
            P("fsdp", None),
            P("fsdp", None),
            P("fsdp"),
            P("fsdp", None),
            P("fsdp"),
            P("fsdp"),
            P("fsdp"),
            P("fsdp", None),
            P("fsdp"),
            P("fsdp", None),
            P("fsdp"),
            P("fsdp"),
            P("fsdp"),
        ),
        check_vma=False,
    )
```

```python
from functools import partial

import jax
import jax.numpy as jnp
from jax import lax
from jax.experimental import pallas as pl
from jax.experimental.pallas import tpu as pltpu
from jax.sharding import PartitionSpec as P

D = 768
H = 12
HD = 64
SEQ_MB = 1
MICRO = 2


EPSILON = 1e-05
NEG_FILL = -1e30
SCALE = 0.125
ROOT_HALF = 0.7071067811865476
INV_ROOT_TAU = 0.3989422804014327
key_block = 512


def matmul(left_side, right_side):
    return jnp.dot(left_side, right_side, preferred_element_type=jnp.float32)


def left_product(left_side, right_side):
    return lax.dot_general(
        left_side, right_side, (((0,), (0,)), ((), ())), preferred_element_type=jnp.float32
    )


def right_product(left_side, right_side):
    return lax.dot_general(
        left_side, right_side, (((1,), (1,)), ((), ())), preferred_element_type=jnp.float32
    )


def split_heads(token_rows):
    return token_rows.reshape(token_rows.shape[0], token_rows.shape[1], H, HD)


def head_scores(query_rows, key_rows):
    return (
        jnp.einsum(
            "bqhd,bkhd->bhqk",
            split_heads(query_rows),
            split_heads(key_rows),
            preferred_element_type=jnp.float32,
        )
        * SCALE
    )


def live_mask(seq_lens, first_pos, num_rows):
    return (first_pos + lax.iota(jnp.int32, num_rows))[None, :] < seq_lens[:, None]


def layer_norm(resid, norm_gain, norm_bias):
    row_mean = jnp.mean(resid, axis=-1, keepdims=True)
    centered = resid - row_mean
    inv_std = lax.rsqrt(jnp.mean(centered * centered, axis=-1, keepdims=True) + EPSILON)
    normed = centered * inv_std
    return (normed * norm_gain + norm_bias, normed, inv_std)


def norm_back(grad_out, normed, inv_std, norm_gain):
    grad_norm = grad_out * norm_gain
    grad_in = inv_std * (
        grad_norm
        - jnp.mean(grad_norm, axis=-1, keepdims=True)
        - normed * jnp.mean(grad_norm * normed, axis=-1, keepdims=True)
    )
    return (grad_in, jnp.sum(grad_out * normed, axis=0), jnp.sum(grad_out, axis=0))


def gelu_exact(pre_act):
    return 0.5 * pre_act * (1.0 + lax.erf(pre_act * ROOT_HALF))


def gelu_slope(pre_act):
    return 0.5 * (1.0 + lax.erf(pre_act * ROOT_HALF)) + pre_act * INV_ROOT_TAU * jnp.exp(
        -0.5 * pre_act * pre_act
    )


def in_blocks(step_fn, running, pieces):
    num_rows = pieces[0].shape[1]

    def advance(block_index, current):
        offset = block_index * key_block
        sliced = tuple(
            (lax.dynamic_slice_in_dim(member, offset, key_block, 1) for member in pieces)
        )
        return step_fn(current, sliced, offset)

    return lax.fori_loop(0, num_rows // key_block, advance, running)


def attend_step(running, sliced, first_pos, queries, seq_lens, skip_empty):
    key_rows, value_rows = sliced
    live_keys = live_mask(seq_lens, first_pos, key_rows.shape[1])
    run_max, run_sum, run_out = running
    key_mask = live_keys[:, None, None, :]
    scores = jnp.where(key_mask, head_scores(queries, key_rows), NEG_FILL)
    new_max = jnp.maximum(run_max, jnp.max(scores, axis=-1))
    weights = jnp.where(key_mask, jnp.exp(scores - new_max[..., None]), 0.0)
    rescale = jnp.exp(run_max - new_max)
    new_sum = run_sum * rescale + jnp.sum(weights, axis=-1)
    new_out = run_out * rescale[..., None] + jnp.einsum(
        "bhqk,bkhd->bhqd",
        weights.astype(jnp.bfloat16),
        split_heads(value_rows),
        preferred_element_type=jnp.float32,
    )
    return (new_max, new_sum, new_out)


def query_grad_step(
    running,
    sliced,
    first_pos,
    queries,
    grad_context,
    log_total,
    row_delta,
    seq_lens,
    live_queries,
    skip_empty,
):
    key_rows, value_rows = sliced
    live_keys = live_mask(seq_lens, first_pos, key_rows.shape[1])
    key_mask = live_keys[:, None, None, :]
    probabilities = jnp.where(
        key_mask, jnp.exp(head_scores(queries, key_rows) - log_total[..., None]), 0.0
    )
    grad_probs = jnp.einsum(
        "bqhd,bkhd->bhqk",
        split_heads(grad_context),
        split_heads(value_rows),
        preferred_element_type=jnp.float32,
    )
    grad_scores = (probabilities * (grad_probs - row_delta[..., None])).astype(jnp.bfloat16)
    return running + jnp.einsum(
        "bhqk,bkhd->bqhd", grad_scores, split_heads(key_rows), preferred_element_type=jnp.float32
    )


def key_grad_step(
    running,
    sliced,
    first_pos,
    key_rows,
    value_rows,
    stat_total,
    stat_delta,
    seq_lens,
    live_keys,
    skip_empty,
):
    query_rows, grad_rows = sliced
    num_rows = query_rows.shape[1]
    grad_k, grad_v = running
    log_total = lax.dynamic_slice_in_dim(stat_total, first_pos, num_rows, 1).transpose(0, 2, 1)
    row_delta = lax.dynamic_slice_in_dim(stat_delta, first_pos, num_rows, 1).transpose(0, 2, 1)
    key_mask = live_keys[:, None, None, :]
    probabilities = jnp.where(
        key_mask, jnp.exp(head_scores(query_rows, key_rows) - log_total[..., None]), 0.0
    )
    grad_probs = jnp.einsum(
        "bqhd,bkhd->bhqk",
        split_heads(grad_rows),
        split_heads(value_rows),
        preferred_element_type=jnp.float32,
    )
    grad_scores = (probabilities * (grad_probs - row_delta[..., None])).astype(jnp.bfloat16)
    grad_v = grad_v + jnp.einsum(
        "bhqk,bqhd->bkhd",
        probabilities.astype(jnp.bfloat16),
        split_heads(grad_rows),
        preferred_element_type=jnp.float32,
    )
    grad_k = grad_k + jnp.einsum(
        "bhqk,bqhd->bkhd", grad_scores, split_heads(query_rows), preferred_element_type=jnp.float32
    )
    return (grad_k, grad_v)


def body(
    inputs,
    cotangent,
    lengths,
    w_query,
    b_query,
    w_key,
    w_value,
    b_value,
    w_output,
    b_output,
    gain_one,
    bias_one,
    w_inner,
    b_inner,
    w_outer,
    b_outer,
    gain_two,
    bias_two,
):
    gathered = (
        lax.all_gather(w_query, "fsdp", axis=0, tiled=True),
        lax.all_gather(b_query, "fsdp", axis=0, tiled=True),
        lax.all_gather(w_key, "fsdp", axis=0, tiled=True),
        lax.all_gather(w_value, "fsdp", axis=0, tiled=True),
        lax.all_gather(b_value, "fsdp", axis=0, tiled=True),
        lax.all_gather(w_output, "fsdp", axis=0, tiled=True),
        lax.all_gather(b_output, "fsdp", axis=0, tiled=True),
        lax.all_gather(gain_one, "fsdp", axis=0, tiled=True),
        lax.all_gather(bias_one, "fsdp", axis=0, tiled=True),
        lax.all_gather(w_inner, "fsdp", axis=0, tiled=True),
        lax.all_gather(b_inner, "fsdp", axis=0, tiled=True),
        lax.all_gather(w_outer, "fsdp", axis=0, tiled=True),
        lax.all_gather(b_outer, "fsdp", axis=0, tiled=True),
        lax.all_gather(gain_two, "fsdp", axis=0, tiled=True),
        lax.all_gather(bias_two, "fsdp", axis=0, tiled=True),
    )
    (
        query_weight,
        query_bias,
        key_weight,
        value_weight,
        value_bias,
        out_weight,
        out_bias,
        gain_first,
        shift_first,
        inner_weight,
        inner_bias,
        outer_weight,
        outer_bias,
        gain_second,
        shift_second,
    ) = gathered
    joint_weight = jnp.concatenate([query_weight, key_weight, value_weight], axis=1)
    joint_bias = jnp.concatenate(
        [
            query_bias.astype(jnp.float32),
            jnp.zeros((D,), jnp.float32),
            value_bias.astype(jnp.float32),
        ]
    )
    out_bias_f = out_bias.astype(jnp.float32)
    inner_bias_f = inner_bias.astype(jnp.float32)
    outer_bias_f = outer_bias.astype(jnp.float32)
    gain_first_f = gain_first.astype(jnp.float32)
    shift_first_f = shift_first.astype(jnp.float32)
    gain_second_f = gain_second.astype(jnp.float32)
    shift_second_f = shift_second.astype(jnp.float32)
    seq_dev = inputs.shape[1]
    row_count = SEQ_MB * seq_dev
    positions = lax.axis_index("ctx") * seq_dev + lax.iota(jnp.int32, seq_dev)
    accum = None
    out_list = []
    grad_list = []
    for micro_index in range(MICRO):
        first_seq = micro_index * SEQ_MB
        seq_lens = lengths[first_seq : first_seq + SEQ_MB]
        token_rows = inputs[first_seq : first_seq + SEQ_MB].reshape(row_count, D)
        grad_rows = (
            cotangent[first_seq : first_seq + SEQ_MB].reshape(row_count, D).astype(jnp.float32)
        )
        query_ok = positions[None, :] < seq_lens[:, None]
        row_keep = query_ok.reshape(row_count, 1).astype(jnp.float32)
        projected = (matmul(token_rows, joint_weight) + joint_bias).astype(jnp.bfloat16)
        queries = projected[:, :D].reshape(SEQ_MB, seq_dev, D)
        keys_local = projected[:, D : 2 * D].reshape(SEQ_MB, seq_dev, D)
        values_local = projected[:, 2 * D :].reshape(SEQ_MB, seq_dev, D)
        start_state = (
            jnp.full((SEQ_MB, H, seq_dev), NEG_FILL, jnp.float32),
            jnp.zeros((SEQ_MB, H, seq_dev), jnp.float32),
            jnp.zeros((SEQ_MB, H, seq_dev, HD), jnp.float32),
        )
        attend_fn = partial(attend_step, queries=queries, seq_lens=seq_lens, skip_empty=False)
        run_max, run_sum, run_out = in_blocks(
            attend_fn,
            start_state,
            (
                lax.all_gather(keys_local, "ctx", axis=1, tiled=True),
                lax.all_gather(values_local, "ctx", axis=1, tiled=True),
            ),
        )
        attended = run_out / run_sum[..., None]
        log_total = run_max + jnp.log(run_sum)
        context = attended.transpose(0, 2, 1, 3).reshape(row_count, D).astype(jnp.bfloat16)
        first_sum = token_rows.astype(jnp.float32) + matmul(context, out_weight) + out_bias_f
        hidden, normed_one, inv_one = layer_norm(first_sum, gain_first_f, shift_first_f)
        hidden_low = hidden.astype(jnp.bfloat16)
        inner_pre = matmul(hidden_low, inner_weight) + inner_bias_f
        activated = gelu_exact(inner_pre).astype(jnp.bfloat16)
        outer_out = matmul(activated, outer_weight) + outer_bias_f
        result, normed_two, inv_two = layer_norm(hidden + outer_out, gain_second_f, shift_second_f)
        out_list.append(result.astype(jnp.bfloat16).reshape(SEQ_MB, seq_dev, D))
        grad_out = grad_rows * row_keep
        grad_second, grad_gain_b, grad_shift_b = norm_back(
            grad_out, normed_two, inv_two, gain_second_f
        )
        grad_outer = grad_second.astype(jnp.bfloat16)
        grad_outer_w = left_product(activated, grad_outer)
        grad_outer_b = jnp.sum(grad_outer.astype(jnp.float32), axis=0)
        grad_inner = (right_product(grad_outer, outer_weight) * gelu_slope(inner_pre)).astype(
            jnp.bfloat16
        )
        grad_inner_w = left_product(hidden_low, grad_inner)
        grad_inner_b = jnp.sum(grad_inner.astype(jnp.float32), axis=0)
        grad_hidden = grad_second + right_product(grad_inner, inner_weight)
        grad_first, grad_gain_a, grad_shift_a = norm_back(
            grad_hidden, normed_one, inv_one, gain_first_f
        )
        grad_branch = grad_first.astype(jnp.bfloat16)
        grad_out_w = left_product(context, grad_branch)
        grad_out_b = jnp.sum(grad_branch.astype(jnp.float32), axis=0)
        grad_context = (
            right_product(grad_branch, out_weight).astype(jnp.bfloat16).reshape(SEQ_MB, seq_dev, D)
        )
        row_delta = jnp.einsum(
            "bqhd,bhqd->bhq", split_heads(grad_context).astype(jnp.float32), attended
        )
        stat_total, stat_delta = (
            lax.all_gather(log_total.transpose(0, 2, 1), "ctx", axis=1, tiled=True),
            lax.all_gather(row_delta.transpose(0, 2, 1), "ctx", axis=1, tiled=True),
        )
        query_fn = partial(
            query_grad_step,
            queries=queries,
            grad_context=grad_context,
            log_total=log_total,
            row_delta=row_delta,
            seq_lens=seq_lens,
            live_queries=query_ok,
            skip_empty=False,
        )
        key_fn = partial(
            key_grad_step,
            key_rows=keys_local,
            value_rows=values_local,
            stat_total=stat_total,
            stat_delta=stat_delta,
            seq_lens=seq_lens,
            live_keys=query_ok,
            skip_empty=False,
        )
        grad_zero = jnp.zeros((SEQ_MB, seq_dev, H, HD), jnp.float32)
        grad_q = in_blocks(
            query_fn,
            grad_zero,
            (
                lax.all_gather(keys_local, "ctx", axis=1, tiled=True),
                lax.all_gather(values_local, "ctx", axis=1, tiled=True),
            ),
        )
        grad_k, grad_v = in_blocks(
            key_fn,
            (grad_zero, grad_zero),
            (
                lax.all_gather(queries, "ctx", axis=1, tiled=True),
                lax.all_gather(grad_context, "ctx", axis=1, tiled=True),
            ),
        )
        joint_grad = jnp.concatenate(
            [
                (grad_q * SCALE).reshape(row_count, D).astype(jnp.bfloat16),
                (grad_k * SCALE).reshape(row_count, D).astype(jnp.bfloat16),
                grad_v.reshape(row_count, D).astype(jnp.bfloat16),
            ],
            axis=1,
        )
        grad_joint_w = left_product(token_rows, joint_grad)
        grad_joint_b = jnp.sum(joint_grad.astype(jnp.float32), axis=0)
        input_rows = grad_first + right_product(joint_grad, joint_weight)
        grad_list.append(input_rows.reshape(SEQ_MB, seq_dev, D))
        micro_grads = (
            grad_joint_w,
            grad_joint_b,
            grad_out_w,
            grad_out_b,
            grad_gain_a,
            grad_shift_a,
            grad_inner_w,
            grad_inner_b,
            grad_outer_w,
            grad_outer_b,
            grad_gain_b,
            grad_shift_b,
        )
        if accum is None:
            accum = micro_grads
        else:
            accum = tuple((held + fresh for held, fresh in zip(accum, micro_grads)))
    (
        joint_w,
        joint_b,
        out_w,
        out_b,
        gain_a,
        shift_a,
        inner_w,
        inner_b,
        outer_w,
        outer_b,
        gain_b,
        shift_b,
    ) = accum
    grad_set = (
        joint_w[:, :D],
        joint_b[:D],
        joint_w[:, D : 2 * D],
        joint_w[:, 2 * D :],
        joint_b[2 * D :],
        out_w,
        out_b,
        gain_a,
        shift_a,
        inner_w,
        inner_b,
        outer_w,
        outer_b,
        gain_b,
        shift_b,
    )
    shard_grads = (
        lax.psum_scatter(
            grad_set[0].astype(jnp.bfloat16), "fsdp", scatter_dimension=0, tiled=True
        ).astype(jnp.float32),
        lax.psum_scatter(
            grad_set[1].astype(jnp.bfloat16), "fsdp", scatter_dimension=0, tiled=True
        ).astype(jnp.float32),
        lax.psum_scatter(
            grad_set[2].astype(jnp.bfloat16), "fsdp", scatter_dimension=0, tiled=True
        ).astype(jnp.float32),
        lax.psum_scatter(
            grad_set[3].astype(jnp.bfloat16), "fsdp", scatter_dimension=0, tiled=True
        ).astype(jnp.float32),
        lax.psum_scatter(
            grad_set[4].astype(jnp.bfloat16), "fsdp", scatter_dimension=0, tiled=True
        ).astype(jnp.float32),
        lax.psum_scatter(
            grad_set[5].astype(jnp.bfloat16), "fsdp", scatter_dimension=0, tiled=True
        ).astype(jnp.float32),
        lax.psum_scatter(
            grad_set[6].astype(jnp.bfloat16), "fsdp", scatter_dimension=0, tiled=True
        ).astype(jnp.float32),
        lax.psum_scatter(
            grad_set[7].astype(jnp.bfloat16), "fsdp", scatter_dimension=0, tiled=True
        ).astype(jnp.float32),
        lax.psum_scatter(
            grad_set[8].astype(jnp.bfloat16), "fsdp", scatter_dimension=0, tiled=True
        ).astype(jnp.float32),
        lax.psum_scatter(
            grad_set[9].astype(jnp.bfloat16), "fsdp", scatter_dimension=0, tiled=True
        ).astype(jnp.float32),
        lax.psum_scatter(
            grad_set[10].astype(jnp.bfloat16), "fsdp", scatter_dimension=0, tiled=True
        ).astype(jnp.float32),
        lax.psum_scatter(
            grad_set[11].astype(jnp.bfloat16), "fsdp", scatter_dimension=0, tiled=True
        ).astype(jnp.float32),
        lax.psum_scatter(
            grad_set[12].astype(jnp.bfloat16), "fsdp", scatter_dimension=0, tiled=True
        ).astype(jnp.float32),
        lax.psum_scatter(
            grad_set[13].astype(jnp.bfloat16), "fsdp", scatter_dimension=0, tiled=True
        ).astype(jnp.float32),
        lax.psum_scatter(
            grad_set[14].astype(jnp.bfloat16), "fsdp", scatter_dimension=0, tiled=True
        ).astype(jnp.float32),
    )
    summed = lax.psum(
        (
            shard_grads[0],
            shard_grads[1],
            shard_grads[2],
            shard_grads[3],
            shard_grads[4],
            shard_grads[5],
            shard_grads[6],
            shard_grads[7],
            shard_grads[8],
            shard_grads[9],
            shard_grads[10],
            shard_grads[11],
            shard_grads[12],
            shard_grads[13],
            shard_grads[14],
        ),
        "ctx",
    )
    outputs = jnp.concatenate(out_list, axis=0)
    input_grad = jnp.concatenate(grad_list, axis=0)
    return (outputs, input_grad) + tuple(summed)


HALF = D // 2
ROWS = 128


def flat(z, x, y, k):
    return (z * 2 + x) * 4 + y * 2 + k


def table(move):
    return [
        (flat(z, x, y, k), flat(*move(z, x, y, k)))
        for z in range(4)
        for x in range(2)
        for y in range(2)
        for k in range(2)
    ]


def permute(move):
    pairs = table(move)
    return lambda block: lax.ppermute(block, ("ctx", "fsdp"), pairs)


def permute_back(move):
    pairs = [(b, a) for a, b in table(move)]
    return lambda block: lax.ppermute(block, ("ctx", "fsdp"), pairs)


def to_seq(turn):
    return lambda z, x, y, k: (2 * k + (z // 2 + turn) % 2, x, y, z % 2)


swap_core = permute(lambda z, x, y, k: (z, x, y, k ^ 1))
swap_y = permute(lambda z, x, y, k: (z, x, y ^ 1, k))
swap_x = permute(lambda z, x, y, k: (z, x ^ 1, y, k))
swap_z1 = permute(lambda z, x, y, k: (z ^ 1, x, y, k))
swap_z2 = permute(lambda z, x, y, k: (z ^ 2, x, y, k))
seq_send = (permute(to_seq(0)), permute(to_seq(1)))
seq_return = (permute_back(to_seq(0)), permute_back(to_seq(1)))


def low(value):
    return value.astype(jnp.bfloat16)


def wide(value):
    return value.astype(jnp.float32)


def pick(array, index, axis=0):
    return lax.dynamic_index_in_dim(array, index, axis, keepdims=False)


def dot_nt(a, b):
    return lax.dot_general(a, b, (((1,), (1,)), ((), ())), preferred_element_type=jnp.float32)


def dot_tn(a, b):
    return lax.dot_general(a, b, (((0,), (0,)), ((), ())), preferred_element_type=jnp.float32)


def coords(info):
    c, f = info[0] >> 2, info[0] & 3
    return c >> 1, c & 1, f >> 1, f & 1, c, f


def pack_kernel(
    info, lens, rows, grads, w_q, w_k, w_v, w_o, w_in, v0, v1, v2, v3, v4, v5, v6, v7, wide_vec,
    t0, t1, cot, first, half, held,
):
    z, x, _, _, _, _ = coords(info)
    zh = z >> 1
    half[...] = w_in[...]
    t0[...] = rows[zh]
    t1[...] = rows[1 - zh]
    cot[:ROWS] = grads[zh]
    cot[ROWS:] = grads[1 - zh]
    columns = pl.ds(pl.multiple_of(x * HALF, 128), HALF)
    first[:192, :D] = w_o[...]
    for n, weight in enumerate((w_q, w_k, w_v)):
        first[:192, D + HALF * n : D + HALF * n + HALF] = weight[:, columns]
    held[...] = jnp.zeros_like(held)
    for n, vector in enumerate((v0, v1, v2, v3, v4, v5, v6, v7)):
        held[n : n + 1, :192] = wide(vector[...]).reshape(1, 192)
    held[8:9, :] = wide(wide_vec[...]).reshape(1, D)
    lane = lax.broadcasted_iota(jnp.int32, (1, D), 1)
    ends = jnp.zeros((1, D), jnp.int32)
    for n in range(2):
        ends = jnp.where(lane == n, lens[n] >> 7, ends)
        ends = jnp.where(lane == 2 + n, lens[n] & 127, ends)
    held[9:10, :] = wide(ends)
    first[192:, :D] = low(held[...])
    first[192:, D:] = jnp.zeros((16, 3 * HALF), jnp.bfloat16)


def attend_kernel(
    info, b0, b1, b2, b3, b4, b5, b6, b7, s0, s1, s2, s3, w0, w1, w2, w3,
    xs, ws, q_out, k_out, v_out, p_out, cu, cv, cx, key_bias, small, sems,
):
    step = pl.program_id(0)
    z, x, y, k, _, f = coords(info)

    @pl.when(step == 0)
    def _():
        copies = [
            pltpu.make_async_copy(
                piece.at[:192, D:], ws.at[pl.ds(pl.multiple_of(192 * (f ^ n), 64), 192), :], sems.at[n]
            )
            for n, piece in enumerate((w0, w1, w2, w3))
        ]
        blocks = (b0, b1, b2, b3, b4, b5, b6, b7)
        copies += [
            pltpu.make_async_copy(block, xs.at[n * ROWS : (n + 1) * ROWS, :], sems.at[4 + n])
            for n, block in enumerate(blocks)
        ]
        for copy in copies:
            copy.start()
        for n, piece in enumerate((s0, s1, s2, s3)):
            small[f ^ n] = wide(piece[...])
        line = small[2 * y + (z >> 1)][9:10, :]
        lane = lax.broadcasted_iota(jnp.int32, (1, D), 1)
        part = jnp.where(lane == (z & 1), 128.0 * line, 0.0)
        part = part + jnp.where(lane == 2 + (z & 1), line, 0.0)
        end = jnp.sum(part, axis=1, keepdims=True)
        z_low = 2 * (z & 1)
        for n, block in enumerate(blocks):
            z_block = (z_low if n % 2 == 0 else 2 - z_low) + (k if n < 4 else 1 - k)
            x_block = x if n % 4 < 2 else 1 - x
            place = (2 * z_block + x_block) * ROWS + lax.broadcasted_iota(jnp.int32, (1, ROWS), 1)
            key_bias[:, n * ROWS : (n + 1) * ROWS] = jnp.where(wide(place) < end, 0.0, NEG_FILL)
        for copy in copies:
            copy.wait()

        def bias(row):
            return jnp.concatenate(
                [small[2 * x + n][row : row + 1, :192] for n in range(2)], axis=1
            )

        q_out[...] = low(wide(low(matmul(xs[: 4 * ROWS, :], ws[:, :HALF]) + bias(0))) * SCALE)
        k_out[...] = low(matmul(xs[...], ws[:, HALF : 2 * HALF]))
        v_out[...] = low(matmul(xs[...], ws[:, 2 * HALF :]) + bias(1))

    lanes = pl.ds(pl.multiple_of(step * 128, 128), 128)
    first = lax.broadcasted_iota(jnp.int32, (1, 128), 1) < HD
    queries = q_out[:, lanes]
    keys = k_out[:, lanes]
    values = v_out[:, lanes]
    for part in range(2):
        rows = slice(part * 256, part * 256 + 256)
        found = []
        for head in range(2):
            mine = first if head == 0 else jnp.logical_not(first)
            scores = dot_nt(jnp.where(mine, queries[rows], 0), keys) + key_bias[...]
            top = jnp.max(scores, axis=1, keepdims=True)
            weights = jnp.exp(scores - top)
            total = jnp.sum(weights, axis=1, keepdims=True)
            probs = low(weights * (1.0 / total))
            p_out[head, rows, :] = probs
            found.append(matmul(probs, values))
        context = low(jnp.where(first, found[0], found[1]))
        if part == 0:
            cu[...] = context[:ROWS]
            cv[...] = context[ROWS:]
        else:
            cx[0] = context[:ROWS]
            cx[1] = context[ROWS:]


def pair_back(queries_ref, keys, values, probs_ref, grads):
    first = lax.broadcasted_iota(jnp.int32, (1, 128), 1) < HD
    grad_k = jnp.zeros((8 * ROWS, 128), jnp.float32)
    grad_v = jnp.zeros((8 * ROWS, 128), jnp.float32)
    grad_qs = []
    for part in range(2):
        rows = slice(part * 256, part * 256 + 256)
        one, two = grads[2 * part : 2 * part + 2]
        grad_rows = jnp.concatenate([one[...], two[...]], axis=0)
        queries = queries_ref[rows, :]
        grad_q = jnp.zeros((256, 128), jnp.float32)
        for head in range(2):
            mine = first if head == 0 else jnp.logical_not(first)
            grad_mine = jnp.where(mine, grad_rows, 0)
            probs = probs_ref[head, rows, :]
            grad_probs = dot_nt(grad_mine, values)
            product = wide(probs) * grad_probs
            delta = jnp.sum(product, axis=1, keepdims=True)
            grad_scores = low(product - wide(probs) * delta)
            grad_q = grad_q + matmul(grad_scores, jnp.where(mine, keys, 0))
            grad_k = grad_k + dot_tn(grad_scores, jnp.where(mine, queries, 0))
            grad_v = grad_v + dot_tn(probs, grad_mine)
        grad_qs.append(low(grad_q * SCALE))
    return grad_qs, low(grad_k), low(grad_v)


def attend_back_kernel(queries, keys, values, probs, gu, gv, gxu, gxv, dq, dk, dv):
    grad_qs, dk[...], dv[...] = pair_back(
        queries, keys[...], values[...], probs, (gu, gv, gxu, gxv)
    )
    dq[:256, :], dq[256:, :] = grad_qs


def joint_kernel(
    info, xs, dq0, dq1, dq2, dk0, dk1, dk2, dv0, dv1, dv2, keep, send, grads, dw
):
    for n, (q, k, v) in enumerate(((dq0, dk0, dv0), (dq1, dk1, dv1), (dq2, dk2, dv2))):
        start = 128 * n
        grads[: 4 * ROWS, start : start + 128] = q[...]
        grads[:, HALF + start : HALF + start + 128] = k[...]
        grads[:, 2 * HALF + start : 2 * HALF + start + 128] = v[...]
    own = slice(0, 4 * ROWS)
    dw[:, :HALF] = low(dot_tn(xs[own, :], grads[own, :HALF]))
    dw[:, HALF:] = low(dot_tn(xs[...], grads[:, HALF:]))
    col_sums = jnp.concatenate(
        [
            column_sum(wide(grads[own, :HALF])),
            jnp.zeros((1, HALF), jnp.float32),
            column_sum(wide(grads[:, 2 * HALF :])),
        ],
        axis=1,
    )
    tail = low(jnp.where(lax.broadcasted_iota(jnp.int32, (16, 1), 0) == 0, col_sums, 0.0))
    z, _, _, _, _, f = coords(info)
    for n in range(4):
        place = send if n % 2 else keep
        for half in range(2):
            start = pl.multiple_of(192 * (f ^ n) + 96 * half, 32)
            place[n // 2, half ^ (z & 1), :96, :] = dw[pl.ds(start, 96), :]
            place[n // 2, half ^ (z & 1), 96:, :] = tail if half == 0 else tail * 0


def rows_back_kernel(
    ws, dq0, dq1, dq2, dk0, dk1, dk2, dv0, dv1, dv2, dx_own, dx_other, grads
):
    for n, (q, k, v) in enumerate(((dq0, dk0, dv0), (dq1, dk1, dv1), (dq2, dk2, dv2))):
        start = 128 * n
        grads[: 4 * ROWS, start : start + 128] = q[...]
        grads[:, HALF + start : HALF + start + 128] = k[...]
        grads[:, 2 * HALF + start : 2 * HALF + start + 128] = v[...]
    dx_other[...] = low(dot_nt(grads[4 * ROWS :, HALF:], ws[:, HALF:]))
    dx_own[...] = dot_nt(grads[: 4 * ROWS, :], ws[...])


def middle_one_kernel(
    info, cm0, cm1, co0, co1, x0, x1, o0, o1, o2, o3, i0, i1, i2, i3,
    hidden_out, normed_out, inv_out, act, slope, vec,
    ctx, low_rows, small, order, inner_weight, sems,
):
    step = pl.program_id(0)
    _, x, _, _, _, f = coords(info)

    def copy(e, n):
        return pltpu.make_async_copy(
            (i0, i1, i2, i3)[n].at[:, pl.ds(pl.multiple_of(D * (f ^ e), 128), D)],
            inner_weight.at[e, pl.ds(pl.multiple_of(192 * (f ^ n), 64), 192), :],
            sems.at[e, n],
        )

    @pl.when(step == 0)
    def _():
        for e in range(4):
            for n in range(4):
                copy(e, n).start()
        for n, piece in enumerate((o0, o1, o2, o3)):
            small[f ^ n] = wide(piece[192:, :])
            order[n] = wide(piece[192:, :])
        for n in range(8):
            vec[n : n + 1, :] = jnp.concatenate(
                [small[m][n : n + 1, :192] for m in range(4)], axis=1
            )
        for side, (one, two) in enumerate(((cm0, cm1), (co0, co1))):
            rows = jnp.concatenate([one[...], two[...]], axis=0)
            for part in range(2):
                ctx[2 * (x ^ side) + part] = rows[:, 192 * part : 192 * part + 192]
        total = wide(jnp.concatenate([x0[...], x1[...]], axis=0)) + vec[2:3, :]
        for n, piece in enumerate((o0, o1, o2, o3)):
            total = total + matmul(ctx[f ^ n], piece[:192, :])
        hidden, normed, inv = layer_norm(total, vec[3:4, :], vec[4:5, :])
        hidden_out[...] = hidden
        normed_out[...] = normed
        inv_out[...] = inv
        low_rows[...] = low(hidden)

    for n in range(4):
        copy(step, n).wait()
    pre = matmul(low_rows[...], inner_weight[step]) + order[step][8:9, :]
    bell = 0.5 * (1.0 + lax.erf(pre * ROOT_HALF))
    act[0] = low(pre * bell)
    slope[0] = low(bell + pre * INV_ROOT_TAU * jnp.exp(-0.5 * pre * pre))


def norm_grad(grad, normed, inv, gain):
    scaled = grad * gain
    return inv * (
        scaled
        - jnp.mean(scaled, axis=-1, keepdims=True)
        - normed * jnp.mean(scaled * normed, axis=-1, keepdims=True)
    )


def column_sum(value):
    return jnp.sum(value, axis=0, keepdims=True)


def outer_copies(refs, held, sems):
    copies = [
        pltpu.make_async_copy(ref, held.at[n], sems.at[n]) for n, ref in enumerate(refs)
    ]
    for copy in copies:
        copy.start()
    return copies


def middle_two_kernel(
    info, lens, act, act_block, hidden, cot, vec, w0, w1, w2, w3,
    out, second_out, outer_out, sums, keep, send, w_all, w_sem,
):
    step = pl.program_id(0)
    z, x, _, _, c, f = coords(info)

    @pl.when(step == 0)
    def _():
        copies = outer_copies((w0, w1, w2, w3), w_all, w_sem)
        b_2, g_2, s_2 = vec[5:6, :], vec[6:7, :], vec[7:8, :]
        total = hidden[...] + b_2
        for n in range(4):
            copies[n].wait()
            total = total + matmul(act[n], w_all[n])
        result, normed, inv = layer_norm(total, g_2, s_2)
        zh = z >> 1
        out[zh] = low(result[:ROWS])
        out[1 - zh] = low(result[ROWS:])
        row = lax.broadcasted_iota(jnp.int32, (2 * ROWS, 1), 0)
        end = jnp.where(row < ROWS, lens[zh], lens[1 - zh] + ROWS)
        grad = wide(cot[...]) * jnp.where(row + c * ROWS < end, 1.0, 0.0)
        grad_second = norm_grad(grad, normed, inv, g_2)
        second_out[...] = grad_second
        grad_outer = low(grad_second)
        outer_out[...] = grad_outer
        sums[...] = jnp.zeros_like(sums)
        for n, value in enumerate((wide(grad_outer), grad * normed, grad)):
            sums[n : n + 1, :] = column_sum(value)

    @pl.when(step > 0)
    def _():
        grad = low(dot_tn(act_block[0], outer_out[...]))
        for place, wanted in ((send, step < 3), (keep, step >= 3)):

            @pl.when(wanted)
            def _(place=place):
                for n in range(4):
                    place[0, n ^ (2 * x + (z & 1))] = grad[192 * n : 192 * n + 192]


def inner_back_kernel(
    info, outer, slope, w0, w1, w2, w3, inner_out, sums, w_all, sems
):
    f = info[0] & 3
    copies = outer_copies((w0, w1, w2, w3), w_all, sems)
    for e in range(4):
        copies[e].wait()
        inner = low(dot_nt(outer[...], w_all[e]) * wide(slope[e]))
        inner_out[e] = inner
        sums[pl.ds(f ^ e, 1), :] = column_sum(wide(inner))


def middle_three_kernel(
    info, second, inner, normed_one, inv_one, vec, o0, o1, o2, o3, i0, i1, i2, i3,
    first_out, g0, g1, branch_out, sums, o_all, i_all, gc, o_sem, i_sem,
):
    _, x, _, _, _, f = coords(info)
    copies = {}
    for e in range(4):
        columns = pl.ds(pl.multiple_of(D * (f ^ e), 128), D)
        for n, ref in enumerate((i0, i1, i2, i3)):
            rows = pl.ds(pl.multiple_of(192 * (f ^ n), 64), 192)
            copies["i", e, n] = pltpu.make_async_copy(
                ref.at[:, columns], i_all.at[e, rows, :], i_sem.at[e, n]
            )
            copies["i", e, n].start()
    for n, ref in enumerate((o0, o1, o2, o3)):
        copies["o", n] = pltpu.make_async_copy(ref.at[:192, :D], o_all.at[n], o_sem.at[n])
        copies["o", n].start()
    grad_hidden = second[...]
    for e in range(4):
        for n in range(4):
            copies["i", e, n].wait()
        grad_hidden = grad_hidden + dot_nt(inner[e], i_all[e])
    grad_first = norm_grad(grad_hidden, normed_one[...], inv_one[...], vec[3:4, :])
    first_out[...] = grad_first
    branch = low(grad_first)
    branch_out[...] = branch
    for n, value in enumerate((wide(branch), grad_hidden * normed_one[...], grad_hidden)):
        sums[n : n + 1, :] = column_sum(value)
    for n in range(4):
        copies["o", n].wait()
        gc[f ^ n] = low(dot_nt(branch, o_all[n]))
    for side in range(2):
        rows = jnp.concatenate([gc[2 * (x ^ side)], gc[2 * (x ^ side) + 1]], axis=1)
        g0[1 - side] = rows[:ROWS]
        g1[1 - side] = rows[ROWS:]


def middle_four_kernel(
    info, inner, hidden, branch, cm0, cm1, co0, co1, sums_two, sums_in, sums_one,
    keep, send, held, out_held, vec_held,
):
    step = pl.program_id(0)
    _, x, _, _, _, f = coords(info)
    block = f ^ step

    @pl.when(step == 0)
    def _():
        for side, (one, two) in enumerate(((cm0, cm1), (co0, co1))):
            rows = jnp.concatenate([one[...], two[...]], axis=0)
            start = pl.multiple_of(HALF * (x ^ side), 128)
            out_held[pl.ds(start, HALF), :] = low(dot_tn(rows, branch[...]))
        vec_held[...] = jnp.zeros_like(vec_held)
        top = lax.broadcasted_iota(jnp.int32, (16, 1), 0) == 0
        for n in range(4):
            cut = slice(192 * n, 192 * n + 192)
            lines = (
                sums_in[n : n + 1, :],
                jnp.concatenate(
                    [sums_one[m : m + 1, cut] for m in range(3)] + [sums_two[0:1, cut]], axis=1
                ),
                jnp.concatenate(
                    [sums_two[1:2, cut], sums_two[2:3, cut], jnp.zeros((1, HALF), jnp.float32)],
                    axis=1,
                ),
            )
            for m, line in enumerate(lines):
                vec_held[m, n] = low(jnp.where(top, line, 0.0))

    held[...] = low(dot_tn(low(hidden[...]), inner[0]))
    for n in range(4):
        place = send if n % 2 else keep
        start = 192 * (f ^ n)
        place[n // 2, 0, :192, :] = held[pl.ds(pl.multiple_of(start, 64), 192), :]
        place[n // 2, 0, 192:240, :] = out_held[pl.ds(pl.multiple_of(start + 48 * block, 16), 48), :]
        place[n // 2, 0, 240:, :] = vec_held[block, f ^ n]


MIDDLE = 2 * ROWS
BF, FP = jnp.bfloat16, jnp.float32


def whole(shape):
    return pl.BlockSpec(tuple(shape), lambda *_: (0,) * len(shape))


def lane_block(rows, start=0):
    return pl.BlockSpec((rows, 128), lambda step, *_: (0, step + start))


def call(kernel, name, grid, scalars, operands, outs, scratch=(), work=(1, 1), limit=30):
    return pl.pallas_call(
        kernel,
        out_shape=[jax.ShapeDtypeStruct(shape, kind) for shape, kind, _ in outs],
        grid_spec=pltpu.PrefetchScalarGridSpec(
            num_scalar_prefetch=len(scalars),
            grid=(grid,),
            in_specs=[spec or whole(array.shape) for array, spec in operands],
            out_specs=[spec or whole(shape) for shape, _, spec in outs],
            scratch_shapes=list(scratch),
        ),
        compiler_params=pltpu.CompilerParams(
            dimension_semantics=("arbitrary",), vmem_limit_bytes=limit * 1024 * 1024
        ),
        cost_estimate=pl.CostEstimate(
            flops=1000, bytes_accessed=1000, transcendentals=0
        ),
        name=name,
    )(*scalars, *[array for array, _ in operands])


def plain(arrays):
    return [(array, None) for array in arrays]


def anywhere(arrays):
    return [(array, pl.BlockSpec(memory_space=pl.ANY)) for array in arrays]


def probs_block(start=0):
    return pl.BlockSpec((2, 4 * ROWS, 8 * ROWS), lambda step, *_: (step + start, 0, 0))


def pack(info, lens, inputs, cotangent, weights, vectors):
    return call(
        pack_kernel, "pack", 1, (info, lens),
        plain([inputs, cotangent, *weights[:4]])
        + [(weights[4], pl.BlockSpec((192, 2 * D), lambda _, info, lens: (0, (info[0] >> 2) & 1)))]
        + plain(vectors),
        [
            ((ROWS, D), BF, None), ((ROWS, D), BF, None), ((MIDDLE, D), BF, None),
            ((208, D + 3 * HALF), BF, None), ((192, 2 * D), BF, None),
        ],
        [pltpu.VMEM((16, D), FP)], limit=56,
    )


def first_columns(pieces):
    return [(piece, pl.BlockSpec((208, D), lambda *_: (0, 0))) for piece in pieces]


def attend(info, blocks, pieces):
    return call(
        attend_kernel, "attend", 3, (info,),
        anywhere(blocks)
        + [(piece, pl.BlockSpec((16, D), lambda *_: (12, 0))) for piece in pieces]
        + anywhere(pieces),
        [
            ((8 * ROWS, D), BF, None), ((D, 3 * HALF), BF, None), ((4 * ROWS, HALF), BF, None),
            ((8 * ROWS, HALF), BF, None), ((8 * ROWS, HALF), BF, None),
            ((6, 4 * ROWS, 8 * ROWS), BF, probs_block()),
        ]
        + [((ROWS, HALF), BF, lane_block(ROWS))] * 2
        + [((2, ROWS, HALF), BF, pl.BlockSpec((2, ROWS, 128), lambda step, *_: (0, 0, step)))],
        [
            pltpu.VMEM((1, 8 * ROWS), FP), pltpu.VMEM((4, 16, D), FP),
            pltpu.SemaphoreType.DMA((12,)),
        ],
        limit=56,
    )


def attend_back(queries, keys, values, probs, grads, start, pairs):
    return call(
        attend_back_kernel, "attend_back", pairs, (),
        [
            (queries, lane_block(4 * ROWS, start)), (keys, lane_block(8 * ROWS, start)),
            (values, lane_block(8 * ROWS, start)), (probs, probs_block(start)),
        ]
        + [(grad, pl.BlockSpec((None, ROWS, 128), lambda s, n=n: (n, 0, s + start))) for grad, n in grads],
        [
            ((4 * ROWS, 128 * pairs), BF, lane_block(4 * ROWS)),
            ((8 * ROWS, 128 * pairs), BF, lane_block(8 * ROWS)),
            ((8 * ROWS, 128 * pairs), BF, lane_block(8 * ROWS)),
        ],
        (), (4 * pairs, 5 * pairs),
    )


def by_name(pairs):
    return [part for name in zip(*pairs) for part in name]


def joint_grads(info, xs, pairs):
    joint = (2, 2, 112, 3 * HALF)
    return call(
        joint_kernel, "joint_grads", 1, (info,), plain([xs, *by_name(pairs)]),
        [(joint, BF, None), (joint, BF, None)],
        [pltpu.VMEM((8 * ROWS, 3 * HALF), BF), pltpu.VMEM((D, 3 * HALF), BF)],
    )


def rows_back(ws, pairs):
    return call(
        rows_back_kernel, "rows_back", 1, (), plain([ws, *by_name(pairs)]),
        [((4 * ROWS, D), FP, None), ((4 * ROWS, D), BF, None)],
        [pltpu.VMEM((8 * ROWS, 3 * HALF), BF)],
    )


def middle_one(info, ctx, rows, out_p, inner_p):
    block = pl.BlockSpec((1, MIDDLE, D), lambda step, *_: (step, 0, 0))
    return call(
        middle_one_kernel, "middle_one", 4, (info,),
        plain([*ctx, *rows]) + first_columns(out_p) + anywhere(inner_p),
        [
            ((MIDDLE, D), FP, None), ((MIDDLE, D), FP, None), ((MIDDLE, 1), FP, None),
            ((4, MIDDLE, D), BF, block), ((4, MIDDLE, D), BF, block), ((8, D), FP, None),
        ],
        [
            pltpu.VMEM((4, MIDDLE, 192), BF), pltpu.VMEM((MIDDLE, D), BF),
            pltpu.VMEM((4, 16, D), FP), pltpu.VMEM((4, 16, D), FP), pltpu.VMEM((4, D, D), BF),
            pltpu.SemaphoreType.DMA((4, 4)),
        ],
        (4, 10),
    )


def middle_two(info, lens, act, hidden, cot, vec, outer_p):
    def turn(step, *_):
        at = jnp.maximum(step - 1, 0)
        return (jnp.where(at < 2, 2 * at + 1, 2 * at - 4), 0, 0)

    blocks = (2, 4, 192, D)
    return call(
        middle_two_kernel, "middle_two", 5, (info, lens),
        [(act, None), (act, pl.BlockSpec((1, MIDDLE, D), turn))]
        + plain([hidden, cot, vec])
        + anywhere(outer_p),
        [
            ((2, ROWS, D), BF, None), ((MIDDLE, D), FP, None), ((MIDDLE, D), BF, None),
            ((8, D), FP, None),
            (blocks, BF, pl.BlockSpec((1, 4, 192, D), lambda s, *_: (jnp.maximum(s - 3, 0), 0, 0, 0))),
            (blocks, BF, pl.BlockSpec((1, 4, 192, D), lambda s, *_: (jnp.where(s < 2, 0, 1), 0, 0, 0))),
        ],
        [pltpu.VMEM((4, D, D), BF), pltpu.SemaphoreType.DMA((4,))], (4, 10),
    )


def inner_back(info, outer, slope, outer_p):
    return call(
        inner_back_kernel, "inner_back", 1, (info,), plain([outer, slope]) + anywhere(outer_p),
        [((4, MIDDLE, D), BF, None), ((4, D), FP, None)],
        [pltpu.VMEM((4, D, D), BF), pltpu.SemaphoreType.DMA((4,))], (2, 7),
    )


def middle_three(info, second, inner, normed, inv, vec, out_p, inner_p):
    return call(
        middle_three_kernel, "middle_three", 1, (info,),
        plain([second, inner, normed, inv, vec]) + anywhere([*out_p, *inner_p]),
        [((MIDDLE, D), FP, None)]
        + [((2, ROWS, HALF), BF, None)] * 2
        + [((MIDDLE, D), BF, None), ((8, D), FP, None)],
        [
            pltpu.VMEM((4, 192, D), BF), pltpu.VMEM((4, D, D), BF),
            pltpu.VMEM((4, MIDDLE, 192), BF), pltpu.SemaphoreType.DMA((4,)),
            pltpu.SemaphoreType.DMA((4, 4)),
        ],
        (2, 7),
    )


def middle_four(info, inner, hidden, branch, ctx, sums):
    def spot(step, info):
        z, x, _, _, _, f = coords(info)
        return (0, f ^ step ^ (2 * (z & 1) + x), 0, 0)

    block = pl.BlockSpec((2, 1, 256, D), spot)
    return call(
        middle_four_kernel, "middle_four", 4, (info,),
        [(inner, pl.BlockSpec((1, MIDDLE, D), lambda step, *_: (step, 0, 0)))]
        + plain([hidden, branch, *ctx, *sums]),
        [((2, 4, 256, D), BF, block)] * 2,
        [pltpu.VMEM((D, D), BF), pltpu.VMEM((D, D), BF), pltpu.VMEM((4, 4, 16, D), BF)],
        (4, 8),
    )


def place_outer_kernel(info, p0, p1, p2, p3, out):
    z, x, _, _, _, _ = coords(info)
    for n, piece in enumerate((p0, p1, p2, p3)):
        out[pl.ds(pl.multiple_of(192 * (n ^ (2 * x + (z & 1))), 64), 192), :] = wide(piece[...])


def place_inner_kernel(
    info, p0, p1, p2, p3, inner, out, b_in, b_out, g_one, s_one, b_two, g_two, s_two, held
):
    z, x, _, _, _, _ = coords(info)
    for n, piece in enumerate((p0, p1, p2, p3)):
        at = n ^ (2 * (z & 1) + x)
        inner[:, pl.ds(pl.multiple_of(D * at, 128), D)] = wide(piece[:192, :])
        out[pl.ds(pl.multiple_of(48 * at, 16), 48), :] = wide(piece[192:240, :])
        held[at] = wide(piece[240:, :])
    b_in[...] = held[0][0:1, :].reshape(D)
    for n, vector in enumerate((b_out, g_one, s_one, b_two, g_two, s_two)):
        cut = 192 * (n % 4)
        vector[...] = held[1 + n // 4][0:1, cut : cut + 192].reshape(192)


def place_joint_kernel(info, p0, p1, p2, p3, query, key, value, b_query, b_value, held):
    z, x, _, _, _, f = coords(info)
    z_bit = z & 1
    for n, piece in enumerate((p0, p1, p2, p3)):
        rows = pl.ds(pl.multiple_of(96 * (n % 2 ^ z_bit), 32), 96)
        columns = pl.ds(pl.multiple_of(HALF * (n // 2 ^ x), 128), HALF)
        for m, out in enumerate((query, key, value)):
            out[rows, columns] = wide(piece[:96, HALF * m : HALF * m + HALF])
        line = wide(piece[96:, :])
        line = jnp.where(f & 1 == 0, line, jnp.concatenate([line[:, 192:], line[:, :192]], axis=1))
        held[n // 2 ^ x, n % 2 ^ z_bit] = line
    mine = held[f >> 1, 0][0:1, :]
    b_query[...] = mine[:, :192].reshape(192)
    b_value[...] = mine[:, 2 * HALF : 2 * HALF + 192].reshape(192)


def placed(kernel, name, info, pieces, shapes, held=()):
    return call(
        kernel, name, 1, (info,), plain(pieces), [(shape, FP, None) for shape in shapes],
        [pltpu.VMEM(shape, FP) for shape in held], (1, 6),
    )


def unshuffle(array, bit):
    return jnp.where(bit == 0, array, array[::-1])


def tied(values, *events):
    return lax.optimization_barrier((values, events))[0]


def fast_body(
    inputs, cotangent, lengths, w_query, b_query, w_key, w_value, b_value, w_output, b_output,
    gain_one, bias_one, w_inner, b_inner, w_outer, b_outer, gain_two, bias_two,
):
    info = lax.axis_index(("ctx", "fsdp")).astype(jnp.int32).reshape(1)
    zh, x = lax.axis_index("ctx") // 4, lax.axis_index("ctx") % 2

    t0, t1, cot, first, half = pack(
        info, lengths, inputs, cotangent, (w_query, w_key, w_value, w_output, w_inner),
        (b_query, b_value, b_output, gain_one, bias_one, b_outer, gain_two, bias_two, b_inner),
    )

    bu, bv = seq_send[0](t0), seq_send[1](t1)
    first_y, first_k = swap_y(first), swap_core(first)
    half_y = swap_y(half)
    bu, bv, first_k = tied((bu, bv, first_k))
    bxu, bxv, bku = swap_x(bu), swap_x(bv), swap_core(bu)
    bxu, bxv, bku, first_y, half_y = tied((bxu, bxv, bku, first_y, half_y))
    bkv, *rest = [swap_core(b) for b in (bv, bxu, bxv, first_y)]
    bkv, *rest = tied([bkv] + rest)
    blocks = [bu, bv, bxu, bxv, bku, bkv, *rest[:2]]
    first_p = [first, first_k, first_y, rest[2]]
    outer_y = swap_y(tied(w_outer, half_y))
    half_x = swap_x(tied(half_y, bkv))
    xs, ws, queries, keys, values, probs, cu, cv, cx = attend(info, blocks, first_p)

    cu, cv, cx, half_x = tied((cu, cv, cx, half_x))
    cu, cv = seq_return[0](cu), seq_return[1](cv)
    cx = swap_x(cx)
    inner_y = jnp.where(
        x == 0, jnp.concatenate([half_y, half_x], 1), jnp.concatenate([half_x, half_y], 1)
    )
    cu, cv, cx, outer_y, inner_y = tied((cu, cv, cx, outer_y, inner_y))
    cxu, cxv = seq_return[0](cx[0]), seq_return[1](cx[1])
    inner_k, inner_ky = swap_core(tied(w_inner, cx)), swap_core(inner_y)
    cxu, cxv, inner_k, inner_ky = tied((cxu, cxv, inner_k, inner_ky))
    outer_k, outer_ky = swap_core(tied(w_outer, cxu)), swap_core(tied(outer_y, cxu))
    ctx = [cu, cv, cxu, cxv]
    inner_p = [w_inner, inner_k, inner_y, inner_ky]
    hidden, normed, inv, act, slope, vec = middle_one(info, ctx, [t0, t1], first_p, inner_p)
    act, outer_k, outer_ky = tied((act, outer_k, outer_ky))
    outer_p = [w_outer, outer_k, outer_y, outer_ky]
    outputs, second_grad, outer, sums_two, o_keep, o_send = middle_two(
        info, lengths, act, hidden, cot, vec, outer_p
    )
    o_came = swap_core(o_send)
    inner, sums_in = inner_back(info, outer, slope, outer_p)
    o_came, inner = tied((o_came, inner))
    o_y = low(wide(o_keep[1, :2]) + wide(o_came[1, :2]))
    o_z = low(wide(o_keep[:, 3]) + wide(o_came[:, 3]))
    inner, o_y, o_z = tied((inner, o_y, o_z))
    o_y, o_z = swap_y(o_y), swap_z1(o_z)
    grad_first, g0, g1, branch, sums_one = middle_three(
        info, second_grad, inner, normed, inv, vec, first_p, inner_p
    )
    g0, g1 = seq_send[0](g0), seq_send[1](g1)
    i_keep, i_send = middle_four(
        info, inner, hidden, branch, ctx, (sums_two, sums_in, sums_one)
    )
    g0, g1, i_send, o_y, o_z = tied((g0, g1, i_send, o_y, o_z))
    go = jnp.stack([g0[0], g1[0]])
    go, o_y, o_z, i_send = tied((go, o_y, o_z, i_send))
    go = swap_x(go)
    i_came = swap_core(i_send)
    o_z2 = swap_z1(low(wide(o_keep[0, 1]) + wide(o_came[0, 1]) + wide(o_y[1])))
    o_y2 = swap_y(low(wide(o_keep[1, 2]) + wide(o_came[1, 2]) + wide(o_z[1])))
    go, i_came, o_z2, o_y2 = tied((go, i_came, o_z2, o_y2))
    o_one = wide(o_keep[0, 0]) + wide(o_came[0, 0]) + wide(o_y[0]) + wide(o_z2)
    o_two = low(wide(o_keep[0, 2]) + wide(o_came[0, 2]) + wide(o_z[0]) + wide(o_y2))
    i_y = low(wide(i_keep[1, :2]) + wide(i_came[1, :2]))
    i_x = low(wide(i_keep[:, 3]) + wide(i_came[:, 3]))
    go, i_y, i_x = tied((go, i_y, i_x))
    i_y, i_x = swap_y(i_y), swap_x(i_x)
    grads = [(g0, 1), (g1, 1), (go, 0), (go, 1)]
    pair_0 = attend_back(queries, keys, values, probs, grads, 0, 1)
    pair_1 = attend_back(tied(queries, pair_0), keys, values, probs, grads, 1, 1)
    pair_2 = attend_back(tied(queries, pair_1), keys, values, probs, grads, 2, 1)
    pairs = (pair_0, pair_1, pair_2)
    dx_own, dx_other = rows_back(ws, pairs)
    dx_own, dx_other, i_y, i_x = tied((dx_own, dx_other, i_y, i_x))
    i_x2 = swap_x(low(wide(i_keep[0, 1]) + wide(i_came[0, 1]) + wide(i_y[1])))
    i_y2 = swap_y(low(wide(i_keep[1, 2]) + wide(i_came[1, 2]) + wide(i_x[1])))
    j_keep, j_send = joint_grads(info, tied(xs, dx_other), pairs)
    j_keep, j_send, i_x2, i_y2 = tied((j_keep, j_send, i_x2, i_y2))
    o_came = swap_x(tied(o_two, j_send))
    i_one = wide(i_keep[0, 0]) + wide(i_came[0, 0]) + wide(i_y[0]) + wide(i_x2)
    i_two = low(wide(i_keep[0, 2]) + wide(i_came[0, 2]) + wide(i_x[0]) + wide(i_y2))
    i_came = swap_z1(i_two)
    j_came, dx_came = swap_core(j_send), swap_core(dx_other)
    j_came, dx_came, i_came, o_came = tied((j_came, dx_came, i_came, o_came))
    o_sum = low(o_one + wide(o_came))
    o_came = swap_z2(o_sum)
    i_sum = low(i_one + wide(i_came))
    dx = dx_own[: 2 * ROWS] + wide(dx_came[: 2 * ROWS])
    dx_send = low(dx_own[2 * ROWS :] + wide(dx_came[2 * ROWS :]))
    j_y = swap_y(low(wide(j_keep[1, :, :56]) + wide(j_came[1, :, :56])))
    j_z = swap_z1(low(wide(j_keep[:, 1, 56:]) + wide(j_came[:, 1, 56:])))
    j_one = wide(j_keep[0, :, :56]) + wide(j_came[0, :, :56])
    j_two = wide(j_keep[:, 0, 56:]) + wide(j_came[:, 0, 56:])
    i_came = swap_z2(i_sum)
    dx_came = swap_x(dx_send)
    j_y, j_z, dx_came, o_came = tied((j_y, j_z, dx_came, o_came))
    j_one, j_two = j_one + wide(j_y), j_two + wide(j_z)
    dx = low(dx + wide(dx_came))
    o_sum = low(wide(o_sum) + wide(o_came))
    j_z, j_y = swap_z1(low(j_one[1])), swap_y(low(j_two[1]))
    o_x, o_z = swap_x(o_sum), swap_z1(o_sum)
    j_z, j_y, o_x, o_z, i_came = tied((j_z, j_y, o_x, o_z, i_came))
    j_sum = low(jnp.concatenate([j_one[0] + wide(j_z), j_two[0] + wide(j_y)], axis=0))
    i_sum = low(wide(i_sum) + wide(i_came))
    j_came = swap_z2(j_sum)
    i_z, i_x, o_zx = swap_z1(i_sum), swap_x(i_sum), swap_x(tied(o_z, i_sum))
    j_came, i_z, i_x, o_zx = tied((j_came, i_z, i_x, o_zx))
    j_sum = low(wide(j_sum) + wide(j_came))
    j_x, j_z = swap_x(j_sum), swap_z1(j_sum)
    i_zx = swap_x(i_z)
    dx0, dx1 = seq_return[0](tied(dx[:ROWS], i_z)), seq_return[1](tied(dx[ROWS:], i_z))
    (outer_grad,) = placed(place_outer_kernel, "place_outer", info, tied([o_sum, o_z, o_x, o_zx], j_sum), [(D, D)])
    j_x, j_z, i_zx, dx0, dx1, outer_grad = tied((j_x, j_z, i_zx, dx0, dx1, outer_grad))
    j_zx = swap_x(j_z)
    input_grad = grad_first + wide(jnp.concatenate([dx0, dx1], axis=0))
    input_grad = unshuffle(input_grad.reshape(2, ROWS, D), zh)
    inner_grad, out_grad, grad_b1, grad_bo, grad_g1, grad_s1, grad_b2, grad_g2, grad_s2 = placed(
        place_inner_kernel, "place_inner", info, [i_sum, i_x, i_z, i_zx],
        [(192, 4 * D), (192, D), (D,)] + [(192,)] * 6, [(4, 16, D)],
    )
    q_grad, k_grad, v_grad, grad_bq, grad_bv = placed(
        place_joint_kernel, "place_joint", info, [j_sum, j_z, j_x, j_zx],
        [(192, D)] * 3 + [(192,)] * 2, [(2, 2, 16, 3 * HALF)],
    )
    return (
        outputs, input_grad, q_grad, grad_bq, k_grad, v_grad, grad_bv, out_grad, grad_bo,
        grad_g1, grad_s1, inner_grad, grad_b1, outer_grad, grad_b2, grad_g2, grad_s2,
    )


def solution(mesh):
    placed = (
        P("fsdp", "ctx", None),
        P("fsdp", "ctx", None),
        P("fsdp"),
        P("fsdp", None),
        P("fsdp"),
        P("fsdp", None),
        P("fsdp", None),
        P("fsdp"),
        P("fsdp", None),
        P("fsdp"),
        P("fsdp"),
        P("fsdp"),
        P("fsdp", None),
        P("fsdp"),
        P("fsdp", None),
        P("fsdp"),
        P("fsdp"),
        P("fsdp"),
    )
    fast = dict(mesh.shape) == {"ctx": 8, "fsdp": 4}
    return jax.shard_map(
        fast_body if fast else body,
        mesh=mesh,
        in_specs=placed,
        out_specs=(
            P("fsdp", "ctx", None),
            P("fsdp", "ctx", None),
            P("fsdp", None),
            P("fsdp"),
            P("fsdp", None),
            P("fsdp", None),
            P("fsdp"),
            P("fsdp", None),
            P("fsdp"),
            P("fsdp"),
            P("fsdp"),
            P("fsdp", None),
            P("fsdp"),
            P("fsdp", None),
            P("fsdp"),
            P("fsdp"),
            P("fsdp"),
        ),
        check_vma=False,
    )
```

```python
from functools import partial

import jax
import jax.numpy as jnp
from jax import lax
from jax.experimental import pallas as pl
from jax.experimental.pallas import tpu as pltpu
from jax.sharding import PartitionSpec as P

D = 768
H = 12
HD = 64
SEQ_MB = 1
MICRO = 2


EPSILON = 1e-05
NEG_FILL = -1e30
SCALE = 0.125
ROOT_HALF = 0.7071067811865476
INV_ROOT_TAU = 0.3989422804014327
key_block = 512


def matmul(left_side, right_side):
    return jnp.dot(left_side, right_side, preferred_element_type=jnp.float32)


def left_product(left_side, right_side):
    return lax.dot_general(
        left_side, right_side, (((0,), (0,)), ((), ())), preferred_element_type=jnp.float32
    )


def right_product(left_side, right_side):
    return lax.dot_general(
        left_side, right_side, (((1,), (1,)), ((), ())), preferred_element_type=jnp.float32
    )


def split_heads(token_rows):
    return token_rows.reshape(token_rows.shape[0], token_rows.shape[1], H, HD)


def head_scores(query_rows, key_rows):
    return (
        jnp.einsum(
            "bqhd,bkhd->bhqk",
            split_heads(query_rows),
            split_heads(key_rows),
            preferred_element_type=jnp.float32,
        )
        * SCALE
    )


def live_mask(seq_lens, first_pos, num_rows):
    return (first_pos + lax.iota(jnp.int32, num_rows))[None, :] < seq_lens[:, None]


def layer_norm(resid, norm_gain, norm_bias):
    row_mean = jnp.mean(resid, axis=-1, keepdims=True)
    centered = resid - row_mean
    inv_std = lax.rsqrt(jnp.mean(centered * centered, axis=-1, keepdims=True) + EPSILON)
    normed = centered * inv_std
    return (normed * norm_gain + norm_bias, normed, inv_std)


def norm_back(grad_out, normed, inv_std, norm_gain):
    grad_norm = grad_out * norm_gain
    grad_in = inv_std * (
        grad_norm
        - jnp.mean(grad_norm, axis=-1, keepdims=True)
        - normed * jnp.mean(grad_norm * normed, axis=-1, keepdims=True)
    )
    return (grad_in, jnp.sum(grad_out * normed, axis=0), jnp.sum(grad_out, axis=0))


def gelu_exact(pre_act):
    return 0.5 * pre_act * (1.0 + lax.erf(pre_act * ROOT_HALF))


def gelu_slope(pre_act):
    return 0.5 * (1.0 + lax.erf(pre_act * ROOT_HALF)) + pre_act * INV_ROOT_TAU * jnp.exp(
        -0.5 * pre_act * pre_act
    )


def in_blocks(step_fn, running, pieces):
    num_rows = pieces[0].shape[1]

    def advance(block_index, current):
        offset = block_index * key_block
        sliced = tuple(
            (lax.dynamic_slice_in_dim(member, offset, key_block, 1) for member in pieces)
        )
        return step_fn(current, sliced, offset)

    return lax.fori_loop(0, num_rows // key_block, advance, running)


def attend_step(running, sliced, first_pos, queries, seq_lens, skip_empty):
    key_rows, value_rows = sliced
    live_keys = live_mask(seq_lens, first_pos, key_rows.shape[1])
    run_max, run_sum, run_out = running
    key_mask = live_keys[:, None, None, :]
    scores = jnp.where(key_mask, head_scores(queries, key_rows), NEG_FILL)
    new_max = jnp.maximum(run_max, jnp.max(scores, axis=-1))
    weights = jnp.where(key_mask, jnp.exp(scores - new_max[..., None]), 0.0)
    rescale = jnp.exp(run_max - new_max)
    new_sum = run_sum * rescale + jnp.sum(weights, axis=-1)
    new_out = run_out * rescale[..., None] + jnp.einsum(
        "bhqk,bkhd->bhqd",
        weights.astype(jnp.bfloat16),
        split_heads(value_rows),
        preferred_element_type=jnp.float32,
    )
    return (new_max, new_sum, new_out)


def query_grad_step(
    running,
    sliced,
    first_pos,
    queries,
    grad_context,
    log_total,
    row_delta,
    seq_lens,
    live_queries,
    skip_empty,
):
    key_rows, value_rows = sliced
    live_keys = live_mask(seq_lens, first_pos, key_rows.shape[1])
    key_mask = live_keys[:, None, None, :]
    probabilities = jnp.where(
        key_mask, jnp.exp(head_scores(queries, key_rows) - log_total[..., None]), 0.0
    )
    grad_probs = jnp.einsum(
        "bqhd,bkhd->bhqk",
        split_heads(grad_context),
        split_heads(value_rows),
        preferred_element_type=jnp.float32,
    )
    grad_scores = (probabilities * (grad_probs - row_delta[..., None])).astype(jnp.bfloat16)
    return running + jnp.einsum(
        "bhqk,bkhd->bqhd", grad_scores, split_heads(key_rows), preferred_element_type=jnp.float32
    )


def key_grad_step(
    running,
    sliced,
    first_pos,
    key_rows,
    value_rows,
    stat_total,
    stat_delta,
    seq_lens,
    live_keys,
    skip_empty,
):
    query_rows, grad_rows = sliced
    num_rows = query_rows.shape[1]
    grad_k, grad_v = running
    log_total = lax.dynamic_slice_in_dim(stat_total, first_pos, num_rows, 1).transpose(0, 2, 1)
    row_delta = lax.dynamic_slice_in_dim(stat_delta, first_pos, num_rows, 1).transpose(0, 2, 1)
    key_mask = live_keys[:, None, None, :]
    probabilities = jnp.where(
        key_mask, jnp.exp(head_scores(query_rows, key_rows) - log_total[..., None]), 0.0
    )
    grad_probs = jnp.einsum(
        "bqhd,bkhd->bhqk",
        split_heads(grad_rows),
        split_heads(value_rows),
        preferred_element_type=jnp.float32,
    )
    grad_scores = (probabilities * (grad_probs - row_delta[..., None])).astype(jnp.bfloat16)
    grad_v = grad_v + jnp.einsum(
        "bhqk,bqhd->bkhd",
        probabilities.astype(jnp.bfloat16),
        split_heads(grad_rows),
        preferred_element_type=jnp.float32,
    )
    grad_k = grad_k + jnp.einsum(
        "bhqk,bqhd->bkhd", grad_scores, split_heads(query_rows), preferred_element_type=jnp.float32
    )
    return (grad_k, grad_v)


def body(
    inputs,
    cotangent,
    lengths,
    w_query,
    b_query,
    w_key,
    w_value,
    b_value,
    w_output,
    b_output,
    gain_one,
    bias_one,
    w_inner,
    b_inner,
    w_outer,
    b_outer,
    gain_two,
    bias_two,
):
    gathered = (
        lax.all_gather(w_query, "fsdp", axis=0, tiled=True),
        lax.all_gather(b_query, "fsdp", axis=0, tiled=True),
        lax.all_gather(w_key, "fsdp", axis=0, tiled=True),
        lax.all_gather(w_value, "fsdp", axis=0, tiled=True),
        lax.all_gather(b_value, "fsdp", axis=0, tiled=True),
        lax.all_gather(w_output, "fsdp", axis=0, tiled=True),
        lax.all_gather(b_output, "fsdp", axis=0, tiled=True),
        lax.all_gather(gain_one, "fsdp", axis=0, tiled=True),
        lax.all_gather(bias_one, "fsdp", axis=0, tiled=True),
        lax.all_gather(w_inner, "fsdp", axis=0, tiled=True),
        lax.all_gather(b_inner, "fsdp", axis=0, tiled=True),
        lax.all_gather(w_outer, "fsdp", axis=0, tiled=True),
        lax.all_gather(b_outer, "fsdp", axis=0, tiled=True),
        lax.all_gather(gain_two, "fsdp", axis=0, tiled=True),
        lax.all_gather(bias_two, "fsdp", axis=0, tiled=True),
    )
    (
        query_weight,
        query_bias,
        key_weight,
        value_weight,
        value_bias,
        out_weight,
        out_bias,
        gain_first,
        shift_first,
        inner_weight,
        inner_bias,
        outer_weight,
        outer_bias,
        gain_second,
        shift_second,
    ) = gathered
    joint_weight = jnp.concatenate([query_weight, key_weight, value_weight], axis=1)
    joint_bias = jnp.concatenate(
        [
            query_bias.astype(jnp.float32),
            jnp.zeros((D,), jnp.float32),
            value_bias.astype(jnp.float32),
        ]
    )
    out_bias_f = out_bias.astype(jnp.float32)
    inner_bias_f = inner_bias.astype(jnp.float32)
    outer_bias_f = outer_bias.astype(jnp.float32)
    gain_first_f = gain_first.astype(jnp.float32)
    shift_first_f = shift_first.astype(jnp.float32)
    gain_second_f = gain_second.astype(jnp.float32)
    shift_second_f = shift_second.astype(jnp.float32)
    seq_dev = inputs.shape[1]
    row_count = SEQ_MB * seq_dev
    positions = lax.axis_index("ctx") * seq_dev + lax.iota(jnp.int32, seq_dev)
    accum = None
    out_list = []
    grad_list = []
    for micro_index in range(MICRO):
        first_seq = micro_index * SEQ_MB
        seq_lens = lengths[first_seq : first_seq + SEQ_MB]
        token_rows = inputs[first_seq : first_seq + SEQ_MB].reshape(row_count, D)
        grad_rows = (
            cotangent[first_seq : first_seq + SEQ_MB].reshape(row_count, D).astype(jnp.float32)
        )
        query_ok = positions[None, :] < seq_lens[:, None]
        row_keep = query_ok.reshape(row_count, 1).astype(jnp.float32)
        projected = (matmul(token_rows, joint_weight) + joint_bias).astype(jnp.bfloat16)
        queries = projected[:, :D].reshape(SEQ_MB, seq_dev, D)
        keys_local = projected[:, D : 2 * D].reshape(SEQ_MB, seq_dev, D)
        values_local = projected[:, 2 * D :].reshape(SEQ_MB, seq_dev, D)
        start_state = (
            jnp.full((SEQ_MB, H, seq_dev), NEG_FILL, jnp.float32),
            jnp.zeros((SEQ_MB, H, seq_dev), jnp.float32),
            jnp.zeros((SEQ_MB, H, seq_dev, HD), jnp.float32),
        )
        attend_fn = partial(attend_step, queries=queries, seq_lens=seq_lens, skip_empty=False)
        run_max, run_sum, run_out = in_blocks(
            attend_fn,
            start_state,
            (
                lax.all_gather(keys_local, "ctx", axis=1, tiled=True),
                lax.all_gather(values_local, "ctx", axis=1, tiled=True),
            ),
        )
        attended = run_out / run_sum[..., None]
        log_total = run_max + jnp.log(run_sum)
        context = attended.transpose(0, 2, 1, 3).reshape(row_count, D).astype(jnp.bfloat16)
        first_sum = token_rows.astype(jnp.float32) + matmul(context, out_weight) + out_bias_f
        hidden, normed_one, inv_one = layer_norm(first_sum, gain_first_f, shift_first_f)
        hidden_low = hidden.astype(jnp.bfloat16)
        inner_pre = matmul(hidden_low, inner_weight) + inner_bias_f
        activated = gelu_exact(inner_pre).astype(jnp.bfloat16)
        outer_out = matmul(activated, outer_weight) + outer_bias_f
        result, normed_two, inv_two = layer_norm(hidden + outer_out, gain_second_f, shift_second_f)
        out_list.append(result.astype(jnp.bfloat16).reshape(SEQ_MB, seq_dev, D))
        grad_out = grad_rows * row_keep
        grad_second, grad_gain_b, grad_shift_b = norm_back(
            grad_out, normed_two, inv_two, gain_second_f
        )
        grad_outer = grad_second.astype(jnp.bfloat16)
        grad_outer_w = left_product(activated, grad_outer)
        grad_outer_b = jnp.sum(grad_outer.astype(jnp.float32), axis=0)
        grad_inner = (right_product(grad_outer, outer_weight) * gelu_slope(inner_pre)).astype(
            jnp.bfloat16
        )
        grad_inner_w = left_product(hidden_low, grad_inner)
        grad_inner_b = jnp.sum(grad_inner.astype(jnp.float32), axis=0)
        grad_hidden = grad_second + right_product(grad_inner, inner_weight)
        grad_first, grad_gain_a, grad_shift_a = norm_back(
            grad_hidden, normed_one, inv_one, gain_first_f
        )
        grad_branch = grad_first.astype(jnp.bfloat16)
        grad_out_w = left_product(context, grad_branch)
        grad_out_b = jnp.sum(grad_branch.astype(jnp.float32), axis=0)
        grad_context = (
            right_product(grad_branch, out_weight).astype(jnp.bfloat16).reshape(SEQ_MB, seq_dev, D)
        )
        row_delta = jnp.einsum(
            "bqhd,bhqd->bhq", split_heads(grad_context).astype(jnp.float32), attended
        )
        stat_total, stat_delta = (
            lax.all_gather(log_total.transpose(0, 2, 1), "ctx", axis=1, tiled=True),
            lax.all_gather(row_delta.transpose(0, 2, 1), "ctx", axis=1, tiled=True),
        )
        query_fn = partial(
            query_grad_step,
            queries=queries,
            grad_context=grad_context,
            log_total=log_total,
            row_delta=row_delta,
            seq_lens=seq_lens,
            live_queries=query_ok,
            skip_empty=False,
        )
        key_fn = partial(
            key_grad_step,
            key_rows=keys_local,
            value_rows=values_local,
            stat_total=stat_total,
            stat_delta=stat_delta,
            seq_lens=seq_lens,
            live_keys=query_ok,
            skip_empty=False,
        )
        grad_zero = jnp.zeros((SEQ_MB, seq_dev, H, HD), jnp.float32)
        grad_q = in_blocks(
            query_fn,
            grad_zero,
            (
                lax.all_gather(keys_local, "ctx", axis=1, tiled=True),
                lax.all_gather(values_local, "ctx", axis=1, tiled=True),
            ),
        )
        grad_k, grad_v = in_blocks(
            key_fn,
            (grad_zero, grad_zero),
            (
                lax.all_gather(queries, "ctx", axis=1, tiled=True),
                lax.all_gather(grad_context, "ctx", axis=1, tiled=True),
            ),
        )
        joint_grad = jnp.concatenate(
            [
                (grad_q * SCALE).reshape(row_count, D).astype(jnp.bfloat16),
                (grad_k * SCALE).reshape(row_count, D).astype(jnp.bfloat16),
                grad_v.reshape(row_count, D).astype(jnp.bfloat16),
            ],
            axis=1,
        )
        grad_joint_w = left_product(token_rows, joint_grad)
        grad_joint_b = jnp.sum(joint_grad.astype(jnp.float32), axis=0)
        input_rows = grad_first + right_product(joint_grad, joint_weight)
        grad_list.append(input_rows.reshape(SEQ_MB, seq_dev, D))
        micro_grads = (
            grad_joint_w,
            grad_joint_b,
            grad_out_w,
            grad_out_b,
            grad_gain_a,
            grad_shift_a,
            grad_inner_w,
            grad_inner_b,
            grad_outer_w,
            grad_outer_b,
            grad_gain_b,
            grad_shift_b,
        )
        if accum is None:
            accum = micro_grads
        else:
            accum = tuple((held + fresh for held, fresh in zip(accum, micro_grads)))
    (
        joint_w,
        joint_b,
        out_w,
        out_b,
        gain_a,
        shift_a,
        inner_w,
        inner_b,
        outer_w,
        outer_b,
        gain_b,
        shift_b,
    ) = accum
    grad_set = (
        joint_w[:, :D],
        joint_b[:D],
        joint_w[:, D : 2 * D],
        joint_w[:, 2 * D :],
        joint_b[2 * D :],
        out_w,
        out_b,
        gain_a,
        shift_a,
        inner_w,
        inner_b,
        outer_w,
        outer_b,
        gain_b,
        shift_b,
    )
    shard_grads = (
        lax.psum_scatter(
            grad_set[0].astype(jnp.bfloat16), "fsdp", scatter_dimension=0, tiled=True
        ).astype(jnp.float32),
        lax.psum_scatter(
            grad_set[1].astype(jnp.bfloat16), "fsdp", scatter_dimension=0, tiled=True
        ).astype(jnp.float32),
        lax.psum_scatter(
            grad_set[2].astype(jnp.bfloat16), "fsdp", scatter_dimension=0, tiled=True
        ).astype(jnp.float32),
        lax.psum_scatter(
            grad_set[3].astype(jnp.bfloat16), "fsdp", scatter_dimension=0, tiled=True
        ).astype(jnp.float32),
        lax.psum_scatter(
            grad_set[4].astype(jnp.bfloat16), "fsdp", scatter_dimension=0, tiled=True
        ).astype(jnp.float32),
        lax.psum_scatter(
            grad_set[5].astype(jnp.bfloat16), "fsdp", scatter_dimension=0, tiled=True
        ).astype(jnp.float32),
        lax.psum_scatter(
            grad_set[6].astype(jnp.bfloat16), "fsdp", scatter_dimension=0, tiled=True
        ).astype(jnp.float32),
        lax.psum_scatter(
            grad_set[7].astype(jnp.bfloat16), "fsdp", scatter_dimension=0, tiled=True
        ).astype(jnp.float32),
        lax.psum_scatter(
            grad_set[8].astype(jnp.bfloat16), "fsdp", scatter_dimension=0, tiled=True
        ).astype(jnp.float32),
        lax.psum_scatter(
            grad_set[9].astype(jnp.bfloat16), "fsdp", scatter_dimension=0, tiled=True
        ).astype(jnp.float32),
        lax.psum_scatter(
            grad_set[10].astype(jnp.bfloat16), "fsdp", scatter_dimension=0, tiled=True
        ).astype(jnp.float32),
        lax.psum_scatter(
            grad_set[11].astype(jnp.bfloat16), "fsdp", scatter_dimension=0, tiled=True
        ).astype(jnp.float32),
        lax.psum_scatter(
            grad_set[12].astype(jnp.bfloat16), "fsdp", scatter_dimension=0, tiled=True
        ).astype(jnp.float32),
        lax.psum_scatter(
            grad_set[13].astype(jnp.bfloat16), "fsdp", scatter_dimension=0, tiled=True
        ).astype(jnp.float32),
        lax.psum_scatter(
            grad_set[14].astype(jnp.bfloat16), "fsdp", scatter_dimension=0, tiled=True
        ).astype(jnp.float32),
    )
    summed = lax.psum(
        (
            shard_grads[0],
            shard_grads[1],
            shard_grads[2],
            shard_grads[3],
            shard_grads[4],
            shard_grads[5],
            shard_grads[6],
            shard_grads[7],
            shard_grads[8],
            shard_grads[9],
            shard_grads[10],
            shard_grads[11],
            shard_grads[12],
            shard_grads[13],
            shard_grads[14],
        ),
        "ctx",
    )
    outputs = jnp.concatenate(out_list, axis=0)
    input_grad = jnp.concatenate(grad_list, axis=0)
    return (outputs, input_grad) + tuple(summed)


HALF = D // 2
ROWS = 128


def flat(z, x, y, k):
    return (z * 2 + x) * 4 + y * 2 + k


def table(move):
    return [
        (flat(z, x, y, k), flat(*move(z, x, y, k)))
        for z in range(4)
        for x in range(2)
        for y in range(2)
        for k in range(2)
    ]


def permute(move):
    pairs = table(move)
    return lambda block: lax.ppermute(block, ("ctx", "fsdp"), pairs)


def permute_back(move):
    pairs = [(b, a) for a, b in table(move)]
    return lambda block: lax.ppermute(block, ("ctx", "fsdp"), pairs)


def to_seq(turn):
    return lambda z, x, y, k: (2 * k + (z // 2 + turn) % 2, x, y, z % 2)


swap_core = permute(lambda z, x, y, k: (z, x, y, k ^ 1))
swap_y = permute(lambda z, x, y, k: (z, x, y ^ 1, k))
swap_x = permute(lambda z, x, y, k: (z, x ^ 1, y, k))
swap_z1 = permute(lambda z, x, y, k: (z ^ 1, x, y, k))
swap_xz = permute(lambda z, x, y, k: (z ^ 1, x ^ 1, y, k))
swap_z2 = permute(lambda z, x, y, k: (z ^ 2, x, y, k))
seq_send = (permute(to_seq(0)), permute(to_seq(1)))
seq_return = (permute_back(to_seq(0)), permute_back(to_seq(1)))


def low(value):
    return value.astype(jnp.bfloat16)


def wide(value):
    return value.astype(jnp.float32)


def pick(array, index, axis=0):
    return lax.dynamic_index_in_dim(array, index, axis, keepdims=False)


def dot_nt(a, b):
    return lax.dot_general(a, b, (((1,), (1,)), ((), ())), preferred_element_type=jnp.float32)


def dot_tn(a, b):
    return lax.dot_general(a, b, (((0,), (0,)), ((), ())), preferred_element_type=jnp.float32)


def coords(info):
    c, f = info[0] >> 2, info[0] & 3
    return c >> 1, c & 1, f >> 1, f & 1, c, f


def pack_kernel(
    info, lens, rows, grads, w_q, w_k, w_v, w_o, w_in, v0, v1, v2, v3, v4, v5, v6, v7, wide_vec,
    t0, t1, cot, first, half, held,
):
    z, x, _, _, _, _ = coords(info)
    zh = z >> 1
    half[...] = w_in[...]
    t0[...] = rows[zh]
    t1[...] = rows[1 - zh]
    cot[:ROWS] = grads[zh]
    cot[ROWS:] = grads[1 - zh]
    columns = pl.ds(pl.multiple_of(x * HALF, 128), HALF)
    first[:192, :D] = w_o[...]
    for n, weight in enumerate((w_q, w_k, w_v)):
        first[:192, D + HALF * n : D + HALF * n + HALF] = weight[:, columns]
    held[...] = jnp.zeros_like(held)
    for n, vector in enumerate((v0, v1, v2, v3, v4, v5, v6, v7)):
        held[n : n + 1, :192] = wide(vector[...]).reshape(1, 192)
    held[8:9, :] = wide(wide_vec[...]).reshape(1, D)
    lane = lax.broadcasted_iota(jnp.int32, (1, D), 1)
    ends = jnp.zeros((1, D), jnp.int32)
    for n in range(2):
        ends = jnp.where(lane == n, lens[n] >> 7, ends)
        ends = jnp.where(lane == 2 + n, lens[n] & 127, ends)
    held[9:10, :] = wide(ends)
    first[192:, :D] = low(held[...])
    first[192:, D:] = jnp.zeros((16, 3 * HALF), jnp.bfloat16)


def attend_kernel(
    info, b0, b1, b2, b3, b4, b5, b6, b7, s0, s1, s2, s3, w0, w1, w2, w3,
    xs, ws, q_out, k_out, v_out, p_out, cu, cv, cx, key_bias, small, sems,
):
    step = pl.program_id(0)
    z, x, y, k, _, f = coords(info)

    @pl.when(step == 0)
    def _():
        copies = [
            pltpu.make_async_copy(
                piece.at[:192, D:], ws.at[pl.ds(pl.multiple_of(192 * (f ^ n), 64), 192), :], sems.at[n]
            )
            for n, piece in enumerate((w0, w1, w2, w3))
        ]
        blocks = (b0, b1, b2, b3, b4, b5, b6, b7)
        copies += [
            pltpu.make_async_copy(block, xs.at[n * ROWS : (n + 1) * ROWS, :], sems.at[4 + n])
            for n, block in enumerate(blocks)
        ]
        for copy in copies:
            copy.start()
        for n, piece in enumerate((s0, s1, s2, s3)):
            small[f ^ n] = wide(piece[...])
        line = small[2 * y + (z >> 1)][9:10, :]
        lane = lax.broadcasted_iota(jnp.int32, (1, D), 1)
        part = jnp.where(lane == (z & 1), 128.0 * line, 0.0)
        part = part + jnp.where(lane == 2 + (z & 1), line, 0.0)
        end = jnp.sum(part, axis=1, keepdims=True)
        z_low = 2 * (z & 1)
        for n, block in enumerate(blocks):
            z_block = (z_low if n % 2 == 0 else 2 - z_low) + (k if n < 4 else 1 - k)
            x_block = x if n % 4 < 2 else 1 - x
            place = (2 * z_block + x_block) * ROWS + lax.broadcasted_iota(jnp.int32, (1, ROWS), 1)
            key_bias[:, n * ROWS : (n + 1) * ROWS] = jnp.where(wide(place) < end, 0.0, NEG_FILL)
        for copy in copies:
            copy.wait()

        def bias(row):
            return jnp.concatenate(
                [small[2 * x + n][row : row + 1, :192] for n in range(2)], axis=1
            )

        q_out[...] = low(wide(low(matmul(xs[: 4 * ROWS, :], ws[:, :HALF]) + bias(0))) * SCALE)
        k_out[...] = low(matmul(xs[...], ws[:, HALF : 2 * HALF]))
        v_out[...] = low(matmul(xs[...], ws[:, 2 * HALF :]) + bias(1))

    lanes = pl.ds(pl.multiple_of(step * 128, 128), 128)
    first = lax.broadcasted_iota(jnp.int32, (1, 128), 1) < HD
    queries = q_out[:, lanes]
    keys = k_out[:, lanes]
    values = v_out[:, lanes]
    for part in range(2):
        rows = slice(part * 256, part * 256 + 256)
        found = []
        for head in range(2):
            mine = first if head == 0 else jnp.logical_not(first)
            scores = dot_nt(jnp.where(mine, queries[rows], 0), keys) + key_bias[...]
            top = jnp.max(scores, axis=1, keepdims=True)
            weights = jnp.exp(scores - top)
            total = jnp.sum(weights, axis=1, keepdims=True)
            probs = low(weights * (1.0 / total))
            p_out[head, rows, :] = probs
            found.append(matmul(probs, values))
        context = low(jnp.where(first, found[0], found[1]))
        if part == 0:
            cu[...] = context[:ROWS]
            cv[...] = context[ROWS:]
        else:
            cx[0] = context[:ROWS]
            cx[1] = context[ROWS:]


def pair_back(queries_ref, keys, values, probs_ref, grads):
    first = lax.broadcasted_iota(jnp.int32, (1, 128), 1) < HD
    grad_k = jnp.zeros((8 * ROWS, 128), jnp.float32)
    grad_v = jnp.zeros((8 * ROWS, 128), jnp.float32)
    grad_qs = []
    for part in range(2):
        rows = slice(part * 256, part * 256 + 256)
        one, two = grads[2 * part : 2 * part + 2]
        grad_rows = jnp.concatenate([one[...], two[...]], axis=0)
        queries = queries_ref[rows, :]
        grad_q = jnp.zeros((256, 128), jnp.float32)
        for head in range(2):
            mine = first if head == 0 else jnp.logical_not(first)
            grad_mine = jnp.where(mine, grad_rows, 0)
            probs = probs_ref[head, rows, :]
            grad_probs = dot_nt(grad_mine, values)
            product = wide(probs) * grad_probs
            delta = jnp.sum(product, axis=1, keepdims=True)
            grad_scores = low(product - wide(probs) * delta)
            grad_q = grad_q + matmul(grad_scores, jnp.where(mine, keys, 0))
            grad_k = grad_k + dot_tn(grad_scores, jnp.where(mine, queries, 0))
            grad_v = grad_v + dot_tn(probs, grad_mine)
        grad_qs.append(low(grad_q * SCALE))
    return grad_qs, low(grad_k), low(grad_v)


def attend_back_kernel(queries, keys, values, probs, gu, gv, gxu, gxv, dq, dk, dv):
    grad_qs, dk[...], dv[...] = pair_back(
        queries, keys[...], values[...], probs, (gu, gv, gxu, gxv)
    )
    dq[:256, :], dq[256:, :] = grad_qs


def joint_kernel(
    info, xs, dq0, dq1, dq2, dk0, dk1, dk2, dv0, dv1, dv2, keep, send, grads, dw
):
    for n, (q, k, v) in enumerate(((dq0, dk0, dv0), (dq1, dk1, dv1), (dq2, dk2, dv2))):
        start = 128 * n
        grads[: 4 * ROWS, start : start + 128] = q[...]
        grads[:, HALF + start : HALF + start + 128] = k[...]
        grads[:, 2 * HALF + start : 2 * HALF + start + 128] = v[...]
    own = slice(0, 4 * ROWS)
    dw[:, :HALF] = low(dot_tn(xs[own, :], grads[own, :HALF]))
    dw[:, HALF:] = low(dot_tn(xs[...], grads[:, HALF:]))
    col_sums = jnp.concatenate(
        [
            column_sum(wide(grads[own, :HALF])),
            jnp.zeros((1, HALF), jnp.float32),
            column_sum(wide(grads[:, 2 * HALF :])),
        ],
        axis=1,
    )
    tail = low(jnp.where(lax.broadcasted_iota(jnp.int32, (16, 1), 0) == 0, col_sums, 0.0))
    z, _, _, _, _, f = coords(info)
    for n in range(4):
        place = send if n % 2 else keep
        for half in range(2):
            start = pl.multiple_of(192 * (f ^ n) + 96 * half, 32)
            place[n // 2, half ^ (z & 1), :96, :] = dw[pl.ds(start, 96), :]
            place[n // 2, half ^ (z & 1), 96:, :] = tail if half == 0 else tail * 0


def rows_back_kernel(
    ws, dq0, dq1, dq2, dk0, dk1, dk2, dv0, dv1, dv2, dx_own, dx_other, grads
):
    for n, (q, k, v) in enumerate(((dq0, dk0, dv0), (dq1, dk1, dv1), (dq2, dk2, dv2))):
        start = 128 * n
        grads[: 4 * ROWS, start : start + 128] = q[...]
        grads[:, HALF + start : HALF + start + 128] = k[...]
        grads[:, 2 * HALF + start : 2 * HALF + start + 128] = v[...]
    dx_other[...] = low(dot_nt(grads[4 * ROWS :, HALF:], ws[:, HALF:]))
    dx_own[...] = dot_nt(grads[: 4 * ROWS, :], ws[...])


def middle_one_kernel(
    info, cm0, cm1, co0, co1, x0, x1, o0, o1, o2, o3, i0, i1, i2, i3,
    hidden_out, normed_out, inv_out, act, slope, vec,
    ctx, low_rows, small, order, inner_weight, sems,
):
    step = pl.program_id(0)
    _, x, _, _, _, f = coords(info)

    def copy(e, n):
        return pltpu.make_async_copy(
            (i0, i1, i2, i3)[n].at[:, pl.ds(pl.multiple_of(D * (f ^ e), 128), D)],
            inner_weight.at[e, pl.ds(pl.multiple_of(192 * (f ^ n), 64), 192), :],
            sems.at[e, n],
        )

    @pl.when(step == 0)
    def _():
        for e in range(4):
            for n in range(4):
                copy(e, n).start()
        for n, piece in enumerate((o0, o1, o2, o3)):
            small[f ^ n] = wide(piece[192:, :])
            order[n] = wide(piece[192:, :])
        for n in range(8):
            vec[n : n + 1, :] = jnp.concatenate(
                [small[m][n : n + 1, :192] for m in range(4)], axis=1
            )
        for side, (one, two) in enumerate(((cm0, cm1), (co0, co1))):
            rows = jnp.concatenate([one[...], two[...]], axis=0)
            for part in range(2):
                ctx[2 * (x ^ side) + part] = rows[:, 192 * part : 192 * part + 192]
        total = wide(jnp.concatenate([x0[...], x1[...]], axis=0)) + vec[2:3, :]
        for n, piece in enumerate((o0, o1, o2, o3)):
            total = total + matmul(ctx[f ^ n], piece[:192, :])
        hidden, normed, inv = layer_norm(total, vec[3:4, :], vec[4:5, :])
        hidden_out[...] = hidden
        normed_out[...] = normed
        inv_out[...] = inv
        low_rows[...] = low(hidden)

    for n in range(4):
        copy(step, n).wait()
    pre = matmul(low_rows[...], inner_weight[step]) + order[step][8:9, :]
    bell = 0.5 * (1.0 + lax.erf(pre * ROOT_HALF))
    act[0] = low(pre * bell)
    slope[0] = low(bell + pre * INV_ROOT_TAU * jnp.exp(-0.5 * pre * pre))


def norm_grad(grad, normed, inv, gain):
    scaled = grad * gain
    return inv * (
        scaled
        - jnp.mean(scaled, axis=-1, keepdims=True)
        - normed * jnp.mean(scaled * normed, axis=-1, keepdims=True)
    )


def column_sum(value):
    return jnp.sum(value, axis=0, keepdims=True)


def outer_copies(refs, held, sems):
    copies = [
        pltpu.make_async_copy(ref, held.at[n], sems.at[n]) for n, ref in enumerate(refs)
    ]
    for copy in copies:
        copy.start()
    return copies


def middle_two_kernel(
    info, lens, act, act_block, hidden, cot, vec, w0, w1, w2, w3,
    out, second_out, outer_out, sums, keep, send, w_all, w_sem,
):
    step = pl.program_id(0)
    z, x, _, _, c, f = coords(info)

    @pl.when(step == 0)
    def _():
        copies = outer_copies((w0, w1, w2, w3), w_all, w_sem)
        b_2, g_2, s_2 = vec[5:6, :], vec[6:7, :], vec[7:8, :]
        total = hidden[...] + b_2
        for n in range(4):
            copies[n].wait()
            total = total + matmul(act[n], w_all[n])
        result, normed, inv = layer_norm(total, g_2, s_2)
        zh = z >> 1
        out[zh] = low(result[:ROWS])
        out[1 - zh] = low(result[ROWS:])
        row = lax.broadcasted_iota(jnp.int32, (2 * ROWS, 1), 0)
        end = jnp.where(row < ROWS, lens[zh], lens[1 - zh] + ROWS)
        grad = wide(cot[...]) * jnp.where(row + c * ROWS < end, 1.0, 0.0)
        grad_second = norm_grad(grad, normed, inv, g_2)
        second_out[...] = grad_second
        grad_outer = low(grad_second)
        outer_out[...] = grad_outer
        sums[...] = jnp.zeros_like(sums)
        for n, value in enumerate((wide(grad_outer), grad * normed, grad)):
            sums[n : n + 1, :] = column_sum(value)

    @pl.when(step > 0)
    def _():
        grad = low(dot_tn(act_block[0], outer_out[...]))
        for place, wanted in ((send, step < 3), (keep, step >= 3)):

            @pl.when(wanted)
            def _(place=place):
                for n in range(4):
                    place[0, n ^ (2 * x + (z & 1))] = grad[192 * n : 192 * n + 192]


def inner_back_kernel(
    info, outer, slope, w0, w1, w2, w3, inner_out, sums, w_all, sems
):
    f = info[0] & 3
    copies = outer_copies((w0, w1, w2, w3), w_all, sems)
    for e in range(4):
        copies[e].wait()
        inner = low(dot_nt(outer[...], w_all[e]) * wide(slope[e]))
        inner_out[e] = inner
        sums[pl.ds(f ^ e, 1), :] = column_sum(wide(inner))


def middle_three_kernel(
    info, second, inner, normed_one, inv_one, vec, o0, o1, o2, o3, i0, i1, i2, i3,
    first_out, g0, g1, branch_out, sums, o_all, i_all, gc, o_sem, i_sem,
):
    _, x, _, _, _, f = coords(info)
    copies = {}
    for e in range(4):
        columns = pl.ds(pl.multiple_of(D * (f ^ e), 128), D)
        for n, ref in enumerate((i0, i1, i2, i3)):
            rows = pl.ds(pl.multiple_of(192 * (f ^ n), 64), 192)
            copies["i", e, n] = pltpu.make_async_copy(
                ref.at[:, columns], i_all.at[e, rows, :], i_sem.at[e, n]
            )
            copies["i", e, n].start()
    for n, ref in enumerate((o0, o1, o2, o3)):
        copies["o", n] = pltpu.make_async_copy(ref.at[:192, :D], o_all.at[n], o_sem.at[n])
        copies["o", n].start()
    grad_hidden = second[...]
    for e in range(4):
        for n in range(4):
            copies["i", e, n].wait()
        grad_hidden = grad_hidden + dot_nt(inner[e], i_all[e])
    grad_first = norm_grad(grad_hidden, normed_one[...], inv_one[...], vec[3:4, :])
    first_out[...] = grad_first
    branch = low(grad_first)
    branch_out[...] = branch
    for n, value in enumerate((wide(branch), grad_hidden * normed_one[...], grad_hidden)):
        sums[n : n + 1, :] = column_sum(value)
    for n in range(4):
        copies["o", n].wait()
        gc[f ^ n] = low(dot_nt(branch, o_all[n]))
    for side in range(2):
        rows = jnp.concatenate([gc[2 * (x ^ side)], gc[2 * (x ^ side) + 1]], axis=1)
        g0[1 - side] = rows[:ROWS]
        g1[1 - side] = rows[ROWS:]


def middle_four_kernel(
    info, inner, hidden, branch, cm0, cm1, co0, co1, sums_two, sums_in, sums_one,
    keep, send, held, out_held, vec_held,
):
    step = pl.program_id(0)
    _, x, _, _, _, f = coords(info)
    block = f ^ step

    @pl.when(step == 0)
    def _():
        for side, (one, two) in enumerate(((cm0, cm1), (co0, co1))):
            rows = jnp.concatenate([one[...], two[...]], axis=0)
            start = pl.multiple_of(HALF * (x ^ side), 128)
            out_held[pl.ds(start, HALF), :] = low(dot_tn(rows, branch[...]))
        vec_held[...] = jnp.zeros_like(vec_held)
        top = lax.broadcasted_iota(jnp.int32, (16, 1), 0) == 0
        for n in range(4):
            cut = slice(192 * n, 192 * n + 192)
            lines = (
                sums_in[n : n + 1, :],
                jnp.concatenate(
                    [sums_one[m : m + 1, cut] for m in range(3)] + [sums_two[0:1, cut]], axis=1
                ),
                jnp.concatenate(
                    [sums_two[1:2, cut], sums_two[2:3, cut], jnp.zeros((1, HALF), jnp.float32)],
                    axis=1,
                ),
            )
            for m, line in enumerate(lines):
                vec_held[m, n] = low(jnp.where(top, line, 0.0))

    held[...] = low(dot_tn(low(hidden[...]), inner[0]))
    for n in range(4):
        place = send if n % 2 else keep
        start = 192 * (f ^ n)
        place[n // 2, 0, :192, :] = held[pl.ds(pl.multiple_of(start, 64), 192), :]
        place[n // 2, 0, 192:240, :] = out_held[pl.ds(pl.multiple_of(start + 48 * block, 16), 48), :]
        place[n // 2, 0, 240:, :] = vec_held[block, f ^ n]


MIDDLE = 2 * ROWS
BF, FP = jnp.bfloat16, jnp.float32


def whole(shape):
    return pl.BlockSpec(tuple(shape), lambda *_: (0,) * len(shape))


def lane_block(rows, start=0):
    return pl.BlockSpec((rows, 128), lambda step, *_: (0, step + start))


def call(kernel, name, grid, scalars, operands, outs, scratch=(), work=(1, 1), limit=30):
    return pl.pallas_call(
        kernel,
        out_shape=[jax.ShapeDtypeStruct(shape, kind) for shape, kind, _ in outs],
        grid_spec=pltpu.PrefetchScalarGridSpec(
            num_scalar_prefetch=len(scalars),
            grid=(grid,),
            in_specs=[spec or whole(array.shape) for array, spec in operands],
            out_specs=[spec or whole(shape) for shape, _, spec in outs],
            scratch_shapes=list(scratch),
        ),
        compiler_params=pltpu.CompilerParams(
            dimension_semantics=("arbitrary",), vmem_limit_bytes=limit * 1024 * 1024
        ),
        cost_estimate=pl.CostEstimate(
            flops=1000, bytes_accessed=1000, transcendentals=0
        ),
        name=name,
    )(*scalars, *[array for array, _ in operands])


def plain(arrays):
    return [(array, None) for array in arrays]


def anywhere(arrays):
    return [(array, pl.BlockSpec(memory_space=pl.ANY)) for array in arrays]


def probs_block(start=0):
    return pl.BlockSpec((2, 4 * ROWS, 8 * ROWS), lambda step, *_: (step + start, 0, 0))


def pack(info, lens, inputs, cotangent, weights, vectors):
    return call(
        pack_kernel, "pack", 1, (info, lens),
        plain([inputs, cotangent, *weights[:4]])
        + [(weights[4], pl.BlockSpec((192, 2 * D), lambda _, info, lens: (0, (info[0] >> 2) & 1)))]
        + plain(vectors),
        [
            ((ROWS, D), BF, None), ((ROWS, D), BF, None), ((MIDDLE, D), BF, None),
            ((208, D + 3 * HALF), BF, None), ((192, 2 * D), BF, None),
        ],
        [pltpu.VMEM((16, D), FP)], limit=56,
    )


def first_columns(pieces):
    return [(piece, pl.BlockSpec((208, D), lambda *_: (0, 0))) for piece in pieces]


def attend(info, blocks, pieces):
    return call(
        attend_kernel, "attend", 3, (info,),
        anywhere(blocks)
        + [(piece, pl.BlockSpec((16, D), lambda *_: (12, 0))) for piece in pieces]
        + anywhere(pieces),
        [
            ((8 * ROWS, D), BF, None), ((D, 3 * HALF), BF, None), ((4 * ROWS, HALF), BF, None),
            ((8 * ROWS, HALF), BF, None), ((8 * ROWS, HALF), BF, None),
            ((6, 4 * ROWS, 8 * ROWS), BF, probs_block()),
        ]
        + [((ROWS, HALF), BF, lane_block(ROWS))] * 2
        + [((2, ROWS, HALF), BF, pl.BlockSpec((2, ROWS, 128), lambda step, *_: (0, 0, step)))],
        [
            pltpu.VMEM((1, 8 * ROWS), FP), pltpu.VMEM((4, 16, D), FP),
            pltpu.SemaphoreType.DMA((12,)),
        ],
        limit=56,
    )


def attend_back(queries, keys, values, probs, grads, start, pairs):
    return call(
        attend_back_kernel, "attend_back", pairs, (),
        [
            (queries, lane_block(4 * ROWS, start)), (keys, lane_block(8 * ROWS, start)),
            (values, lane_block(8 * ROWS, start)), (probs, probs_block(start)),
        ]
        + [(grad, pl.BlockSpec((None, ROWS, 128), lambda s, n=n: (n, 0, s + start))) for grad, n in grads],
        [
            ((4 * ROWS, 128 * pairs), BF, lane_block(4 * ROWS)),
            ((8 * ROWS, 128 * pairs), BF, lane_block(8 * ROWS)),
            ((8 * ROWS, 128 * pairs), BF, lane_block(8 * ROWS)),
        ],
        (), (4 * pairs, 5 * pairs),
    )


def by_name(pairs):
    return [part for name in zip(*pairs) for part in name]


def joint_grads(info, xs, pairs):
    joint = (2, 2, 112, 3 * HALF)
    return call(
        joint_kernel, "joint_grads", 1, (info,), plain([xs, *by_name(pairs)]),
        [(joint, BF, None), (joint, BF, None)],
        [pltpu.VMEM((8 * ROWS, 3 * HALF), BF), pltpu.VMEM((D, 3 * HALF), BF)],
    )


def rows_back(ws, pairs):
    return call(
        rows_back_kernel, "rows_back", 1, (), plain([ws, *by_name(pairs)]),
        [((4 * ROWS, D), FP, None), ((4 * ROWS, D), BF, None)],
        [pltpu.VMEM((8 * ROWS, 3 * HALF), BF)],
    )


def middle_one(info, ctx, rows, out_p, inner_p):
    block = pl.BlockSpec((1, MIDDLE, D), lambda step, *_: (step, 0, 0))
    return call(
        middle_one_kernel, "middle_one", 4, (info,),
        plain([*ctx, *rows]) + first_columns(out_p) + anywhere(inner_p),
        [
            ((MIDDLE, D), FP, None), ((MIDDLE, D), FP, None), ((MIDDLE, 1), FP, None),
            ((4, MIDDLE, D), BF, block), ((4, MIDDLE, D), BF, block), ((8, D), FP, None),
        ],
        [
            pltpu.VMEM((4, MIDDLE, 192), BF), pltpu.VMEM((MIDDLE, D), BF),
            pltpu.VMEM((4, 16, D), FP), pltpu.VMEM((4, 16, D), FP), pltpu.VMEM((4, D, D), BF),
            pltpu.SemaphoreType.DMA((4, 4)),
        ],
        (4, 10),
    )


def middle_two(info, lens, act, hidden, cot, vec, outer_p):
    def turn(step, *_):
        at = jnp.maximum(step - 1, 0)
        return (jnp.where(at < 2, 2 * at + 1, 2 * at - 4), 0, 0)

    blocks = (2, 4, 192, D)
    return call(
        middle_two_kernel, "middle_two", 5, (info, lens),
        [(act, None), (act, pl.BlockSpec((1, MIDDLE, D), turn))]
        + plain([hidden, cot, vec])
        + anywhere(outer_p),
        [
            ((2, ROWS, D), BF, None), ((MIDDLE, D), FP, None), ((MIDDLE, D), BF, None),
            ((8, D), FP, None),
            (blocks, BF, pl.BlockSpec((1, 4, 192, D), lambda s, *_: (jnp.maximum(s - 3, 0), 0, 0, 0))),
            (blocks, BF, pl.BlockSpec((1, 4, 192, D), lambda s, *_: (jnp.where(s < 2, 0, 1), 0, 0, 0))),
        ],
        [pltpu.VMEM((4, D, D), BF), pltpu.SemaphoreType.DMA((4,))], (4, 10),
    )


def inner_back(info, outer, slope, outer_p):
    return call(
        inner_back_kernel, "inner_back", 1, (info,), plain([outer, slope]) + anywhere(outer_p),
        [((4, MIDDLE, D), BF, None), ((4, D), FP, None)],
        [pltpu.VMEM((4, D, D), BF), pltpu.SemaphoreType.DMA((4,))], (2, 7),
    )


def middle_three(info, second, inner, normed, inv, vec, out_p, inner_p):
    return call(
        middle_three_kernel, "middle_three", 1, (info,),
        plain([second, inner, normed, inv, vec]) + anywhere([*out_p, *inner_p]),
        [((MIDDLE, D), FP, None)]
        + [((2, ROWS, HALF), BF, None)] * 2
        + [((MIDDLE, D), BF, None), ((8, D), FP, None)],
        [
            pltpu.VMEM((4, 192, D), BF), pltpu.VMEM((4, D, D), BF),
            pltpu.VMEM((4, MIDDLE, 192), BF), pltpu.SemaphoreType.DMA((4,)),
            pltpu.SemaphoreType.DMA((4, 4)),
        ],
        (2, 7),
    )


def middle_four(info, inner, hidden, branch, ctx, sums):
    def spot(step, info):
        z, x, _, _, _, f = coords(info)
        return (0, f ^ step ^ (2 * (z & 1) + x), 0, 0)

    block = pl.BlockSpec((2, 1, 256, D), spot)
    return call(
        middle_four_kernel, "middle_four", 4, (info,),
        [(inner, pl.BlockSpec((1, MIDDLE, D), lambda step, *_: (step, 0, 0)))]
        + plain([hidden, branch, *ctx, *sums]),
        [((2, 4, 256, D), BF, block)] * 2,
        [pltpu.VMEM((D, D), BF), pltpu.VMEM((D, D), BF), pltpu.VMEM((4, 4, 16, D), BF)],
        (4, 8),
    )


def place_outer_kernel(info, p0, p1, p2, p3, out):
    z, x, _, _, _, _ = coords(info)
    for n, piece in enumerate((p0, p1, p2, p3)):
        out[pl.ds(pl.multiple_of(192 * (n ^ (2 * x + (z & 1))), 64), 192), :] = wide(piece[...])


def place_inner_kernel(
    info, p0, p1, p2, p3, inner, out, b_in, b_out, g_one, s_one, b_two, g_two, s_two, held
):
    z, x, _, _, _, _ = coords(info)
    for n, piece in enumerate((p0, p1, p2, p3)):
        at = n ^ (2 * (z & 1) + x)
        inner[:, pl.ds(pl.multiple_of(D * at, 128), D)] = wide(piece[:192, :])
        out[pl.ds(pl.multiple_of(48 * at, 16), 48), :] = wide(piece[192:240, :])
        held[at] = wide(piece[240:, :])
    b_in[...] = held[0][0:1, :].reshape(D)
    for n, vector in enumerate((b_out, g_one, s_one, b_two, g_two, s_two)):
        cut = 192 * (n % 4)
        vector[...] = held[1 + n // 4][0:1, cut : cut + 192].reshape(192)


def place_joint_kernel(info, p0, p1, p2, p3, query, key, value, b_query, b_value, held):
    z, x, _, _, _, f = coords(info)
    z_bit = z & 1
    for n, piece in enumerate((p0, p1, p2, p3)):
        rows = pl.ds(pl.multiple_of(96 * (n % 2 ^ z_bit), 32), 96)
        columns = pl.ds(pl.multiple_of(HALF * (n // 2 ^ x), 128), HALF)
        for m, out in enumerate((query, key, value)):
            out[rows, columns] = wide(piece[:96, HALF * m : HALF * m + HALF])
        line = wide(piece[96:, :])
        line = jnp.where(f & 1 == 0, line, jnp.concatenate([line[:, 192:], line[:, :192]], axis=1))
        held[n // 2 ^ x, n % 2 ^ z_bit] = line
    mine = held[f >> 1, 0][0:1, :]
    b_query[...] = mine[:, :192].reshape(192)
    b_value[...] = mine[:, 2 * HALF : 2 * HALF + 192].reshape(192)


def placed(kernel, name, info, pieces, shapes, held=()):
    return call(
        kernel, name, 1, (info,), plain(pieces), [(shape, FP, None) for shape in shapes],
        [pltpu.VMEM(shape, FP) for shape in held], (1, 6),
    )


def unshuffle(array, bit):
    return jnp.where(bit == 0, array, array[::-1])


def tied(values, *events):
    return lax.optimization_barrier((values, events))[0]


ROW_A, ROW_B = 96, 144


def fast_body(
    inputs, cotangent, lengths, w_query, b_query, w_key, w_value, b_value, w_output, b_output,
    gain_one, bias_one, w_inner, b_inner, w_outer, b_outer, gain_two, bias_two,
):
    info = lax.axis_index(("ctx", "fsdp")).astype(jnp.int32).reshape(1)
    zh, x = lax.axis_index("ctx") // 4, lax.axis_index("ctx") % 2

    t0, t1, cot, first, half = pack(
        info, lengths, inputs, cotangent, (w_query, w_key, w_value, w_output, w_inner),
        (b_query, b_value, b_output, gain_one, bias_one, b_outer, gain_two, bias_two, b_inner),
    )

    bu, bv = seq_send[0](t0), seq_send[1](t1)
    first_y, first_k = swap_y(first), swap_core(first)
    half_y = swap_y(half)
    bu, bv, first_k = tied((bu, bv, first_k))
    bxu, bxv, bku = swap_x(bu), swap_x(bv), swap_core(bu)
    bxu, bxv, bku, first_y, half_y = tied((bxu, bxv, bku, first_y, half_y))
    bkv, *rest = [swap_core(b) for b in (bv, bxu, bxv, first_y)]
    bkv, *rest = tied([bkv] + rest)
    blocks = [bu, bv, bxu, bxv, bku, bkv, *rest[:2]]
    first_p = [first, first_k, first_y, rest[2]]
    outer_y = swap_y(tied(w_outer, half_y))
    half_x = swap_x(tied(half_y, bkv))
    xs, ws, queries, keys, values, probs, cu, cv, cx = attend(info, blocks, first_p)

    cu, cv, cx, half_x = tied((cu, cv, cx, half_x))
    cu, cv = seq_return[0](cu), seq_return[1](cv)
    cx = swap_x(cx)
    inner_y = jnp.where(
        x == 0, jnp.concatenate([half_y, half_x], 1), jnp.concatenate([half_x, half_y], 1)
    )
    cu, cv, cx, outer_y, inner_y = tied((cu, cv, cx, outer_y, inner_y))
    cxu, cxv = seq_return[0](cx[0]), seq_return[1](cx[1])
    inner_k, inner_ky = swap_core(tied(w_inner, cx)), swap_core(inner_y)
    cxu, cxv, inner_k, inner_ky = tied((cxu, cxv, inner_k, inner_ky))
    outer_k, outer_ky = swap_core(tied(w_outer, cxu)), swap_core(tied(outer_y, cxu))
    ctx = [cu, cv, cxu, cxv]
    inner_p = [w_inner, inner_k, inner_y, inner_ky]
    hidden, normed, inv, act, slope, vec = middle_one(info, ctx, [t0, t1], first_p, inner_p)
    act, outer_k, outer_ky = tied((act, outer_k, outer_ky))
    outer_p = [w_outer, outer_k, outer_y, outer_ky]
    outputs, second_grad, outer, sums_two, o_keep, o_send = middle_two(
        info, lengths, act, hidden, cot, vec, outer_p
    )
    o_came = swap_core(o_send)
    inner, sums_in = inner_back(info, outer, slope, outer_p)
    o_came, inner = tied((o_came, inner))
    o_y = low(wide(o_keep[1, :2]) + wide(o_came[1, :2]))
    o_z = low(wide(o_keep[:, 3]) + wide(o_came[:, 3]))
    inner, o_y, o_z = tied((inner, o_y, o_z))
    o_y, o_z = swap_y(o_y), swap_z1(o_z)
    grad_first, g0, g1, branch, sums_one = middle_three(
        info, second_grad, inner, normed, inv, vec, first_p, inner_p
    )
    g0, g1 = seq_send[0](g0), seq_send[1](g1)
    i_keep, i_send = middle_four(
        info, inner, hidden, branch, ctx, (sums_two, sums_in, sums_one)
    )
    g0, g1, i_send, o_y, o_z = tied((g0, g1, i_send, o_y, o_z))
    go = jnp.stack([g0[0], g1[0]])
    go, o_y, o_z, i_send = tied((go, o_y, o_z, i_send))
    go = swap_x(go)
    i_came = swap_core(i_send)
    o_z2 = swap_z1(low(wide(o_keep[0, 1]) + wide(o_came[0, 1]) + wide(o_y[1])))
    o_y2 = swap_y(low(wide(o_keep[1, 2]) + wide(o_came[1, 2]) + wide(o_z[1])))
    go, i_came, o_z2, o_y2 = tied((go, i_came, o_z2, o_y2))
    o_one = wide(o_keep[0, 0]) + wide(o_came[0, 0]) + wide(o_y[0]) + wide(o_z2)
    o_two = low(wide(o_keep[0, 2]) + wide(o_came[0, 2]) + wide(o_z[0]) + wide(o_y2))
    i_keep, i_came = (a.reshape(2, 2, 2, 256, D) for a in (i_keep, i_came))

    def summed(*spot):
        return wide(i_keep[spot]) + wide(i_came[spot])

    every, one_a, one_b, one_c = slice(None), slice(0, ROW_A), slice(ROW_A, ROW_B), slice(ROW_B, 256)
    i_y, i_x = low(summed(1, every, every, one_a)), low(summed(every, every, 1, one_b))
    i_z = low(summed(every, 1, every, one_c))
    go, i_y, i_x, i_z, o_two = tied((go, i_y, i_x, i_z, o_two))
    i_y, i_x, i_z = swap_y(i_y), swap_x(i_x), swap_z1(i_z)
    o_came = swap_x(o_two)
    grads = [(g0, 1), (g1, 1), (go, 0), (go, 1)]
    pair_0 = attend_back(queries, keys, values, probs, grads, 0, 1)
    pair_1 = attend_back(tied(queries, pair_0), keys, values, probs, grads, 1, 1)
    pair_2 = attend_back(tied(queries, pair_1), keys, values, probs, grads, 2, 1)
    pairs = (pair_0, pair_1, pair_2)
    dx_own, dx_other = rows_back(ws, pairs)
    dx_own, dx_other, i_y, i_x, i_z, o_came = tied((dx_own, dx_other, i_y, i_x, i_z, o_came))
    part_a = summed(0, every, every, one_a) + wide(i_y)
    part_b = summed(every, every, 0, one_b) + wide(i_x)
    part_c = summed(every, 0, every, one_c) + wide(i_z)
    i_z2, i_y2, i_x2 = swap_z1(low(part_a[1])), swap_y(low(part_b[1])), swap_x(low(part_c[:, 1]))
    o_sum = low(o_one + wide(o_came))
    j_keep, j_send = joint_grads(info, tied(xs, dx_other), pairs)
    j_keep, j_send, i_x2, i_y2, i_z2 = tied((j_keep, j_send, i_x2, i_y2, i_z2))
    j_came, dx_came = swap_core(j_send), swap_core(dx_other)
    o_came = swap_z2(tied(o_sum, j_send))
    part_a, part_b, part_c = part_a[0] + wide(i_z2), part_b[0] + wide(i_y2), part_c[:, 0] + wide(i_x2)
    i_x3, i_z3, i_y3 = swap_x(low(part_a[1])), swap_z1(low(part_b[1])), swap_y(low(part_c[1]))
    j_came, dx_came, i_x3, i_z3, i_y3 = tied((j_came, dx_came, i_x3, i_z3, i_y3))
    i_sum = [part_a[0] + wide(i_x3), part_b[0] + wide(i_z3), part_c[0] + wide(i_y3)]
    i_sum = low(jnp.concatenate(i_sum, axis=0))
    dx = dx_own[: 2 * ROWS] + wide(dx_came[: 2 * ROWS])
    dx_send = low(dx_own[2 * ROWS :] + wide(dx_came[2 * ROWS :]))
    j_y = swap_y(low(wide(j_keep[1, :, :56]) + wide(j_came[1, :, :56])))
    j_z = swap_z1(low(wide(j_keep[:, 1, 56:]) + wide(j_came[:, 1, 56:])))
    j_one = wide(j_keep[0, :, :56]) + wide(j_came[0, :, :56])
    j_two = wide(j_keep[:, 0, 56:]) + wide(j_came[:, 0, 56:])
    i_came = swap_z2(i_sum)
    dx_came = swap_x(dx_send)
    j_y, j_z, dx_came, o_came = tied((j_y, j_z, dx_came, o_came))
    j_one, j_two = j_one + wide(j_y), j_two + wide(j_z)
    dx = low(dx + wide(dx_came))
    o_sum = low(wide(o_sum) + wide(o_came))
    j_z, j_y = swap_z1(low(j_one[1])), swap_y(low(j_two[1]))
    o_x, o_z = swap_x(o_sum), swap_z1(o_sum)
    j_z, j_y, o_x, o_z, i_came = tied((j_z, j_y, o_x, o_z, i_came))
    j_sum = low(jnp.concatenate([j_one[0] + wide(j_z), j_two[0] + wide(j_y)], axis=0))
    i_sum = low(wide(i_sum) + wide(i_came))
    j_came = swap_z2(j_sum)
    i_z, i_x, o_zx = swap_z1(i_sum), swap_x(i_sum), swap_x(tied(o_z, i_sum))
    j_came, i_z, i_x, o_zx = tied((j_came, i_z, i_x, o_zx))
    j_sum = low(wide(j_sum) + wide(j_came))
    j_x, j_z = swap_x(j_sum), swap_z1(j_sum)
    i_zx = swap_x(i_z)
    dx0, dx1 = seq_return[0](tied(dx[:ROWS], i_z)), seq_return[1](tied(dx[ROWS:], i_z))
    (outer_grad,) = placed(place_outer_kernel, "place_outer", info, tied([o_sum, o_z, o_x, o_zx], j_sum), [(D, D)])
    j_x, j_z, i_zx, dx0, dx1, outer_grad = tied((j_x, j_z, i_zx, dx0, dx1, outer_grad))
    j_zx = swap_x(j_z)
    input_grad = grad_first + wide(jnp.concatenate([dx0, dx1], axis=0))
    input_grad = unshuffle(input_grad.reshape(2, ROWS, D), zh)
    inner_grad, out_grad, grad_b1, grad_bo, grad_g1, grad_s1, grad_b2, grad_g2, grad_s2 = placed(
        place_inner_kernel, "place_inner", info, [i_sum, i_x, i_z, i_zx],
        [(192, 4 * D), (192, D), (D,)] + [(192,)] * 6, [(4, 16, D)],
    )
    q_grad, k_grad, v_grad, grad_bq, grad_bv = placed(
        place_joint_kernel, "place_joint", info, [j_sum, j_z, j_x, j_zx],
        [(192, D)] * 3 + [(192,)] * 2, [(2, 2, 16, 3 * HALF)],
    )
    return (
        outputs, input_grad, q_grad, grad_bq, k_grad, v_grad, grad_bv, out_grad, grad_bo,
        grad_g1, grad_s1, inner_grad, grad_b1, outer_grad, grad_b2, grad_g2, grad_s2,
    )


def solution(mesh):
    placed = (
        P("fsdp", "ctx", None),
        P("fsdp", "ctx", None),
        P("fsdp"),
        P("fsdp", None),
        P("fsdp"),
        P("fsdp", None),
        P("fsdp", None),
        P("fsdp"),
        P("fsdp", None),
        P("fsdp"),
        P("fsdp"),
        P("fsdp"),
        P("fsdp", None),
        P("fsdp"),
        P("fsdp", None),
        P("fsdp"),
        P("fsdp"),
        P("fsdp"),
    )
    fast = dict(mesh.shape) == {"ctx": 8, "fsdp": 4}
    return jax.shard_map(
        fast_body if fast else body,
        mesh=mesh,
        in_specs=placed,
        out_specs=(
            P("fsdp", "ctx", None),
            P("fsdp", "ctx", None),
            P("fsdp", None),
            P("fsdp"),
            P("fsdp", None),
            P("fsdp", None),
            P("fsdp"),
            P("fsdp", None),
            P("fsdp"),
            P("fsdp"),
            P("fsdp"),
            P("fsdp", None),
            P("fsdp"),
            P("fsdp", None),
            P("fsdp"),
            P("fsdp"),
            P("fsdp"),
        ),
        check_vma=False,
    )
```

```python
from functools import partial

import jax
import jax.numpy as jnp
from jax import lax
from jax.experimental import pallas as pl
from jax.experimental.pallas import tpu as pltpu
from jax.sharding import PartitionSpec as P

D = 768
H = 12
HD = 64
SEQ_MB = 1
MICRO = 2


EPSILON = 1e-05
NEG_FILL = -1e30
SCALE = 0.125
ROOT_HALF = 0.7071067811865476
INV_ROOT_TAU = 0.3989422804014327
key_block = 512


def matmul(left_side, right_side):
    return jnp.dot(left_side, right_side, preferred_element_type=jnp.float32)


def left_product(left_side, right_side):
    return lax.dot_general(
        left_side, right_side, (((0,), (0,)), ((), ())), preferred_element_type=jnp.float32
    )


def right_product(left_side, right_side):
    return lax.dot_general(
        left_side, right_side, (((1,), (1,)), ((), ())), preferred_element_type=jnp.float32
    )


def split_heads(token_rows):
    return token_rows.reshape(token_rows.shape[0], token_rows.shape[1], H, HD)


def head_scores(query_rows, key_rows):
    return (
        jnp.einsum(
            "bqhd,bkhd->bhqk",
            split_heads(query_rows),
            split_heads(key_rows),
            preferred_element_type=jnp.float32,
        )
        * SCALE
    )


def live_mask(seq_lens, first_pos, num_rows):
    return (first_pos + lax.iota(jnp.int32, num_rows))[None, :] < seq_lens[:, None]


def layer_norm(resid, norm_gain, norm_bias):
    row_mean = jnp.mean(resid, axis=-1, keepdims=True)
    centered = resid - row_mean
    inv_std = lax.rsqrt(jnp.mean(centered * centered, axis=-1, keepdims=True) + EPSILON)
    normed = centered * inv_std
    return (normed * norm_gain + norm_bias, normed, inv_std)


def norm_back(grad_out, normed, inv_std, norm_gain):
    grad_norm = grad_out * norm_gain
    grad_in = inv_std * (
        grad_norm
        - jnp.mean(grad_norm, axis=-1, keepdims=True)
        - normed * jnp.mean(grad_norm * normed, axis=-1, keepdims=True)
    )
    return (grad_in, jnp.sum(grad_out * normed, axis=0), jnp.sum(grad_out, axis=0))


def gelu_exact(pre_act):
    return 0.5 * pre_act * (1.0 + lax.erf(pre_act * ROOT_HALF))


def gelu_slope(pre_act):
    return 0.5 * (1.0 + lax.erf(pre_act * ROOT_HALF)) + pre_act * INV_ROOT_TAU * jnp.exp(
        -0.5 * pre_act * pre_act
    )


def in_blocks(step_fn, running, pieces):
    num_rows = pieces[0].shape[1]

    def advance(block_index, current):
        offset = block_index * key_block
        sliced = tuple(
            (lax.dynamic_slice_in_dim(member, offset, key_block, 1) for member in pieces)
        )
        return step_fn(current, sliced, offset)

    return lax.fori_loop(0, num_rows // key_block, advance, running)


def attend_step(running, sliced, first_pos, queries, seq_lens, skip_empty):
    key_rows, value_rows = sliced
    live_keys = live_mask(seq_lens, first_pos, key_rows.shape[1])
    run_max, run_sum, run_out = running
    key_mask = live_keys[:, None, None, :]
    scores = jnp.where(key_mask, head_scores(queries, key_rows), NEG_FILL)
    new_max = jnp.maximum(run_max, jnp.max(scores, axis=-1))
    weights = jnp.where(key_mask, jnp.exp(scores - new_max[..., None]), 0.0)
    rescale = jnp.exp(run_max - new_max)
    new_sum = run_sum * rescale + jnp.sum(weights, axis=-1)
    new_out = run_out * rescale[..., None] + jnp.einsum(
        "bhqk,bkhd->bhqd",
        weights.astype(jnp.bfloat16),
        split_heads(value_rows),
        preferred_element_type=jnp.float32,
    )
    return (new_max, new_sum, new_out)


def query_grad_step(
    running,
    sliced,
    first_pos,
    queries,
    grad_context,
    log_total,
    row_delta,
    seq_lens,
    live_queries,
    skip_empty,
):
    key_rows, value_rows = sliced
    live_keys = live_mask(seq_lens, first_pos, key_rows.shape[1])
    key_mask = live_keys[:, None, None, :]
    probabilities = jnp.where(
        key_mask, jnp.exp(head_scores(queries, key_rows) - log_total[..., None]), 0.0
    )
    grad_probs = jnp.einsum(
        "bqhd,bkhd->bhqk",
        split_heads(grad_context),
        split_heads(value_rows),
        preferred_element_type=jnp.float32,
    )
    grad_scores = (probabilities * (grad_probs - row_delta[..., None])).astype(jnp.bfloat16)
    return running + jnp.einsum(
        "bhqk,bkhd->bqhd", grad_scores, split_heads(key_rows), preferred_element_type=jnp.float32
    )


def key_grad_step(
    running,
    sliced,
    first_pos,
    key_rows,
    value_rows,
    stat_total,
    stat_delta,
    seq_lens,
    live_keys,
    skip_empty,
):
    query_rows, grad_rows = sliced
    num_rows = query_rows.shape[1]
    grad_k, grad_v = running
    log_total = lax.dynamic_slice_in_dim(stat_total, first_pos, num_rows, 1).transpose(0, 2, 1)
    row_delta = lax.dynamic_slice_in_dim(stat_delta, first_pos, num_rows, 1).transpose(0, 2, 1)
    key_mask = live_keys[:, None, None, :]
    probabilities = jnp.where(
        key_mask, jnp.exp(head_scores(query_rows, key_rows) - log_total[..., None]), 0.0
    )
    grad_probs = jnp.einsum(
        "bqhd,bkhd->bhqk",
        split_heads(grad_rows),
        split_heads(value_rows),
        preferred_element_type=jnp.float32,
    )
    grad_scores = (probabilities * (grad_probs - row_delta[..., None])).astype(jnp.bfloat16)
    grad_v = grad_v + jnp.einsum(
        "bhqk,bqhd->bkhd",
        probabilities.astype(jnp.bfloat16),
        split_heads(grad_rows),
        preferred_element_type=jnp.float32,
    )
    grad_k = grad_k + jnp.einsum(
        "bhqk,bqhd->bkhd", grad_scores, split_heads(query_rows), preferred_element_type=jnp.float32
    )
    return (grad_k, grad_v)


def body(
    inputs,
    cotangent,
    lengths,
    w_query,
    b_query,
    w_key,
    w_value,
    b_value,
    w_output,
    b_output,
    gain_one,
    bias_one,
    w_inner,
    b_inner,
    w_outer,
    b_outer,
    gain_two,
    bias_two,
):
    gathered = (
        lax.all_gather(w_query, "fsdp", axis=0, tiled=True),
        lax.all_gather(b_query, "fsdp", axis=0, tiled=True),
        lax.all_gather(w_key, "fsdp", axis=0, tiled=True),
        lax.all_gather(w_value, "fsdp", axis=0, tiled=True),
        lax.all_gather(b_value, "fsdp", axis=0, tiled=True),
        lax.all_gather(w_output, "fsdp", axis=0, tiled=True),
        lax.all_gather(b_output, "fsdp", axis=0, tiled=True),
        lax.all_gather(gain_one, "fsdp", axis=0, tiled=True),
        lax.all_gather(bias_one, "fsdp", axis=0, tiled=True),
        lax.all_gather(w_inner, "fsdp", axis=0, tiled=True),
        lax.all_gather(b_inner, "fsdp", axis=0, tiled=True),
        lax.all_gather(w_outer, "fsdp", axis=0, tiled=True),
        lax.all_gather(b_outer, "fsdp", axis=0, tiled=True),
        lax.all_gather(gain_two, "fsdp", axis=0, tiled=True),
        lax.all_gather(bias_two, "fsdp", axis=0, tiled=True),
    )
    (
        query_weight,
        query_bias,
        key_weight,
        value_weight,
        value_bias,
        out_weight,
        out_bias,
        gain_first,
        shift_first,
        inner_weight,
        inner_bias,
        outer_weight,
        outer_bias,
        gain_second,
        shift_second,
    ) = gathered
    joint_weight = jnp.concatenate([query_weight, key_weight, value_weight], axis=1)
    joint_bias = jnp.concatenate(
        [
            query_bias.astype(jnp.float32),
            jnp.zeros((D,), jnp.float32),
            value_bias.astype(jnp.float32),
        ]
    )
    out_bias_f = out_bias.astype(jnp.float32)
    inner_bias_f = inner_bias.astype(jnp.float32)
    outer_bias_f = outer_bias.astype(jnp.float32)
    gain_first_f = gain_first.astype(jnp.float32)
    shift_first_f = shift_first.astype(jnp.float32)
    gain_second_f = gain_second.astype(jnp.float32)
    shift_second_f = shift_second.astype(jnp.float32)
    seq_dev = inputs.shape[1]
    row_count = SEQ_MB * seq_dev
    positions = lax.axis_index("ctx") * seq_dev + lax.iota(jnp.int32, seq_dev)
    accum = None
    out_list = []
    grad_list = []
    for micro_index in range(MICRO):
        first_seq = micro_index * SEQ_MB
        seq_lens = lengths[first_seq : first_seq + SEQ_MB]
        token_rows = inputs[first_seq : first_seq + SEQ_MB].reshape(row_count, D)
        grad_rows = (
            cotangent[first_seq : first_seq + SEQ_MB].reshape(row_count, D).astype(jnp.float32)
        )
        query_ok = positions[None, :] < seq_lens[:, None]
        row_keep = query_ok.reshape(row_count, 1).astype(jnp.float32)
        projected = (matmul(token_rows, joint_weight) + joint_bias).astype(jnp.bfloat16)
        queries = projected[:, :D].reshape(SEQ_MB, seq_dev, D)
        keys_local = projected[:, D : 2 * D].reshape(SEQ_MB, seq_dev, D)
        values_local = projected[:, 2 * D :].reshape(SEQ_MB, seq_dev, D)
        start_state = (
            jnp.full((SEQ_MB, H, seq_dev), NEG_FILL, jnp.float32),
            jnp.zeros((SEQ_MB, H, seq_dev), jnp.float32),
            jnp.zeros((SEQ_MB, H, seq_dev, HD), jnp.float32),
        )
        attend_fn = partial(attend_step, queries=queries, seq_lens=seq_lens, skip_empty=False)
        run_max, run_sum, run_out = in_blocks(
            attend_fn,
            start_state,
            (
                lax.all_gather(keys_local, "ctx", axis=1, tiled=True),
                lax.all_gather(values_local, "ctx", axis=1, tiled=True),
            ),
        )
        attended = run_out / run_sum[..., None]
        log_total = run_max + jnp.log(run_sum)
        context = attended.transpose(0, 2, 1, 3).reshape(row_count, D).astype(jnp.bfloat16)
        first_sum = token_rows.astype(jnp.float32) + matmul(context, out_weight) + out_bias_f
        hidden, normed_one, inv_one = layer_norm(first_sum, gain_first_f, shift_first_f)
        hidden_low = hidden.astype(jnp.bfloat16)
        inner_pre = matmul(hidden_low, inner_weight) + inner_bias_f
        activated = gelu_exact(inner_pre).astype(jnp.bfloat16)
        outer_out = matmul(activated, outer_weight) + outer_bias_f
        result, normed_two, inv_two = layer_norm(hidden + outer_out, gain_second_f, shift_second_f)
        out_list.append(result.astype(jnp.bfloat16).reshape(SEQ_MB, seq_dev, D))
        grad_out = grad_rows * row_keep
        grad_second, grad_gain_b, grad_shift_b = norm_back(
            grad_out, normed_two, inv_two, gain_second_f
        )
        grad_outer = grad_second.astype(jnp.bfloat16)
        grad_outer_w = left_product(activated, grad_outer)
        grad_outer_b = jnp.sum(grad_outer.astype(jnp.float32), axis=0)
        grad_inner = (right_product(grad_outer, outer_weight) * gelu_slope(inner_pre)).astype(
            jnp.bfloat16
        )
        grad_inner_w = left_product(hidden_low, grad_inner)
        grad_inner_b = jnp.sum(grad_inner.astype(jnp.float32), axis=0)
        grad_hidden = grad_second + right_product(grad_inner, inner_weight)
        grad_first, grad_gain_a, grad_shift_a = norm_back(
            grad_hidden, normed_one, inv_one, gain_first_f
        )
        grad_branch = grad_first.astype(jnp.bfloat16)
        grad_out_w = left_product(context, grad_branch)
        grad_out_b = jnp.sum(grad_branch.astype(jnp.float32), axis=0)
        grad_context = (
            right_product(grad_branch, out_weight).astype(jnp.bfloat16).reshape(SEQ_MB, seq_dev, D)
        )
        row_delta = jnp.einsum(
            "bqhd,bhqd->bhq", split_heads(grad_context).astype(jnp.float32), attended
        )
        stat_total, stat_delta = (
            lax.all_gather(log_total.transpose(0, 2, 1), "ctx", axis=1, tiled=True),
            lax.all_gather(row_delta.transpose(0, 2, 1), "ctx", axis=1, tiled=True),
        )
        query_fn = partial(
            query_grad_step,
            queries=queries,
            grad_context=grad_context,
            log_total=log_total,
            row_delta=row_delta,
            seq_lens=seq_lens,
            live_queries=query_ok,
            skip_empty=False,
        )
        key_fn = partial(
            key_grad_step,
            key_rows=keys_local,
            value_rows=values_local,
            stat_total=stat_total,
            stat_delta=stat_delta,
            seq_lens=seq_lens,
            live_keys=query_ok,
            skip_empty=False,
        )
        grad_zero = jnp.zeros((SEQ_MB, seq_dev, H, HD), jnp.float32)
        grad_q = in_blocks(
            query_fn,
            grad_zero,
            (
                lax.all_gather(keys_local, "ctx", axis=1, tiled=True),
                lax.all_gather(values_local, "ctx", axis=1, tiled=True),
            ),
        )
        grad_k, grad_v = in_blocks(
            key_fn,
            (grad_zero, grad_zero),
            (
                lax.all_gather(queries, "ctx", axis=1, tiled=True),
                lax.all_gather(grad_context, "ctx", axis=1, tiled=True),
            ),
        )
        joint_grad = jnp.concatenate(
            [
                (grad_q * SCALE).reshape(row_count, D).astype(jnp.bfloat16),
                (grad_k * SCALE).reshape(row_count, D).astype(jnp.bfloat16),
                grad_v.reshape(row_count, D).astype(jnp.bfloat16),
            ],
            axis=1,
        )
        grad_joint_w = left_product(token_rows, joint_grad)
        grad_joint_b = jnp.sum(joint_grad.astype(jnp.float32), axis=0)
        input_rows = grad_first + right_product(joint_grad, joint_weight)
        grad_list.append(input_rows.reshape(SEQ_MB, seq_dev, D))
        micro_grads = (
            grad_joint_w,
            grad_joint_b,
            grad_out_w,
            grad_out_b,
            grad_gain_a,
            grad_shift_a,
            grad_inner_w,
            grad_inner_b,
            grad_outer_w,
            grad_outer_b,
            grad_gain_b,
            grad_shift_b,
        )
        if accum is None:
            accum = micro_grads
        else:
            accum = tuple((held + fresh for held, fresh in zip(accum, micro_grads)))
    (
        joint_w,
        joint_b,
        out_w,
        out_b,
        gain_a,
        shift_a,
        inner_w,
        inner_b,
        outer_w,
        outer_b,
        gain_b,
        shift_b,
    ) = accum
    grad_set = (
        joint_w[:, :D],
        joint_b[:D],
        joint_w[:, D : 2 * D],
        joint_w[:, 2 * D :],
        joint_b[2 * D :],
        out_w,
        out_b,
        gain_a,
        shift_a,
        inner_w,
        inner_b,
        outer_w,
        outer_b,
        gain_b,
        shift_b,
    )
    shard_grads = (
        lax.psum_scatter(
            grad_set[0].astype(jnp.bfloat16), "fsdp", scatter_dimension=0, tiled=True
        ).astype(jnp.float32),
        lax.psum_scatter(
            grad_set[1].astype(jnp.bfloat16), "fsdp", scatter_dimension=0, tiled=True
        ).astype(jnp.float32),
        lax.psum_scatter(
            grad_set[2].astype(jnp.bfloat16), "fsdp", scatter_dimension=0, tiled=True
        ).astype(jnp.float32),
        lax.psum_scatter(
            grad_set[3].astype(jnp.bfloat16), "fsdp", scatter_dimension=0, tiled=True
        ).astype(jnp.float32),
        lax.psum_scatter(
            grad_set[4].astype(jnp.bfloat16), "fsdp", scatter_dimension=0, tiled=True
        ).astype(jnp.float32),
        lax.psum_scatter(
            grad_set[5].astype(jnp.bfloat16), "fsdp", scatter_dimension=0, tiled=True
        ).astype(jnp.float32),
        lax.psum_scatter(
            grad_set[6].astype(jnp.bfloat16), "fsdp", scatter_dimension=0, tiled=True
        ).astype(jnp.float32),
        lax.psum_scatter(
            grad_set[7].astype(jnp.bfloat16), "fsdp", scatter_dimension=0, tiled=True
        ).astype(jnp.float32),
        lax.psum_scatter(
            grad_set[8].astype(jnp.bfloat16), "fsdp", scatter_dimension=0, tiled=True
        ).astype(jnp.float32),
        lax.psum_scatter(
            grad_set[9].astype(jnp.bfloat16), "fsdp", scatter_dimension=0, tiled=True
        ).astype(jnp.float32),
        lax.psum_scatter(
            grad_set[10].astype(jnp.bfloat16), "fsdp", scatter_dimension=0, tiled=True
        ).astype(jnp.float32),
        lax.psum_scatter(
            grad_set[11].astype(jnp.bfloat16), "fsdp", scatter_dimension=0, tiled=True
        ).astype(jnp.float32),
        lax.psum_scatter(
            grad_set[12].astype(jnp.bfloat16), "fsdp", scatter_dimension=0, tiled=True
        ).astype(jnp.float32),
        lax.psum_scatter(
            grad_set[13].astype(jnp.bfloat16), "fsdp", scatter_dimension=0, tiled=True
        ).astype(jnp.float32),
        lax.psum_scatter(
            grad_set[14].astype(jnp.bfloat16), "fsdp", scatter_dimension=0, tiled=True
        ).astype(jnp.float32),
    )
    summed = lax.psum(
        (
            shard_grads[0],
            shard_grads[1],
            shard_grads[2],
            shard_grads[3],
            shard_grads[4],
            shard_grads[5],
            shard_grads[6],
            shard_grads[7],
            shard_grads[8],
            shard_grads[9],
            shard_grads[10],
            shard_grads[11],
            shard_grads[12],
            shard_grads[13],
            shard_grads[14],
        ),
        "ctx",
    )
    outputs = jnp.concatenate(out_list, axis=0)
    input_grad = jnp.concatenate(grad_list, axis=0)
    return (outputs, input_grad) + tuple(summed)


HALF = D // 2
ROWS = 128


def flat(z, x, y, k):
    return (z * 2 + x) * 4 + y * 2 + k


def table(move):
    return [
        (flat(z, x, y, k), flat(*move(z, x, y, k)))
        for z in range(4)
        for x in range(2)
        for y in range(2)
        for k in range(2)
    ]


def permute(move):
    pairs = table(move)
    return lambda block: lax.ppermute(block, ("ctx", "fsdp"), pairs)


def permute_back(move):
    pairs = [(b, a) for a, b in table(move)]
    return lambda block: lax.ppermute(block, ("ctx", "fsdp"), pairs)


def to_seq(turn):
    return lambda z, x, y, k: (2 * k + (z // 2 + turn) % 2, x, y, z % 2)


swap_core = permute(lambda z, x, y, k: (z, x, y, k ^ 1))
swap_y = permute(lambda z, x, y, k: (z, x, y ^ 1, k))
swap_x = permute(lambda z, x, y, k: (z, x ^ 1, y, k))
swap_z1 = permute(lambda z, x, y, k: (z ^ 1, x, y, k))
swap_xz = permute(lambda z, x, y, k: (z ^ 1, x ^ 1, y, k))
swap_z2 = permute(lambda z, x, y, k: (z ^ 2, x, y, k))
seq_send = (permute(to_seq(0)), permute(to_seq(1)))
seq_return = (permute_back(to_seq(0)), permute_back(to_seq(1)))


def low(value):
    return value.astype(jnp.bfloat16)


def wide(value):
    return value.astype(jnp.float32)


def pick(array, index, axis=0):
    return lax.dynamic_index_in_dim(array, index, axis, keepdims=False)


def dot_nt(a, b):
    return lax.dot_general(a, b, (((1,), (1,)), ((), ())), preferred_element_type=jnp.float32)


def dot_tn(a, b):
    return lax.dot_general(a, b, (((0,), (0,)), ((), ())), preferred_element_type=jnp.float32)


def coords(info):
    c, f = info[0] >> 2, info[0] & 3
    return c >> 1, c & 1, f >> 1, f & 1, c, f


def pack_kernel(
    info, lens, rows, grads, w_q, w_k, w_v, w_o, w_in, v0, v1, v2, v3, v4, v5, v6, v7, wide_vec,
    t0, t1, cot, first, half, held,
):
    z, x, _, _, _, _ = coords(info)
    zh = z >> 1
    half[...] = w_in[...]
    t0[...] = rows[zh]
    t1[...] = rows[1 - zh]
    cot[:ROWS] = grads[zh]
    cot[ROWS:] = grads[1 - zh]
    columns = pl.ds(pl.multiple_of(x * HALF, 128), HALF)
    first[:192, :D] = w_o[...]
    for n, weight in enumerate((w_q, w_k, w_v)):
        first[:192, D + HALF * n : D + HALF * n + HALF] = weight[:, columns]
    held[...] = jnp.zeros_like(held)
    for n, vector in enumerate((v0, v1, v2, v3, v4, v5, v6, v7)):
        held[n : n + 1, :192] = wide(vector[...]).reshape(1, 192)
    held[8:9, :] = wide(wide_vec[...]).reshape(1, D)
    lane = lax.broadcasted_iota(jnp.int32, (1, D), 1)
    ends = jnp.zeros((1, D), jnp.int32)
    for n in range(2):
        ends = jnp.where(lane == n, lens[n] >> 7, ends)
        ends = jnp.where(lane == 2 + n, lens[n] & 127, ends)
    held[9:10, :] = wide(ends)
    first[192:, :D] = low(held[...])
    first[192:, D:] = jnp.zeros((16, 3 * HALF), jnp.bfloat16)


def attend_kernel(
    info, b0, b1, b2, b3, b4, b5, b6, b7, s0, s1, s2, s3, w0, w1, w2, w3,
    xs, ws, q_out, k_out, v_out, p_out, cu, cv, cx, key_bias, small, sems,
):
    step = pl.program_id(0)
    z, x, y, k, _, f = coords(info)

    @pl.when(step == 0)
    def _():
        copies = [
            pltpu.make_async_copy(
                piece.at[:192, D:], ws.at[pl.ds(pl.multiple_of(192 * (f ^ n), 64), 192), :], sems.at[n]
            )
            for n, piece in enumerate((w0, w1, w2, w3))
        ]
        blocks = (b0, b1, b2, b3, b4, b5, b6, b7)
        copies += [
            pltpu.make_async_copy(block, xs.at[n * ROWS : (n + 1) * ROWS, :], sems.at[4 + n])
            for n, block in enumerate(blocks)
        ]
        for copy in copies:
            copy.start()
        for n, piece in enumerate((s0, s1, s2, s3)):
            small[f ^ n] = wide(piece[...])
        line = small[2 * y + (z >> 1)][9:10, :]
        lane = lax.broadcasted_iota(jnp.int32, (1, D), 1)
        part = jnp.where(lane == (z & 1), 128.0 * line, 0.0)
        part = part + jnp.where(lane == 2 + (z & 1), line, 0.0)
        end = jnp.sum(part, axis=1, keepdims=True)
        z_low = 2 * (z & 1)
        for n, block in enumerate(blocks):
            z_block = (z_low if n % 2 == 0 else 2 - z_low) + (k if n < 4 else 1 - k)
            x_block = x if n % 4 < 2 else 1 - x
            place = (2 * z_block + x_block) * ROWS + lax.broadcasted_iota(jnp.int32, (1, ROWS), 1)
            key_bias[:, n * ROWS : (n + 1) * ROWS] = jnp.where(wide(place) < end, 0.0, NEG_FILL)
        for copy in copies:
            copy.wait()

        def bias(row):
            return jnp.concatenate(
                [small[2 * x + n][row : row + 1, :192] for n in range(2)], axis=1
            )

        q_out[...] = low(wide(low(matmul(xs[: 4 * ROWS, :], ws[:, :HALF]) + bias(0))) * SCALE)
        k_out[...] = low(matmul(xs[...], ws[:, HALF : 2 * HALF]))
        v_out[...] = low(matmul(xs[...], ws[:, 2 * HALF :]) + bias(1))

    lanes = pl.ds(pl.multiple_of(step * 128, 128), 128)
    first = lax.broadcasted_iota(jnp.int32, (1, 128), 1) < HD
    queries = q_out[:, lanes]
    keys = k_out[:, lanes]
    values = v_out[:, lanes]
    for part in range(2):
        rows = slice(part * 256, part * 256 + 256)
        found = []
        for head in range(2):
            mine = first if head == 0 else jnp.logical_not(first)
            scores = dot_nt(jnp.where(mine, queries[rows], 0), keys) + key_bias[...]
            top = jnp.max(scores, axis=1, keepdims=True)
            weights = jnp.exp(scores - top)
            total = jnp.sum(weights, axis=1, keepdims=True)
            probs = low(weights * (1.0 / total))
            p_out[head, rows, :] = probs
            found.append(matmul(probs, values))
        context = low(jnp.where(first, found[0], found[1]))
        if part == 0:
            cu[...] = context[:ROWS]
            cv[...] = context[ROWS:]
        else:
            cx[0] = context[:ROWS]
            cx[1] = context[ROWS:]


def pair_back(queries_ref, keys, values, probs_ref, grads):
    first = lax.broadcasted_iota(jnp.int32, (1, 128), 1) < HD
    grad_k = jnp.zeros((8 * ROWS, 128), jnp.float32)
    grad_v = jnp.zeros((8 * ROWS, 128), jnp.float32)
    grad_qs = []
    for part in range(2):
        rows = slice(part * 256, part * 256 + 256)
        one, two = grads[2 * part : 2 * part + 2]
        grad_rows = jnp.concatenate([one[...], two[...]], axis=0)
        queries = queries_ref[rows, :]
        grad_q = jnp.zeros((256, 128), jnp.float32)
        for head in range(2):
            mine = first if head == 0 else jnp.logical_not(first)
            grad_mine = jnp.where(mine, grad_rows, 0)
            probs = probs_ref[head, rows, :]
            grad_probs = dot_nt(grad_mine, values)
            product = wide(probs) * grad_probs
            delta = jnp.sum(product, axis=1, keepdims=True)
            grad_scores = low(product - wide(probs) * delta)
            grad_q = grad_q + matmul(grad_scores, jnp.where(mine, keys, 0))
            grad_k = grad_k + dot_tn(grad_scores, jnp.where(mine, queries, 0))
            grad_v = grad_v + dot_tn(probs, grad_mine)
        grad_qs.append(low(grad_q * SCALE))
    return grad_qs, low(grad_k), low(grad_v)


def attend_back_kernel(queries, keys, values, probs, gu, gv, gxu, gxv, dq, dk, dv):
    grad_qs, dk[...], dv[...] = pair_back(
        queries, keys[...], values[...], probs, (gu, gv, gxu, gxv)
    )
    dq[:256, :], dq[256:, :] = grad_qs


def joint_kernel(
    info, xs, dq0, dq1, dq2, dk0, dk1, dk2, dv0, dv1, dv2, keep, send, grads, dw
):
    for n, (q, k, v) in enumerate(((dq0, dk0, dv0), (dq1, dk1, dv1), (dq2, dk2, dv2))):
        start = 128 * n
        grads[: 4 * ROWS, start : start + 128] = q[...]
        grads[:, HALF + start : HALF + start + 128] = k[...]
        grads[:, 2 * HALF + start : 2 * HALF + start + 128] = v[...]
    own = slice(0, 4 * ROWS)
    dw[:, :HALF] = low(dot_tn(xs[own, :], grads[own, :HALF]))
    dw[:, HALF:] = low(dot_tn(xs[...], grads[:, HALF:]))
    col_sums = jnp.concatenate(
        [
            column_sum(wide(grads[own, :HALF])),
            jnp.zeros((1, HALF), jnp.float32),
            column_sum(wide(grads[:, 2 * HALF :])),
        ],
        axis=1,
    )
    tail = low(jnp.where(lax.broadcasted_iota(jnp.int32, (16, 1), 0) == 0, col_sums, 0.0))
    z, _, _, _, _, f = coords(info)
    for n in range(4):
        place = send if n % 2 else keep
        for half in range(2):
            start = pl.multiple_of(192 * (f ^ n) + 96 * half, 32)
            place[n // 2, half ^ (z & 1), :96, :] = dw[pl.ds(start, 96), :]
            place[n // 2, half ^ (z & 1), 96:, :] = tail if half == 0 else tail * 0


def rows_back_kernel(
    ws, dq0, dq1, dq2, dk0, dk1, dk2, dv0, dv1, dv2, dx_own, dx_other, grads
):
    for n, (q, k, v) in enumerate(((dq0, dk0, dv0), (dq1, dk1, dv1), (dq2, dk2, dv2))):
        start = 128 * n
        grads[: 4 * ROWS, start : start + 128] = q[...]
        grads[:, HALF + start : HALF + start + 128] = k[...]
        grads[:, 2 * HALF + start : 2 * HALF + start + 128] = v[...]
    dx_other[...] = low(dot_nt(grads[4 * ROWS :, HALF:], ws[:, HALF:]))
    dx_own[...] = dot_nt(grads[: 4 * ROWS, :], ws[...])


def middle_one_kernel(
    info, cm0, cm1, co0, co1, x0, x1, o0, o1, o2, o3, i0, i1, i2, i3,
    hidden_out, normed_out, inv_out, act, slope, vec,
    ctx, low_rows, small, order, inner_weight, sems,
):
    step = pl.program_id(0)
    _, x, _, _, _, f = coords(info)

    def copy(e, n):
        return pltpu.make_async_copy(
            (i0, i1, i2, i3)[n].at[:, pl.ds(pl.multiple_of(D * (f ^ e), 128), D)],
            inner_weight.at[e, pl.ds(pl.multiple_of(192 * (f ^ n), 64), 192), :],
            sems.at[e, n],
        )

    @pl.when(step == 0)
    def _():
        for e in range(4):
            for n in range(4):
                copy(e, n).start()
        for n, piece in enumerate((o0, o1, o2, o3)):
            small[f ^ n] = wide(piece[192:, :])
            order[n] = wide(piece[192:, :])
        for n in range(8):
            vec[n : n + 1, :] = jnp.concatenate(
                [small[m][n : n + 1, :192] for m in range(4)], axis=1
            )
        for side, (one, two) in enumerate(((cm0, cm1), (co0, co1))):
            rows = jnp.concatenate([one[...], two[...]], axis=0)
            for part in range(2):
                ctx[2 * (x ^ side) + part] = rows[:, 192 * part : 192 * part + 192]
        total = wide(jnp.concatenate([x0[...], x1[...]], axis=0)) + vec[2:3, :]
        for n, piece in enumerate((o0, o1, o2, o3)):
            total = total + matmul(ctx[f ^ n], piece[:192, :])
        hidden, normed, inv = layer_norm(total, vec[3:4, :], vec[4:5, :])
        hidden_out[...] = hidden
        normed_out[...] = normed
        inv_out[...] = inv
        low_rows[...] = low(hidden)

    for n in range(4):
        copy(step, n).wait()
    pre = matmul(low_rows[...], inner_weight[step]) + order[step][8:9, :]
    bell = 0.5 * (1.0 + lax.erf(pre * ROOT_HALF))
    act[0] = low(pre * bell)
    slope[0] = low(bell + pre * INV_ROOT_TAU * jnp.exp(-0.5 * pre * pre))


def norm_grad(grad, normed, inv, gain):
    scaled = grad * gain
    return inv * (
        scaled
        - jnp.mean(scaled, axis=-1, keepdims=True)
        - normed * jnp.mean(scaled * normed, axis=-1, keepdims=True)
    )


def column_sum(value):
    return jnp.sum(value, axis=0, keepdims=True)


def outer_copies(refs, held, sems):
    copies = [
        pltpu.make_async_copy(ref, held.at[n], sems.at[n]) for n, ref in enumerate(refs)
    ]
    for copy in copies:
        copy.start()
    return copies


def middle_two_kernel(
    info, lens, act, act_block, hidden, cot, vec, w0, w1, w2, w3,
    out, second_out, outer_out, sums, keep, send, w_all, w_sem,
):
    step = pl.program_id(0)
    z, x, _, _, c, f = coords(info)

    @pl.when(step == 0)
    def _():
        copies = outer_copies((w0, w1, w2, w3), w_all, w_sem)
        b_2, g_2, s_2 = vec[5:6, :], vec[6:7, :], vec[7:8, :]
        total = hidden[...] + b_2
        for n in range(4):
            copies[n].wait()
            total = total + matmul(act[n], w_all[n])
        result, normed, inv = layer_norm(total, g_2, s_2)
        zh = z >> 1
        out[zh] = low(result[:ROWS])
        out[1 - zh] = low(result[ROWS:])
        row = lax.broadcasted_iota(jnp.int32, (2 * ROWS, 1), 0)
        end = jnp.where(row < ROWS, lens[zh], lens[1 - zh] + ROWS)
        grad = wide(cot[...]) * jnp.where(row + c * ROWS < end, 1.0, 0.0)
        grad_second = norm_grad(grad, normed, inv, g_2)
        second_out[...] = grad_second
        grad_outer = low(grad_second)
        outer_out[...] = grad_outer
        sums[...] = jnp.zeros_like(sums)
        for n, value in enumerate((wide(grad_outer), grad * normed, grad)):
            sums[n : n + 1, :] = column_sum(value)

    @pl.when(step > 0)
    def _():
        grad = low(dot_tn(act_block[0], outer_out[...]))
        for place, wanted in ((send, step < 3), (keep, step >= 3)):

            @pl.when(wanted)
            def _(place=place):
                for n in range(4):
                    place[0, n ^ (2 * x + (z & 1))] = grad[192 * n : 192 * n + 192]


def inner_back_kernel(
    info, outer, slope, w0, w1, w2, w3, inner_out, sums, w_all, sems
):
    f = info[0] & 3
    copies = outer_copies((w0, w1, w2, w3), w_all, sems)
    for e in range(4):
        copies[e].wait()
        inner = low(dot_nt(outer[...], w_all[e]) * wide(slope[e]))
        inner_out[e] = inner
        sums[pl.ds(f ^ e, 1), :] = column_sum(wide(inner))


def middle_three_kernel(
    info, second, inner, normed_one, inv_one, vec, o0, o1, o2, o3, i0, i1, i2, i3,
    first_out, g0, g1, branch_out, sums, o_all, i_all, gc, o_sem, i_sem,
):
    _, x, _, _, _, f = coords(info)
    copies = {}
    for e in range(4):
        columns = pl.ds(pl.multiple_of(D * (f ^ e), 128), D)
        for n, ref in enumerate((i0, i1, i2, i3)):
            rows = pl.ds(pl.multiple_of(192 * (f ^ n), 64), 192)
            copies["i", e, n] = pltpu.make_async_copy(
                ref.at[:, columns], i_all.at[e, rows, :], i_sem.at[e, n]
            )
            copies["i", e, n].start()
    for n, ref in enumerate((o0, o1, o2, o3)):
        copies["o", n] = pltpu.make_async_copy(ref.at[:192, :D], o_all.at[n], o_sem.at[n])
        copies["o", n].start()
    grad_hidden = second[...]
    for e in range(4):
        for n in range(4):
            copies["i", e, n].wait()
        grad_hidden = grad_hidden + dot_nt(inner[e], i_all[e])
    grad_first = norm_grad(grad_hidden, normed_one[...], inv_one[...], vec[3:4, :])
    first_out[...] = grad_first
    branch = low(grad_first)
    branch_out[...] = branch
    for n, value in enumerate((wide(branch), grad_hidden * normed_one[...], grad_hidden)):
        sums[n : n + 1, :] = column_sum(value)
    for n in range(4):
        copies["o", n].wait()
        gc[f ^ n] = low(dot_nt(branch, o_all[n]))
    for side in range(2):
        rows = jnp.concatenate([gc[2 * (x ^ side)], gc[2 * (x ^ side) + 1]], axis=1)
        g0[1 - side] = rows[:ROWS]
        g1[1 - side] = rows[ROWS:]


def middle_four_kernel(
    info, inner, hidden, branch, cm0, cm1, co0, co1, sums_two, sums_in, sums_one,
    keep, send, held, out_held, vec_held,
):
    step = pl.program_id(0)
    _, x, _, _, _, f = coords(info)
    block = f ^ step

    @pl.when(step == 0)
    def _():
        for side, (one, two) in enumerate(((cm0, cm1), (co0, co1))):
            rows = jnp.concatenate([one[...], two[...]], axis=0)
            start = pl.multiple_of(HALF * (x ^ side), 128)
            out_held[pl.ds(start, HALF), :] = low(dot_tn(rows, branch[...]))
        vec_held[...] = jnp.zeros_like(vec_held)
        top = lax.broadcasted_iota(jnp.int32, (16, 1), 0) == 0
        for n in range(4):
            cut = slice(192 * n, 192 * n + 192)
            lines = (
                sums_in[n : n + 1, :],
                jnp.concatenate(
                    [sums_one[m : m + 1, cut] for m in range(3)] + [sums_two[0:1, cut]], axis=1
                ),
                jnp.concatenate(
                    [sums_two[1:2, cut], sums_two[2:3, cut], jnp.zeros((1, HALF), jnp.float32)],
                    axis=1,
                ),
            )
            for m, line in enumerate(lines):
                vec_held[m, n] = low(jnp.where(top, line, 0.0))

    held[...] = low(dot_tn(low(hidden[...]), inner[0]))
    for n in range(4):
        place = send if n % 2 else keep
        start = 192 * (f ^ n)
        place[n // 2, 0, :192, :] = held[pl.ds(pl.multiple_of(start, 64), 192), :]
        place[n // 2, 0, 192:240, :] = out_held[pl.ds(pl.multiple_of(start + 48 * block, 16), 48), :]
        place[n // 2, 0, 240:, :] = vec_held[block, f ^ n]


MIDDLE = 2 * ROWS
BF, FP = jnp.bfloat16, jnp.float32


def whole(shape):
    return pl.BlockSpec(tuple(shape), lambda *_: (0,) * len(shape))


def lane_block(rows, start=0):
    return pl.BlockSpec((rows, 128), lambda step, *_: (0, step + start))


def call(kernel, name, grid, scalars, operands, outs, scratch=(), work=(1, 1), limit=30):
    return pl.pallas_call(
        kernel,
        out_shape=[jax.ShapeDtypeStruct(shape, kind) for shape, kind, _ in outs],
        grid_spec=pltpu.PrefetchScalarGridSpec(
            num_scalar_prefetch=len(scalars),
            grid=(grid,),
            in_specs=[spec or whole(array.shape) for array, spec in operands],
            out_specs=[spec or whole(shape) for shape, _, spec in outs],
            scratch_shapes=list(scratch),
        ),
        compiler_params=pltpu.CompilerParams(
            dimension_semantics=("arbitrary",), vmem_limit_bytes=limit * 1024 * 1024
        ),
        cost_estimate=pl.CostEstimate(
            flops=1000, bytes_accessed=1000, transcendentals=0
        ),
        name=name,
    )(*scalars, *[array for array, _ in operands])


def plain(arrays):
    return [(array, None) for array in arrays]


def anywhere(arrays):
    return [(array, pl.BlockSpec(memory_space=pl.ANY)) for array in arrays]


def probs_block(start=0):
    return pl.BlockSpec((2, 4 * ROWS, 8 * ROWS), lambda step, *_: (step + start, 0, 0))


def pack(info, lens, inputs, cotangent, weights, vectors):
    return call(
        pack_kernel, "pack", 1, (info, lens),
        plain([inputs, cotangent, *weights[:4]])
        + [(weights[4], pl.BlockSpec((192, 2 * D), lambda _, info, lens: (0, (info[0] >> 2) & 1)))]
        + plain(vectors),
        [
            ((ROWS, D), BF, None), ((ROWS, D), BF, None), ((MIDDLE, D), BF, None),
            ((208, D + 3 * HALF), BF, None), ((192, 2 * D), BF, None),
        ],
        [pltpu.VMEM((16, D), FP)], limit=56,
    )


def first_columns(pieces):
    return [(piece, pl.BlockSpec((208, D), lambda *_: (0, 0))) for piece in pieces]


def attend(info, blocks, pieces):
    return call(
        attend_kernel, "attend", 3, (info,),
        anywhere(blocks)
        + [(piece, pl.BlockSpec((16, D), lambda *_: (12, 0))) for piece in pieces]
        + anywhere(pieces),
        [
            ((8 * ROWS, D), BF, None), ((D, 3 * HALF), BF, None), ((4 * ROWS, HALF), BF, None),
            ((8 * ROWS, HALF), BF, None), ((8 * ROWS, HALF), BF, None),
            ((6, 4 * ROWS, 8 * ROWS), BF, probs_block()),
        ]
        + [((ROWS, HALF), BF, lane_block(ROWS))] * 2
        + [((2, ROWS, HALF), BF, pl.BlockSpec((2, ROWS, 128), lambda step, *_: (0, 0, step)))],
        [
            pltpu.VMEM((1, 8 * ROWS), FP), pltpu.VMEM((4, 16, D), FP),
            pltpu.SemaphoreType.DMA((12,)),
        ],
        limit=56,
    )


def attend_back(queries, keys, values, probs, grads, start, pairs):
    return call(
        attend_back_kernel, "attend_back", pairs, (),
        [
            (queries, lane_block(4 * ROWS, start)), (keys, lane_block(8 * ROWS, start)),
            (values, lane_block(8 * ROWS, start)), (probs, probs_block(start)),
        ]
        + [(grad, pl.BlockSpec((None, ROWS, 128), lambda s, n=n: (n, 0, s + start))) for grad, n in grads],
        [
            ((4 * ROWS, 128 * pairs), BF, lane_block(4 * ROWS)),
            ((8 * ROWS, 128 * pairs), BF, lane_block(8 * ROWS)),
            ((8 * ROWS, 128 * pairs), BF, lane_block(8 * ROWS)),
        ],
        (), (4 * pairs, 5 * pairs),
    )


def by_name(pairs):
    return [part for name in zip(*pairs) for part in name]


def joint_grads(info, xs, pairs):
    joint = (2, 2, 112, 3 * HALF)
    return call(
        joint_kernel, "joint_grads", 1, (info,), plain([xs, *by_name(pairs)]),
        [(joint, BF, None), (joint, BF, None)],
        [pltpu.VMEM((8 * ROWS, 3 * HALF), BF), pltpu.VMEM((D, 3 * HALF), BF)],
    )


def rows_back(ws, pairs):
    return call(
        rows_back_kernel, "rows_back", 1, (), plain([ws, *by_name(pairs)]),
        [((4 * ROWS, D), FP, None), ((4 * ROWS, D), BF, None)],
        [pltpu.VMEM((8 * ROWS, 3 * HALF), BF)],
    )


def middle_one(info, ctx, rows, out_p, inner_p):
    block = pl.BlockSpec((1, MIDDLE, D), lambda step, *_: (step, 0, 0))
    return call(
        middle_one_kernel, "middle_one", 4, (info,),
        plain([*ctx, *rows]) + first_columns(out_p) + anywhere(inner_p),
        [
            ((MIDDLE, D), FP, None), ((MIDDLE, D), FP, None), ((MIDDLE, 1), FP, None),
            ((4, MIDDLE, D), BF, block), ((4, MIDDLE, D), BF, block), ((8, D), FP, None),
        ],
        [
            pltpu.VMEM((4, MIDDLE, 192), BF), pltpu.VMEM((MIDDLE, D), BF),
            pltpu.VMEM((4, 16, D), FP), pltpu.VMEM((4, 16, D), FP), pltpu.VMEM((4, D, D), BF),
            pltpu.SemaphoreType.DMA((4, 4)),
        ],
        (4, 10),
    )


def middle_two(info, lens, act, hidden, cot, vec, outer_p):
    def turn(step, *_):
        at = jnp.maximum(step - 1, 0)
        return (jnp.where(at < 2, 2 * at + 1, 2 * at - 4), 0, 0)

    blocks = (2, 4, 192, D)
    return call(
        middle_two_kernel, "middle_two", 5, (info, lens),
        [(act, None), (act, pl.BlockSpec((1, MIDDLE, D), turn))]
        + plain([hidden, cot, vec])
        + anywhere(outer_p),
        [
            ((2, ROWS, D), BF, None), ((MIDDLE, D), FP, None), ((MIDDLE, D), BF, None),
            ((8, D), FP, None),
            (blocks, BF, pl.BlockSpec((1, 4, 192, D), lambda s, *_: (jnp.maximum(s - 3, 0), 0, 0, 0))),
            (blocks, BF, pl.BlockSpec((1, 4, 192, D), lambda s, *_: (jnp.where(s < 2, 0, 1), 0, 0, 0))),
        ],
        [pltpu.VMEM((4, D, D), BF), pltpu.SemaphoreType.DMA((4,))], (4, 10),
    )


def inner_back(info, outer, slope, outer_p):
    return call(
        inner_back_kernel, "inner_back", 1, (info,), plain([outer, slope]) + anywhere(outer_p),
        [((4, MIDDLE, D), BF, None), ((4, D), FP, None)],
        [pltpu.VMEM((4, D, D), BF), pltpu.SemaphoreType.DMA((4,))], (2, 7),
    )


def middle_three(info, second, inner, normed, inv, vec, out_p, inner_p):
    return call(
        middle_three_kernel, "middle_three", 1, (info,),
        plain([second, inner, normed, inv, vec]) + anywhere([*out_p, *inner_p]),
        [((MIDDLE, D), FP, None)]
        + [((2, ROWS, HALF), BF, None)] * 2
        + [((MIDDLE, D), BF, None), ((8, D), FP, None)],
        [
            pltpu.VMEM((4, 192, D), BF), pltpu.VMEM((4, D, D), BF),
            pltpu.VMEM((4, MIDDLE, 192), BF), pltpu.SemaphoreType.DMA((4,)),
            pltpu.SemaphoreType.DMA((4, 4)),
        ],
        (2, 7),
    )


def middle_four(info, inner, hidden, branch, ctx, sums):
    def spot(step, info):
        z, x, _, _, _, f = coords(info)
        return (0, f ^ step ^ (2 * (z & 1) + x), 0, 0)

    block = pl.BlockSpec((2, 1, 256, D), spot)
    return call(
        middle_four_kernel, "middle_four", 4, (info,),
        [(inner, pl.BlockSpec((1, MIDDLE, D), lambda step, *_: (step, 0, 0)))]
        + plain([hidden, branch, *ctx, *sums]),
        [((2, 4, 256, D), BF, block)] * 2,
        [pltpu.VMEM((D, D), BF), pltpu.VMEM((D, D), BF), pltpu.VMEM((4, 4, 16, D), BF)],
        (4, 8),
    )


def place_outer_kernel(info, p0, p1, p2, p3, out):
    z, x, _, _, _, _ = coords(info)
    for n, piece in enumerate((p0, p1, p2, p3)):
        out[pl.ds(pl.multiple_of(192 * (n ^ (2 * x + (z & 1))), 64), 192), :] = wide(piece[...])


def place_inner_kernel(
    info, p0, p1, p2, p3, inner, out, b_in, b_out, g_one, s_one, b_two, g_two, s_two, held
):
    z, x, _, _, _, _ = coords(info)
    for n, piece in enumerate((p0, p1, p2, p3)):
        at = n ^ (2 * (z & 1) + x)
        inner[:, pl.ds(pl.multiple_of(D * at, 128), D)] = wide(piece[:192, :])
        out[pl.ds(pl.multiple_of(48 * at, 16), 48), :] = wide(piece[192:240, :])
        held[at] = wide(piece[240:, :])
    b_in[...] = held[0][0:1, :].reshape(D)
    for n, vector in enumerate((b_out, g_one, s_one, b_two, g_two, s_two)):
        cut = 192 * (n % 4)
        vector[...] = held[1 + n // 4][0:1, cut : cut + 192].reshape(192)


def place_joint_kernel(info, p0, p1, p2, p3, query, key, value, b_query, b_value, held):
    z, x, _, _, _, f = coords(info)
    z_bit = z & 1
    for n, piece in enumerate((p0, p1, p2, p3)):
        rows = pl.ds(pl.multiple_of(96 * (n % 2 ^ z_bit), 32), 96)
        columns = pl.ds(pl.multiple_of(HALF * (n // 2 ^ x), 128), HALF)
        for m, out in enumerate((query, key, value)):
            out[rows, columns] = wide(piece[:96, HALF * m : HALF * m + HALF])
        line = wide(piece[96:, :])
        line = jnp.where(f & 1 == 0, line, jnp.concatenate([line[:, 192:], line[:, :192]], axis=1))
        held[n // 2 ^ x, n % 2 ^ z_bit] = line
    mine = held[f >> 1, 0][0:1, :]
    b_query[...] = mine[:, :192].reshape(192)
    b_value[...] = mine[:, 2 * HALF : 2 * HALF + 192].reshape(192)


def placed(kernel, name, info, pieces, shapes, held=()):
    return call(
        kernel, name, 1, (info,), plain(pieces), [(shape, FP, None) for shape in shapes],
        [pltpu.VMEM(shape, FP) for shape in held], (1, 6),
    )


def unshuffle(array, bit):
    return jnp.where(bit == 0, array, array[::-1])


def tied(values, *events):
    return lax.optimization_barrier((values, events))[0]


ROW_A, ROW_B = 96, 144


def fast_body(
    inputs, cotangent, lengths, w_query, b_query, w_key, w_value, b_value, w_output, b_output,
    gain_one, bias_one, w_inner, b_inner, w_outer, b_outer, gain_two, bias_two,
):
    info = lax.axis_index(("ctx", "fsdp")).astype(jnp.int32).reshape(1)
    zh, x = lax.axis_index("ctx") // 4, lax.axis_index("ctx") % 2

    t0, t1, cot, first, half = pack(
        info, lengths, inputs, cotangent, (w_query, w_key, w_value, w_output, w_inner),
        (b_query, b_value, b_output, gain_one, bias_one, b_outer, gain_two, bias_two, b_inner),
    )

    bu, bv = seq_send[0](t0), seq_send[1](t1)
    first_y, first_k = swap_y(first), swap_core(first)
    half_y = swap_y(half)
    bu, bv, first_k = tied((bu, bv, first_k))
    bxu, bxv, bku = swap_x(bu), swap_x(bv), swap_core(bu)
    bxu, bxv, bku, first_y, half_y = tied((bxu, bxv, bku, first_y, half_y))
    bkv, *rest = [swap_core(b) for b in (bv, bxu, bxv, first_y)]
    bkv, *rest = tied([bkv] + rest)
    blocks = [bu, bv, bxu, bxv, bku, bkv, *rest[:2]]
    first_p = [first, first_k, first_y, rest[2]]
    outer_y = swap_y(tied(w_outer, half_y))
    half_x = swap_x(tied(half_y, bkv))
    xs, ws, queries, keys, values, probs, cu, cv, cx = attend(info, blocks, first_p)

    cu, cv, cx, half_x = tied((cu, cv, cx, half_x))
    cu, cv = seq_return[0](cu), seq_return[1](cv)
    cx = swap_x(cx)
    inner_y = jnp.where(
        x == 0, jnp.concatenate([half_y, half_x], 1), jnp.concatenate([half_x, half_y], 1)
    )
    cu, cv, cx, outer_y, inner_y = tied((cu, cv, cx, outer_y, inner_y))
    cxu, cxv = seq_return[0](cx[0]), seq_return[1](cx[1])
    inner_k, inner_ky = swap_core(tied(w_inner, cx)), swap_core(inner_y)
    cxu, cxv, inner_k, inner_ky = tied((cxu, cxv, inner_k, inner_ky))
    outer_k, outer_ky = swap_core(tied(w_outer, cxu)), swap_core(tied(outer_y, cxu))
    ctx = [cu, cv, cxu, cxv]
    inner_p = [w_inner, inner_k, inner_y, inner_ky]
    hidden, normed, inv, act, slope, vec = middle_one(info, ctx, [t0, t1], first_p, inner_p)
    act, outer_k, outer_ky = tied((act, outer_k, outer_ky))
    outer_p = [w_outer, outer_k, outer_y, outer_ky]
    outputs, second_grad, outer, sums_two, o_keep, o_send = middle_two(
        info, lengths, act, hidden, cot, vec, outer_p
    )
    o_came = swap_core(o_send)
    inner, sums_in = inner_back(info, outer, slope, outer_p)
    o_came, inner = tied((o_came, inner))
    o_y = low(wide(o_keep[1, :2]) + wide(o_came[1, :2]))
    o_z = low(wide(o_keep[:, 3]) + wide(o_came[:, 3]))
    inner, o_y, o_z = tied((inner, o_y, o_z))
    o_y, o_z = swap_y(o_y), swap_z1(o_z)
    grad_first, g0, g1, branch, sums_one = middle_three(
        info, second_grad, inner, normed, inv, vec, first_p, inner_p
    )
    g0, g1 = seq_send[0](g0), seq_send[1](g1)
    i_keep, i_send = middle_four(
        info, inner, hidden, branch, ctx, (sums_two, sums_in, sums_one)
    )
    g0, g1, i_send, o_y, o_z = tied((g0, g1, i_send, o_y, o_z))
    go = jnp.stack([g0[0], g1[0]])
    go, o_y, o_z, i_send = tied((go, o_y, o_z, i_send))
    go = swap_x(go)
    i_came = swap_core(i_send)
    o_z2 = swap_z1(low(wide(o_keep[0, 1]) + wide(o_came[0, 1]) + wide(o_y[1])))
    o_y2 = swap_y(low(wide(o_keep[1, 2]) + wide(o_came[1, 2]) + wide(o_z[1])))
    go, i_came, o_z2, o_y2 = tied((go, i_came, o_z2, o_y2))
    o_one = wide(o_keep[0, 0]) + wide(o_came[0, 0]) + wide(o_y[0]) + wide(o_z2)
    o_two = low(wide(o_keep[0, 2]) + wide(o_came[0, 2]) + wide(o_z[0]) + wide(o_y2))
    i_keep, i_came = (a.reshape(2, 2, 2, 256, D) for a in (i_keep, i_came))

    def summed(*spot):
        return wide(i_keep[spot]) + wide(i_came[spot])

    every, one_a, one_b, one_c = slice(None), slice(0, ROW_A), slice(ROW_A, ROW_B), slice(ROW_B, 256)
    i_y, i_x = low(summed(1, every, every, one_a)), low(summed(every, every, 1, one_b))
    i_z = low(summed(every, 1, every, one_c))
    go, i_y, i_x, i_z, o_two = tied((go, i_y, i_x, i_z, o_two))
    i_y, i_x, i_z = swap_y(i_y), swap_x(i_x), swap_z1(i_z)
    o_came = swap_x(o_two)
    grads = [(g0, 1), (g1, 1), (go, 0), (go, 1)]
    pair_0 = attend_back(queries, keys, values, probs, grads, 0, 1)
    pair_1 = attend_back(tied(queries, pair_0), keys, values, probs, grads, 1, 1)
    pair_2 = attend_back(tied(queries, pair_1), keys, values, probs, grads, 2, 1)
    pairs = (pair_0, pair_1, pair_2)
    dx_own, dx_other = rows_back(ws, pairs)
    dx_own, dx_other, i_y, i_x, i_z, o_came = tied((dx_own, dx_other, i_y, i_x, i_z, o_came))
    part_a = summed(0, every, every, one_a) + wide(i_y)
    part_b = summed(every, every, 0, one_b) + wide(i_x)
    part_c = summed(every, 0, every, one_c) + wide(i_z)
    i_z2, i_y2, i_x2 = swap_z1(low(part_a[1])), swap_y(low(part_b[1])), swap_x(low(part_c[:, 1]))
    o_sum = low(o_one + wide(o_came))
    dx_came = swap_core(dx_other)
    o_came = swap_z2(o_sum)
    j_keep, j_send = joint_grads(info, tied(xs, dx_other), pairs)
    j_keep, j_send, i_x2, i_y2, i_z2, dx_came = tied((j_keep, j_send, i_x2, i_y2, i_z2, dx_came))
    j_came = swap_core(j_send)
    part_a, part_b, part_c = part_a[0] + wide(i_z2), part_b[0] + wide(i_y2), part_c[:, 0] + wide(i_x2)
    i_x3, i_z3, i_y3 = swap_x(low(part_a[1])), swap_z1(low(part_b[1])), swap_y(low(part_c[1]))
    j_came, i_x3, i_z3, i_y3, o_came = tied((j_came, i_x3, i_z3, i_y3, o_came))
    o_sum = low(wide(o_sum) + wide(o_came))
    i_sum = [part_a[0] + wide(i_x3), part_b[0] + wide(i_z3), part_c[0] + wide(i_y3)]
    i_sum = low(jnp.concatenate(i_sum, axis=0))
    dx = dx_own[: 2 * ROWS] + wide(dx_came[: 2 * ROWS])
    dx_send = low(dx_own[2 * ROWS :] + wide(dx_came[2 * ROWS :]))
    j_y = swap_y(low(wide(j_keep[1, :, :56]) + wide(j_came[1, :, :56])))
    j_z = swap_z1(low(wide(j_keep[:, 1, 56:]) + wide(j_came[:, 1, 56:])))
    j_one = wide(j_keep[0, :, :56]) + wide(j_came[0, :, :56])
    j_two = wide(j_keep[:, 0, 56:]) + wide(j_came[:, 0, 56:])
    i_came = swap_z2(i_sum)
    dx_came = swap_x(dx_send)
    j_y, j_z, dx_came = tied((j_y, j_z, dx_came))
    j_one, j_two = j_one + wide(j_y), j_two + wide(j_z)
    dx = low(dx + wide(dx_came))
    j_z, j_y = swap_z1(low(j_one[1])), swap_y(low(j_two[1]))
    o_x, o_z = swap_x(o_sum), swap_z1(o_sum)
    j_z, j_y, o_x, o_z, i_came = tied((j_z, j_y, o_x, o_z, i_came))
    j_sum = low(jnp.concatenate([j_one[0] + wide(j_z), j_two[0] + wide(j_y)], axis=0))
    i_sum = low(wide(i_sum) + wide(i_came))
    j_came = swap_z2(j_sum)
    i_z, i_x, o_zx = swap_z1(i_sum), swap_x(i_sum), swap_x(tied(o_z, i_sum))
    j_came, i_z, i_x, o_zx = tied((j_came, i_z, i_x, o_zx))
    j_sum = low(wide(j_sum) + wide(j_came))
    j_x, j_z = swap_x(j_sum), swap_z1(j_sum)
    i_zx = swap_x(i_z)
    dx0, dx1 = seq_return[0](tied(dx[:ROWS], i_z)), seq_return[1](tied(dx[ROWS:], i_z))
    (outer_grad,) = placed(place_outer_kernel, "place_outer", info, tied([o_sum, o_z, o_x, o_zx], j_sum), [(D, D)])
    j_x, j_z, i_zx, dx0, dx1, outer_grad = tied((j_x, j_z, i_zx, dx0, dx1, outer_grad))
    j_zx = swap_x(j_z)
    input_grad = grad_first + wide(jnp.concatenate([dx0, dx1], axis=0))
    input_grad = unshuffle(input_grad.reshape(2, ROWS, D), zh)
    inner_grad, out_grad, grad_b1, grad_bo, grad_g1, grad_s1, grad_b2, grad_g2, grad_s2 = placed(
        place_inner_kernel, "place_inner", info, [i_sum, i_x, i_z, i_zx],
        [(192, 4 * D), (192, D), (D,)] + [(192,)] * 6, [(4, 16, D)],
    )
    q_grad, k_grad, v_grad, grad_bq, grad_bv = placed(
        place_joint_kernel, "place_joint", info, [j_sum, j_z, j_x, j_zx],
        [(192, D)] * 3 + [(192,)] * 2, [(2, 2, 16, 3 * HALF)],
    )
    return (
        outputs, input_grad, q_grad, grad_bq, k_grad, v_grad, grad_bv, out_grad, grad_bo,
        grad_g1, grad_s1, inner_grad, grad_b1, outer_grad, grad_b2, grad_g2, grad_s2,
    )


def solution(mesh):
    placed = (
        P("fsdp", "ctx", None),
        P("fsdp", "ctx", None),
        P("fsdp"),
        P("fsdp", None),
        P("fsdp"),
        P("fsdp", None),
        P("fsdp", None),
        P("fsdp"),
        P("fsdp", None),
        P("fsdp"),
        P("fsdp"),
        P("fsdp"),
        P("fsdp", None),
        P("fsdp"),
        P("fsdp", None),
        P("fsdp"),
        P("fsdp"),
        P("fsdp"),
    )
    fast = dict(mesh.shape) == {"ctx": 8, "fsdp": 4}
    return jax.shard_map(
        fast_body if fast else body,
        mesh=mesh,
        in_specs=placed,
        out_specs=(
            P("fsdp", "ctx", None),
            P("fsdp", "ctx", None),
            P("fsdp", None),
            P("fsdp"),
            P("fsdp", None),
            P("fsdp", None),
            P("fsdp"),
            P("fsdp", None),
            P("fsdp"),
            P("fsdp"),
            P("fsdp"),
            P("fsdp", None),
            P("fsdp"),
            P("fsdp", None),
            P("fsdp"),
            P("fsdp"),
            P("fsdp"),
        ),
        check_vma=False,
    )
```

```python
from functools import partial

import jax
import jax.numpy as jnp
from jax import lax
from jax.experimental import pallas as pl
from jax.experimental.pallas import tpu as pltpu
from jax.sharding import PartitionSpec as P

D = 768
H = 12
HD = 64
SEQ_MB = 1
MICRO = 2


EPSILON = 1e-05
NEG_FILL = -1e30
SCALE = 0.125
ROOT_HALF = 0.7071067811865476
INV_ROOT_TAU = 0.3989422804014327
key_block = 512


def matmul(left_side, right_side):
    return jnp.dot(left_side, right_side, preferred_element_type=jnp.float32)


def left_product(left_side, right_side):
    return lax.dot_general(
        left_side, right_side, (((0,), (0,)), ((), ())), preferred_element_type=jnp.float32
    )


def right_product(left_side, right_side):
    return lax.dot_general(
        left_side, right_side, (((1,), (1,)), ((), ())), preferred_element_type=jnp.float32
    )


def split_heads(token_rows):
    return token_rows.reshape(token_rows.shape[0], token_rows.shape[1], H, HD)


def head_scores(query_rows, key_rows):
    return (
        jnp.einsum(
            "bqhd,bkhd->bhqk",
            split_heads(query_rows),
            split_heads(key_rows),
            preferred_element_type=jnp.float32,
        )
        * SCALE
    )


def live_mask(seq_lens, first_pos, num_rows):
    return (first_pos + lax.iota(jnp.int32, num_rows))[None, :] < seq_lens[:, None]


def layer_norm(resid, norm_gain, norm_bias):
    row_mean = jnp.mean(resid, axis=-1, keepdims=True)
    centered = resid - row_mean
    inv_std = lax.rsqrt(jnp.mean(centered * centered, axis=-1, keepdims=True) + EPSILON)
    normed = centered * inv_std
    return (normed * norm_gain + norm_bias, normed, inv_std)


def norm_back(grad_out, normed, inv_std, norm_gain):
    grad_norm = grad_out * norm_gain
    grad_in = inv_std * (
        grad_norm
        - jnp.mean(grad_norm, axis=-1, keepdims=True)
        - normed * jnp.mean(grad_norm * normed, axis=-1, keepdims=True)
    )
    return (grad_in, jnp.sum(grad_out * normed, axis=0), jnp.sum(grad_out, axis=0))


def gelu_exact(pre_act):
    return 0.5 * pre_act * (1.0 + lax.erf(pre_act * ROOT_HALF))


def gelu_slope(pre_act):
    return 0.5 * (1.0 + lax.erf(pre_act * ROOT_HALF)) + pre_act * INV_ROOT_TAU * jnp.exp(
        -0.5 * pre_act * pre_act
    )


def in_blocks(step_fn, running, pieces):
    num_rows = pieces[0].shape[1]

    def advance(block_index, current):
        offset = block_index * key_block
        sliced = tuple(
            (lax.dynamic_slice_in_dim(member, offset, key_block, 1) for member in pieces)
        )
        return step_fn(current, sliced, offset)

    return lax.fori_loop(0, num_rows // key_block, advance, running)


def attend_step(running, sliced, first_pos, queries, seq_lens, skip_empty):
    key_rows, value_rows = sliced
    live_keys = live_mask(seq_lens, first_pos, key_rows.shape[1])
    run_max, run_sum, run_out = running
    key_mask = live_keys[:, None, None, :]
    scores = jnp.where(key_mask, head_scores(queries, key_rows), NEG_FILL)
    new_max = jnp.maximum(run_max, jnp.max(scores, axis=-1))
    weights = jnp.where(key_mask, jnp.exp(scores - new_max[..., None]), 0.0)
    rescale = jnp.exp(run_max - new_max)
    new_sum = run_sum * rescale + jnp.sum(weights, axis=-1)
    new_out = run_out * rescale[..., None] + jnp.einsum(
        "bhqk,bkhd->bhqd",
        weights.astype(jnp.bfloat16),
        split_heads(value_rows),
        preferred_element_type=jnp.float32,
    )
    return (new_max, new_sum, new_out)


def query_grad_step(
    running,
    sliced,
    first_pos,
    queries,
    grad_context,
    log_total,
    row_delta,
    seq_lens,
    live_queries,
    skip_empty,
):
    key_rows, value_rows = sliced
    live_keys = live_mask(seq_lens, first_pos, key_rows.shape[1])
    key_mask = live_keys[:, None, None, :]
    probabilities = jnp.where(
        key_mask, jnp.exp(head_scores(queries, key_rows) - log_total[..., None]), 0.0
    )
    grad_probs = jnp.einsum(
        "bqhd,bkhd->bhqk",
        split_heads(grad_context),
        split_heads(value_rows),
        preferred_element_type=jnp.float32,
    )
    grad_scores = (probabilities * (grad_probs - row_delta[..., None])).astype(jnp.bfloat16)
    return running + jnp.einsum(
        "bhqk,bkhd->bqhd", grad_scores, split_heads(key_rows), preferred_element_type=jnp.float32
    )


def key_grad_step(
    running,
    sliced,
    first_pos,
    key_rows,
    value_rows,
    stat_total,
    stat_delta,
    seq_lens,
    live_keys,
    skip_empty,
):
    query_rows, grad_rows = sliced
    num_rows = query_rows.shape[1]
    grad_k, grad_v = running
    log_total = lax.dynamic_slice_in_dim(stat_total, first_pos, num_rows, 1).transpose(0, 2, 1)
    row_delta = lax.dynamic_slice_in_dim(stat_delta, first_pos, num_rows, 1).transpose(0, 2, 1)
    key_mask = live_keys[:, None, None, :]
    probabilities = jnp.where(
        key_mask, jnp.exp(head_scores(query_rows, key_rows) - log_total[..., None]), 0.0
    )
    grad_probs = jnp.einsum(
        "bqhd,bkhd->bhqk",
        split_heads(grad_rows),
        split_heads(value_rows),
        preferred_element_type=jnp.float32,
    )
    grad_scores = (probabilities * (grad_probs - row_delta[..., None])).astype(jnp.bfloat16)
    grad_v = grad_v + jnp.einsum(
        "bhqk,bqhd->bkhd",
        probabilities.astype(jnp.bfloat16),
        split_heads(grad_rows),
        preferred_element_type=jnp.float32,
    )
    grad_k = grad_k + jnp.einsum(
        "bhqk,bqhd->bkhd", grad_scores, split_heads(query_rows), preferred_element_type=jnp.float32
    )
    return (grad_k, grad_v)


def body(
    inputs,
    cotangent,
    lengths,
    w_query,
    b_query,
    w_key,
    w_value,
    b_value,
    w_output,
    b_output,
    gain_one,
    bias_one,
    w_inner,
    b_inner,
    w_outer,
    b_outer,
    gain_two,
    bias_two,
):
    gathered = (
        lax.all_gather(w_query, "fsdp", axis=0, tiled=True),
        lax.all_gather(b_query, "fsdp", axis=0, tiled=True),
        lax.all_gather(w_key, "fsdp", axis=0, tiled=True),
        lax.all_gather(w_value, "fsdp", axis=0, tiled=True),
        lax.all_gather(b_value, "fsdp", axis=0, tiled=True),
        lax.all_gather(w_output, "fsdp", axis=0, tiled=True),
        lax.all_gather(b_output, "fsdp", axis=0, tiled=True),
        lax.all_gather(gain_one, "fsdp", axis=0, tiled=True),
        lax.all_gather(bias_one, "fsdp", axis=0, tiled=True),
        lax.all_gather(w_inner, "fsdp", axis=0, tiled=True),
        lax.all_gather(b_inner, "fsdp", axis=0, tiled=True),
        lax.all_gather(w_outer, "fsdp", axis=0, tiled=True),
        lax.all_gather(b_outer, "fsdp", axis=0, tiled=True),
        lax.all_gather(gain_two, "fsdp", axis=0, tiled=True),
        lax.all_gather(bias_two, "fsdp", axis=0, tiled=True),
    )
    (
        query_weight,
        query_bias,
        key_weight,
        value_weight,
        value_bias,
        out_weight,
        out_bias,
        gain_first,
        shift_first,
        inner_weight,
        inner_bias,
        outer_weight,
        outer_bias,
        gain_second,
        shift_second,
    ) = gathered
    joint_weight = jnp.concatenate([query_weight, key_weight, value_weight], axis=1)
    joint_bias = jnp.concatenate(
        [
            query_bias.astype(jnp.float32),
            jnp.zeros((D,), jnp.float32),
            value_bias.astype(jnp.float32),
        ]
    )
    out_bias_f = out_bias.astype(jnp.float32)
    inner_bias_f = inner_bias.astype(jnp.float32)
    outer_bias_f = outer_bias.astype(jnp.float32)
    gain_first_f = gain_first.astype(jnp.float32)
    shift_first_f = shift_first.astype(jnp.float32)
    gain_second_f = gain_second.astype(jnp.float32)
    shift_second_f = shift_second.astype(jnp.float32)
    seq_dev = inputs.shape[1]
    row_count = SEQ_MB * seq_dev
    positions = lax.axis_index("ctx") * seq_dev + lax.iota(jnp.int32, seq_dev)
    accum = None
    out_list = []
    grad_list = []
    for micro_index in range(MICRO):
        first_seq = micro_index * SEQ_MB
        seq_lens = lengths[first_seq : first_seq + SEQ_MB]
        token_rows = inputs[first_seq : first_seq + SEQ_MB].reshape(row_count, D)
        grad_rows = (
            cotangent[first_seq : first_seq + SEQ_MB].reshape(row_count, D).astype(jnp.float32)
        )
        query_ok = positions[None, :] < seq_lens[:, None]
        row_keep = query_ok.reshape(row_count, 1).astype(jnp.float32)
        projected = (matmul(token_rows, joint_weight) + joint_bias).astype(jnp.bfloat16)
        queries = projected[:, :D].reshape(SEQ_MB, seq_dev, D)
        keys_local = projected[:, D : 2 * D].reshape(SEQ_MB, seq_dev, D)
        values_local = projected[:, 2 * D :].reshape(SEQ_MB, seq_dev, D)
        start_state = (
            jnp.full((SEQ_MB, H, seq_dev), NEG_FILL, jnp.float32),
            jnp.zeros((SEQ_MB, H, seq_dev), jnp.float32),
            jnp.zeros((SEQ_MB, H, seq_dev, HD), jnp.float32),
        )
        attend_fn = partial(attend_step, queries=queries, seq_lens=seq_lens, skip_empty=False)
        run_max, run_sum, run_out = in_blocks(
            attend_fn,
            start_state,
            (
                lax.all_gather(keys_local, "ctx", axis=1, tiled=True),
                lax.all_gather(values_local, "ctx", axis=1, tiled=True),
            ),
        )
        attended = run_out / run_sum[..., None]
        log_total = run_max + jnp.log(run_sum)
        context = attended.transpose(0, 2, 1, 3).reshape(row_count, D).astype(jnp.bfloat16)
        first_sum = token_rows.astype(jnp.float32) + matmul(context, out_weight) + out_bias_f
        hidden, normed_one, inv_one = layer_norm(first_sum, gain_first_f, shift_first_f)
        hidden_low = hidden.astype(jnp.bfloat16)
        inner_pre = matmul(hidden_low, inner_weight) + inner_bias_f
        activated = gelu_exact(inner_pre).astype(jnp.bfloat16)
        outer_out = matmul(activated, outer_weight) + outer_bias_f
        result, normed_two, inv_two = layer_norm(hidden + outer_out, gain_second_f, shift_second_f)
        out_list.append(result.astype(jnp.bfloat16).reshape(SEQ_MB, seq_dev, D))
        grad_out = grad_rows * row_keep
        grad_second, grad_gain_b, grad_shift_b = norm_back(
            grad_out, normed_two, inv_two, gain_second_f
        )
        grad_outer = grad_second.astype(jnp.bfloat16)
        grad_outer_w = left_product(activated, grad_outer)
        grad_outer_b = jnp.sum(grad_outer.astype(jnp.float32), axis=0)
        grad_inner = (right_product(grad_outer, outer_weight) * gelu_slope(inner_pre)).astype(
            jnp.bfloat16
        )
        grad_inner_w = left_product(hidden_low, grad_inner)
        grad_inner_b = jnp.sum(grad_inner.astype(jnp.float32), axis=0)
        grad_hidden = grad_second + right_product(grad_inner, inner_weight)
        grad_first, grad_gain_a, grad_shift_a = norm_back(
            grad_hidden, normed_one, inv_one, gain_first_f
        )
        grad_branch = grad_first.astype(jnp.bfloat16)
        grad_out_w = left_product(context, grad_branch)
        grad_out_b = jnp.sum(grad_branch.astype(jnp.float32), axis=0)
        grad_context = (
            right_product(grad_branch, out_weight).astype(jnp.bfloat16).reshape(SEQ_MB, seq_dev, D)
        )
        row_delta = jnp.einsum(
            "bqhd,bhqd->bhq", split_heads(grad_context).astype(jnp.float32), attended
        )
        stat_total, stat_delta = (
            lax.all_gather(log_total.transpose(0, 2, 1), "ctx", axis=1, tiled=True),
            lax.all_gather(row_delta.transpose(0, 2, 1), "ctx", axis=1, tiled=True),
        )
        query_fn = partial(
            query_grad_step,
            queries=queries,
            grad_context=grad_context,
            log_total=log_total,
            row_delta=row_delta,
            seq_lens=seq_lens,
            live_queries=query_ok,
            skip_empty=False,
        )
        key_fn = partial(
            key_grad_step,
            key_rows=keys_local,
            value_rows=values_local,
            stat_total=stat_total,
            stat_delta=stat_delta,
            seq_lens=seq_lens,
            live_keys=query_ok,
            skip_empty=False,
        )
        grad_zero = jnp.zeros((SEQ_MB, seq_dev, H, HD), jnp.float32)
        grad_q = in_blocks(
            query_fn,
            grad_zero,
            (
                lax.all_gather(keys_local, "ctx", axis=1, tiled=True),
                lax.all_gather(values_local, "ctx", axis=1, tiled=True),
            ),
        )
        grad_k, grad_v = in_blocks(
            key_fn,
            (grad_zero, grad_zero),
            (
                lax.all_gather(queries, "ctx", axis=1, tiled=True),
                lax.all_gather(grad_context, "ctx", axis=1, tiled=True),
            ),
        )
        joint_grad = jnp.concatenate(
            [
                (grad_q * SCALE).reshape(row_count, D).astype(jnp.bfloat16),
                (grad_k * SCALE).reshape(row_count, D).astype(jnp.bfloat16),
                grad_v.reshape(row_count, D).astype(jnp.bfloat16),
            ],
            axis=1,
        )
        grad_joint_w = left_product(token_rows, joint_grad)
        grad_joint_b = jnp.sum(joint_grad.astype(jnp.float32), axis=0)
        input_rows = grad_first + right_product(joint_grad, joint_weight)
        grad_list.append(input_rows.reshape(SEQ_MB, seq_dev, D))
        micro_grads = (
            grad_joint_w,
            grad_joint_b,
            grad_out_w,
            grad_out_b,
            grad_gain_a,
            grad_shift_a,
            grad_inner_w,
            grad_inner_b,
            grad_outer_w,
            grad_outer_b,
            grad_gain_b,
            grad_shift_b,
        )
        if accum is None:
            accum = micro_grads
        else:
            accum = tuple((held + fresh for held, fresh in zip(accum, micro_grads)))
    (
        joint_w,
        joint_b,
        out_w,
        out_b,
        gain_a,
        shift_a,
        inner_w,
        inner_b,
        outer_w,
        outer_b,
        gain_b,
        shift_b,
    ) = accum
    grad_set = (
        joint_w[:, :D],
        joint_b[:D],
        joint_w[:, D : 2 * D],
        joint_w[:, 2 * D :],
        joint_b[2 * D :],
        out_w,
        out_b,
        gain_a,
        shift_a,
        inner_w,
        inner_b,
        outer_w,
        outer_b,
        gain_b,
        shift_b,
    )
    shard_grads = (
        lax.psum_scatter(
            grad_set[0].astype(jnp.bfloat16), "fsdp", scatter_dimension=0, tiled=True
        ).astype(jnp.float32),
        lax.psum_scatter(
            grad_set[1].astype(jnp.bfloat16), "fsdp", scatter_dimension=0, tiled=True
        ).astype(jnp.float32),
        lax.psum_scatter(
            grad_set[2].astype(jnp.bfloat16), "fsdp", scatter_dimension=0, tiled=True
        ).astype(jnp.float32),
        lax.psum_scatter(
            grad_set[3].astype(jnp.bfloat16), "fsdp", scatter_dimension=0, tiled=True
        ).astype(jnp.float32),
        lax.psum_scatter(
            grad_set[4].astype(jnp.bfloat16), "fsdp", scatter_dimension=0, tiled=True
        ).astype(jnp.float32),
        lax.psum_scatter(
            grad_set[5].astype(jnp.bfloat16), "fsdp", scatter_dimension=0, tiled=True
        ).astype(jnp.float32),
        lax.psum_scatter(
            grad_set[6].astype(jnp.bfloat16), "fsdp", scatter_dimension=0, tiled=True
        ).astype(jnp.float32),
        lax.psum_scatter(
            grad_set[7].astype(jnp.bfloat16), "fsdp", scatter_dimension=0, tiled=True
        ).astype(jnp.float32),
        lax.psum_scatter(
            grad_set[8].astype(jnp.bfloat16), "fsdp", scatter_dimension=0, tiled=True
        ).astype(jnp.float32),
        lax.psum_scatter(
            grad_set[9].astype(jnp.bfloat16), "fsdp", scatter_dimension=0, tiled=True
        ).astype(jnp.float32),
        lax.psum_scatter(
            grad_set[10].astype(jnp.bfloat16), "fsdp", scatter_dimension=0, tiled=True
        ).astype(jnp.float32),
        lax.psum_scatter(
            grad_set[11].astype(jnp.bfloat16), "fsdp", scatter_dimension=0, tiled=True
        ).astype(jnp.float32),
        lax.psum_scatter(
            grad_set[12].astype(jnp.bfloat16), "fsdp", scatter_dimension=0, tiled=True
        ).astype(jnp.float32),
        lax.psum_scatter(
            grad_set[13].astype(jnp.bfloat16), "fsdp", scatter_dimension=0, tiled=True
        ).astype(jnp.float32),
        lax.psum_scatter(
            grad_set[14].astype(jnp.bfloat16), "fsdp", scatter_dimension=0, tiled=True
        ).astype(jnp.float32),
    )
    summed = lax.psum(
        (
            shard_grads[0],
            shard_grads[1],
            shard_grads[2],
            shard_grads[3],
            shard_grads[4],
            shard_grads[5],
            shard_grads[6],
            shard_grads[7],
            shard_grads[8],
            shard_grads[9],
            shard_grads[10],
            shard_grads[11],
            shard_grads[12],
            shard_grads[13],
            shard_grads[14],
        ),
        "ctx",
    )
    outputs = jnp.concatenate(out_list, axis=0)
    input_grad = jnp.concatenate(grad_list, axis=0)
    return (outputs, input_grad) + tuple(summed)


HALF = D // 2
ROWS = 128


def flat(z, x, y, k):
    return (z * 2 + x) * 4 + y * 2 + k


def table(move):
    return [
        (flat(z, x, y, k), flat(*move(z, x, y, k)))
        for z in range(4)
        for x in range(2)
        for y in range(2)
        for k in range(2)
    ]


def permute(move):
    pairs = table(move)
    return lambda block: lax.ppermute(block, ("ctx", "fsdp"), pairs)


def permute_back(move):
    pairs = [(b, a) for a, b in table(move)]
    return lambda block: lax.ppermute(block, ("ctx", "fsdp"), pairs)


def to_seq(turn):
    return lambda z, x, y, k: (2 * k + (z // 2 + turn) % 2, x, y, z % 2)


swap_core = permute(lambda z, x, y, k: (z, x, y, k ^ 1))
swap_y = permute(lambda z, x, y, k: (z, x, y ^ 1, k))
swap_x = permute(lambda z, x, y, k: (z, x ^ 1, y, k))
swap_z1 = permute(lambda z, x, y, k: (z ^ 1, x, y, k))
swap_xz = permute(lambda z, x, y, k: (z ^ 1, x ^ 1, y, k))
swap_z2 = permute(lambda z, x, y, k: (z ^ 2, x, y, k))
seq_send = (permute(to_seq(0)), permute(to_seq(1)))
seq_return = (permute_back(to_seq(0)), permute_back(to_seq(1)))


def low(value):
    return value.astype(jnp.bfloat16)


def wide(value):
    return value.astype(jnp.float32)


def pick(array, index, axis=0):
    return lax.dynamic_index_in_dim(array, index, axis, keepdims=False)


def dot_nt(a, b):
    return lax.dot_general(a, b, (((1,), (1,)), ((), ())), preferred_element_type=jnp.float32)


def dot_tn(a, b):
    return lax.dot_general(a, b, (((0,), (0,)), ((), ())), preferred_element_type=jnp.float32)


def coords(info):
    c, f = info[0] >> 2, info[0] & 3
    return c >> 1, c & 1, f >> 1, f & 1, c, f


def pack_kernel(
    info, lens, rows, grads, w_q, w_k, w_v, w_o, w_in, v0, v1, v2, v3, v4, v5, v6, v7, wide_vec,
    t0, t1, cot, first, half, held,
):
    z, x, _, _, _, _ = coords(info)
    zh = z >> 1
    half[...] = w_in[...]
    t0[...] = rows[zh]
    t1[...] = rows[1 - zh]
    cot[:ROWS] = grads[zh]
    cot[ROWS:] = grads[1 - zh]
    columns = pl.ds(pl.multiple_of(x * HALF, 128), HALF)
    first[:192, :D] = w_o[...]
    for n, weight in enumerate((w_q, w_k, w_v)):
        first[:192, D + HALF * n : D + HALF * n + HALF] = weight[:, columns]
    held[...] = jnp.zeros_like(held)
    for n, vector in enumerate((v0, v1, v2, v3, v4, v5, v6, v7)):
        held[n : n + 1, :192] = wide(vector[...]).reshape(1, 192)
    held[8:9, :] = wide(wide_vec[...]).reshape(1, D)
    lane = lax.broadcasted_iota(jnp.int32, (1, D), 1)
    ends = jnp.zeros((1, D), jnp.int32)
    for n in range(2):
        ends = jnp.where(lane == n, lens[n] >> 7, ends)
        ends = jnp.where(lane == 2 + n, lens[n] & 127, ends)
    held[9:10, :] = wide(ends)
    first[192:, :D] = low(held[...])
    first[192:, D:] = jnp.zeros((16, 3 * HALF), jnp.bfloat16)


def attend_kernel(
    info, b0, b1, b2, b3, b4, b5, b6, b7, s0, s1, s2, s3, w0, w1, w2, w3,
    xs, ws, q_out, k_out, v_out, p_out, cu, cv, cx, key_bias, small, sems,
):
    step = pl.program_id(0)
    z, x, y, k, _, f = coords(info)

    @pl.when(step == 0)
    def _():
        copies = [
            pltpu.make_async_copy(
                piece.at[:192, D:], ws.at[pl.ds(pl.multiple_of(192 * (f ^ n), 64), 192), :], sems.at[n]
            )
            for n, piece in enumerate((w0, w1, w2, w3))
        ]
        blocks = (b0, b1, b2, b3, b4, b5, b6, b7)
        copies += [
            pltpu.make_async_copy(block, xs.at[n * ROWS : (n + 1) * ROWS, :], sems.at[4 + n])
            for n, block in enumerate(blocks)
        ]
        for copy in copies:
            copy.start()
        for n, piece in enumerate((s0, s1, s2, s3)):
            small[f ^ n] = wide(piece[...])
        line = small[2 * y + (z >> 1)][9:10, :]
        lane = lax.broadcasted_iota(jnp.int32, (1, D), 1)
        part = jnp.where(lane == (z & 1), 128.0 * line, 0.0)
        part = part + jnp.where(lane == 2 + (z & 1), line, 0.0)
        end = jnp.sum(part, axis=1, keepdims=True)
        z_low = 2 * (z & 1)
        for n, block in enumerate(blocks):
            z_block = (z_low if n % 2 == 0 else 2 - z_low) + (k if n < 4 else 1 - k)
            x_block = x if n % 4 < 2 else 1 - x
            place = (2 * z_block + x_block) * ROWS + lax.broadcasted_iota(jnp.int32, (1, ROWS), 1)
            key_bias[:, n * ROWS : (n + 1) * ROWS] = jnp.where(wide(place) < end, 0.0, NEG_FILL)
        for copy in copies:
            copy.wait()

        def bias(row):
            return jnp.concatenate(
                [small[2 * x + n][row : row + 1, :192] for n in range(2)], axis=1
            )

        q_out[...] = low(wide(low(matmul(xs[: 4 * ROWS, :], ws[:, :HALF]) + bias(0))) * SCALE)
        k_out[...] = low(matmul(xs[...], ws[:, HALF : 2 * HALF]))
        v_out[...] = low(matmul(xs[...], ws[:, 2 * HALF :]) + bias(1))

    lanes = pl.ds(pl.multiple_of(step * 128, 128), 128)
    first = lax.broadcasted_iota(jnp.int32, (1, 128), 1) < HD
    queries = q_out[:, lanes]
    keys = k_out[:, lanes]
    values = v_out[:, lanes]
    for part in range(2):
        rows = slice(part * 256, part * 256 + 256)
        found = []
        for head in range(2):
            mine = first if head == 0 else jnp.logical_not(first)
            scores = dot_nt(jnp.where(mine, queries[rows], 0), keys) + key_bias[...]
            top = jnp.max(scores, axis=1, keepdims=True)
            weights = jnp.exp(scores - top)
            total = jnp.sum(weights, axis=1, keepdims=True)
            probs = low(weights * (1.0 / total))
            p_out[head, rows, :] = probs
            found.append(matmul(probs, values))
        context = low(jnp.where(first, found[0], found[1]))
        if part == 0:
            cu[...] = context[:ROWS]
            cv[...] = context[ROWS:]
        else:
            cx[0] = context[:ROWS]
            cx[1] = context[ROWS:]


def pair_back(queries_ref, keys, values, probs_ref, grads):
    first = lax.broadcasted_iota(jnp.int32, (1, 128), 1) < HD
    grad_k = jnp.zeros((8 * ROWS, 128), jnp.float32)
    grad_v = jnp.zeros((8 * ROWS, 128), jnp.float32)
    grad_qs = []
    for part in range(2):
        rows = slice(part * 256, part * 256 + 256)
        one, two = grads[2 * part : 2 * part + 2]
        grad_rows = jnp.concatenate([one[...], two[...]], axis=0)
        queries = queries_ref[rows, :]
        grad_q = jnp.zeros((256, 128), jnp.float32)
        for head in range(2):
            mine = first if head == 0 else jnp.logical_not(first)
            grad_mine = jnp.where(mine, grad_rows, 0)
            probs = probs_ref[head, rows, :]
            grad_probs = dot_nt(grad_mine, values)
            product = wide(probs) * grad_probs
            delta = jnp.sum(product, axis=1, keepdims=True)
            grad_scores = low(product - wide(probs) * delta)
            grad_q = grad_q + matmul(grad_scores, jnp.where(mine, keys, 0))
            grad_k = grad_k + dot_tn(grad_scores, jnp.where(mine, queries, 0))
            grad_v = grad_v + dot_tn(probs, grad_mine)
        grad_qs.append(low(grad_q * SCALE))
    return grad_qs, low(grad_k), low(grad_v)


def attend_back_kernel(queries, keys, values, probs, gu, gv, gxu, gxv, dq, dk, dv):
    grad_qs, dk[...], dv[...] = pair_back(
        queries, keys[...], values[...], probs, (gu, gv, gxu, gxv)
    )
    dq[:256, :], dq[256:, :] = grad_qs


def joint_kernel(
    info, xs, dq0, dq1, dq2, dk0, dk1, dk2, dv0, dv1, dv2, keep, send, grads, dw
):
    for n, (q, k, v) in enumerate(((dq0, dk0, dv0), (dq1, dk1, dv1), (dq2, dk2, dv2))):
        start = 128 * n
        grads[: 4 * ROWS, start : start + 128] = q[...]
        grads[:, HALF + start : HALF + start + 128] = k[...]
        grads[:, 2 * HALF + start : 2 * HALF + start + 128] = v[...]
    own = slice(0, 4 * ROWS)
    dw[:, :HALF] = low(dot_tn(xs[own, :], grads[own, :HALF]))
    dw[:, HALF:] = low(dot_tn(xs[...], grads[:, HALF:]))
    col_sums = jnp.concatenate(
        [
            column_sum(wide(grads[own, :HALF])),
            jnp.zeros((1, HALF), jnp.float32),
            column_sum(wide(grads[:, 2 * HALF :])),
        ],
        axis=1,
    )
    tail = low(jnp.where(lax.broadcasted_iota(jnp.int32, (8, 1), 0) == 0, col_sums, 0.0))
    z, _, _, _, _, f = coords(info)
    for n in range(4):
        place = send if n % 2 else keep
        for half in range(2):
            start = pl.multiple_of(192 * (f ^ n) + 96 * half, 32)
            place[n // 2, half ^ (z & 1), :96, :] = dw[pl.ds(start, 96), :]
            place[n // 2, half ^ (z & 1), 96:, :] = tail if half == 0 else tail * 0


def rows_back_kernel(
    ws, dq0, dq1, dq2, dk0, dk1, dk2, dv0, dv1, dv2, dx_own, dx_other, grads
):
    for n, (q, k, v) in enumerate(((dq0, dk0, dv0), (dq1, dk1, dv1), (dq2, dk2, dv2))):
        start = 128 * n
        grads[: 4 * ROWS, start : start + 128] = q[...]
        grads[:, HALF + start : HALF + start + 128] = k[...]
        grads[:, 2 * HALF + start : 2 * HALF + start + 128] = v[...]
    dx_other[...] = low(dot_nt(grads[4 * ROWS :, HALF:], ws[:, HALF:]))
    dx_own[...] = dot_nt(grads[: 4 * ROWS, :], ws[...])


def middle_one_kernel(
    info, cm0, cm1, co0, co1, x0, x1, o0, o1, o2, o3, i0, i1, i2, i3,
    hidden_out, normed_out, inv_out, act, slope, vec,
    ctx, low_rows, small, order, inner_weight, sems,
):
    step = pl.program_id(0)
    _, x, _, _, _, f = coords(info)

    def copy(e, n):
        return pltpu.make_async_copy(
            (i0, i1, i2, i3)[n].at[:, pl.ds(pl.multiple_of(D * (f ^ e), 128), D)],
            inner_weight.at[e, pl.ds(pl.multiple_of(192 * (f ^ n), 64), 192), :],
            sems.at[e, n],
        )

    @pl.when(step == 0)
    def _():
        for e in range(4):
            for n in range(4):
                copy(e, n).start()
        for n, piece in enumerate((o0, o1, o2, o3)):
            small[f ^ n] = wide(piece[192:, :])
            order[n] = wide(piece[192:, :])
        for n in range(8):
            vec[n : n + 1, :] = jnp.concatenate(
                [small[m][n : n + 1, :192] for m in range(4)], axis=1
            )
        for side, (one, two) in enumerate(((cm0, cm1), (co0, co1))):
            rows = jnp.concatenate([one[...], two[...]], axis=0)
            for part in range(2):
                ctx[2 * (x ^ side) + part] = rows[:, 192 * part : 192 * part + 192]
        total = wide(jnp.concatenate([x0[...], x1[...]], axis=0)) + vec[2:3, :]
        for n, piece in enumerate((o0, o1, o2, o3)):
            total = total + matmul(ctx[f ^ n], piece[:192, :])
        hidden, normed, inv = layer_norm(total, vec[3:4, :], vec[4:5, :])
        hidden_out[...] = hidden
        normed_out[...] = normed
        inv_out[...] = inv
        low_rows[...] = low(hidden)

    for n in range(4):
        copy(step, n).wait()
    pre = matmul(low_rows[...], inner_weight[step]) + order[step][8:9, :]
    bell = 0.5 * (1.0 + lax.erf(pre * ROOT_HALF))
    act[0] = low(pre * bell)
    slope[0] = low(bell + pre * INV_ROOT_TAU * jnp.exp(-0.5 * pre * pre))


def norm_grad(grad, normed, inv, gain):
    scaled = grad * gain
    return inv * (
        scaled
        - jnp.mean(scaled, axis=-1, keepdims=True)
        - normed * jnp.mean(scaled * normed, axis=-1, keepdims=True)
    )


def column_sum(value):
    return jnp.sum(value, axis=0, keepdims=True)


def outer_copies(refs, held, sems):
    copies = [
        pltpu.make_async_copy(ref, held.at[n], sems.at[n]) for n, ref in enumerate(refs)
    ]
    for copy in copies:
        copy.start()
    return copies


def middle_two_kernel(
    info, lens, act, act_block, hidden, cot, vec, w0, w1, w2, w3,
    out, second_out, outer_out, sums, keep, send, w_all, w_sem,
):
    step = pl.program_id(0)
    z, x, _, _, c, f = coords(info)

    @pl.when(step == 0)
    def _():
        copies = outer_copies((w0, w1, w2, w3), w_all, w_sem)
        b_2, g_2, s_2 = vec[5:6, :], vec[6:7, :], vec[7:8, :]
        total = hidden[...] + b_2
        for n in range(4):
            copies[n].wait()
            total = total + matmul(act[n], w_all[n])
        result, normed, inv = layer_norm(total, g_2, s_2)
        zh = z >> 1
        out[zh] = low(result[:ROWS])
        out[1 - zh] = low(result[ROWS:])
        row = lax.broadcasted_iota(jnp.int32, (2 * ROWS, 1), 0)
        end = jnp.where(row < ROWS, lens[zh], lens[1 - zh] + ROWS)
        grad = wide(cot[...]) * jnp.where(row + c * ROWS < end, 1.0, 0.0)
        grad_second = norm_grad(grad, normed, inv, g_2)
        second_out[...] = grad_second
        grad_outer = low(grad_second)
        outer_out[...] = grad_outer
        sums[...] = jnp.zeros_like(sums)
        for n, value in enumerate((wide(grad_outer), grad * normed, grad)):
            sums[n : n + 1, :] = column_sum(value)

    @pl.when(step > 0)
    def _():
        grad = low(dot_tn(act_block[0], outer_out[...]))
        for place, wanted in ((send, step < 3), (keep, step >= 3)):

            @pl.when(wanted)
            def _(place=place):
                for n in range(4):
                    place[0, n ^ (2 * x + (z & 1))] = grad[192 * n : 192 * n + 192]


def inner_back_kernel(
    info, outer, slope, w0, w1, w2, w3, inner_out, sums, w_all, sems
):
    f = info[0] & 3
    copies = outer_copies((w0, w1, w2, w3), w_all, sems)
    for e in range(4):
        copies[e].wait()
        inner = low(dot_nt(outer[...], w_all[e]) * wide(slope[e]))
        inner_out[e] = inner
        sums[pl.ds(f ^ e, 1), :] = column_sum(wide(inner))


def middle_three_kernel(
    info, second, inner, normed_one, inv_one, vec, o0, o1, o2, o3, i0, i1, i2, i3,
    first_out, g0, g1, branch_out, sums, o_all, i_all, gc, o_sem, i_sem,
):
    _, x, _, _, _, f = coords(info)
    copies = {}
    for e in range(4):
        columns = pl.ds(pl.multiple_of(D * (f ^ e), 128), D)
        for n, ref in enumerate((i0, i1, i2, i3)):
            rows = pl.ds(pl.multiple_of(192 * (f ^ n), 64), 192)
            copies["i", e, n] = pltpu.make_async_copy(
                ref.at[:, columns], i_all.at[e, rows, :], i_sem.at[e, n]
            )
            copies["i", e, n].start()
    for n, ref in enumerate((o0, o1, o2, o3)):
        copies["o", n] = pltpu.make_async_copy(ref.at[:192, :D], o_all.at[n], o_sem.at[n])
        copies["o", n].start()
    grad_hidden = second[...]
    for e in range(4):
        for n in range(4):
            copies["i", e, n].wait()
        grad_hidden = grad_hidden + dot_nt(inner[e], i_all[e])
    grad_first = norm_grad(grad_hidden, normed_one[...], inv_one[...], vec[3:4, :])
    first_out[...] = grad_first
    branch = low(grad_first)
    branch_out[...] = branch
    for n, value in enumerate((wide(branch), grad_hidden * normed_one[...], grad_hidden)):
        sums[n : n + 1, :] = column_sum(value)
    for n in range(4):
        copies["o", n].wait()
        gc[f ^ n] = low(dot_nt(branch, o_all[n]))
    for side in range(2):
        rows = jnp.concatenate([gc[2 * (x ^ side)], gc[2 * (x ^ side) + 1]], axis=1)
        g0[1 - side] = rows[:ROWS]
        g1[1 - side] = rows[ROWS:]


def middle_four_kernel(
    info, inner, hidden, branch, cm0, cm1, co0, co1, sums_two, sums_in, sums_one,
    keep, send, held, out_held, vec_held,
):
    step = pl.program_id(0)
    _, x, _, _, _, f = coords(info)
    block = f ^ step

    @pl.when(step == 0)
    def _():
        for side, (one, two) in enumerate(((cm0, cm1), (co0, co1))):
            rows = jnp.concatenate([one[...], two[...]], axis=0)
            start = pl.multiple_of(HALF * (x ^ side), 128)
            out_held[pl.ds(start, HALF), :] = low(dot_tn(rows, branch[...]))
        vec_held[...] = jnp.zeros_like(vec_held)
        top = lax.broadcasted_iota(jnp.int32, (16, 1), 0) == 0
        for n in range(4):
            cut = slice(192 * n, 192 * n + 192)
            lines = (
                sums_in[n : n + 1, :],
                jnp.concatenate(
                    [sums_one[m : m + 1, cut] for m in range(3)] + [sums_two[0:1, cut]], axis=1
                ),
                jnp.concatenate(
                    [sums_two[1:2, cut], sums_two[2:3, cut], jnp.zeros((1, HALF), jnp.float32)],
                    axis=1,
                ),
            )
            for m, line in enumerate(lines):
                vec_held[m, n] = low(jnp.where(top, line, 0.0))

    held[...] = low(dot_tn(low(hidden[...]), inner[0]))
    for n in range(4):
        place = send if n % 2 else keep
        start = 192 * (f ^ n)
        place[n // 2, 0, :192, :] = held[pl.ds(pl.multiple_of(start, 64), 192), :]
        place[n // 2, 0, 192:240, :] = out_held[pl.ds(pl.multiple_of(start + 48 * block, 16), 48), :]
        place[n // 2, 0, 240:, :] = vec_held[block, f ^ n]


MIDDLE = 2 * ROWS
BF, FP = jnp.bfloat16, jnp.float32


def whole(shape):
    return pl.BlockSpec(tuple(shape), lambda *_: (0,) * len(shape))


def lane_block(rows, start=0):
    return pl.BlockSpec((rows, 128), lambda step, *_: (0, step + start))


def call(kernel, name, grid, scalars, operands, outs, scratch=(), work=(1, 1), limit=30):
    return pl.pallas_call(
        kernel,
        out_shape=[jax.ShapeDtypeStruct(shape, kind) for shape, kind, _ in outs],
        grid_spec=pltpu.PrefetchScalarGridSpec(
            num_scalar_prefetch=len(scalars),
            grid=(grid,),
            in_specs=[spec or whole(array.shape) for array, spec in operands],
            out_specs=[spec or whole(shape) for shape, _, spec in outs],
            scratch_shapes=list(scratch),
        ),
        compiler_params=pltpu.CompilerParams(
            dimension_semantics=("arbitrary",), vmem_limit_bytes=limit * 1024 * 1024
        ),
        cost_estimate=pl.CostEstimate(
            flops=1000, bytes_accessed=1000, transcendentals=0
        ),
        name=name,
    )(*scalars, *[array for array, _ in operands])


def plain(arrays):
    return [(array, None) for array in arrays]


def anywhere(arrays):
    return [(array, pl.BlockSpec(memory_space=pl.ANY)) for array in arrays]


def probs_block(start=0):
    return pl.BlockSpec((2, 4 * ROWS, 8 * ROWS), lambda step, *_: (step + start, 0, 0))


def pack(info, lens, inputs, cotangent, weights, vectors):
    return call(
        pack_kernel, "pack", 1, (info, lens),
        plain([inputs, cotangent, *weights[:4]])
        + [(weights[4], pl.BlockSpec((192, 2 * D), lambda _, info, lens: (0, (info[0] >> 2) & 1)))]
        + plain(vectors),
        [
            ((ROWS, D), BF, None), ((ROWS, D), BF, None), ((MIDDLE, D), BF, None),
            ((208, D + 3 * HALF), BF, None), ((192, 2 * D), BF, None),
        ],
        [pltpu.VMEM((16, D), FP)], limit=56,
    )


def first_columns(pieces):
    return [(piece, pl.BlockSpec((208, D), lambda *_: (0, 0))) for piece in pieces]


def attend(info, blocks, pieces):
    return call(
        attend_kernel, "attend", 3, (info,),
        anywhere(blocks)
        + [(piece, pl.BlockSpec((16, D), lambda *_: (12, 0))) for piece in pieces]
        + anywhere(pieces),
        [
            ((8 * ROWS, D), BF, None), ((D, 3 * HALF), BF, None), ((4 * ROWS, HALF), BF, None),
            ((8 * ROWS, HALF), BF, None), ((8 * ROWS, HALF), BF, None),
            ((6, 4 * ROWS, 8 * ROWS), BF, probs_block()),
        ]
        + [((ROWS, HALF), BF, lane_block(ROWS))] * 2
        + [((2, ROWS, HALF), BF, pl.BlockSpec((2, ROWS, 128), lambda step, *_: (0, 0, step)))],
        [
            pltpu.VMEM((1, 8 * ROWS), FP), pltpu.VMEM((4, 16, D), FP),
            pltpu.SemaphoreType.DMA((12,)),
        ],
        limit=56,
    )


def attend_back(queries, keys, values, probs, grads, start, pairs):
    return call(
        attend_back_kernel, "attend_back", pairs, (),
        [
            (queries, lane_block(4 * ROWS, start)), (keys, lane_block(8 * ROWS, start)),
            (values, lane_block(8 * ROWS, start)), (probs, probs_block(start)),
        ]
        + [(grad, pl.BlockSpec((None, ROWS, 128), lambda s, n=n: (n, 0, s + start))) for grad, n in grads],
        [
            ((4 * ROWS, 128 * pairs), BF, lane_block(4 * ROWS)),
            ((8 * ROWS, 128 * pairs), BF, lane_block(8 * ROWS)),
            ((8 * ROWS, 128 * pairs), BF, lane_block(8 * ROWS)),
        ],
        (), (4 * pairs, 5 * pairs),
    )


def by_name(pairs):
    return [part for name in zip(*pairs) for part in name]


def joint_grads(info, xs, pairs):
    joint = (2, 2, 104, 3 * HALF)
    return call(
        joint_kernel, "joint_grads", 1, (info,), plain([xs, *by_name(pairs)]),
        [(joint, BF, None), (joint, BF, None)],
        [pltpu.VMEM((8 * ROWS, 3 * HALF), BF), pltpu.VMEM((D, 3 * HALF), BF)],
    )


def rows_back(ws, pairs):
    return call(
        rows_back_kernel, "rows_back", 1, (), plain([ws, *by_name(pairs)]),
        [((4 * ROWS, D), FP, None), ((4 * ROWS, D), BF, None)],
        [pltpu.VMEM((8 * ROWS, 3 * HALF), BF)],
    )


def middle_one(info, ctx, rows, out_p, inner_p):
    block = pl.BlockSpec((1, MIDDLE, D), lambda step, *_: (step, 0, 0))
    return call(
        middle_one_kernel, "middle_one", 4, (info,),
        plain([*ctx, *rows]) + first_columns(out_p) + anywhere(inner_p),
        [
            ((MIDDLE, D), FP, None), ((MIDDLE, D), FP, None), ((MIDDLE, 1), FP, None),
            ((4, MIDDLE, D), BF, block), ((4, MIDDLE, D), BF, block), ((8, D), FP, None),
        ],
        [
            pltpu.VMEM((4, MIDDLE, 192), BF), pltpu.VMEM((MIDDLE, D), BF),
            pltpu.VMEM((4, 16, D), FP), pltpu.VMEM((4, 16, D), FP), pltpu.VMEM((4, D, D), BF),
            pltpu.SemaphoreType.DMA((4, 4)),
        ],
        (4, 10),
    )


def middle_two(info, lens, act, hidden, cot, vec, outer_p):
    def turn(step, *_):
        at = jnp.maximum(step - 1, 0)
        return (jnp.where(at < 2, 2 * at + 1, 2 * at - 4), 0, 0)

    blocks = (2, 4, 192, D)
    return call(
        middle_two_kernel, "middle_two", 5, (info, lens),
        [(act, None), (act, pl.BlockSpec((1, MIDDLE, D), turn))]
        + plain([hidden, cot, vec])
        + anywhere(outer_p),
        [
            ((2, ROWS, D), BF, None), ((MIDDLE, D), FP, None), ((MIDDLE, D), BF, None),
            ((8, D), FP, None),
            (blocks, BF, pl.BlockSpec((1, 4, 192, D), lambda s, *_: (jnp.maximum(s - 3, 0), 0, 0, 0))),
            (blocks, BF, pl.BlockSpec((1, 4, 192, D), lambda s, *_: (jnp.where(s < 2, 0, 1), 0, 0, 0))),
        ],
        [pltpu.VMEM((4, D, D), BF), pltpu.SemaphoreType.DMA((4,))], (4, 10),
    )


def inner_back(info, outer, slope, outer_p):
    return call(
        inner_back_kernel, "inner_back", 1, (info,), plain([outer, slope]) + anywhere(outer_p),
        [((4, MIDDLE, D), BF, None), ((4, D), FP, None)],
        [pltpu.VMEM((4, D, D), BF), pltpu.SemaphoreType.DMA((4,))], (2, 7),
    )


def middle_three(info, second, inner, normed, inv, vec, out_p, inner_p):
    return call(
        middle_three_kernel, "middle_three", 1, (info,),
        plain([second, inner, normed, inv, vec]) + anywhere([*out_p, *inner_p]),
        [((MIDDLE, D), FP, None)]
        + [((2, ROWS, HALF), BF, None)] * 2
        + [((MIDDLE, D), BF, None), ((8, D), FP, None)],
        [
            pltpu.VMEM((4, 192, D), BF), pltpu.VMEM((4, D, D), BF),
            pltpu.VMEM((4, MIDDLE, 192), BF), pltpu.SemaphoreType.DMA((4,)),
            pltpu.SemaphoreType.DMA((4, 4)),
        ],
        (2, 7),
    )


def middle_four(info, inner, hidden, branch, ctx, sums):
    def spot(step, info):
        z, x, _, _, _, f = coords(info)
        return (0, f ^ step ^ (2 * (z & 1) + x), 0, 0)

    block = pl.BlockSpec((2, 1, 256, D), spot)
    return call(
        middle_four_kernel, "middle_four", 4, (info,),
        [(inner, pl.BlockSpec((1, MIDDLE, D), lambda step, *_: (step, 0, 0)))]
        + plain([hidden, branch, *ctx, *sums]),
        [((2, 4, 256, D), BF, block)] * 2,
        [pltpu.VMEM((D, D), BF), pltpu.VMEM((D, D), BF), pltpu.VMEM((4, 4, 16, D), BF)],
        (4, 8),
    )


def place_outer_kernel(info, p0, p1, p2, p3, out):
    z, x, _, _, _, _ = coords(info)
    for n, piece in enumerate((p0, p1, p2, p3)):
        out[pl.ds(pl.multiple_of(192 * (n ^ (2 * x + (z & 1))), 64), 192), :] = wide(piece[...])


def place_inner_kernel(
    info, p0, p1, p2, p3, inner, out, b_in, b_out, g_one, s_one, b_two, g_two, s_two, held
):
    z, x, _, _, _, _ = coords(info)
    for n, piece in enumerate((p0, p1, p2, p3)):
        at = n ^ (2 * (z & 1) + x)
        inner[:, pl.ds(pl.multiple_of(D * at, 128), D)] = wide(piece[:192, :])
        out[pl.ds(pl.multiple_of(48 * at, 16), 48), :] = wide(piece[192:240, :])
        held[at] = wide(piece[240:, :])
    b_in[...] = held[0][0:1, :].reshape(D)
    for n, vector in enumerate((b_out, g_one, s_one, b_two, g_two, s_two)):
        cut = 192 * (n % 4)
        vector[...] = held[1 + n // 4][0:1, cut : cut + 192].reshape(192)


def place_joint_kernel(info, p0, p1, p2, p3, query, key, value, b_query, b_value, held):
    z, x, _, _, _, f = coords(info)
    z_bit = z & 1
    for n, piece in enumerate((p0, p1, p2, p3)):
        rows = pl.ds(pl.multiple_of(96 * (n % 2 ^ z_bit), 32), 96)
        columns = pl.ds(pl.multiple_of(HALF * (n // 2 ^ x), 128), HALF)
        for m, out in enumerate((query, key, value)):
            out[rows, columns] = wide(piece[:96, HALF * m : HALF * m + HALF])
        line = wide(piece[96:, :])
        line = jnp.where(f & 1 == 0, line, jnp.concatenate([line[:, 192:], line[:, :192]], axis=1))
        held[n // 2 ^ x, n % 2 ^ z_bit] = line
    mine = held[f >> 1, 0][0:1, :]
    b_query[...] = mine[:, :192].reshape(192)
    b_value[...] = mine[:, 2 * HALF : 2 * HALF + 192].reshape(192)


def placed(kernel, name, info, pieces, shapes, held=()):
    return call(
        kernel, name, 1, (info,), plain(pieces), [(shape, FP, None) for shape in shapes],
        [pltpu.VMEM(shape, FP) for shape in held], (1, 6),
    )


def unshuffle(array, bit):
    return jnp.where(bit == 0, array, array[::-1])


def tied(values, *events):
    return lax.optimization_barrier((values, events))[0]


ROW_A, ROW_B = 96, 144


def fast_body(
    inputs, cotangent, lengths, w_query, b_query, w_key, w_value, b_value, w_output, b_output,
    gain_one, bias_one, w_inner, b_inner, w_outer, b_outer, gain_two, bias_two,
):
    info = lax.axis_index(("ctx", "fsdp")).astype(jnp.int32).reshape(1)
    zh, x = lax.axis_index("ctx") // 4, lax.axis_index("ctx") % 2

    t0, t1, cot, first, half = pack(
        info, lengths, inputs, cotangent, (w_query, w_key, w_value, w_output, w_inner),
        (b_query, b_value, b_output, gain_one, bias_one, b_outer, gain_two, bias_two, b_inner),
    )

    bu, bv = seq_send[0](t0), seq_send[1](t1)
    first_y, first_k = swap_y(first), swap_core(first)
    half_y = swap_y(half)
    bu, bv, first_k = tied((bu, bv, first_k))
    bxu, bxv, bku = swap_x(bu), swap_x(bv), swap_core(bu)
    bxu, bxv, bku, first_y, half_y = tied((bxu, bxv, bku, first_y, half_y))
    bkv, *rest = [swap_core(b) for b in (bv, bxu, bxv, first_y)]
    bkv, *rest = tied([bkv] + rest)
    blocks = [bu, bv, bxu, bxv, bku, bkv, *rest[:2]]
    first_p = [first, first_k, first_y, rest[2]]
    outer_y = swap_y(tied(w_outer, half_y))
    half_x = swap_x(tied(half_y, bkv))
    xs, ws, queries, keys, values, probs, cu, cv, cx = attend(info, blocks, first_p)

    cu, cv, cx, half_x = tied((cu, cv, cx, half_x))
    cu, cv = seq_return[0](cu), seq_return[1](cv)
    cx = swap_x(cx)
    inner_y = jnp.where(
        x == 0, jnp.concatenate([half_y, half_x], 1), jnp.concatenate([half_x, half_y], 1)
    )
    cu, cv, cx, outer_y, inner_y = tied((cu, cv, cx, outer_y, inner_y))
    cxu, cxv = seq_return[0](cx[0]), seq_return[1](cx[1])
    inner_k, inner_ky = swap_core(tied(w_inner, cx)), swap_core(inner_y)
    cxu, cxv, inner_k, inner_ky = tied((cxu, cxv, inner_k, inner_ky))
    outer_k, outer_ky = swap_core(tied(w_outer, cxu)), swap_core(tied(outer_y, cxu))
    ctx = [cu, cv, cxu, cxv]
    inner_p = [w_inner, inner_k, inner_y, inner_ky]
    hidden, normed, inv, act, slope, vec = middle_one(info, ctx, [t0, t1], first_p, inner_p)
    act, outer_k, outer_ky = tied((act, outer_k, outer_ky))
    outer_p = [w_outer, outer_k, outer_y, outer_ky]
    outputs, second_grad, outer, sums_two, o_keep, o_send = middle_two(
        info, lengths, act, hidden, cot, vec, outer_p
    )
    o_came = swap_core(o_send)
    inner, sums_in = inner_back(info, outer, slope, outer_p)
    o_came, inner = tied((o_came, inner))
    o_y = low(wide(o_keep[1, :2]) + wide(o_came[1, :2]))
    o_z = low(wide(o_keep[:, 3]) + wide(o_came[:, 3]))
    inner, o_y, o_z = tied((inner, o_y, o_z))
    o_y, o_z = swap_y(o_y), swap_z1(o_z)
    grad_first, g0, g1, branch, sums_one = middle_three(
        info, second_grad, inner, normed, inv, vec, first_p, inner_p
    )
    g0, g1 = seq_send[0](g0), seq_send[1](g1)
    i_keep, i_send = middle_four(
        info, inner, hidden, branch, ctx, (sums_two, sums_in, sums_one)
    )
    g0, g1, i_send, o_y, o_z = tied((g0, g1, i_send, o_y, o_z))
    go = jnp.stack([g0[0], g1[0]])
    go, o_y, o_z, i_send = tied((go, o_y, o_z, i_send))
    go = swap_x(go)
    i_came = swap_core(i_send)
    o_z2 = swap_z1(low(wide(o_keep[0, 1]) + wide(o_came[0, 1]) + wide(o_y[1])))
    o_y2 = swap_y(low(wide(o_keep[1, 2]) + wide(o_came[1, 2]) + wide(o_z[1])))
    go, i_came, o_z2, o_y2 = tied((go, i_came, o_z2, o_y2))
    o_one = wide(o_keep[0, 0]) + wide(o_came[0, 0]) + wide(o_y[0]) + wide(o_z2)
    o_two = low(wide(o_keep[0, 2]) + wide(o_came[0, 2]) + wide(o_z[0]) + wide(o_y2))
    i_keep, i_came = (a.reshape(2, 2, 2, 256, D) for a in (i_keep, i_came))

    def summed(*spot):
        return wide(i_keep[spot]) + wide(i_came[spot])

    every, one_a, one_b, one_c = slice(None), slice(0, ROW_A), slice(ROW_A, ROW_B), slice(ROW_B, 256)
    i_y, i_x = low(summed(1, every, every, one_a)), low(summed(every, every, 1, one_b))
    i_z = low(summed(every, 1, every, one_c))
    go, i_y, i_x, i_z, o_two = tied((go, i_y, i_x, i_z, o_two))
    i_y, i_x, i_z = swap_y(i_y), swap_x(i_x), swap_z1(i_z)
    o_came = swap_x(o_two)
    grads = [(g0, 1), (g1, 1), (go, 0), (go, 1)]
    pair_0 = attend_back(queries, keys, values, probs, grads, 0, 1)
    pair_1 = attend_back(tied(queries, pair_0), keys, values, probs, grads, 1, 1)
    pair_2 = attend_back(tied(queries, pair_1), keys, values, probs, grads, 2, 1)
    pairs = (pair_0, pair_1, pair_2)
    dx_own, dx_other = rows_back(ws, pairs)
    dx_own, dx_other, i_y, i_x, i_z, o_came = tied((dx_own, dx_other, i_y, i_x, i_z, o_came))
    part_a = summed(0, every, every, one_a) + wide(i_y)
    part_b = summed(every, every, 0, one_b) + wide(i_x)
    part_c = summed(every, 0, every, one_c) + wide(i_z)
    i_z2, i_y2, i_x2 = swap_z1(low(part_a[1])), swap_y(low(part_b[1])), swap_x(low(part_c[:, 1]))
    o_sum = low(o_one + wide(o_came))
    dx_came = swap_core(dx_other)
    o_came = swap_z2(o_sum)
    j_keep, j_send = joint_grads(info, tied(xs, dx_other), pairs)
    j_keep, j_send, i_x2, i_y2, i_z2, dx_came = tied((j_keep, j_send, i_x2, i_y2, i_z2, dx_came))
    j_came = swap_core(j_send)
    part_a, part_b, part_c = part_a[0] + wide(i_z2), part_b[0] + wide(i_y2), part_c[:, 0] + wide(i_x2)
    i_x3, i_z3, i_y3 = swap_x(low(part_a[1])), swap_z1(low(part_b[1])), swap_y(low(part_c[1]))
    j_came, i_x3, i_z3, i_y3, o_came = tied((j_came, i_x3, i_z3, i_y3, o_came))
    o_sum = low(wide(o_sum) + wide(o_came))
    i_sum = [part_a[0] + wide(i_x3), part_b[0] + wide(i_z3), part_c[0] + wide(i_y3)]
    i_sum = low(jnp.concatenate(i_sum, axis=0))
    dx = dx_own[: 2 * ROWS] + wide(dx_came[: 2 * ROWS])
    dx_send = low(dx_own[2 * ROWS :] + wide(dx_came[2 * ROWS :]))
    j_y = swap_y(low(wide(j_keep[1, :, :48]) + wide(j_came[1, :, :48])))
    j_z = swap_z1(low(wide(j_keep[:, 1, 48:]) + wide(j_came[:, 1, 48:])))
    j_one = wide(j_keep[0, :, :48]) + wide(j_came[0, :, :48])
    j_two = wide(j_keep[:, 0, 48:]) + wide(j_came[:, 0, 48:])
    i_came = swap_z2(i_sum)
    dx_came = swap_x(dx_send)
    j_y, j_z, dx_came = tied((j_y, j_z, dx_came))
    j_one, j_two = j_one + wide(j_y), j_two + wide(j_z)
    dx = low(dx + wide(dx_came))
    j_z, j_y = swap_z1(low(j_one[1])), swap_y(low(j_two[1]))
    o_x, o_z = swap_x(o_sum), swap_z1(o_sum)
    j_z, j_y, o_x, o_z, i_came = tied((j_z, j_y, o_x, o_z, i_came))
    j_sum = low(jnp.concatenate([j_one[0] + wide(j_z), j_two[0] + wide(j_y)], axis=0))
    i_sum = low(wide(i_sum) + wide(i_came))
    j_came = swap_z2(j_sum)
    i_z, i_x, o_zx = swap_z1(i_sum), swap_x(i_sum), swap_x(tied(o_z, i_sum))
    j_came, i_z, i_x, o_zx = tied((j_came, i_z, i_x, o_zx))
    j_sum = low(wide(j_sum) + wide(j_came))
    j_x, j_z = swap_x(j_sum), swap_z1(j_sum)
    i_zx = swap_x(i_z)
    dx0, dx1 = seq_return[0](tied(dx[:ROWS], i_z)), seq_return[1](tied(dx[ROWS:], i_z))
    (outer_grad,) = placed(place_outer_kernel, "place_outer", info, tied([o_sum, o_z, o_x, o_zx], j_sum), [(D, D)])
    j_x, j_z, i_zx, dx0, dx1, outer_grad = tied((j_x, j_z, i_zx, dx0, dx1, outer_grad))
    j_zx = swap_x(j_z)
    input_grad = grad_first + wide(jnp.concatenate([dx0, dx1], axis=0))
    input_grad = unshuffle(input_grad.reshape(2, ROWS, D), zh)
    inner_grad, out_grad, grad_b1, grad_bo, grad_g1, grad_s1, grad_b2, grad_g2, grad_s2 = placed(
        place_inner_kernel, "place_inner", info, [i_sum, i_x, i_z, i_zx],
        [(192, 4 * D), (192, D), (D,)] + [(192,)] * 6, [(4, 16, D)],
    )
    q_grad, k_grad, v_grad, grad_bq, grad_bv = placed(
        place_joint_kernel, "place_joint", info, [j_sum, j_z, j_x, j_zx],
        [(192, D)] * 3 + [(192,)] * 2, [(2, 2, 8, 3 * HALF)],
    )
    return (
        outputs, input_grad, q_grad, grad_bq, k_grad, v_grad, grad_bv, out_grad, grad_bo,
        grad_g1, grad_s1, inner_grad, grad_b1, outer_grad, grad_b2, grad_g2, grad_s2,
    )


def solution(mesh):
    placed = (
        P("fsdp", "ctx", None),
        P("fsdp", "ctx", None),
        P("fsdp"),
        P("fsdp", None),
        P("fsdp"),
        P("fsdp", None),
        P("fsdp", None),
        P("fsdp"),
        P("fsdp", None),
        P("fsdp"),
        P("fsdp"),
        P("fsdp"),
        P("fsdp", None),
        P("fsdp"),
        P("fsdp", None),
        P("fsdp"),
        P("fsdp"),
        P("fsdp"),
    )
    fast = dict(mesh.shape) == {"ctx": 8, "fsdp": 4}
    return jax.shard_map(
        fast_body if fast else body,
        mesh=mesh,
        in_specs=placed,
        out_specs=(
            P("fsdp", "ctx", None),
            P("fsdp", "ctx", None),
            P("fsdp", None),
            P("fsdp"),
            P("fsdp", None),
            P("fsdp", None),
            P("fsdp"),
            P("fsdp", None),
            P("fsdp"),
            P("fsdp"),
            P("fsdp"),
            P("fsdp", None),
            P("fsdp"),
            P("fsdp", None),
            P("fsdp"),
            P("fsdp"),
            P("fsdp"),
        ),
        check_vma=False,
    )
```
